32 devices in a mesh: rep: 16 (over z, x, core), fsdp: 2 (over y).
Axes of the slice: x: 2, y: 2, z: 4, core: 2. Of those that a mesh axis runs over, the one named last changes fastest.
Arguments:
- tokens: bfloat16 [31520, 512], P(('rep', 'fsdp')), may hold values from -6 to 6
- cotangent: bfloat16 [31520, 512], P(('rep', 'fsdp')), may hold values from -6 to 6
- routes: int32 [31520, 2], P(('rep', 'fsdp')), may hold values from 0 to 31, all different within a row
- image_count: int32 [32], P(('rep', 'fsdp')), may hold values from 2 to 5, as said below
- capacity: int32 [32], P(('rep', 'fsdp')), may hold values from 40 to 80, as said below
- norm1_gain: bfloat16 [512], P('fsdp'), may hold values from 0.5 to 1.5
- norm1_bias: bfloat16 [512], P('fsdp'), may hold values from -1.25 to 1.25
- w_qkv: bfloat16 [512, 1536], P('fsdp'), may hold values from -0.25 to 0.25
- bias_q: bfloat16 [512], P('fsdp'), may hold values from -1.25 to 1.25
- bias_v: bfloat16 [512], P('fsdp'), may hold values from -1.25 to 1.25
- w_out: bfloat16 [512, 512], P('fsdp'), may hold values from -0.75 to 0.75
- bias_out: bfloat16 [512], P('fsdp'), may hold values from -0.625 to 0.625
- norm2_gain: bfloat16 [512], P('fsdp'), may hold values from 0.5 to 1.5
- norm2_bias: bfloat16 [512], P('fsdp'), may hold values from -1.25 to 1.25
- w_router: bfloat16 [512, 32], P('fsdp'), may hold values from -0.1875 to 0.1875
- expert_in: bfloat16 [32, 512, 2048], P('fsdp'), may hold values from -0.25 to 0.25
- expert_in_bias: bfloat16 [32, 2048], P('fsdp'), may hold values from -1.25 to 1.25
- expert_out: bfloat16 [32, 2048, 512], P('fsdp'), may hold values from -0.1875 to 0.1875
- expert_out_bias: bfloat16 [32, 512], P('fsdp'), may hold values from -0.625 to 0.625
Outputs:
- outputs: bfloat16 [31520, 512], P(('rep', 'fsdp'))
- grad_tokens: float32 [31520, 512], P(('rep', 'fsdp'))
- balance_loss: float32 [], replicated
- grad_norm1_gain: float32 [512], P('fsdp')
- grad_norm1_bias: float32 [512], P('fsdp')
- grad_w_qkv: float32 [512, 1536], P('fsdp')
- grad_bias_q: float32 [512], P('fsdp')
- grad_bias_v: float32 [512], P('fsdp')
- grad_w_out: float32 [512, 512], P('fsdp')
- grad_bias_out: float32 [512], P('fsdp')
- grad_norm2_gain: float32 [512], P('fsdp')
- grad_norm2_bias: float32 [512], P('fsdp')
- grad_w_router: float32 [512, 32], P('fsdp')
- grad_expert_in: float32 [32, 512, 2048], P('fsdp', None, 'rep')
- grad_expert_in_bias: float32 [32, 2048], P('fsdp', 'rep')
- grad_expert_out: float32 [32, 2048, 512], P('fsdp', 'rep')
- grad_expert_out_bias: float32 [32, 512], P('fsdp', 'rep')
The draws below stay inside these ranges and needn't reach their ends.
Inputs may be any that keep to these rules, and one draw needn't show every extreme that they name: `image_count`: every device holds at least one image; some device holds 5. `capacity`: some device may fill 80 slots of each expert.
All inputs are finite; a program needn't handle non-finite values.
Results may differ from the reference program's by a relative error of at most 0.015.
Values may be sent and summed in bfloat16 or wider, within the bound.
A program may use at most 384 MiB of HBM per device.

```python
import jax
import jax.numpy as jnp
from jax import lax

D = 512
HEADS = 8
HEAD_DIM = 64
FF = 2048
EXPERTS = 32
IMG_TOK = 197
IMG_DEV = 5
TOK_DEV = 985
TOKENS = 31520
CAP = 80
N_REP = 16
N_FSDP = 2
DEVICES = 32


def draw_image_count(key, part):
    counts = jax.random.randint(key, (DEVICES,), max(1, IMG_DEV // 2), IMG_DEV + 1)
    chosen = jax.random.randint(jax.random.fold_in(key, 7), (), 0, DEVICES)
    return jnp.where(jnp.arange(DEVICES) == chosen, IMG_DEV, counts).astype(jnp.int32)


def draw_capacity(key, part):
    limits = jax.random.randint(key, (DEVICES,), CAP // 2, CAP + 1)
    chosen = jax.random.randint(jax.random.fold_in(key, 11), (), 0, DEVICES)
    return jnp.where(jnp.arange(DEVICES) == chosen, CAP, limits).astype(jnp.int32)


def shard_levels(rng, extent, split, smallest, top_value):
    level, own = 1.0, jax.random.fold_in(rng, 6)
    for axis_at, shards_of in split:
        draws = jnp.exp(jax.random.uniform(jax.random.fold_in(own, axis_at), (shards_of,), jnp.float32, smallest / len(split), top_value / len(split)))
        level = level * jnp.repeat(draws, extent[axis_at] // shards_of).reshape([-1 if axis == axis_at else 1 for axis in range(len(extent))])
    return level


def different_ones(rng, rows, amount, top, lift):
    ranking = jax.random.permutation(jax.random.fold_in(rng, 1), amount)
    boost = ranking
    for power in range(3):
        boost = boost * boost // amount
    boost = boost * lift // amount
    tickets = jax.random.randint(jax.random.fold_in(rng, 2), (rows, amount), 0, 4096) + boost
    holders = jax.random.permutation(jax.random.fold_in(rng, 3), rows)[jnp.arange(amount) % rows]
    tickets = jnp.where(jnp.arange(rows)[:, None] == holders[None, :], 1 << 14, tickets)
    priority = tickets * amount + jnp.arange(amount)
    return lax.top_k(priority.astype(jnp.int32), top)[1].astype(jnp.int32)


def scatter_about(rng, dims, spread, reach, split=(), kind=jnp.bfloat16):
    values = jax.random.normal(rng, dims, jnp.float32) * spread
    if len(split) > 0:
        values = shard_levels(rng, dims, split, -0.22, 0.18) * values
    return jnp.clip(values, min=-reach, max=reach).astype(kind)


def setup_inputs(seed: int = 0) -> dict:
    key_of = jax.random.split(jax.random.key(seed), 20)
    tokens = scatter_about(key_of[0], (TOKENS, D), 1.0, 6.0, ((0, 32),))
    cotangent = scatter_about(key_of[1], (TOKENS, D), 1.0, 6.0, ((0, 32),))
    routes = different_ones(key_of[2], TOKENS, EXPERTS, 2, 512)
    image_count = draw_image_count(jax.random.fold_in(key_of[19], 71), 0)
    capacity = draw_capacity(jax.random.fold_in(key_of[19], 71), 0)
    norm1_gain = jnp.clip(1.0 + 0.1 * jax.random.normal(key_of[5], (D,), jnp.float32), 0.5, 1.5).astype(jnp.bfloat16)
    norm1_bias = scatter_about(key_of[6], (D,), 0.2, 1.25, ((0, 2),))
    w_qkv = scatter_about(key_of[7], (D, 3 * D), D ** -0.5, 0.25, ((0, 2),))
    bias_q = scatter_about(key_of[8], (D,), 0.2, 1.25, ((0, 2),))
    bias_v = scatter_about(key_of[9], (D,), 0.2, 1.25, ((0, 2),))
    w_out = scatter_about(key_of[10], (D, D), (D // 8) ** -0.5, 0.75, ((0, 2),))
    bias_out = scatter_about(key_of[11], (D,), 0.1, 0.625, ((0, 2),))
    norm2_gain = jnp.clip(1.0 + 0.1 * jax.random.normal(key_of[12], (D,), jnp.float32), 0.5, 1.5).astype(jnp.bfloat16)
    norm2_bias = scatter_about(key_of[13], (D,), 0.2, 1.25, ((0, 2),))
    w_router = scatter_about(key_of[14], (D, EXPERTS), (2 * D) ** -0.5, 0.1875, ((0, 2),))
    expert_in = scatter_about(key_of[15], (EXPERTS, D, FF), D ** -0.5, 0.25, ((0, 2),))
    expert_in_bias = scatter_about(key_of[16], (EXPERTS, FF), 0.2, 1.25, ((0, 2),))
    expert_out = scatter_about(key_of[17], (EXPERTS, FF, D), (FF // 2) ** -0.5, 0.1875, ((0, 2),))
    expert_out_bias = scatter_about(key_of[18], (EXPERTS, D), 0.1, 0.625, ((0, 2),))
    return dict(tokens=tokens, cotangent=cotangent, routes=routes, image_count=image_count, capacity=capacity, norm1_gain=norm1_gain, norm1_bias=norm1_bias, w_qkv=w_qkv, bias_q=bias_q, bias_v=bias_v, w_out=w_out, bias_out=bias_out, norm2_gain=norm2_gain, norm2_bias=norm2_bias, w_router=w_router, expert_in=expert_in, expert_in_bias=expert_in_bias, expert_out=expert_out, expert_out_bias=expert_out_bias)


@jax.custom_vjp
def low(v):
    return lax.optimization_barrier(v.astype(jnp.bfloat16)).astype(jnp.float32)

@jax.custom_vjp
def low_back(v):
    return v

def low_keep(v):
    return (low(v), None)

def low_pass(kept, grad):
    return (grad,)

def back_keep(v):
    return (v, None)

def back_low(kept, grad):
    return (low(grad),)
low.defvjp(low_keep, low_pass)
low_back.defvjp(back_keep, back_low)

def matmul(left, right):
    return jnp.dot(left, right, precision=lax.Precision.HIGHEST)

def norm_rows(values, norm_gain, offset):
    average = lax.optimization_barrier(jnp.mean(values, axis=-1, keepdims=True))
    centred = values - average
    variance = lax.optimization_barrier(jnp.mean(centred * centred, axis=-1, keepdims=True))
    return centred * lax.rsqrt(variance + 1e-06) * norm_gain + offset

def slot_table(choices, alive_mask, limit):
    pair_expert = jnp.concatenate([choices[:, 0], choices[:, 1]]).astype(jnp.int32)
    live_pairs = jnp.concatenate([alive_mask, alive_mask])
    expert_ids = jnp.arange(EXPERTS, dtype=jnp.int32)
    onehot = ((pair_expert[:, None] == expert_ids[None, :]) & live_pairs[:, None]).astype(jnp.int32)
    before = jnp.cumsum(onehot, axis=0) - onehot
    position = lax.optimization_barrier(jnp.sum(before * onehot, axis=1)).astype(jnp.int32)
    kept_pairs = live_pairs & (position < limit)
    pair_slot = (pair_expert * CAP + position).astype(jnp.int32)
    pair_token = jnp.concatenate([jnp.arange(TOK_DEV, dtype=jnp.int32), jnp.arange(TOK_DEV, dtype=jnp.int32)])
    slot_owner = jnp.full((EXPERTS * CAP,), TOK_DEV, jnp.int32)
    target = jnp.where(kept_pairs, pair_slot, EXPERTS * CAP).astype(jnp.int32)
    slot_owner = slot_owner.at[target].set(pair_token, mode='drop')
    safe_slot = jnp.where(kept_pairs, pair_slot, 0).astype(jnp.int32)
    return (slot_owner, kept_pairs, safe_slot)

def reference(tokens, cotangent, routes, image_count, capacity, norm1_gain, norm1_bias, w_qkv, bias_q, bias_v, w_out, bias_out, norm2_gain, norm2_bias, w_router, expert_in, expert_in_bias, expert_out, expert_out_bias):
    device_count = N_REP * N_FSDP
    score_scale = HEAD_DIM ** (-0.5)
    image_rows = jnp.arange(TOK_DEV, dtype=jnp.int32) // IMG_TOK
    alive_mask = image_rows[None, :] < image_count[:, None]
    route_blocks = routes.reshape(device_count, TOK_DEV, 2)
    slot_owner, kept_pairs, safe_slot = jax.vmap(slot_table)(route_blocks, alive_mask, capacity)
    alive_float = alive_mask.astype(jnp.float32)
    expert_ids = jnp.arange(EXPERTS, dtype=jnp.int32)
    first_hot = (route_blocks[:, :, 0:1] == expert_ids[None, None, :]).astype(jnp.float32)
    second_hot = (route_blocks[:, :, 1:2] == expert_ids[None, None, :]).astype(jnp.float32)
    load_counts = lax.optimization_barrier(jnp.sum((first_hot + second_hot) * alive_float[:, :, None], axis=(0, 1)))
    live_total = jnp.sum(alive_float)
    share = load_counts / (2.0 * live_total)
    same_image = image_rows[:, None] == image_rows[None, :]

    def forward(inputs, params):
        gain_one, shift_one, qkv_full, query_bias, value_bias, out_full, out_bias, gain_two, shift_two, router_full, in_weight, in_bias, out_weight, out_bias_expert = params
        bias_row = jnp.concatenate([query_bias, jnp.zeros_like(query_bias), value_bias])

        def front(block_rows):
            normed = low(norm_rows(block_rows, gain_one, shift_one))
            packed = low(low_back(matmul(normed, qkv_full) + bias_row))
            queries = packed[:, :D].reshape(TOK_DEV, HEADS, HEAD_DIM)
            all_keys = packed[:, D:2 * D].reshape(TOK_DEV, HEADS, HEAD_DIM)
            valued = packed[:, 2 * D:].reshape(TOK_DEV, HEADS, HEAD_DIM)
            scores = jnp.einsum('qhd,khd->hqk', queries, all_keys, precision=lax.Precision.HIGHEST) * score_scale
            scores = low_back(scores)
            scores = jnp.where(same_image[None], scores, -1e+30)
            row_peak = lax.optimization_barrier(jnp.max(scores, axis=-1, keepdims=True))
            exp_scores = jnp.exp(scores - row_peak)
            attn_weights = low(exp_scores / lax.optimization_barrier(jnp.sum(exp_scores, axis=-1, keepdims=True)))
            mixed_rows = jnp.einsum('hqk,khd->qhd', attn_weights, valued, precision=lax.Precision.HIGHEST).reshape(TOK_DEV, D)
            mixed_rows = low(low_back(mixed_rows))
            attended = low_back(matmul(mixed_rows, out_full) + out_bias)
            middle = block_rows + attended
            second = low(norm_rows(middle, gain_two, shift_two))
            logits = low_back(matmul(second, router_full))
            return (middle, second, jax.nn.softmax(logits, axis=-1))
        blocks = inputs.reshape(device_count, TOK_DEV, D)
        middle, second, router_probs = lax.map(jax.checkpoint(front), blocks)
        padded = jnp.concatenate([second, jnp.zeros((device_count, 1, D), jnp.float32)], axis=1)

        def take_rows(rows_in, picks):
            return rows_in[picks]
        slots = jax.vmap(take_rows)(padded, slot_owner)
        slots = slots.reshape(device_count, EXPERTS, CAP, D).transpose(1, 0, 2, 3).reshape(EXPERTS, device_count * CAP, D)
        slots = low_back(slots)

        def expert_block(bundle):
            rows_in, first_w, first_b, second_w, second_b = bundle
            raised = low_back(matmul(rows_in, first_w) + first_b)
            active = low(jax.nn.gelu(raised))
            return low(low_back(matmul(active, second_w) + second_b))
        produced = lax.map(jax.checkpoint(expert_block), (slots, in_weight, in_bias, out_weight, out_bias_expert))
        produced = produced.reshape(EXPERTS, device_count, CAP, D).transpose(1, 0, 2, 3).reshape(device_count, EXPERTS * CAP, D)
        pair_rows = jax.vmap(take_rows)(produced, safe_slot)
        pick_one = lax.optimization_barrier(jnp.sum(router_probs * first_hot, axis=-1))
        pick_two = lax.optimization_barrier(jnp.sum(router_probs * second_hot, axis=-1))
        pick_total = pick_one + pick_two
        pair_weight = jnp.concatenate([pick_one / pick_total, pick_two / pick_total], axis=1) * kept_pairs.astype(jnp.float32)
        expert_sum = lax.optimization_barrier(jnp.sum((pair_rows * pair_weight[:, :, None]).reshape(device_count, 2, TOK_DEV, D), axis=1))
        result = alive_float[:, :, None] * (middle + expert_sum)
        prob_total = lax.optimization_barrier(jnp.sum(router_probs * alive_float[:, :, None], axis=(0, 1)))
        loss = EXPERTS * jnp.sum(share * prob_total / live_total)
        return (result.reshape(device_count * TOK_DEV, D), loss)
    params = tuple((member.astype(jnp.float32) for member in (norm1_gain, norm1_bias, w_qkv, bias_q, bias_v, w_out, bias_out, norm2_gain, norm2_bias, w_router, expert_in, expert_in_bias, expert_out, expert_out_bias)))
    inputs = tokens.astype(jnp.float32)
    (result, loss), back_fn = jax.vjp(forward, inputs, params)
    grad_inputs, grad_params = back_fn((cotangent.astype(jnp.float32), jnp.ones((), jnp.float32)))
    return (result.astype(jnp.bfloat16), grad_inputs, loss) + tuple(grad_params)
```

```python
import functools

import jax
import jax.numpy as jnp
from jax import lax
from jax.experimental import pallas as pl
from jax.experimental.pallas import tpu as pltpu
from jax.sharding import PartitionSpec as P

HEADS = 8
HEAD_DIM = 64
EXPERTS = 32
IMG_TOK = 197
CAP = 80


def norm_rows(values, norm_gain, offset):
    average = jnp.mean(values, axis=-1, keepdims=True)
    centred = values - average
    variance = jnp.mean(centred * centred, axis=-1, keepdims=True)
    return centred * lax.rsqrt(variance + 1e-06) * norm_gain + offset


def slot_table(choices, alive_mask, limit, row_total):
    pair_expert = jnp.concatenate([choices[:, 0], choices[:, 1]])
    live_pairs = jnp.concatenate([alive_mask, alive_mask])
    expert_ids = jnp.arange(EXPERTS, dtype=jnp.int32)
    onehot = ((pair_expert[:, None] == expert_ids[None, :]) & live_pairs[:, None]).astype(jnp.int32)
    before = jnp.cumsum(onehot, axis=0) - onehot
    position = jnp.sum(before * onehot, axis=1)
    kept_pairs = live_pairs & (position < limit)
    pair_slot = pair_expert * CAP + position
    pair_token = jnp.concatenate(
        [jnp.arange(row_total, dtype=jnp.int32), jnp.arange(row_total, dtype=jnp.int32)]
    )
    slot_owner = jnp.full((EXPERTS * CAP,), row_total, jnp.int32)
    target = jnp.where(kept_pairs, pair_slot, EXPERTS * CAP)
    slot_owner = slot_owner.at[target].set(pair_token, mode="drop")
    safe_slot = jnp.where(kept_pairs, pair_slot, 0)
    return (slot_owner, kept_pairs, safe_slot, target, onehot, pair_slot)


def expert_grads_by_sum(received, grad_raised_low, active_low, grad_received):
    local_in = jnp.einsum(
        "esd,esf->edf", received, grad_raised_low, preferred_element_type=jnp.float32
    )
    local_in_bias = jnp.sum(grad_raised_low.astype(jnp.float32), axis=1)
    local_out = jnp.einsum(
        "esf,esd->efd", active_low, grad_received, preferred_element_type=jnp.float32
    )
    local_out_bias = jnp.sum(grad_received.astype(jnp.float32), axis=1)
    grad_in_weight, grad_in_bias, grad_out_weight, grad_out_expert_bias = (
        lax.psum_scatter(local_in, "rep", scatter_dimension=2, tiled=True),
        lax.psum_scatter(local_in_bias, "rep", scatter_dimension=1, tiled=True),
        lax.psum_scatter(local_out, "rep", scatter_dimension=1, tiled=True),
        lax.psum_scatter(local_out_bias, "rep", scatter_dimension=1, tiled=True),
    )
    return grad_in_weight, grad_in_bias, grad_out_weight, grad_out_expert_bias


def expert_grads_by_slice(
    rows, cots, kept_pairs, pair_slot, slot_gate, first, first_bias, second
):
    axes = ("rep", "fsdp")
    device = lax.axis_index("rep")
    core = device % 2
    local = first.shape[0]
    total, width = rows.shape
    groups = [[i for i in range(32) if (i >> 1) % 2 == c] for c in (0, 1)]
    pad = -total % 16

    def spread(value):
        return lax.all_gather(value, axes, axis=0, tiled=False, axis_index_groups=groups)

    ids = jnp.where(kept_pairs, pair_slot, -1).reshape(2, total)
    ids_all = spread(jnp.pad(ids, ((0, 0), (0, pad)), constant_values=-1))
    cots_all = spread(jnp.pad(cots, ((0, pad), (0, 0))))
    rows_all = spread(jnp.pad(rows, ((0, pad), (0, 0))))
    gates_all = spread(slot_gate.reshape(2, local, CAP))
    mine = lax.axis_index("fsdp")
    gates_mine = lax.dynamic_index_in_dim(gates_all, mine, axis=1, keepdims=False)
    gates_mine = gates_mine.transpose(1, 0, 2).reshape(local, 1, -1)
    base = (mine * (local * CAP)).reshape(1)
    row_slots = gather_slots(base, rows_all, ids_all, local, CAP)
    cot_slots = gather_slots(base, cots_all, ids_all, local, CAP)
    where = jnp.stack([device // 2, core]).astype(jnp.int32)
    keep_in, send_in, keep_out, send_out, d_bias, d_out_bias = slice_grads(
        where, row_slots, cot_slots, gates_mine, first, first_bias, second
    )
    swap = [(i, i ^ 1) for i in range(16)]
    got_in, got_out, got_bias, got_out_bias = (
        lax.ppermute(v, "rep", swap) for v in (send_in, send_out, d_bias, d_out_bias)
    )
    bias = (d_bias + got_bias)[:, 0]
    out_bias = (d_out_bias + got_out_bias)[:, 0]
    half = bias.shape[1] // 2
    piece = width // 16
    return (
        keep_in + got_in.astype(jnp.float32),
        lax.dynamic_slice_in_dim(bias, core * half, half, axis=1),
        keep_out + got_out.astype(jnp.float32),
        lax.dynamic_slice_in_dim(out_bias, device * piece, piece, axis=1),
    )


def gather_body(base_ref, rows_ref, ids_ref, out_ref):
    experts, _, cap, width = out_ref.shape
    slots = experts * cap
    tokens = rows_ref.shape[1]
    slot = lax.broadcasted_iota(jnp.int32, (slots, tokens), 0) + base_ref[0]
    ids = ids_ref[0]
    hit = (slot == ids[0:1, :]) | (slot == ids[1:2, :])
    pick = jnp.where(hit, 1.0, 0.0).astype(jnp.bfloat16)
    got = jnp.dot(pick, rows_ref[0], preferred_element_type=jnp.float32)
    out_ref[...] = got.astype(jnp.bfloat16).reshape(experts, 1, cap, width)


def gather_slots(base, rows, ids, experts, cap):
    senders, tokens, width = rows.shape
    return pl.pallas_call(
        gather_body,
        grid_spec=pltpu.PrefetchScalarGridSpec(
            num_scalar_prefetch=1,
            grid=(senders,),
            in_specs=[
                pl.BlockSpec((1, tokens, width), lambda d, b: (d, 0, 0)),
                pl.BlockSpec((1, 2, tokens), lambda d, b: (d, 0, 0)),
            ],
            out_specs=pl.BlockSpec((experts, 1, cap, width), lambda d, b: (0, d, 0, 0)),
        ),
        out_shape=jax.ShapeDtypeStruct((experts, senders, cap, width), jnp.bfloat16),
        cost_estimate=pl.CostEstimate(
            flops=2 * senders * experts * cap * tokens * width,
            bytes_accessed=2 * senders * (tokens + experts * cap) * width,
            transcendentals=0,
        ),
        name="gather_slots",
    )(base, rows, ids)


def gelu_pair(value):
    root = 0.7978845608028654
    square = value * value
    bend = jnp.tanh(root * value * (1.0 + 0.044715 * square))
    half = 0.5 * (1.0 + bend)
    slope = half + 0.5 * value * (1.0 - bend * bend) * root * (1.0 + 3 * 0.044715 * square)
    return value * half, slope


def slice_grads_body(
    where_ref, row_ref, cot_ref, gate_ref, in_ref, in_bias_ref, out_ref, keep_in, send_in, keep_out, send_out, d_bias, d_out_bias
):
    core = where_ref[1]
    width = row_ref.shape[-1]
    rows = row_ref[...].reshape(-1, width)
    gate = jnp.transpose(jnp.broadcast_to(gate_ref[0], (8, rows.shape[0])))[:, 0:1]
    grads = (cot_ref[...].reshape(-1, width).astype(jnp.float32) * gate).astype(jnp.bfloat16)
    first = in_ref[0]
    second = out_ref[0]
    raised = jnp.dot(rows, first, preferred_element_type=jnp.float32) + in_bias_ref[0].astype(
        jnp.float32
    )
    active, slope = gelu_pair(raised)
    active = active.astype(jnp.bfloat16)
    back = lax.dot_general(
        grads, second, (((1,), (1,)), ((), ())), preferred_element_type=jnp.float32
    )
    draised = (back * slope).astype(jnp.bfloat16)
    over_rows = (((0,), (0,)), ((), ()))
    g_in = lax.dot_general(rows, draised, over_rows, preferred_element_type=jnp.float32)
    g_out = lax.dot_general(active, grads, over_rows, preferred_element_type=jnp.float32)
    half = g_in.shape[1] // 2
    first_core = core == 0
    keep_in[0] = jnp.where(first_core, g_in[:, :half], g_in[:, half:])
    send_in[0] = jnp.where(first_core, g_in[:, half:], g_in[:, :half]).astype(jnp.bfloat16)
    keep_out[0] = jnp.where(first_core, g_out[:half], g_out[half:])
    send_out[0] = jnp.where(first_core, g_out[half:], g_out[:half]).astype(jnp.bfloat16)
    d_bias[0] = jnp.sum(draised.astype(jnp.float32), axis=0, keepdims=True)
    d_out_bias[0] = jnp.sum(grads.astype(jnp.float32), axis=0, keepdims=True)


def slice_grads(where, rows, cots, gates, first, first_bias, second):
    experts, senders, cap, width = rows.shape
    hidden = first.shape[2]
    part = 256
    half = part // 2
    f32 = jnp.float32
    return pl.pallas_call(
        slice_grads_body,
        grid_spec=pltpu.PrefetchScalarGridSpec(
            num_scalar_prefetch=1,
            grid=(experts,),
            in_specs=[
                pl.BlockSpec((1, senders, cap, width), lambda e, w: (e, 0, 0, 0)),
                pl.BlockSpec((1, senders, cap, width), lambda e, w: (e, 0, 0, 0)),
                pl.BlockSpec((1, 1, senders * cap), lambda e, w: (e, 0, 0)),
                pl.BlockSpec((1, width, part), lambda e, w: (e, 0, w[0])),
                pl.BlockSpec((1, 1, part), lambda e, w: (e, 0, w[0])),
                pl.BlockSpec((1, part, width), lambda e, w: (e, w[0], 0)),
            ],
            out_specs=[
                pl.BlockSpec((1, width, half), lambda e, w: (e, 0, 0)),
                pl.BlockSpec((1, width, half), lambda e, w: (e, 0, 0)),
                pl.BlockSpec((1, half, width), lambda e, w: (e, 0, 0)),
                pl.BlockSpec((1, half, width), lambda e, w: (e, 0, 0)),
                pl.BlockSpec((1, 1, part), lambda e, w: (e, 0, 0)),
                pl.BlockSpec((1, 1, width), lambda e, w: (e, 0, 0)),
            ],
        ),
        out_shape=[
            jax.ShapeDtypeStruct((experts, width, half), f32),
            jax.ShapeDtypeStruct((experts, width, half), jnp.bfloat16),
            jax.ShapeDtypeStruct((experts, half, width), f32),
            jax.ShapeDtypeStruct((experts, half, width), jnp.bfloat16),
            jax.ShapeDtypeStruct((experts, 1, part), f32),
            jax.ShapeDtypeStruct((experts, 1, width), f32),
        ],
        cost_estimate=pl.CostEstimate(
            flops=8 * experts * senders * cap * width * part,
            bytes_accessed=4 * experts * (senders * cap * width + 3 * width * part),
            transcendentals=experts * senders * cap * part,
        ),
        name="slice_grads",
    )(where, rows, cots, gates, first, first_bias.reshape(experts, 1, hidden), second)


def shards(
    fast,
    tokens,
    cotangent,
    routes,
    image_count,
    capacity,
    norm1_gain,
    norm1_bias,
    w_qkv,
    bias_q,
    bias_v,
    w_out,
    bias_out,
    norm2_gain,
    norm2_bias,
    w_router,
    expert_in,
    expert_in_bias,
    expert_out,
    expert_out_bias,
):
    rows_count = tokens.shape[0]
    model_width = tokens.shape[1]
    image_total = rows_count // IMG_TOK
    score_scale = HEAD_DIM ** (-0.5)
    image_rows = jnp.arange(rows_count, dtype=jnp.int32) // IMG_TOK
    alive_mask = image_rows < image_count[0]
    alive_float = alive_mask.astype(jnp.float32)[:, None]
    slot_owner, kept_pairs, safe_slot, target, onehot, pair_slot = slot_table(
        routes, alive_mask, capacity[0], rows_count
    )
    kept_float = kept_pairs.astype(jnp.float32)
    load_local = jnp.sum(onehot.astype(jnp.float32), axis=0)
    live_local = jnp.sum(alive_float)
    load_total, live_total = lax.psum((load_local, live_local), ("rep", "fsdp"))
    gathered = (
        lax.all_gather(norm1_gain, "fsdp", axis=0, tiled=True),
        lax.all_gather(norm1_bias, "fsdp", axis=0, tiled=True),
        lax.all_gather(w_qkv, "fsdp", axis=0, tiled=True),
        lax.all_gather(bias_q, "fsdp", axis=0, tiled=True),
        lax.all_gather(bias_v, "fsdp", axis=0, tiled=True),
        lax.all_gather(w_out, "fsdp", axis=0, tiled=True),
        lax.all_gather(bias_out, "fsdp", axis=0, tiled=True),
        lax.all_gather(norm2_gain, "fsdp", axis=0, tiled=True),
        lax.all_gather(norm2_bias, "fsdp", axis=0, tiled=True),
        lax.all_gather(w_router, "fsdp", axis=0, tiled=True),
    )
    (
        gain_one,
        shift_one,
        qkv_full,
        query_bias,
        value_bias,
        out_full,
        out_bias,
        gain_two,
        shift_two,
        router_full,
    ) = gathered
    gain_one = gain_one.astype(jnp.float32)
    shift_one = shift_one.astype(jnp.float32)
    gain_two = gain_two.astype(jnp.float32)
    shift_two = shift_two.astype(jnp.float32)
    inputs = tokens.astype(jnp.float32)
    normed = norm_rows(inputs, gain_one, shift_one)
    normed_low = normed.astype(jnp.bfloat16)
    bias_row = jnp.concatenate([query_bias, jnp.zeros_like(query_bias), value_bias]).astype(
        jnp.float32
    )
    packed_low = (
        jnp.dot(normed_low, qkv_full, preferred_element_type=jnp.float32) + bias_row
    ).astype(jnp.bfloat16)
    image_shape = (image_total, IMG_TOK, HEADS, HEAD_DIM)
    queries = packed_low[:, :model_width].reshape(image_shape)
    all_keys = packed_low[:, model_width : 2 * model_width].reshape(image_shape)
    valued = packed_low[:, 2 * model_width :].reshape(image_shape)

    def score_block():
        return (
            jnp.einsum("iqhd,ikhd->hiqk", queries, all_keys, preferred_element_type=jnp.float32)
            * score_scale
        )

    scores = score_block()
    row_peak = jnp.max(scores, axis=-1, keepdims=True)
    exp_scores = jnp.exp(scores - row_peak)
    totals = jnp.sum(exp_scores, axis=-1, keepdims=True)
    log_total = row_peak + jnp.log(totals)
    attn_low = (exp_scores / totals).astype(jnp.bfloat16)
    mixed_low = (
        jnp.einsum("hiqk,ikhd->iqhd", attn_low, valued, preferred_element_type=jnp.float32)
        .reshape(rows_count, model_width)
        .astype(jnp.bfloat16)
    )
    middle = (
        inputs
        + jnp.dot(mixed_low, out_full, preferred_element_type=jnp.float32)
        + out_bias.astype(jnp.float32)
    )
    second_low = norm_rows(middle, gain_two, shift_two).astype(jnp.bfloat16)
    logits = jnp.dot(second_low, router_full, preferred_element_type=jnp.float32)
    expert_ids = jnp.arange(EXPERTS, dtype=jnp.int32)
    first_hot = (routes[:, 0:1] == expert_ids[None, :]).astype(jnp.float32)
    second_hot = (routes[:, 1:2] == expert_ids[None, :]).astype(jnp.float32)

    def gate_terms(logit_rows):
        router_probs = jax.nn.softmax(logit_rows, axis=-1)
        pick_one = jnp.sum(router_probs * first_hot, axis=-1)
        pick_two = jnp.sum(router_probs * second_hot, axis=-1)
        pick_total = pick_one + pick_two
        return (pick_one / pick_total, pick_two / pick_total, router_probs)

    (gate_first, gate_second, router_probs), gate_back = jax.vjp(gate_terms, logits)
    padded_rows = jnp.concatenate([second_low, jnp.zeros((1, model_width), jnp.bfloat16)], axis=0)
    sent_rows = padded_rows[slot_owner].reshape(EXPERTS, CAP, model_width)
    received = lax.all_to_all(sent_rows, "fsdp", split_axis=0, concat_axis=1, tiled=True)
    raised = (
        jnp.einsum("esd,edf->esf", received, expert_in, preferred_element_type=jnp.float32)
        + expert_in_bias.astype(jnp.float32)[:, None, :]
    )
    active, gelu_back = jax.vjp(jax.nn.gelu, raised)
    active_low = active.astype(jnp.bfloat16)
    produced = (
        jnp.einsum("esf,efd->esd", active_low, expert_out, preferred_element_type=jnp.float32)
        + expert_out_bias.astype(jnp.float32)[:, None, :]
    ).astype(jnp.bfloat16)
    returned = lax.all_to_all(produced, "fsdp", split_axis=1, concat_axis=0, tiled=True).reshape(
        EXPERTS * CAP, model_width
    )
    pair_rows = returned[safe_slot].astype(jnp.float32)
    pair_weight = jnp.concatenate([gate_first, gate_second]) * kept_float
    expert_sum = jnp.sum(
        (pair_rows * pair_weight[:, None]).reshape(2, rows_count, model_width), axis=0
    )
    outputs = (alive_float * (middle + expert_sum)).astype(jnp.bfloat16)
    upstream = cotangent.astype(jnp.float32) * alive_float
    pair_grad = jnp.concatenate([upstream, upstream], axis=0)
    gate_grads = jnp.sum(pair_grad * pair_rows, axis=1) * kept_float
    slot_gate = jnp.zeros((EXPERTS * CAP,), jnp.float32).at[target].set(pair_weight, mode="drop")
    padded_grad = jnp.concatenate([upstream, jnp.zeros((1, model_width), jnp.float32)], axis=0)
    slot_grads = (
        (padded_grad[slot_owner] * slot_gate[:, None])
        .astype(jnp.bfloat16)
        .reshape(EXPERTS, CAP, model_width)
    )
    grad_received = lax.all_to_all(slot_grads, "fsdp", split_axis=0, concat_axis=1, tiled=True)
    grad_active = jnp.einsum(
        "esd,efd->esf", grad_received, expert_out, preferred_element_type=jnp.float32
    )
    (grad_raised,) = gelu_back(grad_active)
    grad_raised_low = grad_raised.astype(jnp.bfloat16)
    grad_rows = jnp.einsum(
        "esf,edf->esd", grad_raised_low, expert_in, preferred_element_type=jnp.float32
    ).astype(jnp.bfloat16)
    back_rows = lax.all_to_all(grad_rows, "fsdp", split_axis=1, concat_axis=0, tiled=True).reshape(
        EXPERTS * CAP, model_width
    )
    expert_part = jnp.sum(
        (back_rows[safe_slot].astype(jnp.float32) * kept_float[:, None]).reshape(
            2, rows_count, model_width
        ),
        axis=0,
    )
    if fast:
        grad_in_weight, grad_in_bias, grad_out_weight, grad_out_expert_bias = expert_grads_by_slice(
            second_low, cotangent, kept_pairs, pair_slot, slot_gate, expert_in, expert_in_bias, expert_out
        )
    else:
        grad_in_weight, grad_in_bias, grad_out_weight, grad_out_expert_bias = expert_grads_by_sum(
            received, grad_raised_low, active_low, grad_received
        )
    prob_local = jnp.sum(router_probs * alive_float, axis=0)
    prob_total = lax.psum(prob_local, ("rep", "fsdp"))
    share = load_total / (2.0 * live_total)
    balance_loss = EXPERTS * jnp.sum(share * prob_total / live_total)
    aux_grad = alive_float * (EXPERTS * share / live_total)[None, :]
    (grad_logits,) = gate_back((gate_grads[:rows_count], gate_grads[rows_count:], aux_grad))
    grad_logits_low = grad_logits.astype(jnp.bfloat16)
    grad_router = jnp.dot(second_low.T, grad_logits_low, preferred_element_type=jnp.float32)
    grad_second = (
        jnp.dot(grad_logits_low, router_full.T, preferred_element_type=jnp.float32) + expert_part
    )
    _, norm_two_back = jax.vjp(norm_rows, middle, gain_two, shift_two)
    grad_mid_norm, grad_gain_two, grad_shift_two = norm_two_back(grad_second)
    grad_middle = upstream + grad_mid_norm
    grad_att_low = grad_middle.astype(jnp.bfloat16)
    grad_out_proj = jnp.dot(mixed_low.T, grad_att_low, preferred_element_type=jnp.float32)
    grad_out_bias = jnp.sum(grad_att_low.astype(jnp.float32), axis=0)
    grad_mixed = (
        jnp.dot(grad_att_low, out_full.T, preferred_element_type=jnp.float32)
        .astype(jnp.bfloat16)
        .reshape(image_shape)
    )
    recomputed = jnp.exp(score_block() - log_total)
    grad_weights = jnp.einsum(
        "iqhd,ikhd->hiqk", grad_mixed, valued, preferred_element_type=jnp.float32
    )
    grad_values = jnp.einsum(
        "hiqk,iqhd->ikhd",
        recomputed.astype(jnp.bfloat16),
        grad_mixed,
        preferred_element_type=jnp.float32,
    )
    inner_sum = jnp.sum(grad_weights * recomputed, axis=-1, keepdims=True)
    grad_scores = (recomputed * (grad_weights - inner_sum)).astype(jnp.bfloat16)
    grad_queries = (
        jnp.einsum("hiqk,ikhd->iqhd", grad_scores, all_keys, preferred_element_type=jnp.float32)
        * score_scale
    )
    grad_keys = (
        jnp.einsum("hiqk,iqhd->ikhd", grad_scores, queries, preferred_element_type=jnp.float32)
        * score_scale
    )
    grad_packed_low = jnp.concatenate(
        [
            grad_queries.reshape(rows_count, model_width),
            grad_keys.reshape(rows_count, model_width),
            grad_values.reshape(rows_count, model_width),
        ],
        axis=1,
    ).astype(jnp.bfloat16)
    grad_qkv = jnp.dot(normed_low.T, grad_packed_low, preferred_element_type=jnp.float32)
    packed_sums = jnp.sum(grad_packed_low.astype(jnp.float32), axis=0)
    grad_query_bias = packed_sums[:model_width]
    grad_value_bias = packed_sums[2 * model_width :]
    grad_normed = jnp.dot(grad_packed_low, qkv_full.T, preferred_element_type=jnp.float32)
    _, norm_one_back = jax.vjp(norm_rows, inputs, gain_one, shift_one)
    grad_input_norm, grad_gain_one, grad_shift_one = norm_one_back(grad_normed)
    grad_tokens = grad_middle + grad_input_norm
    local_grads = (
        grad_gain_one,
        grad_shift_one,
        grad_qkv,
        grad_query_bias,
        grad_value_bias,
        grad_out_proj,
        grad_out_bias,
        grad_gain_two,
        grad_shift_two,
        grad_router,
    )
    shares = (
        lax.psum_scatter(local_grads[0], "fsdp", scatter_dimension=0, tiled=True),
        lax.psum_scatter(local_grads[1], "fsdp", scatter_dimension=0, tiled=True),
        lax.psum_scatter(local_grads[2], "fsdp", scatter_dimension=0, tiled=True),
        lax.psum_scatter(local_grads[3], "fsdp", scatter_dimension=0, tiled=True),
        lax.psum_scatter(local_grads[4], "fsdp", scatter_dimension=0, tiled=True),
        lax.psum_scatter(local_grads[5], "fsdp", scatter_dimension=0, tiled=True),
        lax.psum_scatter(local_grads[6], "fsdp", scatter_dimension=0, tiled=True),
        lax.psum_scatter(local_grads[7], "fsdp", scatter_dimension=0, tiled=True),
        lax.psum_scatter(local_grads[8], "fsdp", scatter_dimension=0, tiled=True),
        lax.psum_scatter(local_grads[9], "fsdp", scatter_dimension=0, tiled=True),
    )
    owned = lax.psum(
        (
            shares[0],
            shares[1],
            shares[2],
            shares[3],
            shares[4],
            shares[5],
            shares[6],
            shares[7],
            shares[8],
            shares[9],
        ),
        "rep",
    )
    return (
        (outputs, grad_tokens, balance_loss)
        + tuple(owned)
        + (grad_in_weight, grad_in_bias, grad_out_weight, grad_out_expert_bias)
    )


def solution(mesh):
    in_specs = (
        P(("rep", "fsdp"), None),
        P(("rep", "fsdp"), None),
        P(("rep", "fsdp"), None),
        P(("rep", "fsdp")),
        P(("rep", "fsdp")),
        P("fsdp"),
        P("fsdp"),
        P("fsdp", None),
        P("fsdp"),
        P("fsdp"),
        P("fsdp", None),
        P("fsdp"),
        P("fsdp"),
        P("fsdp"),
        P("fsdp", None),
        P("fsdp", None, None),
        P("fsdp", None),
        P("fsdp", None, None),
        P("fsdp", None),
    )
    out_specs = (
        P(("rep", "fsdp"), None),
        P(("rep", "fsdp"), None),
        P(),
        P("fsdp"),
        P("fsdp"),
        P("fsdp", None),
        P("fsdp"),
        P("fsdp"),
        P("fsdp", None),
        P("fsdp"),
        P("fsdp"),
        P("fsdp"),
        P("fsdp", None),
        P("fsdp", None, "rep"),
        P("fsdp", "rep"),
        P("fsdp", "rep", None),
        P("fsdp", "rep"),
    )
    fast = mesh.shape["rep"] == 16 and mesh.shape["fsdp"] == 2
    return jax.shard_map(functools.partial(shards, fast), mesh=mesh, in_specs=in_specs, out_specs=out_specs, check_vma=False)
```

```python
import jax
import jax.numpy as jnp
from jax import lax
from jax.experimental import pallas as pl
from jax.experimental.pallas import tpu as pltpu
from jax.sharding import PartitionSpec as P

HEADS = 8
HEAD_DIM = 64
EXPERTS = 32
IMG_TOK = 197
CAP = 80


def norm_rows(values, norm_gain, offset):
    average = jnp.mean(values, axis=-1, keepdims=True)
    centred = values - average
    variance = jnp.mean(centred * centred, axis=-1, keepdims=True)
    return centred * lax.rsqrt(variance + 1e-06) * norm_gain + offset


def slot_table(choices, alive_mask, limit, row_total):
    pair_expert = jnp.concatenate([choices[:, 0], choices[:, 1]])
    live_pairs = jnp.concatenate([alive_mask, alive_mask])
    expert_ids = jnp.arange(EXPERTS, dtype=jnp.int32)
    onehot = ((pair_expert[:, None] == expert_ids[None, :]) & live_pairs[:, None]).astype(jnp.int32)
    before = jnp.cumsum(onehot, axis=0) - onehot
    position = jnp.sum(before * onehot, axis=1)
    kept_pairs = live_pairs & (position < limit)
    pair_slot = pair_expert * CAP + position
    pair_token = jnp.concatenate(
        [jnp.arange(row_total, dtype=jnp.int32), jnp.arange(row_total, dtype=jnp.int32)]
    )
    slot_owner = jnp.full((EXPERTS * CAP,), row_total, jnp.int32)
    target = jnp.where(kept_pairs, pair_slot, EXPERTS * CAP)
    slot_owner = slot_owner.at[target].set(pair_token, mode="drop")
    safe_slot = jnp.where(kept_pairs, pair_slot, 0)
    return (slot_owner, kept_pairs, safe_slot, target, onehot)


def shards(
    tokens,
    cotangent,
    routes,
    image_count,
    capacity,
    norm1_gain,
    norm1_bias,
    w_qkv,
    bias_q,
    bias_v,
    w_out,
    bias_out,
    norm2_gain,
    norm2_bias,
    w_router,
    expert_in,
    expert_in_bias,
    expert_out,
    expert_out_bias,
):
    rows_count = tokens.shape[0]
    model_width = tokens.shape[1]
    image_total = rows_count // IMG_TOK
    score_scale = HEAD_DIM ** (-0.5)
    image_rows = jnp.arange(rows_count, dtype=jnp.int32) // IMG_TOK
    alive_mask = image_rows < image_count[0]
    alive_float = alive_mask.astype(jnp.float32)[:, None]
    slot_owner, kept_pairs, safe_slot, target, onehot = slot_table(
        routes, alive_mask, capacity[0], rows_count
    )
    kept_float = kept_pairs.astype(jnp.float32)
    load_local = jnp.sum(onehot.astype(jnp.float32), axis=0)
    live_local = jnp.sum(alive_float)
    load_total, live_total = lax.psum((load_local, live_local), ("rep", "fsdp"))
    gathered = (
        lax.all_gather(norm1_gain, "fsdp", axis=0, tiled=True),
        lax.all_gather(norm1_bias, "fsdp", axis=0, tiled=True),
        lax.all_gather(w_qkv, "fsdp", axis=0, tiled=True),
        lax.all_gather(bias_q, "fsdp", axis=0, tiled=True),
        lax.all_gather(bias_v, "fsdp", axis=0, tiled=True),
        lax.all_gather(w_out, "fsdp", axis=0, tiled=True),
        lax.all_gather(bias_out, "fsdp", axis=0, tiled=True),
        lax.all_gather(norm2_gain, "fsdp", axis=0, tiled=True),
        lax.all_gather(norm2_bias, "fsdp", axis=0, tiled=True),
        lax.all_gather(w_router, "fsdp", axis=0, tiled=True),
    )
    (
        gain_one,
        shift_one,
        qkv_full,
        query_bias,
        value_bias,
        out_full,
        out_bias,
        gain_two,
        shift_two,
        router_full,
    ) = gathered
    gain_one = gain_one.astype(jnp.float32)
    shift_one = shift_one.astype(jnp.float32)
    gain_two = gain_two.astype(jnp.float32)
    shift_two = shift_two.astype(jnp.float32)
    inputs = tokens.astype(jnp.float32)
    normed = norm_rows(inputs, gain_one, shift_one)
    normed_low = normed.astype(jnp.bfloat16)
    bias_row = jnp.concatenate([query_bias, jnp.zeros_like(query_bias), value_bias]).astype(
        jnp.float32
    )
    packed_low = (
        jnp.dot(normed_low, qkv_full, preferred_element_type=jnp.float32) + bias_row
    ).astype(jnp.bfloat16)
    image_shape = (image_total, IMG_TOK, HEADS, HEAD_DIM)
    queries = packed_low[:, :model_width].reshape(image_shape)
    all_keys = packed_low[:, model_width : 2 * model_width].reshape(image_shape)
    valued = packed_low[:, 2 * model_width :].reshape(image_shape)

    def score_block():
        return (
            jnp.einsum("iqhd,ikhd->hiqk", queries, all_keys, preferred_element_type=jnp.float32)
            * score_scale
        )

    scores = score_block()
    row_peak = jnp.max(scores, axis=-1, keepdims=True)
    exp_scores = jnp.exp(scores - row_peak)
    totals = jnp.sum(exp_scores, axis=-1, keepdims=True)
    log_total = row_peak + jnp.log(totals)
    attn_low = (exp_scores / totals).astype(jnp.bfloat16)
    mixed_low = (
        jnp.einsum("hiqk,ikhd->iqhd", attn_low, valued, preferred_element_type=jnp.float32)
        .reshape(rows_count, model_width)
        .astype(jnp.bfloat16)
    )
    middle = (
        inputs
        + jnp.dot(mixed_low, out_full, preferred_element_type=jnp.float32)
        + out_bias.astype(jnp.float32)
    )
    second_low = norm_rows(middle, gain_two, shift_two).astype(jnp.bfloat16)
    logits = jnp.dot(second_low, router_full, preferred_element_type=jnp.float32)
    expert_ids = jnp.arange(EXPERTS, dtype=jnp.int32)
    first_hot = (routes[:, 0:1] == expert_ids[None, :]).astype(jnp.float32)
    second_hot = (routes[:, 1:2] == expert_ids[None, :]).astype(jnp.float32)

    def gate_terms(logit_rows):
        router_probs = jax.nn.softmax(logit_rows, axis=-1)
        pick_one = jnp.sum(router_probs * first_hot, axis=-1)
        pick_two = jnp.sum(router_probs * second_hot, axis=-1)
        pick_total = pick_one + pick_two
        return (pick_one / pick_total, pick_two / pick_total, router_probs)

    (gate_first, gate_second, router_probs), gate_back = jax.vjp(gate_terms, logits)
    padded_rows = jnp.concatenate([second_low, jnp.zeros((1, model_width), jnp.bfloat16)], axis=0)
    sent_rows = padded_rows[slot_owner].reshape(EXPERTS, CAP, model_width)
    received = lax.all_to_all(sent_rows, "fsdp", split_axis=0, concat_axis=1, tiled=True)
    raised = (
        jnp.einsum("esd,edf->esf", received, expert_in, preferred_element_type=jnp.float32)
        + expert_in_bias.astype(jnp.float32)[:, None, :]
    )
    active, gelu_back = jax.vjp(jax.nn.gelu, raised)
    active_low = active.astype(jnp.bfloat16)
    produced = (
        jnp.einsum("esf,efd->esd", active_low, expert_out, preferred_element_type=jnp.float32)
        + expert_out_bias.astype(jnp.float32)[:, None, :]
    ).astype(jnp.bfloat16)
    returned = lax.all_to_all(produced, "fsdp", split_axis=1, concat_axis=0, tiled=True).reshape(
        EXPERTS * CAP, model_width
    )
    pair_rows = returned[safe_slot].astype(jnp.float32)
    pair_weight = jnp.concatenate([gate_first, gate_second]) * kept_float
    expert_sum = jnp.sum(
        (pair_rows * pair_weight[:, None]).reshape(2, rows_count, model_width), axis=0
    )
    outputs = (alive_float * (middle + expert_sum)).astype(jnp.bfloat16)
    upstream = cotangent.astype(jnp.float32) * alive_float
    pair_grad = jnp.concatenate([upstream, upstream], axis=0)
    gate_grads = jnp.sum(pair_grad * pair_rows, axis=1) * kept_float
    slot_gate = jnp.zeros((EXPERTS * CAP,), jnp.float32).at[target].set(pair_weight, mode="drop")
    padded_grad = jnp.concatenate([upstream, jnp.zeros((1, model_width), jnp.float32)], axis=0)
    slot_grads = (
        (padded_grad[slot_owner] * slot_gate[:, None])
        .astype(jnp.bfloat16)
        .reshape(EXPERTS, CAP, model_width)
    )
    grad_received = lax.all_to_all(slot_grads, "fsdp", split_axis=0, concat_axis=1, tiled=True)
    grad_active = jnp.einsum(
        "esd,efd->esf", grad_received, expert_out, preferred_element_type=jnp.float32
    )
    (grad_raised,) = gelu_back(grad_active)
    grad_raised_low = grad_raised.astype(jnp.bfloat16)
    grad_rows = jnp.einsum(
        "esf,edf->esd", grad_raised_low, expert_in, preferred_element_type=jnp.float32
    ).astype(jnp.bfloat16)
    back_rows = lax.all_to_all(grad_rows, "fsdp", split_axis=1, concat_axis=0, tiled=True).reshape(
        EXPERTS * CAP, model_width
    )
    expert_part = jnp.sum(
        (back_rows[safe_slot].astype(jnp.float32) * kept_float[:, None]).reshape(
            2, rows_count, model_width
        ),
        axis=0,
    )
    local_in = jnp.einsum(
        "esd,esf->edf", received, grad_raised_low, preferred_element_type=jnp.float32
    )
    local_in_bias = jnp.sum(grad_raised_low.astype(jnp.float32), axis=1)
    local_out = jnp.einsum(
        "esf,esd->efd", active_low, grad_received, preferred_element_type=jnp.float32
    )
    local_out_bias = jnp.sum(grad_received.astype(jnp.float32), axis=1)
    grad_in_weight, grad_in_bias, grad_out_weight, grad_out_expert_bias = (
        lax.psum_scatter(local_in, "rep", scatter_dimension=2, tiled=True),
        lax.psum_scatter(local_in_bias, "rep", scatter_dimension=1, tiled=True),
        lax.psum_scatter(local_out, "rep", scatter_dimension=1, tiled=True),
        lax.psum_scatter(local_out_bias, "rep", scatter_dimension=1, tiled=True),
    )
    prob_local = jnp.sum(router_probs * alive_float, axis=0)
    prob_total = lax.psum(prob_local, ("rep", "fsdp"))
    share = load_total / (2.0 * live_total)
    balance_loss = EXPERTS * jnp.sum(share * prob_total / live_total)
    aux_grad = alive_float * (EXPERTS * share / live_total)[None, :]
    (grad_logits,) = gate_back((gate_grads[:rows_count], gate_grads[rows_count:], aux_grad))
    grad_logits_low = grad_logits.astype(jnp.bfloat16)
    grad_router = jnp.dot(second_low.T, grad_logits_low, preferred_element_type=jnp.float32)
    grad_second = (
        jnp.dot(grad_logits_low, router_full.T, preferred_element_type=jnp.float32) + expert_part
    )
    _, norm_two_back = jax.vjp(norm_rows, middle, gain_two, shift_two)
    grad_mid_norm, grad_gain_two, grad_shift_two = norm_two_back(grad_second)
    grad_middle = upstream + grad_mid_norm
    grad_att_low = grad_middle.astype(jnp.bfloat16)
    grad_out_proj = jnp.dot(mixed_low.T, grad_att_low, preferred_element_type=jnp.float32)
    grad_out_bias = jnp.sum(grad_att_low.astype(jnp.float32), axis=0)
    grad_mixed = (
        jnp.dot(grad_att_low, out_full.T, preferred_element_type=jnp.float32)
        .astype(jnp.bfloat16)
        .reshape(image_shape)
    )
    recomputed = jnp.exp(score_block() - log_total)
    grad_weights = jnp.einsum(
        "iqhd,ikhd->hiqk", grad_mixed, valued, preferred_element_type=jnp.float32
    )
    grad_values = jnp.einsum(
        "hiqk,iqhd->ikhd",
        recomputed.astype(jnp.bfloat16),
        grad_mixed,
        preferred_element_type=jnp.float32,
    )
    inner_sum = jnp.sum(grad_weights * recomputed, axis=-1, keepdims=True)
    grad_scores = (recomputed * (grad_weights - inner_sum)).astype(jnp.bfloat16)
    grad_queries = (
        jnp.einsum("hiqk,ikhd->iqhd", grad_scores, all_keys, preferred_element_type=jnp.float32)
        * score_scale
    )
    grad_keys = (
        jnp.einsum("hiqk,iqhd->ikhd", grad_scores, queries, preferred_element_type=jnp.float32)
        * score_scale
    )
    grad_packed_low = jnp.concatenate(
        [
            grad_queries.reshape(rows_count, model_width),
            grad_keys.reshape(rows_count, model_width),
            grad_values.reshape(rows_count, model_width),
        ],
        axis=1,
    ).astype(jnp.bfloat16)
    grad_qkv = jnp.dot(normed_low.T, grad_packed_low, preferred_element_type=jnp.float32)
    packed_sums = jnp.sum(grad_packed_low.astype(jnp.float32), axis=0)
    grad_query_bias = packed_sums[:model_width]
    grad_value_bias = packed_sums[2 * model_width :]
    grad_normed = jnp.dot(grad_packed_low, qkv_full.T, preferred_element_type=jnp.float32)
    _, norm_one_back = jax.vjp(norm_rows, inputs, gain_one, shift_one)
    grad_input_norm, grad_gain_one, grad_shift_one = norm_one_back(grad_normed)
    grad_tokens = grad_middle + grad_input_norm
    local_grads = (
        grad_gain_one,
        grad_shift_one,
        grad_qkv,
        grad_query_bias,
        grad_value_bias,
        grad_out_proj,
        grad_out_bias,
        grad_gain_two,
        grad_shift_two,
        grad_router,
    )
    shares = (
        lax.psum_scatter(local_grads[0], "fsdp", scatter_dimension=0, tiled=True),
        lax.psum_scatter(local_grads[1], "fsdp", scatter_dimension=0, tiled=True),
        lax.psum_scatter(local_grads[2], "fsdp", scatter_dimension=0, tiled=True),
        lax.psum_scatter(local_grads[3], "fsdp", scatter_dimension=0, tiled=True),
        lax.psum_scatter(local_grads[4], "fsdp", scatter_dimension=0, tiled=True),
        lax.psum_scatter(local_grads[5], "fsdp", scatter_dimension=0, tiled=True),
        lax.psum_scatter(local_grads[6], "fsdp", scatter_dimension=0, tiled=True),
        lax.psum_scatter(local_grads[7], "fsdp", scatter_dimension=0, tiled=True),
        lax.psum_scatter(local_grads[8], "fsdp", scatter_dimension=0, tiled=True),
        lax.psum_scatter(local_grads[9], "fsdp", scatter_dimension=0, tiled=True),
    )
    owned = lax.psum(
        (
            shares[0],
            shares[1],
            shares[2],
            shares[3],
            shares[4],
            shares[5],
            shares[6],
            shares[7],
            shares[8],
            shares[9],
        ),
        "rep",
    )
    return (
        (outputs, grad_tokens, balance_loss)
        + tuple(owned)
        + (grad_in_weight, grad_in_bias, grad_out_weight, grad_out_expert_bias)
    )


def gelu_pair(value):
    root = 0.7978845608028654
    square = value * value
    bend = jnp.tanh(root * value * (1.0 + 0.044715 * square))
    half = 0.5 * (1.0 + bend)
    slope = half + 0.5 * value * (1.0 - bend * bend) * root * (1.0 + 3 * 0.044715 * square)
    return value * half, slope


def slice_grads_body(where_ref, *refs, senders):
    parts, refs = refs[: sum(senders)], refs[sum(senders) :]
    in_ref, in_bias_ref, out_ref, keep_in, send_in, keep_out, send_out, d_bias, d_out_bias = refs
    core = where_ref[1]
    width = in_ref.shape[1]

    def stacked(pieces):
        return jnp.concatenate([piece[...].reshape(-1, width) for piece in pieces], axis=0)

    rows = stacked(parts[: senders[0]])
    grads = stacked(parts[senders[0] :])
    first = in_ref[0]
    second = out_ref[0]
    raised = jnp.dot(rows, first, preferred_element_type=jnp.float32) + in_bias_ref[0].astype(
        jnp.float32
    )
    active, slope = gelu_pair(raised)
    active = active.astype(jnp.bfloat16)
    back = lax.dot_general(
        grads, second, (((1,), (1,)), ((), ())), preferred_element_type=jnp.float32
    )
    draised = (back * slope).astype(jnp.bfloat16)
    over_rows = (((0,), (0,)), ((), ()))
    g_in = lax.dot_general(rows, draised, over_rows, preferred_element_type=jnp.float32)
    g_out = lax.dot_general(active, grads, over_rows, preferred_element_type=jnp.float32)
    half = g_in.shape[1] // 2
    first_core = core == 0
    keep_in[0] = jnp.where(first_core, g_in[:, :half], g_in[:, half:])
    send_in[0] = jnp.where(first_core, g_in[:, half:], g_in[:, :half]).astype(jnp.bfloat16)
    keep_out[0] = jnp.where(first_core, g_out[:half], g_out[half:])
    send_out[0] = jnp.where(first_core, g_out[half:], g_out[:half]).astype(jnp.bfloat16)
    d_bias[0] = jnp.sum(draised.astype(jnp.float32), axis=0, keepdims=True)
    d_out_bias[0] = jnp.sum(grads.astype(jnp.float32), axis=0, keepdims=True)


def slice_grads(where, rows, grads, first, first_bias, second):
    experts, width, hidden = first.shape
    cap = rows[0].shape[2]
    slots = cap * sum(piece.shape[1] for piece in rows)
    part = 256
    half = part // 2
    f32 = jnp.float32
    return pl.pallas_call(
        lambda *refs: slice_grads_body(*refs, senders=(len(rows), len(grads))),
        grid_spec=pltpu.PrefetchScalarGridSpec(
            num_scalar_prefetch=1,
            grid=(experts,),
            in_specs=[
                pl.BlockSpec((1,) + piece.shape[1:], lambda e, w: (e, 0, 0, 0)) for piece in (*rows, *grads)
            ]
            + [
                pl.BlockSpec((1, width, part), lambda e, w: (e, 0, w[0])),
                pl.BlockSpec((1, 1, part), lambda e, w: (e, 0, w[0])),
                pl.BlockSpec((1, part, width), lambda e, w: (e, w[0], 0)),
            ],
            out_specs=[
                pl.BlockSpec((1, width, half), lambda e, w: (e, 0, 0)),
                pl.BlockSpec((1, width, half), lambda e, w: (e, 0, 0)),
                pl.BlockSpec((1, half, width), lambda e, w: (e, 0, 0)),
                pl.BlockSpec((1, half, width), lambda e, w: (e, 0, 0)),
                pl.BlockSpec((1, 1, part), lambda e, w: (e, 0, 0)),
                pl.BlockSpec((1, 1, width), lambda e, w: (e, 0, 0)),
            ],
        ),
        out_shape=[
            jax.ShapeDtypeStruct((experts, width, half), f32),
            jax.ShapeDtypeStruct((experts, width, half), jnp.bfloat16),
            jax.ShapeDtypeStruct((experts, half, width), f32),
            jax.ShapeDtypeStruct((experts, half, width), jnp.bfloat16),
            jax.ShapeDtypeStruct((experts, 1, part), f32),
            jax.ShapeDtypeStruct((experts, 1, width), f32),
        ],
        cost_estimate=pl.CostEstimate(
            flops=8 * experts * slots * width * part,
            bytes_accessed=4 * experts * (slots * width + 3 * width * part),
            transcendentals=experts * slots * part,
        ),
        name="slice_grads",
    )(where, *rows, *grads, first, first_bias.reshape(experts, 1, hidden), second)


F32 = jnp.float32
BF16 = jnp.bfloat16
PAD = 208
ROOT_AXES = ("rep", "fsdp")
OVER_COLS = (((1,), (1,)), ((), ()))
OVER_ROWS = (((0,), (0,)), ((), ()))


def dot(left, right):
    return jnp.dot(left, right, preferred_element_type=F32)


def dot_cols(left, right):
    return lax.dot_general(left, right, OVER_COLS, preferred_element_type=F32)


def dot_rows(left, right):
    return lax.dot_general(left, right, OVER_ROWS, preferred_element_type=F32)


def iota(shape, axis):
    return lax.broadcasted_iota(jnp.int32, shape, axis)


def resident(shape):
    return pl.BlockSpec(shape, lambda *_: (0,) * len(shape))


def by_image(*shape):
    return pl.BlockSpec((1,) + shape, lambda i, *_: (i,) + (0,) * len(shape))


def scalar_spec():
    return pl.BlockSpec(memory_space=pltpu.SMEM)


def partner(link):
    device, side = lax.axis_index("rep"), lax.axis_index("fsdp")
    if link == "y":
        return {"rep": device, "fsdp": 1 - side}
    depth = device // 4
    step = {
        "core": 1 - 2 * (device % 2),
        "x": 2 - 4 * ((device // 2) % 2),
        "near": 4 - 8 * (depth % 2),
        "inner": 12 - 8 * depth,
    }[link]
    return {"rep": device + step, "fsdp": side}


def only_if(condition, action):
    if condition is None:
        action()
    else:
        pl.when(condition)(action)


class Move:
    def __init__(self, link, source, target, needs=()):
        self.link, self.source, self.target, self.needs = link, source, target, needs

    def roles(self):
        depth = lax.axis_index("rep") // 4
        middle = (depth % 3) > 0
        if self.link == "inner":
            return middle, middle
        if self.link == "outward":
            return middle, (depth % 3) == 0
        return None, None

    def copy(self, refs, send, recv):
        return pltpu.make_async_remote_copy(
            src_ref=self.source(refs),
            dst_ref=self.target(refs),
            send_sem=send,
            recv_sem=recv,
            device_id=partner("near" if self.link == "outward" else self.link),
            device_id_type=pl.DeviceIdType.MESH,
        )


class Traffic:
    def __init__(self, sources, targets, rounds, steps):
        self.sources, self.targets, self.rounds, self.steps = sources, targets, rounds, steps

    def count(self):
        return sum(len(moves) for moves in self.rounds)

    def greet(self):
        links = {("near" if m.link == "outward" else m.link) for moves in self.rounds for m in moves}
        barrier = pltpu.get_barrier_semaphore()
        middle = ((lax.axis_index("rep") // 4) % 3) > 0
        plain = [link for link in ("core", "x", "y", "near") if link in links]
        for link in plain:
            pl.semaphore_signal(barrier, inc=1, device_id=partner(link), device_id_type=pl.DeviceIdType.MESH)
        if "inner" in links:

            @pl.when(middle)
            def _():
                pl.semaphore_signal(
                    barrier, inc=1, device_id=partner("inner"), device_id_type=pl.DeviceIdType.MESH
                )

        if "inner" in links:

            @pl.when(middle)
            def _():
                pl.semaphore_wait(barrier, len(plain) + 1)

            @pl.when(~middle)
            def _():
                if plain:
                    pl.semaphore_wait(barrier, len(plain))

        else:
            pl.semaphore_wait(barrier, len(plain))

    def start(self, which, refs, send, recv, arrived):
        moves = [m for moves in self.rounds for m in moves]
        at = sum(len(moves) for moves in self.rounds[:which])
        for k, move in enumerate(self.rounds[which]):
            for index in move.needs:
                if index not in arrived:
                    arrived.add(index)
                    only_if(moves[index].roles()[1], moves[index].copy(refs, send.at[index], recv.at[index]).wait_recv)
            only_if(move.roles()[0], move.copy(refs, send.at[at + k], recv.at[at + k]).start)

    def finish(self, refs, send, recv, arrived):
        moves = [m for moves in self.rounds for m in moves]
        for index, move in enumerate(moves):
            copy = move.copy(refs, send.at[index], recv.at[index])
            sends, receives = move.roles()
            only_if(sends, copy.wait_send)
            if index not in arrived:
                only_if(receives, copy.wait_recv)


def run(body, args, in_specs, out_specs, out_shape, *, name, grid=(1,), scratch=(), cost=None, traffic=None, ident=None):
    if traffic is None or traffic.count() == 0:
        outs = pl.pallas_call(
            body, grid=grid, in_specs=in_specs, out_specs=out_specs, out_shape=out_shape,
            scratch_shapes=list(scratch), cost_estimate=cost, name=name,
        )(*args)
        return outs, []
    n_in, n_src, n_out, n_dst = len(args), len(traffic.sources), len(out_shape), len(traffic.targets)
    anywhere = pl.BlockSpec(memory_space=pl.ANY)

    def carried(*refs):
        ins, refs = refs[:n_in], refs[n_in:]
        sources, refs = refs[:n_src], refs[n_src:]
        outs, refs = refs[:n_out], refs[n_out:]
        targets, refs = refs[:n_dst], refs[n_dst:]
        held, send, recv = refs[:-2], refs[-2], refs[-1]
        ends = (sources, targets)
        step = pl.program_id(0)
        arrived = set()
        for which, at in enumerate(traffic.steps):

            @pl.when(step == at)
            def _():
                if which == 0:
                    traffic.greet()
                traffic.start(which, ends, send, recv, arrived)

        body(*ins, *outs, *held)

        @pl.when(step == grid[0] - 1)
        def _():
            traffic.finish(ends, send, recv, arrived)

    count = traffic.count()
    outs = pl.pallas_call(
        carried,
        grid=grid,
        in_specs=list(in_specs) + [anywhere] * n_src,
        out_specs=list(out_specs) + [anywhere] * n_dst,
        out_shape=list(out_shape) + list(traffic.targets),
        scratch_shapes=list(scratch) + [pltpu.SemaphoreType.DMA((count,)), pltpu.SemaphoreType.DMA((count,))],
        compiler_params=pltpu.CompilerParams(collective_id=ident, has_side_effects=True),
        cost_estimate=cost,
        name=name,
    )(*args, *traffic.sources)
    return outs[:n_out], outs[n_out:]


def block_hops(balance):
    hops = {
        (0, 1, 0): ("x", (0, 0, 0)),
        (0, 0, 1): ("y", (0, 0, 0)),
        (0, 1, 1): ("x", (0, 0, 1)),
        (1, 0, 0): ("near", (0, 0, 0)),
        (2, 0, 0): ("inner", (0, 0, 0)),
        (3, 0, 0): ("inner", (1, 0, 0)),
        (1, 1, 1): ("near", (0, 1, 1)),
        (2, 1, 1): ("inner", (0, 1, 1)),
        (3, 1, 1): ("x", (3, 0, 1)) if balance else ("inner", (1, 1, 1)),
    }
    for s in (1, 2, 3):
        hops[(s, 1, 0)] = ("x", (s, 0, 0))
        hops[(s, 0, 1)] = ("y", (s, 0, 0))
    return hops


class Network:
    def __init__(self):
        self.have, self.hops, self.weight, self.pieces, self.rank = {}, {}, {}, {}, {}

    def offer(self, name, array, hops, weight=1, rank=0):
        self.hops[name], self.weight[name], self.rank[name] = hops, weight, rank
        self.pieces[name] = array.shape[0]
        for p in range(array.shape[0]):
            self.have[name, (0, 0, 0), p] = (array, p)

    def depth(self, name, block):
        below = [b for b, (_, source) in self.hops[name].items() if source == block]
        own = 2 if block != (0, 0, 0) and self.hops[name][block][0] == "inner" else 1
        return own + max([self.depth(name, b) for b in below], default=0)

    def missing(self):
        return [
            (name, block, p)
            for name in self.hops
            for block in self.hops[name]
            for p in range(self.pieces[name])
            if (name, block, p) not in self.have
        ]

    def complete(self, name, block):
        return all((name, block, p) in self.have for p in range(self.pieces[name]))

    def plan(self, capacities, steps):
        waiting = sorted(
            self.missing(), key=lambda m: (self.rank[m[0]] - (m[0] in "CS" and m[1] == (0, 0, 1)), -self.depth(m[0], m[1]), m[1], m[2])
        )
        landed = {}
        rounds = [[] for _ in capacities]
        load = [dict.fromkeys(("x", "y", "near", "inner"), 0) for _ in capacities]
        for r, capacity in enumerate(capacities):
            for item in waiting:
                name, block, p = item
                if item in landed:
                    continue
                link, source = self.hops[name][block]
                source = (name, source, p)
                if source not in self.have and landed.get(source, r) >= r:
                    continue
                weight = self.weight[name]
                if load[r][link] + weight > capacity:
                    continue
                if link == "inner":
                    if r + 1 >= len(capacities) or load[r + 1]["near"] + weight > capacities[r + 1]:
                        continue
                    load[r + 1]["near"] += weight
                    rounds[r + 1].append(("outward", item, item))
                    landed[item] = r + 1
                else:
                    landed[item] = r
                load[r][link] += weight
                rounds[r].append((link, source, item))
        sources, targets, homes = [], [], {}
        for name, block, p in sorted(landed):
            homes.setdefault((name, block), []).append(p)
        order = list(homes)
        for name, block in order:
            model = self.have[name, (0, 0, 0), 0][0]
            targets.append(jax.ShapeDtypeStruct((len(homes[name, block]),) + model.shape[1:], model.dtype))

        def home(item):
            name, block, p = item
            return order.index((name, block)), homes[name, block].index(p)

        def origin(item):
            if item in landed:
                return (1,) + home(item)
            array, at = self.have[item]
            for k, known in enumerate(sources):
                if known is array:
                    return 0, k, at
            sources.append(array)
            return 0, len(sources) - 1, at

        moves = []
        for chosen in rounds:
            spans = []
            for link, source, item in sorted(chosen):
                a, b = origin(source), home(item)
                if spans:
                    link_, a_, b_, n = spans[-1]
                    if link_ == link and a_[:2] == a[:2] and b_[0] == b[0] and a[2] == a_[2] + n and b[1] == b_[1] + n:
                        spans[-1] = (link, a_, b_, n + 1)
                        continue
                spans.append((link, a, b, 1))
            flat = [m for made in moves for m in made]
            placed = []
            for link, a, b, n in spans:
                needs = [
                    k
                    for k, m in enumerate(flat)
                    if a[0] == 1 and m.home[0] == a[1] and m.home[1] < a[2] + n and a[2] < m.home[1] + m.size
                ]
                placed.append(self.move(link, a, b, n, needs))
            moves.append(placed)
        while moves and not moves[-1]:
            moves.pop()
        traffic = Traffic(sources, targets, moves, steps[: len(moves)])
        return traffic, (order, homes)

    @staticmethod
    def move(link, origin, home, count, needs):
        def source(refs):
            return refs[origin[0]][origin[1]].at[pl.ds(origin[2], count)]

        def target(refs):
            return refs[1][home[0]].at[pl.ds(home[1], count)]

        made = Move(link, source, target, needs)
        made.home, made.size = home, count
        return made

    def land(self, plan, arrays):
        order, homes = plan
        for key, array in zip(order, arrays):
            for at, p in enumerate(homes[key]):
                self.have[key[0], key[1], p] = (array, at)

    def block(self, name, block):
        return [self.have[name, block, p] for p in range(self.pieces[name])]


def standardise(values):
    average = jnp.mean(values, axis=-1, keepdims=True)
    centred = values - average
    variance = jnp.mean(centred * centred, axis=-1, keepdims=True)
    scale = lax.rsqrt(variance + 1e-06)
    return centred * scale, scale


def prep_body(count_ref, cap_ref, tok_ref, cot_ref, route_ref, tok_out, cot_out, route_out, ids_out, load_out, wide, narrow):
    pl.when(pl.program_id(0) == 0)(
        lambda: prep_rows(
            count_ref, cap_ref, tok_ref, cot_ref, route_ref, tok_out, cot_out, route_out, ids_out, load_out, wide, narrow
        )
    )


def prep_rows(count_ref, cap_ref, tok_ref, cot_ref, route_ref, tok_out, cot_out, route_out, ids_out, load_out, wide, narrow):
    images = tok_out.shape[0]
    total = tok_ref.shape[0]
    alive_images = count_ref[0]
    real = iota((PAD, 1), 0) < IMG_TOK

    def split(source, image):
        return source[pl.ds(image * IMG_TOK, PAD), :]

    wide[...] = jnp.zeros_like(wide)
    narrow[...] = jnp.zeros_like(narrow)
    wide[pl.ds(0, total), :] = tok_ref[...].astype(F32)
    for image in range(images):
        tok_out[image] = jnp.where(real, split(wide, image), 0.0).astype(BF16)
    wide[pl.ds(0, total), :] = cot_ref[...].astype(F32)
    narrow[pl.ds(0, total), :] = route_ref[...]
    routes = []
    lives = []
    for image in range(images):
        live = real & (image < alive_images)
        cot_out[image] = jnp.where(live, split(wide, image), 0.0).astype(BF16)
        picked = split(narrow, image)
        route_out[image] = picked
        routes.append(picked)
        lives.append(jnp.where(live, 1, 0))
    routes = jnp.concatenate(routes, axis=0)
    live = jnp.concatenate(lives, axis=0) > 0
    rows = images * PAD
    lane = iota((rows, 128), 1)
    first = (lane == routes[:, 0:1]) & live
    second = (lane == routes[:, 1:2] + EXPERTS) & live
    hot = jnp.where(first | second, 1.0, 0.0)
    below = jnp.where(iota((rows, rows), 0) > iota((rows, rows), 1), 1.0, 0.0).astype(BF16)
    before = dot(below, hot.astype(BF16))
    totals = jnp.sum(hot, axis=0, keepdims=True)
    place_one = jnp.sum(jnp.where(first, before, 0.0), axis=1, keepdims=True)
    place_two = jnp.sum(jnp.where(second, before, 0.0), axis=1, keepdims=True) + jnp.sum(
        jnp.where(lane == routes[:, 1:2], totals, 0.0), axis=1, keepdims=True
    )
    limit = cap_ref[0].astype(F32)
    keep_one = live & (place_one < limit)
    keep_two = live & (place_two < limit)
    slots = jnp.where(lane == 0, jnp.where(keep_one, routes[:, 0:1].astype(F32), -1.0), 0.0)
    slots = jnp.where(lane == 1, jnp.where(keep_one, place_one, 0.0), slots)
    slots = jnp.where(lane == 2, jnp.where(keep_two, routes[:, 1:2].astype(F32), -1.0), slots)
    slots = jnp.where(lane == 3, jnp.where(keep_two, place_two, 0.0), slots)
    for image in range(images):
        ids_out[image] = jnp.transpose(slots[image * PAD : (image + 1) * PAD])[0:8]
    lanes = iota((1, 128), 1)
    tokens_alive = (alive_images * IMG_TOK).astype(F32)
    load_out[0] = jnp.broadcast_to(jnp.where(lanes == 64, tokens_alive, totals), (8, 128))


def weight_traffic(wide, tall):
    def rows(array):
        half = array.shape[0] // 2
        return pl.ds(pl.multiple_of((lax.axis_index("rep") % 2) * half, 8), half)

    def fetch(at, array):
        return Move("y", lambda refs: refs[0][at].at[rows(array)], lambda refs: refs[1][at].at[rows(array)])

    def pass_on(at, array):
        there = lambda refs: refs[1][at].at[rows(array)]
        return Move("core", there, there, [at])

    arrays = (wide, tall)
    targets = [jax.ShapeDtypeStruct(a.shape, a.dtype) for a in arrays]
    rounds = [[make(at, a) for at, a in enumerate(arrays)] for make in (fetch, pass_on)]
    return Traffic(list(arrays), targets, rounds, [0, 1])


def prepare(tokens, cotangent, routes, image_count, capacity, wide, tall, ident):
    total, width = tokens.shape
    images = total // IMG_TOK
    shapes = [
        jax.ShapeDtypeStruct((images, PAD, width), BF16),
        jax.ShapeDtypeStruct((images, PAD, width), BF16),
        jax.ShapeDtypeStruct((images, PAD, 2), jnp.int32),
        jax.ShapeDtypeStruct((images, 8, PAD), F32),
        jax.ShapeDtypeStruct((1, 8, 128), F32),
    ]
    return run(
        prep_body,
        (image_count, capacity, tokens, cotangent, routes),
        [scalar_spec(), scalar_spec()] + [resident(a.shape) for a in (tokens, cotangent, routes)],
        [resident(a.shape) for a in shapes],
        shapes,
        grid=(2,),
        scratch=[pltpu.VMEM((1000, width), F32), pltpu.VMEM((1000, 2), jnp.int32)],
        cost=pl.CostEstimate(flops=300_000_000, bytes_accessed=6_000_000, transcendentals=0),
        name="prepare",
        traffic=weight_traffic(wide, tall),
        ident=ident,
    )


def place_halves(own, far, both):
    mine = lax.axis_index("fsdp")
    both[mine] = own[...]
    both[1 - mine] = far[...]


def vectors(wide_ref):
    return jnp.concatenate([wide_ref[0, 256:272, :256], wide_ref[1, 256:272, :256]], axis=1).astype(F32)


def front_body(
    count_ref, tok_ref, ids_ref, route_ref, wide_own, wide_far, tall_own, tall_far,
    packed_ref, prob_ref, mixed_ref, middle_ref, second_ref, soft_ref, sum_ref, wide_ref, tall_ref,
):
    @pl.when(pl.program_id(0) == 0)
    def _():
        sum_ref[...] = jnp.zeros_like(sum_ref)
        place_halves(wide_own, wide_far, wide_ref)
        place_halves(tall_own, tall_far, tall_ref)

    width = tok_ref.shape[-1]
    vec = vectors(wide_ref)
    inputs = tok_ref[0].astype(F32)
    normed = (standardise(inputs)[0] * vec[0:1] + vec[1:2]).astype(BF16)
    qkv = wide_ref[:, :256, :].reshape(width, 3 * width)
    raw = dot(normed, qkv)
    packed_ref[0, :, :width] = (raw[:, :width] + vec[2:3]).astype(BF16)
    packed_ref[0, :, width : 2 * width] = raw[:, width : 2 * width].astype(BF16)
    packed_ref[0, :, 2 * width :] = (raw[:, 2 * width :] + vec[3:4]).astype(BF16)
    low_lanes = iota((PAD, 128), 1) < HEAD_DIM
    real_key = iota((PAD, PAD), 1) < IMG_TOK
    for pair in range(HEADS // 2):
        at = pair * 128
        query = packed_ref[0, :, at : at + 128] * jnp.asarray(HEAD_DIM**-0.5, BF16)
        keys = packed_ref[0, :, width + at : width + at + 128]
        valued = packed_ref[0, :, 2 * width + at : 2 * width + at + 128]
        got = []
        for side in range(2):
            own = low_lanes if side == 0 else ~low_lanes
            scores = dot_cols(jnp.where(own, query, jnp.zeros_like(query)), keys)
            scores = jnp.where(real_key, scores, -1e30)
            raised = jnp.exp(scores - jnp.max(scores, axis=-1, keepdims=True))
            weights = (raised / jnp.sum(raised, axis=-1, keepdims=True)).astype(BF16)
            prob_ref[0, 2 * pair + side] = weights
            got.append(dot(weights, valued))
        mixed_ref[0, :, at : at + 128] = jnp.where(low_lanes, got[0], got[1]).astype(BF16)
    out_full = tall_ref[:, :, :width].reshape(width, width)
    router = tall_ref[:, :, width : width + 128].reshape(width, 128)
    middle = inputs + dot(mixed_ref[0], out_full) + vec[4:5]
    middle_ref[0] = middle
    second = standardise(middle)[0] * vec[5:6] + vec[6:7]
    lane = iota((PAD, 128), 1)
    logits = jnp.where(lane < EXPERTS, dot(second.astype(BF16), router), -1e30)
    soft = jnp.exp(logits - jnp.max(logits, axis=-1, keepdims=True))
    soft = soft / jnp.sum(soft, axis=-1, keepdims=True)
    route = route_ref[0]
    pick_one = jnp.sum(jnp.where(lane == route[:, 0:1], soft, 0.0), axis=-1, keepdims=True)
    pick_two = jnp.sum(jnp.where(lane == route[:, 1:2], soft, 0.0), axis=-1, keepdims=True)
    both = pick_one + pick_two
    live = (iota((PAD, 1), 0) < IMG_TOK) & (pl.program_id(0) < count_ref[0])
    alive = jnp.where(live, 1.0, 0.0)
    sum_ref[0] += jnp.broadcast_to(jnp.sum(soft * alive, axis=0, keepdims=True), (8, 128))
    soft = jnp.where(lane == EXPERTS + 4, pick_one / both, soft)
    soft = jnp.where(lane == EXPERTS + 5, pick_two / both, soft)
    soft_ref[0] = soft
    gates = jnp.transpose(soft)[EXPERTS : EXPERTS + 8]
    line = iota((8, PAD), 0)
    meta = jnp.where((line == 4) | (line == 5), gates, ids_ref[0])
    meta = jnp.concatenate([meta, jnp.zeros((8, width - PAD), F32)], axis=1)
    second_ref[0] = jnp.concatenate([second[: PAD - 8], meta], axis=0).astype(BF16)


def front(count, tok, ids, routes, wide, tall, traffic, ident):
    images, _, width = tok.shape
    shape = jax.ShapeDtypeStruct
    return run(
        front_body,
        (count, tok, ids, routes, *wide, *tall),
        [scalar_spec(), by_image(PAD, width), by_image(8, PAD), by_image(PAD, 2)]
        + [resident(wide[0].shape)] * 2
        + [resident(tall[0].shape)] * 2,
        [
            by_image(PAD, 3 * width),
            by_image(HEADS, PAD, PAD),
            by_image(PAD, width),
            by_image(PAD, width),
            by_image(PAD, width),
            by_image(PAD, 128),
            resident((1, 8, 128)),
        ],
        [
            shape((images, PAD, 3 * width), BF16),
            shape((images, HEADS, PAD, PAD), BF16),
            shape((images, PAD, width), BF16),
            shape((images, PAD, width), F32),
            shape((images, PAD, width), BF16),
            shape((images, PAD, 128), F32),
            shape((1, 8, 128), F32),
        ],
        grid=(images,),
        scratch=[pltpu.VMEM((2,) + wide[0].shape, BF16), pltpu.VMEM((2,) + tall[0].shape, BF16)],
        cost=pl.CostEstimate(flops=6_000_000_000, bytes_accessed=16_000_000, transcendentals=2_000_000),
        name="front",
        traffic=traffic,
        ident=ident,
    )


def slot_lines(meta):
    return meta[0:1] * CAP + meta[1:2], meta[2:3] * CAP + meta[3:4]


def gather_body(base_ref, *refs, parts, senders):
    arrays, (row_out, grad_out, rows, lines) = refs[:parts], refs[parts:]
    experts, _, cap, width = row_out.shape
    slots = experts * cap
    tokens = rows.shape[0]
    step = pl.program_id(0)
    for k, pair in enumerate(senders):
        for kind, pieces in enumerate(pair):

            @pl.when(step == 2 * k + kind)
            def _():
                for image, (at, position) in enumerate(pieces):
                    value = arrays[at][position]
                    rows[image * PAD : (image + 1) * PAD, :] = value
                    if kind == 0:
                        lines[image] = value[PAD - 16 :, :PAD].astype(F32)[8:]

    meta = jnp.concatenate([lines[image] for image in range(lines.shape[0])], axis=1)
    one, two = slot_lines(meta)
    gated = step % 2 == 1
    weight_one = jnp.where(gated, meta[4:5], 1.0)
    weight_two = jnp.where(gated, meta[5:6], 1.0)
    slot = (iota((slots, tokens), 0) + base_ref[0]).astype(F32)
    pick = jnp.where(slot == one, weight_one, 0.0) + jnp.where(slot == two, weight_two, 0.0)
    got = dot(pick.astype(BF16), rows[...]).astype(BF16).reshape(experts, 1, cap, width)

    @pl.when(step % 2 == 0)
    def _():
        row_out[...] = got

    @pl.when(step % 2 == 1)
    def _():
        grad_out[...] = got


def gather(base, experts, senders, traffic, ident):
    arrays, table = [], []
    for pair in senders:
        table.append([])
        for pieces in pair:
            table[-1].append([])
            for array, position in pieces:
                at = next((k for k, known in enumerate(arrays) if known is array), len(arrays))
                if at == len(arrays):
                    arrays.append(array)
                table[-1][-1].append((at, position))
    width = arrays[0].shape[-1]
    images = len(table[0][0])
    tokens = images * PAD
    count = len(senders)
    shape = jax.ShapeDtypeStruct((experts, count, CAP, width), BF16)
    return run(
        lambda *refs: gather_body(*refs, parts=len(arrays), senders=table),
        (base, *arrays),
        [scalar_spec()]
        + [pl.BlockSpec(a.shape, lambda d: (0, 0, 0), pipeline_mode=pl.Buffered(1)) for a in arrays],
        [pl.BlockSpec((experts, 1, CAP, width), lambda d: (0, d // 2, 0, 0))] * 2,
        [shape, shape],
        grid=(2 * count,),
        scratch=[pltpu.VMEM((tokens, width), BF16), pltpu.VMEM((images, 8, PAD), F32)],
        cost=pl.CostEstimate(
            flops=4 * count * experts * CAP * tokens * width,
            bytes_accessed=4 * count * (tokens + experts * CAP) * width,
            transcendentals=0,
        ),
        name="gather",
        traffic=traffic,
        ident=ident,
    )


def expert_body(row_own, row_far, grad_own, grad_far, in_ref, in_bias_ref, out_ref, out_bias_ref, made_own, made_far, back_own, back_far):
    cap, width = row_own.shape[2:]
    hidden = in_ref.shape[2]
    rows = jnp.concatenate([row_own[0, 0], row_far[0, 0]], axis=0)
    grads = jnp.concatenate([grad_own[0, 0], grad_far[0, 0]], axis=0)
    made = jnp.zeros((2 * cap, width), F32)
    back = jnp.zeros((2 * cap, width), F32)
    chunk = 512
    for at in range(0, hidden, chunk):
        first = in_ref[0, :, at : at + chunk]
        second = out_ref[0, at : at + chunk, :]
        raised = dot(rows, first) + in_bias_ref[0, :, at : at + chunk].astype(F32)
        active, slope = gelu_pair(raised)
        made += dot(active.astype(BF16), second)
        draised = (dot_cols(grads, second) * slope).astype(BF16)
        back += dot_cols(draised, first)
    made = (made + out_bias_ref[0].astype(F32)).astype(BF16)
    back = back.astype(BF16)
    made_own[0], made_far[0] = made[:cap], made[cap:]
    back_own[0], back_far[0] = back[:cap], back[cap:]


def expert_layer(own, far, first, first_bias, second, second_bias, traffic, ident):
    experts, _, cap, width = own[0].shape
    hidden = first.shape[2]
    rows = pl.BlockSpec((1, 1, cap, width), lambda e: (e, 0, 0, 0))
    out = pl.BlockSpec((1, cap, width), lambda e: (e, 0, 0))
    return run(
        expert_body,
        (
            own[0],
            far[0],
            own[1],
            far[1],
            first,
            first_bias.reshape(experts, 1, hidden),
            second,
            second_bias.reshape(experts, 1, width),
        ),
        [rows] * 4 + [by_image(width, hidden), by_image(1, hidden), by_image(hidden, width), by_image(1, width)],
        [out] * 4,
        [jax.ShapeDtypeStruct((experts, cap, width), BF16)] * 4,
        grid=(experts,),
        cost=pl.CostEstimate(
            flops=16 * experts * cap * width * hidden,
            bytes_accessed=4 * experts * width * hidden,
            transcendentals=2 * experts * cap * hidden,
        ),
        name="expert_layer",
        traffic=traffic,
        ident=ident,
    )


def combine_body(base_ref, rows, cot, made_ref, back_ref, sum_ref, row_ref, gate_ref):
    experts, cap, width = made_ref.shape
    slots = experts * cap
    meta = jnp.transpose(rows[PAD - 16 :, :PAD].astype(F32)[8:])
    slot = (iota((PAD, slots), 1) + base_ref[0]).astype(F32)
    one = jnp.where(slot == meta[:, 0:1] * CAP + meta[:, 1:2], 1.0, 0.0).astype(BF16)
    two = jnp.where(slot == meta[:, 2:3] * CAP + meta[:, 3:4], 1.0, 0.0).astype(BF16)
    made = made_ref[...].reshape(slots, width)
    made_one = dot(one, made)
    made_two = dot(two, made)
    sum_ref[0] = (meta[:, 4:5] * made_one + meta[:, 5:6] * made_two).astype(BF16)
    row_ref[0] = dot(one + two, back_ref[...].reshape(slots, width)).astype(BF16)
    cot = cot.astype(F32)
    grad_one = jnp.sum(cot * made_one, axis=1, keepdims=True)
    grad_two = jnp.sum(cot * made_two, axis=1, keepdims=True)
    lane = iota((PAD, 128), 1)
    wide = jnp.where(lane == 0, grad_one, jnp.where(lane == 1, grad_two, 0.0))
    gate_ref[0] = jnp.transpose(wide)[0:8]


def by_piece(pieces, *shape):
    arrays, first = [], []
    for image, (array, position) in enumerate(pieces):
        if not arrays or arrays[-1] is not array:
            arrays.append(array)
            first.append((image, position))
    specs = []
    for array, (image, position) in zip(arrays, first):

        def index(i, *_, image=image, position=position, last=array.shape[0] - 1):
            return (jnp.clip(i - image + position, 0, last),) + (0,) * len(shape)

        specs.append(pl.BlockSpec((1,) + shape, index))

    def read(refs):
        value = refs[0][0]
        for ref, (image, _) in zip(refs[1:], first[1:]):
            value = jnp.where(pl.program_id(0) >= image, ref[0], value)
        return value

    return arrays, specs, read


def combine(base, rows, cots, made, back, traffic, ident):
    width = made.shape[-1]
    images = len(rows)
    experts, cap, _ = made.shape
    row_arrays, row_specs, read_rows = by_piece(rows, PAD, width)
    cot_arrays, cot_specs, read_cots = by_piece(cots, PAD, width)
    split = len(row_arrays)

    def body(base_ref, made_ref, back_ref, *refs):
        inputs, outs = refs[: split + len(cot_arrays)], refs[split + len(cot_arrays) :]
        combine_body(base_ref, read_rows(inputs[:split]), read_cots(inputs[split:]), made_ref, back_ref, *outs)

    return run(
        body,
        (base, made, back, *row_arrays, *cot_arrays),
        [scalar_spec(), resident(made.shape), resident(back.shape), *row_specs, *cot_specs],
        [by_image(PAD, width), by_image(PAD, width), by_image(8, PAD)],
        [
            jax.ShapeDtypeStruct((images, PAD, width), BF16),
            jax.ShapeDtypeStruct((images, PAD, width), BF16),
            jax.ShapeDtypeStruct((images, 8, PAD), F32),
        ],
        grid=(images,),
        cost=pl.CostEstimate(
            flops=6 * images * PAD * experts * cap * width, bytes_accessed=6_000_000, transcendentals=0
        ),
        name="combine",
        traffic=traffic,
        ident=ident,
    )


def norm_back(grads, hat, scale, gain):
    scaled = grads * gain
    inner = jnp.mean(scaled * hat, axis=-1, keepdims=True)
    return scale * (scaled - jnp.mean(scaled, axis=-1, keepdims=True) - hat * inner)


def column_sum(values):
    return jnp.sum(values, axis=0, keepdims=True)


def finish_body(
    count_ref, tok_ref, cot_ref, packed_ref, prob_ref, mixed_ref, middle_ref, second_ref, soft_ref, route_ref,
    row_own, row_far, gate_own, gate_far, aux_ref,
    wide_own, wide_far, tall_own, tall_far, dtok_ref, pack_ref,
    dpacked, wide_ref, tall_ref, dqkv_ref, dout_ref, drouter_ref, dvec_ref,
):
    image = pl.program_id(0)
    width = tok_ref.shape[-1]

    @pl.when(image == 0)
    def _():
        place_halves(wide_own, wide_far, wide_ref)
        place_halves(tall_own, tall_far, tall_ref)

    vec = vectors(wide_ref)
    images = dtok_ref.shape[0] // IMG_TOK

    @pl.when(image == 0)
    def _():
        for ref in (dqkv_ref, dout_ref, drouter_ref, dvec_ref):
            ref[...] = jnp.zeros_like(ref)

    real = iota((PAD, 1), 0) < IMG_TOK
    alive = jnp.where(real & (image < count_ref[0]), 1.0, 0.0)
    middle = middle_ref[0]
    upstream = cot_ref[0].astype(F32)
    soft = soft_ref[0]
    route = route_ref[0]
    lane = iota((PAD, 128), 1)
    gate_grads = jnp.transpose(gate_own[0] + gate_far)
    push = (gate_grads[:, 0:1] - gate_grads[:, 1:2]) * soft[:, EXPERTS + 4 : EXPERTS + 5] * soft[:, EXPERTS + 5 : EXPERTS + 6]
    soft = jnp.where(lane < EXPERTS, soft, 0.0)
    aux = aux_ref[...] * alive
    dlogits = soft * (aux - jnp.sum(soft * aux, axis=-1, keepdims=True))
    dlogits += jnp.where(lane == route[:, 0:1], push, 0.0) - jnp.where(lane == route[:, 1:2], push, 0.0)
    dlogits = dlogits.astype(BF16)
    second = second_ref[0]
    router = tall_ref[:, :, width : width + 128].reshape(width, 128)
    drouter_ref[...] += dot_rows(second, dlogits)
    dsecond = dot_cols(dlogits, router) + (row_own[0].astype(F32) + row_far.astype(F32))
    hat, scale = standardise(middle)
    dmiddle = upstream + norm_back(dsecond, hat, scale, vec[5:6])
    dattn = dmiddle.astype(BF16)
    dvec_ref[4:5] += column_sum(dattn.astype(F32))
    dvec_ref[5:6] += column_sum(dsecond * hat)
    dvec_ref[6:7] += column_sum(dsecond)
    dout_ref[...] += dot_rows(mixed_ref[0], dattn)
    out_full = tall_ref[:, :, :width].reshape(width, width)
    dmixed = dot_cols(dattn, out_full).astype(BF16)
    low_lanes = iota((PAD, 128), 1) < HEAD_DIM
    root = HEAD_DIM**-0.5
    for pair in range(HEADS // 2):
        at = pair * 128
        query = packed_ref[0, :, at : at + 128]
        keys = packed_ref[0, :, width + at : width + at + 128]
        valued = packed_ref[0, :, 2 * width + at : 2 * width + at + 128]
        grads = dmixed[:, at : at + 128]
        parts = []
        for side in range(2):
            own = low_lanes if side == 0 else ~low_lanes
            weights = prob_ref[0, 2 * pair + side]
            dweights = dot_cols(jnp.where(own, grads, jnp.zeros_like(grads)), valued)
            exact = weights.astype(F32)
            inner = jnp.sum(dweights * exact, axis=-1, keepdims=True)
            dscores = (exact * (dweights - inner)).astype(BF16)
            parts.append((dot(dscores, keys), dot_rows(dscores, query), dot_rows(weights, grads)))
        for third, factor in ((0, root), (1, root), (2, 1.0)):
            both = jnp.where(low_lanes, parts[0][third], parts[1][third]) * factor
            dpacked[:, third * width + at : third * width + at + 128] = both.astype(BF16)
    inputs = tok_ref[0].astype(F32)
    hat, scale = standardise(inputs)
    normed = (hat * vec[0:1] + vec[1:2]).astype(BF16)
    packed_grads = dpacked[...]
    dqkv_ref[...] += dot_rows(normed, packed_grads)
    dvec_ref[2:3] += column_sum(packed_grads[:, :width].astype(F32))
    dvec_ref[3:4] += column_sum(packed_grads[:, 2 * width :].astype(F32))
    qkv = wide_ref[:, :256, :].reshape(width, 3 * width)
    dnormed = dot_cols(packed_grads, qkv)
    dvec_ref[0:1] += column_sum(dnormed * hat)
    dvec_ref[1:2] += column_sum(dnormed)
    dtokens = dmiddle + norm_back(dnormed, hat, scale, vec[0:1])
    for k in range(images):

        @pl.when(image == k)
        def _():
            dtok_ref[pl.ds(k * IMG_TOK, IMG_TOK), :] = dtokens[:IMG_TOK]

    @pl.when(image == images - 1)
    def _():
        half = width // 2
        for owner in range(2):
            rows = slice(owner * half, (owner + 1) * half)
            pack_ref[owner, :half, : 3 * width] = dqkv_ref[rows].astype(BF16)
            pack_ref[owner, :half, 3 * width : 4 * width] = dout_ref[rows].astype(BF16)
            pack_ref[owner, :half, 4 * width :] = drouter_ref[rows].astype(BF16)
            pack_ref[owner, half:, :half] = dvec_ref[:, rows].astype(BF16)
            pack_ref[owner, half:, half:] = jnp.zeros((16, 4 * width + 128 - half), BF16)


def finish(count, tok, cot, saved, routes, row_own, row_far, gate_own, gate_far, aux, wide, tall, total, traffic, ident):
    images, _, width = tok.shape
    packed, prob, mixed, middle, second, soft = saved
    shape = jax.ShapeDtypeStruct
    tile = by_image(PAD, width)
    row_arrays, row_specs, read_rows = by_piece(row_far, PAD, width)
    gate_arrays, gate_specs, read_gates = by_piece(gate_far, 8, PAD)
    extra = len(row_arrays) + len(gate_arrays)

    def body(*refs):
        pieces, refs = refs[:extra], list(refs[extra:])
        refs[11:11] = [read_rows(pieces[: len(row_arrays)])]
        refs[13:13] = [read_gates(pieces[len(row_arrays) :])]
        finish_body(*refs)

    pack = (2, width // 2 + 16, 4 * width + 128)
    return run(
        body,
        (
            *row_arrays, *gate_arrays, count, tok, cot, packed, prob, mixed, middle, second, soft, routes,
            row_own, gate_own, aux, *wide, *tall,
        ),
        [
            *row_specs,
            *gate_specs,
            scalar_spec(),
            tile,
            tile,
            by_image(PAD, 3 * width),
            by_image(HEADS, PAD, PAD),
            tile,
            tile,
            tile,
            by_image(PAD, 128),
            by_image(PAD, 2),
            tile,
            by_image(8, PAD),
            resident((1, 128)),
            resident(wide[0].shape),
            resident(wide[0].shape),
            resident(tall[0].shape),
            resident(tall[0].shape),
        ],
        [resident((total, width)), resident(pack)],
        [shape((total, width), F32), shape(pack, BF16)],
        grid=(images,),
        scratch=[
            pltpu.VMEM((PAD, 3 * width), BF16),
            pltpu.VMEM((2,) + wide[0].shape, BF16),
            pltpu.VMEM((2,) + tall[0].shape, BF16),
            pltpu.VMEM((width, 3 * width), F32),
            pltpu.VMEM((width, width), F32),
            pltpu.VMEM((width, 128), F32),
            pltpu.VMEM((16, width), F32),
        ],
        cost=pl.CostEstimate(flops=12_000_000_000, bytes_accessed=24_000_000, transcendentals=0),
        name="finish",
        traffic=traffic,
        ident=ident,
    )


def emit(count, middle, sum_own, sum_far, total):
    images, _, width = middle.shape
    far_arrays, far_specs, read_far = by_piece(sum_far, PAD, width)

    def body(count_ref, middle_ref, own_ref, *refs):
        far, (out_ref, held) = refs[:-2], refs[-2:]
        image = pl.program_id(0)
        live = (iota((PAD, 1), 0) < IMG_TOK) & (image < count_ref[0])
        both = own_ref[0].astype(F32) + read_far(far).astype(F32)
        result = jnp.where(live, 1.0, 0.0) * (middle_ref[0] + both)
        for k in range(images):

            @pl.when(image == k)
            def _():
                held[pl.ds(k * IMG_TOK, IMG_TOK), :] = result[:IMG_TOK]

        @pl.when(image == images - 1)
        def _():
            out_ref[...] = held[pl.ds(0, total), :].astype(BF16)

    tile = by_image(PAD, width)
    return run(
        body,
        (count, middle, sum_own, *far_arrays),
        [scalar_spec(), tile, tile, *far_specs],
        [resident((total, width))],
        [jax.ShapeDtypeStruct((total, width), BF16)],
        grid=(images,),
        scratch=[pltpu.VMEM((1000, width), F32)],
        cost=pl.CostEstimate(flops=2_000_000, bytes_accessed=6_000_000, transcendentals=0),
        name="emit",
    )[0][0]


def by_slice(
    tokens, cotangent, routes, image_count, capacity, norm1_gain, norm1_bias, w_qkv, bias_q, bias_v, w_out, bias_out,
    norm2_gain, norm2_bias, w_router, expert_in, expert_in_bias, expert_out, expert_out_bias,
):
    total, width = tokens.shape
    local = expert_in.shape[0]
    device = lax.axis_index("rep")
    mine = lax.axis_index("fsdp")
    core = device % 2
    small = jnp.stack([norm1_gain, norm1_bias, bias_q, bias_v, bias_out, norm2_gain, norm2_bias])
    small = jnp.pad(small, ((0, 9), (0, 3 * width - small.shape[1])))
    wide = jnp.concatenate([w_qkv, small], axis=0)
    tall = jnp.concatenate([w_out, jnp.pad(w_router, ((0, 0), (0, 128 - EXPERTS)))], axis=1)
    (tok, cot, route, ids, load), (wide_far, tall_far) = prepare(
        tokens, cotangent, routes, image_count, capacity, wide, tall, 0
    )
    wide, tall = (wide, wide_far), (tall, tall_far)
    base = (mine * (local * CAP)).reshape(1)
    net = Network()
    net.offer("C", cot, block_hops(True), 1, 2)
    net.offer("L", load, block_hops(True), 0, 0)
    idents = iter(range(1, 32))

    def staged(kernel, *args, rounds, steps=None):
        traffic, plan = net.plan(rounds, steps or list(range(len(rounds))))
        outs, arrived = kernel(*args, traffic, next(idents))
        net.land(plan, arrived)
        return outs

    own, far = (0, 0, 0), (0, 0, 1)
    packed, prob, mixed, middle, second, soft, soft_sum = staged(
        front, image_count, tok, ids, route, wide, tall, rounds=[2, 2], steps=[0, 3]
    )
    net.offer("S", second, block_hops(False), 1, 2)
    net.offer("P", soft_sum, block_hops(True), 0, 3)

    def sender(block):
        return net.block("S", block), net.block("C", block)

    slots = []
    taken = set()

    def take(blocks, rounds):
        taken.update(blocks)
        outs = staged(gather, base, local, [sender(b) for b in blocks], rounds=rounds)
        slots.append(outs)
        return outs

    def ready():
        return [b for b in block_hops(True) if b not in taken and net.complete("S", b) and net.complete("C", b)]

    slots_own = take([own], [3, 3])
    slots_far = take([far], [1, 1])
    made_own, made_far, back_own, back_far = staged(
        expert_layer, slots_own, slots_far, expert_in, expert_in_bias, expert_out, expert_out_bias,
        rounds=[3, 3, 3, 2], steps=[0, 4, 8, 12],
    )
    sum_far, drow_far, dgate_far = staged(
        combine, base, *sender(far), made_far, back_far, rounds=[1, 1], steps=[0, 3]
    )
    once = {far: ("y", own)}
    net.offer("D", drow_far, once, 1, 0)
    net.offer("G", dgate_far, once, 0, 0)
    net.offer("M", sum_far, once, 1, 4)
    sum_own, drow_own, dgate_own = staged(
        combine, base, *sender(own), made_own, back_own, rounds=[1, 1], steps=[0, 3]
    )
    take(ready()[:2], [1, 1, 1])
    blocks = list(block_hops(True))

    def everyone(name):
        rows = [load if name == "L" else soft_sum] + [array for b in blocks for array, _ in net.block(name, b)]
        mine_sum = jnp.sum(jnp.concatenate(rows, axis=0), axis=0)[0:1]
        return mine_sum + lax.ppermute(mine_sum, "rep", [(i, i ^ 1) for i in range(16)])

    loads = everyone("L")
    live = loads[:, 64:65]
    share = (loads[:, :EXPERTS] + loads[:, EXPERTS : 2 * EXPERTS]) / (2.0 * live)
    aux = jnp.pad(EXPERTS * share / live, ((0, 0), (0, 128 - EXPERTS)))
    grad_tokens, pack = staged(
        finish, image_count, tok, cot, (packed, prob, mixed, middle, second, soft), route, drow_own,
        net.block("D", far), dgate_own, net.block("G", far), aux, wide, tall, total,
        rounds=[1, 2, 1, 2, 1],
    )
    owned = lax.psum_scatter(pack, "fsdp", scatter_dimension=0, tiled=True)
    owned = lax.psum(owned, "rep")[0].astype(F32)
    while len(taken) < 16:
        now = ready()[:4]
        left = bool(net.missing())
        take(now, [2] * (2 * len(now)) if left else [])
    outputs = emit(image_count, middle, sum_own, net.block("M", far), total)
    row_slots = [pair[0] for pair in slots]
    grad_slots = [pair[1] for pair in slots]
    prob_total = everyone("P")
    where = jnp.stack([device // 2, core]).astype(jnp.int32)
    keep_in, send_in, keep_out, send_out, d_bias, d_out_bias = slice_grads(
        where, row_slots, grad_slots, expert_in, expert_in_bias, expert_out
    )
    swap = [(i, i ^ 1) for i in range(16)]
    got_in, got_out, got_bias, got_out_bias = (
        lax.ppermute(v, "rep", swap) for v in (send_in, send_out, d_bias, d_out_bias)
    )
    bias = (d_bias + got_bias)[:, 0]
    out_bias = (d_out_bias + got_out_bias)[:, 0]
    half = bias.shape[1] // 2
    piece = width // 16
    expert_grads = (
        keep_in + got_in.astype(F32),
        lax.dynamic_slice_in_dim(bias, core * half, half, axis=1),
        keep_out + got_out.astype(F32),
        lax.dynamic_slice_in_dim(out_bias, device * piece, piece, axis=1),
    )

    balance_loss = jnp.sum(aux * prob_total)
    half = width // 2
    owned = (
        owned[half, :half],
        owned[half + 1, :half],
        owned[:half, : 3 * width],
        owned[half + 2, :half],
        owned[half + 3, :half],
        owned[:half, 3 * width : 4 * width],
        owned[half + 4, :half],
        owned[half + 5, :half],
        owned[half + 6, :half],
        owned[:half, 4 * width : 4 * width + EXPERTS],
    )
    return (outputs, grad_tokens, balance_loss) + owned + expert_grads


def solution(mesh):
    in_specs = (
        P(("rep", "fsdp"), None),
        P(("rep", "fsdp"), None),
        P(("rep", "fsdp"), None),
        P(("rep", "fsdp")),
        P(("rep", "fsdp")),
        P("fsdp"),
        P("fsdp"),
        P("fsdp", None),
        P("fsdp"),
        P("fsdp"),
        P("fsdp", None),
        P("fsdp"),
        P("fsdp"),
        P("fsdp"),
        P("fsdp", None),
        P("fsdp", None, None),
        P("fsdp", None),
        P("fsdp", None, None),
        P("fsdp", None),
    )
    out_specs = (
        P(("rep", "fsdp"), None),
        P(("rep", "fsdp"), None),
        P(),
        P("fsdp"),
        P("fsdp"),
        P("fsdp", None),
        P("fsdp"),
        P("fsdp"),
        P("fsdp", None),
        P("fsdp"),
        P("fsdp"),
        P("fsdp"),
        P("fsdp", None),
        P("fsdp", None, "rep"),
        P("fsdp", "rep"),
        P("fsdp", "rep", None),
        P("fsdp", "rep"),
    )
    program = by_slice if mesh.shape["rep"] == 16 and mesh.shape["fsdp"] == 2 else shards
    return jax.shard_map(program, mesh=mesh, in_specs=in_specs, out_specs=out_specs, check_vma=False)
```

```python
import jax
import jax.numpy as jnp
from jax import lax
from jax.experimental import pallas as pl
from jax.experimental.pallas import tpu as pltpu
from jax.sharding import PartitionSpec as P

HEADS = 8
HEAD_DIM = 64
EXPERTS = 32
IMG_TOK = 197
CAP = 80


def norm_rows(values, norm_gain, offset):
    average = jnp.mean(values, axis=-1, keepdims=True)
    centred = values - average
    variance = jnp.mean(centred * centred, axis=-1, keepdims=True)
    return centred * lax.rsqrt(variance + 1e-06) * norm_gain + offset


def slot_table(choices, alive_mask, limit, row_total):
    pair_expert = jnp.concatenate([choices[:, 0], choices[:, 1]])
    live_pairs = jnp.concatenate([alive_mask, alive_mask])
    expert_ids = jnp.arange(EXPERTS, dtype=jnp.int32)
    onehot = ((pair_expert[:, None] == expert_ids[None, :]) & live_pairs[:, None]).astype(jnp.int32)
    before = jnp.cumsum(onehot, axis=0) - onehot
    position = jnp.sum(before * onehot, axis=1)
    kept_pairs = live_pairs & (position < limit)
    pair_slot = pair_expert * CAP + position
    pair_token = jnp.concatenate(
        [jnp.arange(row_total, dtype=jnp.int32), jnp.arange(row_total, dtype=jnp.int32)]
    )
    slot_owner = jnp.full((EXPERTS * CAP,), row_total, jnp.int32)
    target = jnp.where(kept_pairs, pair_slot, EXPERTS * CAP)
    slot_owner = slot_owner.at[target].set(pair_token, mode="drop")
    safe_slot = jnp.where(kept_pairs, pair_slot, 0)
    return (slot_owner, kept_pairs, safe_slot, target, onehot)


def shards(
    tokens,
    cotangent,
    routes,
    image_count,
    capacity,
    norm1_gain,
    norm1_bias,
    w_qkv,
    bias_q,
    bias_v,
    w_out,
    bias_out,
    norm2_gain,
    norm2_bias,
    w_router,
    expert_in,
    expert_in_bias,
    expert_out,
    expert_out_bias,
):
    rows_count = tokens.shape[0]
    model_width = tokens.shape[1]
    image_total = rows_count // IMG_TOK
    score_scale = HEAD_DIM ** (-0.5)
    image_rows = jnp.arange(rows_count, dtype=jnp.int32) // IMG_TOK
    alive_mask = image_rows < image_count[0]
    alive_float = alive_mask.astype(jnp.float32)[:, None]
    slot_owner, kept_pairs, safe_slot, target, onehot = slot_table(
        routes, alive_mask, capacity[0], rows_count
    )
    kept_float = kept_pairs.astype(jnp.float32)
    load_local = jnp.sum(onehot.astype(jnp.float32), axis=0)
    live_local = jnp.sum(alive_float)
    load_total, live_total = lax.psum((load_local, live_local), ("rep", "fsdp"))
    gathered = (
        lax.all_gather(norm1_gain, "fsdp", axis=0, tiled=True),
        lax.all_gather(norm1_bias, "fsdp", axis=0, tiled=True),
        lax.all_gather(w_qkv, "fsdp", axis=0, tiled=True),
        lax.all_gather(bias_q, "fsdp", axis=0, tiled=True),
        lax.all_gather(bias_v, "fsdp", axis=0, tiled=True),
        lax.all_gather(w_out, "fsdp", axis=0, tiled=True),
        lax.all_gather(bias_out, "fsdp", axis=0, tiled=True),
        lax.all_gather(norm2_gain, "fsdp", axis=0, tiled=True),
        lax.all_gather(norm2_bias, "fsdp", axis=0, tiled=True),
        lax.all_gather(w_router, "fsdp", axis=0, tiled=True),
    )
    (
        gain_one,
        shift_one,
        qkv_full,
        query_bias,
        value_bias,
        out_full,
        out_bias,
        gain_two,
        shift_two,
        router_full,
    ) = gathered
    gain_one = gain_one.astype(jnp.float32)
    shift_one = shift_one.astype(jnp.float32)
    gain_two = gain_two.astype(jnp.float32)
    shift_two = shift_two.astype(jnp.float32)
    inputs = tokens.astype(jnp.float32)
    normed = norm_rows(inputs, gain_one, shift_one)
    normed_low = normed.astype(jnp.bfloat16)
    bias_row = jnp.concatenate([query_bias, jnp.zeros_like(query_bias), value_bias]).astype(
        jnp.float32
    )
    packed_low = (
        jnp.dot(normed_low, qkv_full, preferred_element_type=jnp.float32) + bias_row
    ).astype(jnp.bfloat16)
    image_shape = (image_total, IMG_TOK, HEADS, HEAD_DIM)
    queries = packed_low[:, :model_width].reshape(image_shape)
    all_keys = packed_low[:, model_width : 2 * model_width].reshape(image_shape)
    valued = packed_low[:, 2 * model_width :].reshape(image_shape)

    def score_block():
        return (
            jnp.einsum("iqhd,ikhd->hiqk", queries, all_keys, preferred_element_type=jnp.float32)
            * score_scale
        )

    scores = score_block()
    row_peak = jnp.max(scores, axis=-1, keepdims=True)
    exp_scores = jnp.exp(scores - row_peak)
    totals = jnp.sum(exp_scores, axis=-1, keepdims=True)
    log_total = row_peak + jnp.log(totals)
    attn_low = (exp_scores / totals).astype(jnp.bfloat16)
    mixed_low = (
        jnp.einsum("hiqk,ikhd->iqhd", attn_low, valued, preferred_element_type=jnp.float32)
        .reshape(rows_count, model_width)
        .astype(jnp.bfloat16)
    )
    middle = (
        inputs
        + jnp.dot(mixed_low, out_full, preferred_element_type=jnp.float32)
        + out_bias.astype(jnp.float32)
    )
    second_low = norm_rows(middle, gain_two, shift_two).astype(jnp.bfloat16)
    logits = jnp.dot(second_low, router_full, preferred_element_type=jnp.float32)
    expert_ids = jnp.arange(EXPERTS, dtype=jnp.int32)
    first_hot = (routes[:, 0:1] == expert_ids[None, :]).astype(jnp.float32)
    second_hot = (routes[:, 1:2] == expert_ids[None, :]).astype(jnp.float32)

    def gate_terms(logit_rows):
        router_probs = jax.nn.softmax(logit_rows, axis=-1)
        pick_one = jnp.sum(router_probs * first_hot, axis=-1)
        pick_two = jnp.sum(router_probs * second_hot, axis=-1)
        pick_total = pick_one + pick_two
        return (pick_one / pick_total, pick_two / pick_total, router_probs)

    (gate_first, gate_second, router_probs), gate_back = jax.vjp(gate_terms, logits)
    padded_rows = jnp.concatenate([second_low, jnp.zeros((1, model_width), jnp.bfloat16)], axis=0)
    sent_rows = padded_rows[slot_owner].reshape(EXPERTS, CAP, model_width)
    received = lax.all_to_all(sent_rows, "fsdp", split_axis=0, concat_axis=1, tiled=True)
    raised = (
        jnp.einsum("esd,edf->esf", received, expert_in, preferred_element_type=jnp.float32)
        + expert_in_bias.astype(jnp.float32)[:, None, :]
    )
    active, gelu_back = jax.vjp(jax.nn.gelu, raised)
    active_low = active.astype(jnp.bfloat16)
    produced = (
        jnp.einsum("esf,efd->esd", active_low, expert_out, preferred_element_type=jnp.float32)
        + expert_out_bias.astype(jnp.float32)[:, None, :]
    ).astype(jnp.bfloat16)
    returned = lax.all_to_all(produced, "fsdp", split_axis=1, concat_axis=0, tiled=True).reshape(
        EXPERTS * CAP, model_width
    )
    pair_rows = returned[safe_slot].astype(jnp.float32)
    pair_weight = jnp.concatenate([gate_first, gate_second]) * kept_float
    expert_sum = jnp.sum(
        (pair_rows * pair_weight[:, None]).reshape(2, rows_count, model_width), axis=0
    )
    outputs = (alive_float * (middle + expert_sum)).astype(jnp.bfloat16)
    upstream = cotangent.astype(jnp.float32) * alive_float
    pair_grad = jnp.concatenate([upstream, upstream], axis=0)
    gate_grads = jnp.sum(pair_grad * pair_rows, axis=1) * kept_float
    slot_gate = jnp.zeros((EXPERTS * CAP,), jnp.float32).at[target].set(pair_weight, mode="drop")
    padded_grad = jnp.concatenate([upstream, jnp.zeros((1, model_width), jnp.float32)], axis=0)
    slot_grads = (
        (padded_grad[slot_owner] * slot_gate[:, None])
        .astype(jnp.bfloat16)
        .reshape(EXPERTS, CAP, model_width)
    )
    grad_received = lax.all_to_all(slot_grads, "fsdp", split_axis=0, concat_axis=1, tiled=True)
    grad_active = jnp.einsum(
        "esd,efd->esf", grad_received, expert_out, preferred_element_type=jnp.float32
    )
    (grad_raised,) = gelu_back(grad_active)
    grad_raised_low = grad_raised.astype(jnp.bfloat16)
    grad_rows = jnp.einsum(
        "esf,edf->esd", grad_raised_low, expert_in, preferred_element_type=jnp.float32
    ).astype(jnp.bfloat16)
    back_rows = lax.all_to_all(grad_rows, "fsdp", split_axis=1, concat_axis=0, tiled=True).reshape(
        EXPERTS * CAP, model_width
    )
    expert_part = jnp.sum(
        (back_rows[safe_slot].astype(jnp.float32) * kept_float[:, None]).reshape(
            2, rows_count, model_width
        ),
        axis=0,
    )
    local_in = jnp.einsum(
        "esd,esf->edf", received, grad_raised_low, preferred_element_type=jnp.float32
    )
    local_in_bias = jnp.sum(grad_raised_low.astype(jnp.float32), axis=1)
    local_out = jnp.einsum(
        "esf,esd->efd", active_low, grad_received, preferred_element_type=jnp.float32
    )
    local_out_bias = jnp.sum(grad_received.astype(jnp.float32), axis=1)
    grad_in_weight, grad_in_bias, grad_out_weight, grad_out_expert_bias = (
        lax.psum_scatter(local_in, "rep", scatter_dimension=2, tiled=True),
        lax.psum_scatter(local_in_bias, "rep", scatter_dimension=1, tiled=True),
        lax.psum_scatter(local_out, "rep", scatter_dimension=1, tiled=True),
        lax.psum_scatter(local_out_bias, "rep", scatter_dimension=1, tiled=True),
    )
    prob_local = jnp.sum(router_probs * alive_float, axis=0)
    prob_total = lax.psum(prob_local, ("rep", "fsdp"))
    share = load_total / (2.0 * live_total)
    balance_loss = EXPERTS * jnp.sum(share * prob_total / live_total)
    aux_grad = alive_float * (EXPERTS * share / live_total)[None, :]
    (grad_logits,) = gate_back((gate_grads[:rows_count], gate_grads[rows_count:], aux_grad))
    grad_logits_low = grad_logits.astype(jnp.bfloat16)
    grad_router = jnp.dot(second_low.T, grad_logits_low, preferred_element_type=jnp.float32)
    grad_second = (
        jnp.dot(grad_logits_low, router_full.T, preferred_element_type=jnp.float32) + expert_part
    )
    _, norm_two_back = jax.vjp(norm_rows, middle, gain_two, shift_two)
    grad_mid_norm, grad_gain_two, grad_shift_two = norm_two_back(grad_second)
    grad_middle = upstream + grad_mid_norm
    grad_att_low = grad_middle.astype(jnp.bfloat16)
    grad_out_proj = jnp.dot(mixed_low.T, grad_att_low, preferred_element_type=jnp.float32)
    grad_out_bias = jnp.sum(grad_att_low.astype(jnp.float32), axis=0)
    grad_mixed = (
        jnp.dot(grad_att_low, out_full.T, preferred_element_type=jnp.float32)
        .astype(jnp.bfloat16)
        .reshape(image_shape)
    )
    recomputed = jnp.exp(score_block() - log_total)
    grad_weights = jnp.einsum(
        "iqhd,ikhd->hiqk", grad_mixed, valued, preferred_element_type=jnp.float32
    )
    grad_values = jnp.einsum(
        "hiqk,iqhd->ikhd",
        recomputed.astype(jnp.bfloat16),
        grad_mixed,
        preferred_element_type=jnp.float32,
    )
    inner_sum = jnp.sum(grad_weights * recomputed, axis=-1, keepdims=True)
    grad_scores = (recomputed * (grad_weights - inner_sum)).astype(jnp.bfloat16)
    grad_queries = (
        jnp.einsum("hiqk,ikhd->iqhd", grad_scores, all_keys, preferred_element_type=jnp.float32)
        * score_scale
    )
    grad_keys = (
        jnp.einsum("hiqk,iqhd->ikhd", grad_scores, queries, preferred_element_type=jnp.float32)
        * score_scale
    )
    grad_packed_low = jnp.concatenate(
        [
            grad_queries.reshape(rows_count, model_width),
            grad_keys.reshape(rows_count, model_width),
            grad_values.reshape(rows_count, model_width),
        ],
        axis=1,
    ).astype(jnp.bfloat16)
    grad_qkv = jnp.dot(normed_low.T, grad_packed_low, preferred_element_type=jnp.float32)
    packed_sums = jnp.sum(grad_packed_low.astype(jnp.float32), axis=0)
    grad_query_bias = packed_sums[:model_width]
    grad_value_bias = packed_sums[2 * model_width :]
    grad_normed = jnp.dot(grad_packed_low, qkv_full.T, preferred_element_type=jnp.float32)
    _, norm_one_back = jax.vjp(norm_rows, inputs, gain_one, shift_one)
    grad_input_norm, grad_gain_one, grad_shift_one = norm_one_back(grad_normed)
    grad_tokens = grad_middle + grad_input_norm
    local_grads = (
        grad_gain_one,
        grad_shift_one,
        grad_qkv,
        grad_query_bias,
        grad_value_bias,
        grad_out_proj,
        grad_out_bias,
        grad_gain_two,
        grad_shift_two,
        grad_router,
    )
    shares = (
        lax.psum_scatter(local_grads[0], "fsdp", scatter_dimension=0, tiled=True),
        lax.psum_scatter(local_grads[1], "fsdp", scatter_dimension=0, tiled=True),
        lax.psum_scatter(local_grads[2], "fsdp", scatter_dimension=0, tiled=True),
        lax.psum_scatter(local_grads[3], "fsdp", scatter_dimension=0, tiled=True),
        lax.psum_scatter(local_grads[4], "fsdp", scatter_dimension=0, tiled=True),
        lax.psum_scatter(local_grads[5], "fsdp", scatter_dimension=0, tiled=True),
        lax.psum_scatter(local_grads[6], "fsdp", scatter_dimension=0, tiled=True),
        lax.psum_scatter(local_grads[7], "fsdp", scatter_dimension=0, tiled=True),
        lax.psum_scatter(local_grads[8], "fsdp", scatter_dimension=0, tiled=True),
        lax.psum_scatter(local_grads[9], "fsdp", scatter_dimension=0, tiled=True),
    )
    owned = lax.psum(
        (
            shares[0],
            shares[1],
            shares[2],
            shares[3],
            shares[4],
            shares[5],
            shares[6],
            shares[7],
            shares[8],
            shares[9],
        ),
        "rep",
    )
    return (
        (outputs, grad_tokens, balance_loss)
        + tuple(owned)
        + (grad_in_weight, grad_in_bias, grad_out_weight, grad_out_expert_bias)
    )


def gelu_pair(value):
    root = 0.7978845608028654
    square = value * value
    bend = jnp.tanh(root * value * (1.0 + 0.044715 * square))
    half = 0.5 * (1.0 + bend)
    slope = half + 0.5 * value * (1.0 - bend * bend) * root * (1.0 + 3 * 0.044715 * square)
    return value * half, slope


def slice_grads_body(*refs, senders):
    parts, refs = refs[: sum(senders)], refs[sum(senders) :]
    in_ref, in_bias_ref, out_ref, keep_in, send_in, keep_out, send_out, d_bias, d_out_bias = refs
    core = lax.axis_index("rep") % 2
    width = in_ref.shape[1]

    def stacked(pieces):
        return jnp.concatenate([piece[...].reshape(-1, width) for piece in pieces], axis=0)

    rows = stacked(parts[: senders[0]])
    grads = stacked(parts[senders[0] :])
    first = in_ref[0]
    second = out_ref[0]
    raised = jnp.dot(rows, first, preferred_element_type=jnp.float32) + in_bias_ref[0].astype(
        jnp.float32
    )
    active, slope = gelu_pair(raised)
    active = active.astype(jnp.bfloat16)
    back = lax.dot_general(
        grads, second, (((1,), (1,)), ((), ())), preferred_element_type=jnp.float32
    )
    draised = (back * slope).astype(jnp.bfloat16)
    over_rows = (((0,), (0,)), ((), ()))
    g_in = lax.dot_general(rows, draised, over_rows, preferred_element_type=jnp.float32)
    g_out = lax.dot_general(active, grads, over_rows, preferred_element_type=jnp.float32)
    half = g_in.shape[1] // 2
    first_core = core == 0
    keep_in[0] = jnp.where(first_core, g_in[:, :half], g_in[:, half:])
    send_in[0] = jnp.where(first_core, g_in[:, half:], g_in[:, :half]).astype(jnp.bfloat16)
    keep_out[0] = jnp.where(first_core, g_out[:half], g_out[half:])
    send_out[0] = jnp.where(first_core, g_out[half:], g_out[:half]).astype(jnp.bfloat16)
    d_bias[0] = jnp.sum(draised.astype(jnp.float32), axis=0, keepdims=True)
    d_out_bias[0] = jnp.sum(grads.astype(jnp.float32), axis=0, keepdims=True)


def slice_grads(rows, grads, first, first_bias, second, chain, ident):
    experts, width, hidden = first.shape
    cap = rows[0].shape[2]
    slots = cap * sum(piece.shape[1] for piece in rows)
    part = 256
    half = part // 2
    f32 = jnp.float32
    def chip():
        return lax.axis_index("rep") // 2

    return run(
        lambda *refs: slice_grads_body(*refs, senders=(len(rows), len(grads))),
        (*rows, *grads, first, first_bias.reshape(experts, 1, hidden), second),
        [pl.BlockSpec((1,) + piece.shape[1:], lambda e: (e, 0, 0, 0)) for piece in (*rows, *grads)]
        + [
            pl.BlockSpec((1, width, part), lambda e: (e, 0, chip())),
            pl.BlockSpec((1, 1, part), lambda e: (e, 0, chip())),
            pl.BlockSpec((1, part, width), lambda e: (e, chip(), 0)),
        ],
        [by_image(width, half)] * 2 + [by_image(half, width)] * 2 + [by_image(1, part), by_image(1, width)],
        [
            jax.ShapeDtypeStruct((experts, width, half), f32),
            jax.ShapeDtypeStruct((experts, width, half), jnp.bfloat16),
            jax.ShapeDtypeStruct((experts, half, width), f32),
            jax.ShapeDtypeStruct((experts, half, width), jnp.bfloat16),
            jax.ShapeDtypeStruct((experts, 1, part), f32),
            jax.ShapeDtypeStruct((experts, 1, width), f32),
        ],
        grid=(experts,),
        cost=pl.CostEstimate(
            flops=8 * experts * slots * width * part,
            bytes_accessed=4 * experts * (slots * width + 3 * width * part),
            transcendentals=experts * slots * part,
        ),
        name="slice_grads",
        chain=chain,
        ident=ident,
    )


F32 = jnp.float32
BF16 = jnp.bfloat16
PAD = 208
ROOT_AXES = ("rep", "fsdp")
OVER_COLS = (((1,), (1,)), ((), ()))
OVER_ROWS = (((0,), (0,)), ((), ()))


def dot(left, right):
    return jnp.dot(left, right, preferred_element_type=F32)


def dot_cols(left, right):
    return lax.dot_general(left, right, OVER_COLS, preferred_element_type=F32)


def dot_rows(left, right):
    return lax.dot_general(left, right, OVER_ROWS, preferred_element_type=F32)


def iota(shape, axis):
    return lax.broadcasted_iota(jnp.int32, shape, axis)


def resident(shape):
    return pl.BlockSpec(shape, lambda *_: (0,) * len(shape))


def by_image(*shape):
    return pl.BlockSpec((1,) + shape, lambda i, *_: (i,) + (0,) * len(shape))


def scalar_spec():
    return pl.BlockSpec(memory_space=pltpu.SMEM)


def partner(link):
    device, side = lax.axis_index("rep"), lax.axis_index("fsdp")
    if link == "y":
        return {"rep": device, "fsdp": 1 - side}
    depth = device // 4
    step = {
        "core": 1 - 2 * (device % 2),
        "x": 2 - 4 * ((device // 2) % 2),
        "near": 4 - 8 * (depth % 2),
        "inner": 12 - 8 * depth,
        "skip": 8 - 16 * (depth // 2),
    }[link]
    return {"rep": device + step, "fsdp": side}


def only_if(condition, action):
    if condition is None:
        action()
    else:
        pl.when(condition)(action)


class Move:
    def __init__(self, link, source, target, needs=()):
        self.link, self.source, self.target, self.needs = link, source, target, needs

    def roles(self):
        depth = lax.axis_index("rep") // 4
        middle = (depth % 3) > 0
        if self.link == "inner":
            return middle, middle
        if self.link in ("outward", "skip"):
            return middle, (depth % 3) == 0
        return None, None

    def copy(self, refs, send, recv):
        return pltpu.make_async_remote_copy(
            src_ref=self.source(refs),
            dst_ref=self.target(refs),
            send_sem=send,
            recv_sem=recv,
            device_id=partner("near" if self.link == "outward" else self.link),
            device_id_type=pl.DeviceIdType.MESH,
        )


class Traffic:
    def __init__(self, sources, targets, rounds, steps):
        self.sources, self.targets, self.rounds, self.steps = sources, targets, rounds, steps

    def count(self):
        return sum(len(moves) for moves in self.rounds)

    def links(self):
        return {("near" if m.link == "outward" else m.link) for moves in self.rounds for m in moves}

    def start(self, which, refs, send, recv, arrived):
        moves = [m for moves in self.rounds for m in moves]
        at = sum(len(moves) for moves in self.rounds[:which])
        for k, move in enumerate(self.rounds[which]):
            for index in move.needs:
                if index not in arrived:
                    arrived.add(index)
                    only_if(moves[index].roles()[1], moves[index].copy(refs, send.at[index], recv.at[index]).wait_recv)
            only_if(move.roles()[0], move.copy(refs, send.at[at + k], recv.at[at + k]).start)

    def finish(self, refs, send, recv, arrived):
        moves = [m for moves in self.rounds for m in moves]
        for index, move in enumerate(moves):
            copy = move.copy(refs, send.at[index], recv.at[index])
            sends, receives = move.roles()
            only_if(sends, copy.wait_send)
            if index not in arrived:
                only_if(receives, copy.wait_recv)


def greet(links):
    barrier = pltpu.get_barrier_semaphore()
    middle = ((lax.axis_index("rep") // 4) % 3) > 0
    plain = [link for link in ("core", "x", "y", "near", "skip") if link in links]
    for link in plain:
        pl.semaphore_signal(barrier, inc=1, device_id=partner(link), device_id_type=pl.DeviceIdType.MESH)
    if "inner" in links:

        @pl.when(middle)
        def _():
            pl.semaphore_signal(
                barrier, inc=1, device_id=partner("inner"), device_id_type=pl.DeviceIdType.MESH
            )

    if "inner" in links:

        @pl.when(middle)
        def _():
            pl.semaphore_wait(barrier, len(plain) + 1)

        @pl.when(~middle)
        def _():
            if plain:
                pl.semaphore_wait(barrier, len(plain))

    else:
        pl.semaphore_wait(barrier, len(plain))


class Chain:
    def __init__(self, args, in_specs, out_specs, out_shape, scratch, links, actions):
        self.args, self.in_specs, self.out_specs, self.out_shape = args, in_specs, out_specs, out_shape
        self.scratch, self.links, self.actions = scratch, links, actions


def run(
    body, args, in_specs, out_specs, out_shape, *,
    name, grid=(1,), scratch=(), cost=None, traffic=None, chain=None, ident=None,
):
    if (traffic is None or traffic.count() == 0) and chain is None:
        outs = pl.pallas_call(
            body, grid=grid, in_specs=in_specs, out_specs=out_specs, out_shape=out_shape,
            scratch_shapes=list(scratch), cost_estimate=cost, name=name,
        )(*args)
        return outs, [], []
    traffic = traffic or Traffic([], [], [], [])
    chain = chain or Chain([], [], [], [], [], set(), [])
    n_in, n_src, n_out, n_dst = len(args), len(traffic.sources), len(out_shape), len(traffic.targets)
    anywhere = pl.BlockSpec(memory_space=pl.ANY)
    sizes = (n_in, n_src, len(chain.args), n_out, n_dst, len(chain.out_shape), len(scratch), len(chain.scratch))
    links = traffic.links() | chain.links

    def carried(*refs):
        groups = []
        for size in sizes:
            groups.append(refs[:size])
            refs = refs[size:]
        ins, sources, chain_in, outs, targets, chain_out, held, chain_held = groups
        ends = (sources, targets)
        step = pl.program_id(0)
        pl.when(step == 0)(lambda: greet(links))
        arrived = set()
        for which, at in enumerate(traffic.steps):

            @pl.when(step == at)
            def _():
                traffic.start(which, ends, *refs, arrived)

        for at, action in chain.actions[:-1]:

            @pl.when(step == at)
            def _():
                action(*chain_in, *chain_out, *chain_held)

        body(*ins, *outs, *held)

        @pl.when(step == grid[0] - 1)
        def _():
            if traffic.count():
                traffic.finish(ends, *refs, arrived)
            if chain.actions:
                chain.actions[-1][1](*chain_in, *chain_out, *chain_held)

    count = traffic.count()
    semaphores = [pltpu.SemaphoreType.DMA((count,))] * 2 if count else []
    outs = pl.pallas_call(
        carried,
        grid=grid,
        in_specs=list(in_specs) + [anywhere] * n_src + list(chain.in_specs),
        out_specs=list(out_specs) + [anywhere] * n_dst + list(chain.out_specs),
        out_shape=list(out_shape) + list(traffic.targets) + list(chain.out_shape),
        scratch_shapes=list(scratch) + list(chain.scratch) + semaphores,
        compiler_params=pltpu.CompilerParams(collective_id=ident, has_side_effects=True),
        cost_estimate=cost,
        name=name,
    )(*args, *traffic.sources, *chain.args)
    return outs[:n_out], outs[n_out : n_out + n_dst], outs[n_out + n_dst :]


COT_PATHS = {
    (0, 0, 1): ("y", (0, 0, 0), -1.500),
    (0, 1, 0): ("x", (0, 0, 0), 3.002),
    (0, 1, 1): ("x", (0, 0, 1), 2.463),
    (1, 0, 0): ("near", (0, 0, 0), 5.503),
    (1, 0, 1): ("y", (1, 0, 0), 0.791),
    (1, 1, 0): ("near", (0, 1, 0), 0.934),
    (1, 1, 1): ("x", (1, 0, 1), 1.171),
    (2, 0, 0): ("reach", (0, 0, 0), 2.419),
    (2, 0, 1): ("y", (2, 0, 0), 2.680),
    (2, 1, 0): ("reach", (0, 1, 0), 0.624),
    (2, 1, 1): ("x", (2, 0, 1), 5.712),
    (3, 0, 0): ("inner", (1, 0, 0), 0.725),
    (3, 0, 1): ("y", (3, 0, 0), 2.905),
    (3, 1, 0): ("x", (3, 0, 0), 4.267),
    (3, 1, 1): ("x", (3, 0, 1), 3.366),
}
ROW_PATHS = {
    (0, 0, 1): ("y", (0, 0, 0), -1.400),
    (0, 1, 0): ("x", (0, 0, 0), 0.507),
    (0, 1, 1): ("x", (0, 0, 1), 3.006),
    (1, 0, 0): ("near", (0, 0, 0), 4.270),
    (1, 0, 1): ("y", (1, 0, 0), 1.765),
    (1, 1, 0): ("near", (0, 1, 0), 5.532),
    (1, 1, 1): ("x", (1, 0, 1), 0.781),
    (2, 0, 0): ("inner", (0, 0, 0), 2.116),
    (2, 0, 1): ("y", (2, 0, 0), 1.823),
    (2, 1, 0): ("x", (2, 0, 0), 0.695),
    (2, 1, 1): ("y", (2, 1, 0), 3.141),
    (3, 0, 0): ("reach", (1, 0, 0), 3.737),
    (3, 0, 1): ("y", (3, 0, 0), 2.332),
    (3, 1, 0): ("inner", (1, 1, 0), 3.735),
    (3, 1, 1): ("x", (3, 0, 1), 4.908),
}
FAR_FIRST = {(0, 0, 1): ("y", (0, 0, 0), -2.0)}
FAR_LAST = {(0, 0, 1): ("y", (0, 0, 0), 5.198)}


class Network:
    def __init__(self):
        self.have, self.hops, self.weight, self.pieces = {}, {}, {}, {}

    def offer(self, name, array, hops, weight=1):
        self.hops[name], self.weight[name] = hops, weight
        self.pieces[name] = array.shape[0]
        for p in range(array.shape[0]):
            self.have[name, (0, 0, 0), p] = (array, p)

    def order(self, item):
        name, block, p = item
        return self.hops[name][block][2], block, p

    def missing(self):
        return [
            (name, block, p)
            for name in self.hops
            for block in self.hops[name]
            for p in range(self.pieces[name])
            if (name, block, p) not in self.have
        ]

    def complete(self, name, block):
        return all((name, block, p) in self.have for p in range(self.pieces[name]))

    def plan(self, room, steps, times):
        waiting = sorted(self.missing(), key=self.order)
        landed, rounds, going = {}, [[] for _ in steps], {}
        free = dict.fromkeys(("x", "y", "near", "inner"), 0.0)
        uses = {"reach": (("inner", 2), ("near", 1))}
        lag = 0.4

        def fill(link, now, weight, horizon):
            spans = [(on, max(free[on], now), n * weight) for on, n in uses.get(link, ((link, 1),))]
            if weight and any(begin >= horizon or begin + length > room + 0.01 for _, begin, length in spans):
                return None
            for on, begin, length in spans:
                if length:
                    free[on] = begin + length
            return max(begin + length for _, begin, length in spans) + lag

        for r, now in enumerate(times):
            horizon = times[r + 1] + 0.5 if r + 1 < len(times) else room
            for item in [i for i, (_, at) in going.items() if at <= now]:
                done = fill("near", now, self.weight[item[0]], horizon)
                if done is not None:
                    rounds[r].append(("outward", item, item))
                    landed[item] = done
                    del going[item]
            for item in waiting:
                name, block, p = item
                if item in landed or item in going:
                    continue
                link, source, _ = self.hops[name][block]
                source = (name, source, p)
                if source not in self.have and landed.get(source, now + 1) > now:
                    continue
                if link == "inner":
                    left = room - max(free["near"], now + 1) - sum(self.weight[i[0]] for i in going)
                    if r + 1 >= len(times) or left < 1 + self.weight[name] or times[-1] < now + self.weight[name] + lag:
                        continue
                done = fill(link, now, self.weight[name], horizon)
                if done is None:
                    continue
                if link == "reach":
                    rounds[r] += [("inner", source, item), ("skip", source, item)]
                else:
                    rounds[r].append((link, source, item))
                if link == "inner":
                    going[item] = (r, done)
                else:
                    landed[item] = done
        for item in list(going):
            rounds[-1].append(("outward", item, item))
            landed[item] = room
        sources, targets, homes = [], [], {}
        for name, block, p in sorted(landed):
            homes.setdefault((name, block), []).append(p)
        order = list(homes)
        for name, block in order:
            model = self.have[name, (0, 0, 0), 0][0]
            targets.append(jax.ShapeDtypeStruct((len(homes[name, block]),) + model.shape[1:], model.dtype))

        def home(item):
            name, block, p = item
            return order.index((name, block)), homes[name, block].index(p)

        def origin(item):
            if item in landed:
                return (1,) + home(item)
            array, at = self.have[item]
            for k, known in enumerate(sources):
                if known is array:
                    return 0, k, at
            sources.append(array)
            return 0, len(sources) - 1, at

        moves = []
        for chosen in rounds:
            spans = []
            for link, source, item in sorted(chosen, key=lambda c: (c[0] not in ("outward", "inner"), *c)):
                a, b = origin(source), home(item)
                if spans:
                    link_, a_, b_, n = spans[-1]
                    if link_ == link and a_[:2] == a[:2] and b_[0] == b[0] and a[2] == a_[2] + n and b[1] == b_[1] + n:
                        spans[-1] = (link, a_, b_, n + 1)
                        continue
                spans.append((link, a, b, 1))
            flat = [m for made in moves for m in made]
            placed = []
            for link, a, b, n in spans:
                needs = [
                    k
                    for k, m in enumerate(flat)
                    if a[0] == 1 and m.home[0] == a[1] and m.home[1] < a[2] + n and a[2] < m.home[1] + m.size
                ]
                placed.append(self.move(link, a, b, n, needs))
            moves.append(placed)
        while moves and not moves[-1]:
            moves.pop()
        traffic = Traffic(sources, targets, moves, steps[: len(moves)])
        return traffic, (order, homes)

    @staticmethod
    def move(link, origin, home, count, needs):
        def source(refs):
            return refs[origin[0]][origin[1]].at[pl.ds(origin[2], count)]

        def target(refs):
            return refs[1][home[0]].at[pl.ds(home[1], count)]

        made = Move(link, source, target, needs)
        made.home, made.size = home, count
        return made

    def land(self, plan, arrays):
        order, homes = plan
        for key, array in zip(order, arrays):
            for at, p in enumerate(homes[key]):
                self.have[key[0], key[1], p] = (array, at)

    def block(self, name, block):
        return [self.have[name, block, p] for p in range(self.pieces[name])]


def evenly(room, steps, length, every=1):
    chosen = list(range(0, steps, every))
    return room, chosen, [step * length for step in chosen]


def gathering(room, senders, extra):
    busy = 2 * senders * 0.45
    times = [0.45 * step for step in range(2 * senders)]
    times += [busy + (step + 1) * max(0.5, room - busy) / (extra + 1) for step in range(extra)]
    return room, list(range(2 * senders + extra)), times


def standardise(values):
    average = jnp.mean(values, axis=-1, keepdims=True)
    centred = values - average
    variance = jnp.mean(centred * centred, axis=-1, keepdims=True)
    scale = lax.rsqrt(variance + 1e-06)
    return centred * scale, scale


def prep_body(count_ref, cap_ref, tok_ref, cot_ref, route_ref, tok_out, cot_out, route_out, ids_out, load_out, wide, narrow):
    pl.when(pl.program_id(0) == 0)(
        lambda: prep_rows(
            count_ref, cap_ref, tok_ref, cot_ref, route_ref, tok_out, cot_out, route_out, ids_out, load_out, wide, narrow
        )
    )


def prep_rows(count_ref, cap_ref, tok_ref, cot_ref, route_ref, tok_out, cot_out, route_out, ids_out, load_out, wide, narrow):
    images = tok_out.shape[0]
    total = tok_ref.shape[0]
    alive_images = count_ref[0]
    real = iota((PAD, 1), 0) < IMG_TOK

    def split(source, image):
        return source[pl.ds(image * IMG_TOK, PAD), :]

    wide[...] = jnp.zeros_like(wide)
    narrow[...] = jnp.zeros_like(narrow)
    wide[pl.ds(0, total), :] = tok_ref[...].astype(F32)
    for image in range(images):
        tok_out[image] = jnp.where(real, split(wide, image), 0.0).astype(BF16)
    wide[pl.ds(0, total), :] = cot_ref[...].astype(F32)
    narrow[pl.ds(0, total), :] = route_ref[...]
    routes = []
    lives = []
    for image in range(images):
        live = real & (image < alive_images)
        cot_out[image] = jnp.where(live, split(wide, image), 0.0).astype(BF16)
        picked = split(narrow, image)
        route_out[image] = picked
        routes.append(picked)
        lives.append(jnp.where(live, 1, 0))
    routes = jnp.concatenate(routes, axis=0)
    live = jnp.concatenate(lives, axis=0) > 0
    rows = images * PAD
    lane = iota((rows, 128), 1)
    first = (lane == routes[:, 0:1]) & live
    second = (lane == routes[:, 1:2] + EXPERTS) & live
    hot = jnp.where(first | second, 1.0, 0.0)
    below = jnp.where(iota((rows, rows), 0) > iota((rows, rows), 1), 1.0, 0.0).astype(BF16)
    before = dot(below, hot.astype(BF16))
    totals = jnp.sum(hot, axis=0, keepdims=True)
    place_one = jnp.sum(jnp.where(first, before, 0.0), axis=1, keepdims=True)
    place_two = jnp.sum(jnp.where(second, before, 0.0), axis=1, keepdims=True) + jnp.sum(
        jnp.where(lane == routes[:, 1:2], totals, 0.0), axis=1, keepdims=True
    )
    limit = cap_ref[0].astype(F32)
    keep_one = live & (place_one < limit)
    keep_two = live & (place_two < limit)
    slots = jnp.where(lane == 0, jnp.where(keep_one, routes[:, 0:1].astype(F32), -1.0), 0.0)
    slots = jnp.where(lane == 1, jnp.where(keep_one, place_one, 0.0), slots)
    slots = jnp.where(lane == 2, jnp.where(keep_two, routes[:, 1:2].astype(F32), -1.0), slots)
    slots = jnp.where(lane == 3, jnp.where(keep_two, place_two, 0.0), slots)
    for image in range(images):
        ids_out[image] = jnp.transpose(slots[image * PAD : (image + 1) * PAD])[0:8]
    lanes = iota((1, 128), 1)
    tokens_alive = (alive_images * IMG_TOK).astype(F32)
    load_out[0] = jnp.broadcast_to(jnp.where(lanes == 64, tokens_alive, totals), (8, 128))


def weight_traffic(wide, tall):
    def rows(array):
        half = array.shape[0] // 2
        return pl.ds(pl.multiple_of((lax.axis_index("rep") % 2) * half, 8), half)

    def fetch(at, array):
        return Move("y", lambda refs: refs[0][at].at[rows(array)], lambda refs: refs[1][at].at[rows(array)])

    def pass_on(at, array):
        there = lambda refs: refs[1][at].at[rows(array)]
        return Move("core", there, there, [at])

    arrays = (wide, tall)
    targets = [jax.ShapeDtypeStruct(a.shape, a.dtype) for a in arrays]
    rounds = [[make(at, a) for at, a in enumerate(arrays)] for make in (fetch, pass_on)]
    return Traffic(list(arrays), targets, rounds, [0, 1])


def prepare(tokens, cotangent, routes, image_count, capacity, wide, tall, ident):
    total, width = tokens.shape
    images = total // IMG_TOK
    shapes = [
        jax.ShapeDtypeStruct((images, PAD, width), BF16),
        jax.ShapeDtypeStruct((images, PAD, width), BF16),
        jax.ShapeDtypeStruct((images, PAD, 2), jnp.int32),
        jax.ShapeDtypeStruct((images, 8, PAD), F32),
        jax.ShapeDtypeStruct((1, 8, 128), F32),
    ]
    return run(
        prep_body,
        (image_count, capacity, tokens, cotangent, routes),
        [scalar_spec(), scalar_spec()] + [resident(a.shape) for a in (tokens, cotangent, routes)],
        [resident(a.shape) for a in shapes],
        shapes,
        grid=(2,),
        scratch=[pltpu.VMEM((1000, width), F32), pltpu.VMEM((1000, 2), jnp.int32)],
        cost=pl.CostEstimate(flops=300_000_000, bytes_accessed=6_000_000, transcendentals=0),
        name="prepare",
        traffic=weight_traffic(wide, tall),
        ident=ident,
    )


def place_halves(own, far, both):
    mine = lax.axis_index("fsdp")
    both[mine] = own[...]
    both[1 - mine] = far[...]


def vectors(wide_ref):
    return jnp.concatenate([wide_ref[0, 256:272, :256], wide_ref[1, 256:272, :256]], axis=1).astype(F32)


def front_body(
    count_ref, tok_ref, ids_ref, route_ref, wide_own, wide_far, tall_own, tall_far,
    packed_ref, prob_ref, mixed_ref, middle_ref, second_ref, soft_ref, sum_ref, wide_ref, tall_ref,
):
    @pl.when(pl.program_id(0) == 0)
    def _():
        sum_ref[...] = jnp.zeros_like(sum_ref)
        place_halves(wide_own, wide_far, wide_ref)
        place_halves(tall_own, tall_far, tall_ref)

    width = tok_ref.shape[-1]
    vec = vectors(wide_ref)
    inputs = tok_ref[0].astype(F32)
    normed = (standardise(inputs)[0] * vec[0:1] + vec[1:2]).astype(BF16)
    qkv = wide_ref[:, :256, :].reshape(width, 3 * width)
    raw = dot(normed, qkv)
    packed_ref[0, :, :width] = (raw[:, :width] + vec[2:3]).astype(BF16)
    packed_ref[0, :, width : 2 * width] = raw[:, width : 2 * width].astype(BF16)
    packed_ref[0, :, 2 * width :] = (raw[:, 2 * width :] + vec[3:4]).astype(BF16)
    low_lanes = iota((PAD, 128), 1) < HEAD_DIM
    real_key = iota((PAD, PAD), 1) < IMG_TOK
    for pair in range(HEADS // 2):
        at = pair * 128
        query = packed_ref[0, :, at : at + 128] * jnp.asarray(HEAD_DIM**-0.5, BF16)
        keys = packed_ref[0, :, width + at : width + at + 128]
        valued = packed_ref[0, :, 2 * width + at : 2 * width + at + 128]
        got = []
        for side in range(2):
            own = low_lanes if side == 0 else ~low_lanes
            scores = dot_cols(jnp.where(own, query, jnp.zeros_like(query)), keys)
            scores = jnp.where(real_key, scores, -1e30)
            raised = jnp.exp(scores - jnp.max(scores, axis=-1, keepdims=True))
            weights = (raised / jnp.sum(raised, axis=-1, keepdims=True)).astype(BF16)
            prob_ref[0, 2 * pair + side] = weights
            got.append(dot(weights, valued))
        mixed_ref[0, :, at : at + 128] = jnp.where(low_lanes, got[0], got[1]).astype(BF16)
    out_full = tall_ref[:, :, :width].reshape(width, width)
    router = tall_ref[:, :, width : width + 128].reshape(width, 128)
    middle = inputs + dot(mixed_ref[0], out_full) + vec[4:5]
    middle_ref[0] = middle
    second = standardise(middle)[0] * vec[5:6] + vec[6:7]
    lane = iota((PAD, 128), 1)
    logits = jnp.where(lane < EXPERTS, dot(second.astype(BF16), router), -1e30)
    soft = jnp.exp(logits - jnp.max(logits, axis=-1, keepdims=True))
    soft = soft / jnp.sum(soft, axis=-1, keepdims=True)
    route = route_ref[0]
    pick_one = jnp.sum(jnp.where(lane == route[:, 0:1], soft, 0.0), axis=-1, keepdims=True)
    pick_two = jnp.sum(jnp.where(lane == route[:, 1:2], soft, 0.0), axis=-1, keepdims=True)
    both = pick_one + pick_two
    live = (iota((PAD, 1), 0) < IMG_TOK) & (pl.program_id(0) < count_ref[0])
    alive = jnp.where(live, 1.0, 0.0)
    sum_ref[0] += jnp.broadcast_to(jnp.sum(soft * alive, axis=0, keepdims=True), (8, 128))
    soft = jnp.where(lane == EXPERTS + 4, pick_one / both, soft)
    soft = jnp.where(lane == EXPERTS + 5, pick_two / both, soft)
    soft_ref[0] = soft
    gates = jnp.transpose(soft)[EXPERTS : EXPERTS + 8]
    line = iota((8, PAD), 0)
    meta = jnp.where((line == 4) | (line == 5), gates, ids_ref[0])
    meta = jnp.concatenate([meta, jnp.zeros((8, width - PAD), F32)], axis=1)
    second_ref[0] = jnp.concatenate([second[: PAD - 8], meta], axis=0).astype(BF16)


def front(count, tok, ids, routes, wide, tall, traffic, ident):
    images, _, width = tok.shape
    shape = jax.ShapeDtypeStruct
    return run(
        front_body,
        (count, tok, ids, routes, *wide, *tall),
        [scalar_spec(), by_image(PAD, width), by_image(8, PAD), by_image(PAD, 2)]
        + [resident(wide[0].shape)] * 2
        + [resident(tall[0].shape)] * 2,
        [
            by_image(PAD, 3 * width),
            by_image(HEADS, PAD, PAD),
            by_image(PAD, width),
            by_image(PAD, width),
            by_image(PAD, width),
            by_image(PAD, 128),
            resident((1, 8, 128)),
        ],
        [
            shape((images, PAD, 3 * width), BF16),
            shape((images, HEADS, PAD, PAD), BF16),
            shape((images, PAD, width), BF16),
            shape((images, PAD, width), F32),
            shape((images, PAD, width), BF16),
            shape((images, PAD, 128), F32),
            shape((1, 8, 128), F32),
        ],
        grid=(images,),
        scratch=[pltpu.VMEM((2,) + wide[0].shape, BF16), pltpu.VMEM((2,) + tall[0].shape, BF16)],
        cost=pl.CostEstimate(flops=6_000_000_000, bytes_accessed=16_000_000, transcendentals=2_000_000),
        name="front",
        traffic=traffic,
        ident=ident,
    )


def slot_lines(meta):
    return meta[0:1] * CAP + meta[1:2], meta[2:3] * CAP + meta[3:4]


def gather_body(base_ref, *refs, parts, senders):
    arrays, (row_out, grad_out, rows, lines) = refs[:parts], refs[parts:]
    experts, _, cap, width = row_out.shape
    slots = experts * cap
    tokens = rows.shape[0]
    step = pl.program_id(0)
    for k, pair in enumerate(senders):
        for kind, pieces in enumerate(pair):

            @pl.when(step == 2 * k + kind)
            def _():
                for image, (at, position) in enumerate(pieces):
                    value = arrays[at][position]
                    rows[image * PAD : (image + 1) * PAD, :] = value
                    if kind == 0:
                        lines[image] = value[PAD - 16 :, :PAD].astype(F32)[8:]

    @pl.when(step < 2 * len(senders))
    def _():
        meta = jnp.concatenate([lines[image] for image in range(lines.shape[0])], axis=1)
        one, two = slot_lines(meta)
        gated = step % 2 == 1
        weight_one = jnp.where(gated, meta[4:5], 1.0)
        weight_two = jnp.where(gated, meta[5:6], 1.0)
        slot = (iota((slots, tokens), 0) + base_ref[0]).astype(F32)
        pick = jnp.where(slot == one, weight_one, 0.0) + jnp.where(slot == two, weight_two, 0.0)
        got = dot(pick.astype(BF16), rows[...]).astype(BF16).reshape(experts, 1, cap, width)

        @pl.when(step % 2 == 0)
        def _():
            row_out[...] = got

        @pl.when(step % 2 == 1)
        def _():
            grad_out[...] = got


def gather(base, experts, senders, extra, traffic, ident, chain=None):
    arrays, table = [], []
    for pair in senders:
        table.append([])
        for pieces in pair:
            table[-1].append([])
            for array, position in pieces:
                at = next((k for k, known in enumerate(arrays) if known is array), len(arrays))
                if at == len(arrays):
                    arrays.append(array)
                table[-1][-1].append((at, position))
    width = arrays[0].shape[-1]
    images = len(table[0][0])
    tokens = images * PAD
    count = len(senders)
    shape = jax.ShapeDtypeStruct((experts, count, CAP, width), BF16)
    return run(
        lambda *refs: gather_body(*refs, parts=len(arrays), senders=table),
        (base, *arrays),
        [scalar_spec()]
        + [pl.BlockSpec(a.shape, lambda d: (0, 0, 0), pipeline_mode=pl.Buffered(1)) for a in arrays],
        [pl.BlockSpec((experts, 1, CAP, width), lambda d: (0, jnp.minimum(d // 2, count - 1), 0, 0))] * 2,
        [shape, shape],
        grid=(2 * count + extra,),
        scratch=[pltpu.VMEM((tokens, width), BF16), pltpu.VMEM((images, 8, PAD), F32)],
        cost=pl.CostEstimate(
            flops=4 * count * experts * CAP * tokens * width,
            bytes_accessed=4 * count * (tokens + experts * CAP) * width,
            transcendentals=0,
        ),
        name="gather",
        traffic=traffic,
        chain=chain,
        ident=ident,
    )


def expert_body(row_own, row_far, grad_own, grad_far, in_ref, in_bias_ref, out_ref, out_bias_ref, made_own, made_far, back_own, back_far):
    cap, width = row_own.shape[2:]
    hidden = in_ref.shape[2]
    rows = jnp.concatenate([row_own[0, 0], row_far[0, 0]], axis=0)
    grads = jnp.concatenate([grad_own[0, 0], grad_far[0, 0]], axis=0)
    made = jnp.zeros((2 * cap, width), F32)
    back = jnp.zeros((2 * cap, width), F32)
    chunk = 512
    for at in range(0, hidden, chunk):
        first = in_ref[0, :, at : at + chunk]
        second = out_ref[0, at : at + chunk, :]
        raised = dot(rows, first) + in_bias_ref[0, :, at : at + chunk].astype(F32)
        active, slope = gelu_pair(raised)
        made += dot(active.astype(BF16), second)
        draised = (dot_cols(grads, second) * slope).astype(BF16)
        back += dot_cols(draised, first)
    made = (made + out_bias_ref[0].astype(F32)).astype(BF16)
    back = back.astype(BF16)
    made_own[0], made_far[0] = made[:cap], made[cap:]
    back_own[0], back_far[0] = back[:cap], back[cap:]


def expert_layer(own, far, first, first_bias, second, second_bias, chain, traffic, ident):
    experts, _, cap, width = own[0].shape
    hidden = first.shape[2]
    rows = pl.BlockSpec((1, 1, cap, width), lambda e: (e, 0, 0, 0))
    out = pl.BlockSpec((1, cap, width), lambda e: (e, 0, 0))
    return run(
        expert_body,
        (
            own[0],
            far[0],
            own[1],
            far[1],
            first,
            first_bias.reshape(experts, 1, hidden),
            second,
            second_bias.reshape(experts, 1, width),
        ),
        [rows] * 4 + [by_image(width, hidden), by_image(1, hidden), by_image(hidden, width), by_image(1, width)],
        [out] * 4,
        [jax.ShapeDtypeStruct((experts, cap, width), BF16)] * 4,
        grid=(experts,),
        cost=pl.CostEstimate(
            flops=16 * experts * cap * width * hidden,
            bytes_accessed=4 * experts * width * hidden,
            transcendentals=2 * experts * cap * hidden,
        ),
        name="expert_layer",
        traffic=traffic,
        chain=chain,
        ident=ident,
    )


def combine_body(base_ref, rows, cot, made_ref, back_ref, sum_ref, row_ref, gate_ref):
    experts, cap, width = made_ref.shape
    slots = experts * cap
    meta = jnp.transpose(rows[PAD - 16 :, :PAD].astype(F32)[8:])
    slot = (iota((PAD, slots), 1) + base_ref[0]).astype(F32)
    one = jnp.where(slot == meta[:, 0:1] * CAP + meta[:, 1:2], 1.0, 0.0).astype(BF16)
    two = jnp.where(slot == meta[:, 2:3] * CAP + meta[:, 3:4], 1.0, 0.0).astype(BF16)
    made = made_ref[...].reshape(slots, width)
    made_one = dot(one, made)
    made_two = dot(two, made)
    sum_ref[0] = (meta[:, 4:5] * made_one + meta[:, 5:6] * made_two).astype(BF16)
    row_ref[0] = dot(one + two, back_ref[...].reshape(slots, width)).astype(BF16)
    cot = cot.astype(F32)
    grad_one = jnp.sum(cot * made_one, axis=1, keepdims=True)
    grad_two = jnp.sum(cot * made_two, axis=1, keepdims=True)
    lane = iota((PAD, 128), 1)
    wide = jnp.where(lane == 0, grad_one, jnp.where(lane == 1, grad_two, 0.0))
    gate_ref[0] = jnp.transpose(wide)[0:8]


def by_piece(pieces, *shape):
    arrays, first = [], []
    for image, (array, position) in enumerate(pieces):
        if not arrays or arrays[-1] is not array:
            arrays.append(array)
            first.append((image, position))
    specs = []
    for array, (image, position) in zip(arrays, first):

        def index(i, *_, image=image, position=position, last=array.shape[0] - 1):
            return (jnp.clip(i - image + position, 0, last),) + (0,) * len(shape)

        specs.append(pl.BlockSpec((1,) + shape, index))

    def read(refs):
        value = refs[0][0]
        for ref, (image, _) in zip(refs[1:], first[1:]):
            value = jnp.where(pl.program_id(0) >= image, ref[0], value)
        return value

    return arrays, specs, read


def combine(base, rows, cots, made, back, traffic, ident):
    width = made.shape[-1]
    images = len(rows)
    experts, cap, _ = made.shape
    row_arrays, row_specs, read_rows = by_piece(rows, PAD, width)
    cot_arrays, cot_specs, read_cots = by_piece(cots, PAD, width)
    split = len(row_arrays)

    def body(base_ref, made_ref, back_ref, *refs):
        inputs, outs = refs[: split + len(cot_arrays)], refs[split + len(cot_arrays) :]
        combine_body(base_ref, read_rows(inputs[:split]), read_cots(inputs[split:]), made_ref, back_ref, *outs)

    return run(
        body,
        (base, made, back, *row_arrays, *cot_arrays),
        [scalar_spec(), resident(made.shape), resident(back.shape), *row_specs, *cot_specs],
        [by_image(PAD, width), by_image(PAD, width), by_image(8, PAD)],
        [
            jax.ShapeDtypeStruct((images, PAD, width), BF16),
            jax.ShapeDtypeStruct((images, PAD, width), BF16),
            jax.ShapeDtypeStruct((images, 8, PAD), F32),
        ],
        grid=(images,),
        cost=pl.CostEstimate(
            flops=6 * images * PAD * experts * cap * width, bytes_accessed=6_000_000, transcendentals=0
        ),
        name="combine",
        traffic=traffic,
        ident=ident,
    )


def norm_back(grads, hat, scale, gain):
    scaled = grads * gain
    inner = jnp.mean(scaled * hat, axis=-1, keepdims=True)
    return scale * (scaled - jnp.mean(scaled, axis=-1, keepdims=True) - hat * inner)


def column_sum(values):
    return jnp.sum(values, axis=0, keepdims=True)


def finish_body(
    count_ref, tok_ref, cot_ref, packed_ref, prob_ref, mixed_ref, middle_ref, second_ref, soft_ref, route_ref,
    row_own, row_far, gate_own, gate_far, aux_ref,
    wide_own, wide_far, tall_own, tall_far, dtok_ref, pack_ref,
    dpacked, wide_ref, tall_ref, dqkv_ref, dout_ref, drouter_ref, dvec_ref,
):
    image = pl.program_id(0)
    width = tok_ref.shape[-1]

    @pl.when(image == 0)
    def _():
        place_halves(wide_own, wide_far, wide_ref)
        place_halves(tall_own, tall_far, tall_ref)

    vec = vectors(wide_ref)
    images = dtok_ref.shape[0] // IMG_TOK

    @pl.when(image == 0)
    def _():
        for ref in (dqkv_ref, dout_ref, drouter_ref, dvec_ref):
            ref[...] = jnp.zeros_like(ref)

    real = iota((PAD, 1), 0) < IMG_TOK
    alive = jnp.where(real & (image < count_ref[0]), 1.0, 0.0)
    middle = middle_ref[0]
    upstream = cot_ref[0].astype(F32)
    soft = soft_ref[0]
    route = route_ref[0]
    lane = iota((PAD, 128), 1)
    gate_grads = jnp.transpose(gate_own[0] + gate_far)
    push = (gate_grads[:, 0:1] - gate_grads[:, 1:2]) * soft[:, EXPERTS + 4 : EXPERTS + 5] * soft[:, EXPERTS + 5 : EXPERTS + 6]
    soft = jnp.where(lane < EXPERTS, soft, 0.0)
    aux = aux_ref[...] * alive
    dlogits = soft * (aux - jnp.sum(soft * aux, axis=-1, keepdims=True))
    dlogits += jnp.where(lane == route[:, 0:1], push, 0.0) - jnp.where(lane == route[:, 1:2], push, 0.0)
    dlogits = dlogits.astype(BF16)
    second = second_ref[0]
    router = tall_ref[:, :, width : width + 128].reshape(width, 128)
    drouter_ref[...] += dot_rows(second, dlogits)
    dsecond = dot_cols(dlogits, router) + (row_own[0].astype(F32) + row_far.astype(F32))
    hat, scale = standardise(middle)
    dmiddle = upstream + norm_back(dsecond, hat, scale, vec[5:6])
    dattn = dmiddle.astype(BF16)
    dvec_ref[EXPERTS + 4 : EXPERTS + 5] += column_sum(dattn.astype(F32))
    dvec_ref[EXPERTS + 5 : EXPERTS + 6] += column_sum(dsecond * hat)
    dvec_ref[EXPERTS + 6 : EXPERTS + 7] += column_sum(dsecond)
    dout_ref[...] += dot_rows(mixed_ref[0], dattn)
    out_full = tall_ref[:, :, :width].reshape(width, width)
    dmixed = dot_cols(dattn, out_full).astype(BF16)
    low_lanes = iota((PAD, 128), 1) < HEAD_DIM
    root = HEAD_DIM**-0.5
    for pair in range(HEADS // 2):
        at = pair * 128
        query = packed_ref[0, :, at : at + 128]
        keys = packed_ref[0, :, width + at : width + at + 128]
        valued = packed_ref[0, :, 2 * width + at : 2 * width + at + 128]
        grads = dmixed[:, at : at + 128]
        parts = []
        for side in range(2):
            own = low_lanes if side == 0 else ~low_lanes
            weights = prob_ref[0, 2 * pair + side]
            dweights = dot_cols(jnp.where(own, grads, jnp.zeros_like(grads)), valued)
            exact = weights.astype(F32)
            inner = jnp.sum(dweights * exact, axis=-1, keepdims=True)
            dscores = (exact * (dweights - inner)).astype(BF16)
            parts.append((dot(dscores, keys), dot_rows(dscores, query), dot_rows(weights, grads)))
        for third, factor in ((0, root), (1, root), (2, 1.0)):
            both = jnp.where(low_lanes, parts[0][third], parts[1][third]) * factor
            dpacked[:, third * width + at : third * width + at + 128] = both.astype(BF16)
    inputs = tok_ref[0].astype(F32)
    hat, scale = standardise(inputs)
    normed = (hat * vec[0:1] + vec[1:2]).astype(BF16)
    packed_grads = dpacked[...]
    dqkv_ref[...] += dot_rows(normed, packed_grads)
    dvec_ref[EXPERTS + 2 : EXPERTS + 3] += column_sum(packed_grads[:, :width].astype(F32))
    dvec_ref[EXPERTS + 3 : EXPERTS + 4] += column_sum(packed_grads[:, 2 * width :].astype(F32))
    qkv = wide_ref[:, :256, :].reshape(width, 3 * width)
    dnormed = dot_cols(packed_grads, qkv)
    dvec_ref[EXPERTS + 0 : EXPERTS + 1] += column_sum(dnormed * hat)
    dvec_ref[EXPERTS + 1 : EXPERTS + 2] += column_sum(dnormed)
    dtokens = dmiddle + norm_back(dnormed, hat, scale, vec[0:1])
    for k in range(images):

        @pl.when(image == k)
        def _():
            dtok_ref[pl.ds(k * IMG_TOK, IMG_TOK), :] = dtokens[:IMG_TOK]

    @pl.when(image == images - 1)
    def _():
        lines = jnp.transpose(dvec_ref[...])
        part = width // 8
        for owner in range(2):
            for half in range(2):
                for quarter in range(2):
                    at = ((owner * 2 + half) * 2 + quarter) * part
                    rows = slice(at, at + part)
                    spot = pack_ref.at[owner, half, quarter]
                    spot[:, : 3 * width] = dqkv_ref[rows].astype(BF16)
                    spot[:, 3 * width : 4 * width] = dout_ref[rows].astype(BF16)
                    spot[:, 4 * width :] = (drouter_ref[rows] + lines[rows]).astype(BF16)


def finish(count, tok, cot, saved, routes, row_own, row_far, gate_own, gate_far, aux, wide, tall, total, traffic, ident):
    images, _, width = tok.shape
    packed, prob, mixed, middle, second, soft = saved
    shape = jax.ShapeDtypeStruct
    tile = by_image(PAD, width)
    row_arrays, row_specs, read_rows = by_piece(row_far, PAD, width)
    gate_arrays, gate_specs, read_gates = by_piece(gate_far, 8, PAD)
    extra = len(row_arrays) + len(gate_arrays)

    def body(*refs):
        pieces, refs = refs[:extra], list(refs[extra:])
        refs[11:11] = [read_rows(pieces[: len(row_arrays)])]
        refs[13:13] = [read_gates(pieces[len(row_arrays) :])]
        finish_body(*refs)

    pack = (2, 2, 2, width // 8, 4 * width + 128)
    return run(
        body,
        (
            *row_arrays, *gate_arrays, count, tok, cot, packed, prob, mixed, middle, second, soft, routes,
            row_own, gate_own, aux, *wide, *tall,
        ),
        [
            *row_specs,
            *gate_specs,
            scalar_spec(),
            tile,
            tile,
            by_image(PAD, 3 * width),
            by_image(HEADS, PAD, PAD),
            tile,
            tile,
            tile,
            by_image(PAD, 128),
            by_image(PAD, 2),
            tile,
            by_image(8, PAD),
            resident((1, 128)),
            resident(wide[0].shape),
            resident(wide[0].shape),
            resident(tall[0].shape),
            resident(tall[0].shape),
        ],
        [resident((total, width)), resident(pack)],
        [shape((total, width), F32), shape(pack, BF16)],
        grid=(images,),
        scratch=[
            pltpu.VMEM((PAD, 3 * width), BF16),
            pltpu.VMEM((2,) + wide[0].shape, BF16),
            pltpu.VMEM((2,) + tall[0].shape, BF16),
            pltpu.VMEM((width, 3 * width), F32),
            pltpu.VMEM((width, width), F32),
            pltpu.VMEM((width, 128), F32),
            pltpu.VMEM((128, width), F32),
        ],
        cost=pl.CostEstimate(flops=12_000_000_000, bytes_accessed=24_000_000, transcendentals=0),
        name="finish",
        traffic=traffic,
        ident=ident,
    )


def add(left, right):
    return (left.astype(F32) + right.astype(F32)).astype(BF16)


class Exchange:
    def __init__(self, send, recv):
        self.send, self.recv = send, recv

    def at(self, index, link, source, target):
        move = Move(link, lambda _: source, lambda _: target)
        return move.roles(), move.copy(None, self.send.at[index], self.recv.at[index])


def begin(make):
    roles, copy = make()
    only_if(roles[0], copy.start)


def end(make):
    roles, copy = make()
    only_if(roles[0], copy.wait_send)
    only_if(roles[1], copy.wait_recv)


def sums_everywhere(load, soft_sum, steps):
    shape = (2,) + load.shape[1:]
    links = ("core", "y", "x", "near", "inner", "outward")

    def copies(load_ref, soft_ref, total, held, got, send, recv):
        made = Exchange(send, recv)
        return [
            lambda k=k, link=link: made.at(k, link, held.at[k], held.at[k] if link == "outward" else got.at[k])
            for k, link in enumerate(links)
        ]

    def first(*refs):
        load_ref, soft_ref, _, held = refs[:4]
        held[0, 0], held[0, 1] = load_ref[0], soft_ref[0]
        begin(copies(*refs)[0])

    def stage(k):
        def action(*refs):
            held, got = refs[3:5]
            end(copies(*refs)[k - 1])
            if links[k] == "outward":

                @pl.when(((lax.axis_index("rep") // 4) % 3) > 0)
                def _():
                    held[k] = held[k - 1] + got[k - 1]

            else:
                held[k] = held[k - 1] + got[k - 1]
            begin(copies(*refs)[k])

        return action

    def last(*refs):
        end(copies(*refs)[5])
        refs[2][...] = refs[3][5]

    return Chain(
        [load, soft_sum],
        [resident(load.shape)] * 2,
        [resident(shape)],
        [jax.ShapeDtypeStruct(shape, F32)],
        [pltpu.VMEM((6,) + shape, F32), pltpu.VMEM((5,) + shape, F32)] + [pltpu.SemaphoreType.DMA((6,))] * 2,
        {"core", "y", "x", "near", "inner"},
        list(zip(steps, [first] + [stage(k) for k in range(1, 6)])) + [(0, last)],
    )


def owner_sums(pack, steps):
    shape = pack.shape[2:]

    def first(pack_ref, part, near_in, half, far_in, send, recv):
        core = lax.axis_index("rep") % 2
        Exchange(send, recv).at(0, "core", pack_ref.at[:, 1 - core], near_in)[1].start()

    def second(pack_ref, part, near_in, half, far_in, send, recv):
        core, mine = lax.axis_index("rep") % 2, lax.axis_index("fsdp")
        Exchange(send, recv).at(0, "core", pack_ref.at[:, 1 - core], near_in)[1].wait()
        half[...] = add(pack_ref[:, core], near_in[...])
        Exchange(send, recv).at(1, "y", half.at[1 - mine], far_in)[1].start()

    def last(pack_ref, part, near_in, half, far_in, send, recv):
        mine = lax.axis_index("fsdp")
        Exchange(send, recv).at(1, "y", half.at[1 - mine], far_in)[1].wait()
        part[...] = add(half[mine], far_in[...])

    return Chain(
        [pack],
        [pl.BlockSpec(pack.shape, lambda *_: (0,) * 5, pipeline_mode=pl.Buffered(1))],
        [resident(shape)],
        [jax.ShapeDtypeStruct(shape, BF16)],
        [pltpu.VMEM((2,) + shape, BF16), pltpu.VMEM((2,) + shape, BF16), pltpu.VMEM(shape, BF16)]
        + [pltpu.SemaphoreType.DMA((2,))] * 2,
        {"core", "y"},
        [(0, first), (1, second), (steps, last)],
    )


def copy_sums(part, steps):
    shape = part.shape[1:]

    def copies(part_ref, total, x_in, held, near_in, line, inner_in, full, send, recv):
        device = lax.axis_index("rep")
        core, side = device % 2, (device // 2) % 2
        made = Exchange(send, recv)
        mine = full.at[core, side]
        plans = [
            ("x", part_ref.at[1 - side], x_in),
            ("near", held, near_in),
            ("inner", line, inner_in),
            ("outward", mine, mine),
            ("x", mine, mine),
            ("core", full.at[core], full.at[core]),
        ]
        return [lambda k=k, plan=plan: made.at(k, *plan) for k, plan in enumerate(plans)]

    def first(*refs):
        begin(copies(*refs)[0])

    def second(*refs):
        part_ref, total, x_in, held = refs[:4]
        steps = copies(*refs)
        end(steps[0])
        side = (lax.axis_index("rep") // 2) % 2
        held[...] = add(part_ref[side], x_in[...])
        begin(steps[1])

    def third(*refs):
        part_ref, total, x_in, held, near_in, line = refs[:6]
        steps = copies(*refs)
        end(steps[1])
        line[...] = add(held[...], near_in[...])
        begin(steps[2])

    def fourth(*refs):
        part_ref, total, x_in, held, near_in, line, inner_in, full = refs[:8]
        steps = copies(*refs)
        device = lax.axis_index("rep")
        middle = ((device // 4) % 3) > 0
        end(steps[2])

        @pl.when(middle)
        def _():
            full[device % 2, (device // 2) % 2] = add(line[...], inner_in[...])

        begin(steps[3])

    def fifth(*refs):
        steps = copies(*refs)
        end(steps[3])
        begin(steps[4])

    def sixth(*refs):
        steps = copies(*refs)
        end(steps[4])
        begin(steps[5])

    def last(*refs):
        total, full = refs[1], refs[7]
        end(copies(*refs)[5])
        total[...] = full[...]

    whole = (2, 2) + shape
    return Chain(
        [part],
        [resident(part.shape)],
        [resident(whole)],
        [jax.ShapeDtypeStruct(whole, BF16)],
        [pltpu.VMEM(shape, BF16)] * 5 + [pltpu.VMEM(whole, BF16)] + [pltpu.SemaphoreType.DMA((6,))] * 2,
        {"core", "x", "near", "inner"},
        list(zip(steps, (first, second, third, fourth, fifth, sixth))) + [(0, last)],
    )


def emit(count, middle, sum_own, sum_far, total):
    images, _, width = middle.shape
    far_arrays, far_specs, read_far = by_piece(sum_far, PAD, width)

    def body(count_ref, middle_ref, own_ref, *refs):
        far, (out_ref, held) = refs[:-2], refs[-2:]
        image = pl.program_id(0)
        live = (iota((PAD, 1), 0) < IMG_TOK) & (image < count_ref[0])
        both = own_ref[0].astype(F32) + read_far(far).astype(F32)
        result = jnp.where(live, 1.0, 0.0) * (middle_ref[0] + both)
        for k in range(images):

            @pl.when(image == k)
            def _():
                held[pl.ds(k * IMG_TOK, IMG_TOK), :] = result[:IMG_TOK]

        @pl.when(image == images - 1)
        def _():
            out_ref[...] = held[pl.ds(0, total), :].astype(BF16)

    tile = by_image(PAD, width)
    return run(
        body,
        (count, middle, sum_own, *far_arrays),
        [scalar_spec(), tile, tile, *far_specs],
        [resident((total, width))],
        [jax.ShapeDtypeStruct((total, width), BF16)],
        grid=(images,),
        scratch=[pltpu.VMEM((1000, width), F32)],
        cost=pl.CostEstimate(flops=2_000_000, bytes_accessed=6_000_000, transcendentals=0),
        name="emit",
    )[0][0]


def by_slice(
    tokens, cotangent, routes, image_count, capacity, norm1_gain, norm1_bias, w_qkv, bias_q, bias_v, w_out, bias_out,
    norm2_gain, norm2_bias, w_router, expert_in, expert_in_bias, expert_out, expert_out_bias,
):
    total, width = tokens.shape
    local = expert_in.shape[0]
    device = lax.axis_index("rep")
    mine = lax.axis_index("fsdp")
    core = device % 2
    small = jnp.stack([norm1_gain, norm1_bias, bias_q, bias_v, bias_out, norm2_gain, norm2_bias])
    small = jnp.pad(small, ((0, 9), (0, 3 * width - small.shape[1])))
    wide = jnp.concatenate([w_qkv, small], axis=0)
    tall = jnp.concatenate([w_out, jnp.pad(w_router, ((0, 0), (0, 128 - EXPERTS)))], axis=1)
    (tok, cot, route, ids, load), (wide_far, tall_far), _ = prepare(
        tokens, cotangent, routes, image_count, capacity, wide, tall, 0
    )
    wide, tall = (wide, wide_far), (tall, tall_far)
    base = (mine * (local * CAP)).reshape(1)
    net = Network()
    net.offer("C", cot, COT_PATHS)
    idents = iter(range(1, 32))

    def staged(kernel, *args, rounds):
        traffic, plan = net.plan(*rounds)
        outs, arrived, chained = kernel(*args, traffic, next(idents))
        net.land(plan, arrived)
        return (*outs, *chained)

    own, far = (0, 0, 0), (0, 0, 1)
    packed, prob, mixed, middle, second, soft, soft_sum = staged(
        front, image_count, tok, ids, route, wide, tall, rounds=evenly(4, 5, 0.68)
    )
    net.offer("S", second, ROW_PATHS)

    def sender(block):
        return net.block("S", block), net.block("C", block)

    slots = []
    taken = set()

    def take(blocks, room, extra):
        taken.update(blocks)
        outs = staged(
            gather, base, local, [sender(b) for b in blocks], extra, rounds=gathering(room, len(blocks), extra)
        )
        slots.append(outs)
        return outs

    def ready():
        return [b for b in COT_PATHS if b not in taken and net.complete("S", b) and net.complete("C", b)]

    slots_own = take([own], 6, 4)
    slots_far = take([far], 2, 1)
    made_own, made_far, back_own, back_far, sums = staged(
        expert_layer, slots_own, slots_far, expert_in, expert_in_bias, expert_out, expert_out_bias,
        sums_everywhere(load, soft_sum, (0, 2, 5, 8, 11, 13)),
        rounds=evenly(11, 16, 0.7, 2),
    )
    sum_far, drow_far, dgate_far = staged(
        combine, base, *sender(far), made_far, back_far, rounds=evenly(2, 5, 0.4, 2)
    )
    net.offer("D", drow_far, FAR_FIRST)
    net.offer("G", dgate_far, FAR_FIRST, 0)
    net.offer("M", sum_far, FAR_LAST)
    sum_own, drow_own, dgate_own = staged(
        combine, base, *sender(own), made_own, back_own, rounds=evenly(2, 5, 0.4, 2)
    )
    take(ready()[:2], 3, 1)
    loads, prob_total = sums[0, 0:1], sums[1, 0:1]
    live = loads[:, 64:65]
    share = (loads[:, :EXPERTS] + loads[:, EXPERTS : 2 * EXPERTS]) / (2.0 * live)
    aux = jnp.pad(EXPERTS * share / live, ((0, 0), (0, 128 - EXPERTS)))
    grad_tokens, pack = staged(
        finish, image_count, tok, cot, (packed, prob, mixed, middle, second, soft), route, drow_own,
        net.block("D", far), dgate_own, net.block("G", far), aux, wide, tall, total,
        rounds=evenly(7, 5, 1.5),
    )
    while True:
        now = ready()[:3]
        if not net.missing() and len(taken) + len(now) == 16:
            break
        take(now, 5, 2)
    traffic, plan = net.plan(0, [0], [0.0])
    taken.update(now)
    outs, arrived, (part,) = gather(
        base, local, [sender(b) for b in now], 0, traffic, next(idents), owner_sums(pack, 2 * len(now))
    )
    net.land(plan, arrived)
    slots.append(outs)
    outputs = emit(image_count, middle, sum_own, net.block("M", far), total)
    row_slots = [pair[0] for pair in slots]
    grad_slots = [pair[1] for pair in slots]
    (keep_in, send_in, keep_out, send_out, d_bias, d_out_bias), _, (owned,) = slice_grads(
        row_slots, grad_slots, expert_in, expert_in_bias, expert_out, copy_sums(part, (0, 3, 6, 9, 12, 15)), next(idents)
    )
    owned = owned.reshape(width // 2, -1).astype(F32)
    swap = [(i, i ^ 1) for i in range(16)]
    got_in, got_out, got_bias, got_out_bias = (
        lax.ppermute(v, "rep", swap) for v in (send_in, send_out, d_bias, d_out_bias)
    )
    bias = (d_bias + got_bias)[:, 0]
    out_bias = (d_out_bias + got_out_bias)[:, 0]
    half = bias.shape[1] // 2
    piece = width // 16
    expert_grads = (
        keep_in + got_in.astype(F32),
        lax.dynamic_slice_in_dim(bias, core * half, half, axis=1),
        keep_out + got_out.astype(F32),
        lax.dynamic_slice_in_dim(out_bias, device * piece, piece, axis=1),
    )

    balance_loss = jnp.sum(aux * prob_total)
    lines = jnp.transpose(owned[:, 4 * width + EXPERTS : 4 * width + EXPERTS + 8])
    owned = (
        lines[0],
        lines[1],
        owned[:, : 3 * width],
        lines[2],
        lines[3],
        owned[:, 3 * width : 4 * width],
        lines[4],
        lines[5],
        lines[6],
        owned[:, 4 * width : 4 * width + EXPERTS],
    )
    return (outputs, grad_tokens, balance_loss) + owned + expert_grads


def solution(mesh):
    in_specs = (
        P(("rep", "fsdp"), None),
        P(("rep", "fsdp"), None),
        P(("rep", "fsdp"), None),
        P(("rep", "fsdp")),
        P(("rep", "fsdp")),
        P("fsdp"),
        P("fsdp"),
        P("fsdp", None),
        P("fsdp"),
        P("fsdp"),
        P("fsdp", None),
        P("fsdp"),
        P("fsdp"),
        P("fsdp"),
        P("fsdp", None),
        P("fsdp", None, None),
        P("fsdp", None),
        P("fsdp", None, None),
        P("fsdp", None),
    )
    out_specs = (
        P(("rep", "fsdp"), None),
        P(("rep", "fsdp"), None),
        P(),
        P("fsdp"),
        P("fsdp"),
        P("fsdp", None),
        P("fsdp"),
        P("fsdp"),
        P("fsdp", None),
        P("fsdp"),
        P("fsdp"),
        P("fsdp"),
        P("fsdp", None),
        P("fsdp", None, "rep"),
        P("fsdp", "rep"),
        P("fsdp", "rep", None),
        P("fsdp", "rep"),
    )
    program = by_slice if mesh.shape["rep"] == 16 and mesh.shape["fsdp"] == 2 else shards
    return jax.shard_map(program, mesh=mesh, in_specs=in_specs, out_specs=out_specs, check_vma=False)
```

```python
import jax
import jax.numpy as jnp
from jax import lax
from jax.experimental import pallas as pl
from jax.experimental.pallas import tpu as pltpu
from jax.sharding import PartitionSpec as P

HEADS = 8
HEAD_DIM = 64
EXPERTS = 32
IMG_TOK = 197
CAP = 80


def norm_rows(values, norm_gain, offset):
    average = jnp.mean(values, axis=-1, keepdims=True)
    centred = values - average
    variance = jnp.mean(centred * centred, axis=-1, keepdims=True)
    return centred * lax.rsqrt(variance + 1e-06) * norm_gain + offset


def slot_table(choices, alive_mask, limit, row_total):
    pair_expert = jnp.concatenate([choices[:, 0], choices[:, 1]])
    live_pairs = jnp.concatenate([alive_mask, alive_mask])
    expert_ids = jnp.arange(EXPERTS, dtype=jnp.int32)
    onehot = ((pair_expert[:, None] == expert_ids[None, :]) & live_pairs[:, None]).astype(jnp.int32)
    before = jnp.cumsum(onehot, axis=0) - onehot
    position = jnp.sum(before * onehot, axis=1)
    kept_pairs = live_pairs & (position < limit)
    pair_slot = pair_expert * CAP + position
    pair_token = jnp.concatenate(
        [jnp.arange(row_total, dtype=jnp.int32), jnp.arange(row_total, dtype=jnp.int32)]
    )
    slot_owner = jnp.full((EXPERTS * CAP,), row_total, jnp.int32)
    target = jnp.where(kept_pairs, pair_slot, EXPERTS * CAP)
    slot_owner = slot_owner.at[target].set(pair_token, mode="drop")
    safe_slot = jnp.where(kept_pairs, pair_slot, 0)
    return (slot_owner, kept_pairs, safe_slot, target, onehot)


def shards(
    tokens,
    cotangent,
    routes,
    image_count,
    capacity,
    norm1_gain,
    norm1_bias,
    w_qkv,
    bias_q,
    bias_v,
    w_out,
    bias_out,
    norm2_gain,
    norm2_bias,
    w_router,
    expert_in,
    expert_in_bias,
    expert_out,
    expert_out_bias,
):
    rows_count = tokens.shape[0]
    model_width = tokens.shape[1]
    image_total = rows_count // IMG_TOK
    score_scale = HEAD_DIM ** (-0.5)
    image_rows = jnp.arange(rows_count, dtype=jnp.int32) // IMG_TOK
    alive_mask = image_rows < image_count[0]
    alive_float = alive_mask.astype(jnp.float32)[:, None]
    slot_owner, kept_pairs, safe_slot, target, onehot = slot_table(
        routes, alive_mask, capacity[0], rows_count
    )
    kept_float = kept_pairs.astype(jnp.float32)
    load_local = jnp.sum(onehot.astype(jnp.float32), axis=0)
    live_local = jnp.sum(alive_float)
    load_total, live_total = lax.psum((load_local, live_local), ("rep", "fsdp"))
    gathered = (
        lax.all_gather(norm1_gain, "fsdp", axis=0, tiled=True),
        lax.all_gather(norm1_bias, "fsdp", axis=0, tiled=True),
        lax.all_gather(w_qkv, "fsdp", axis=0, tiled=True),
        lax.all_gather(bias_q, "fsdp", axis=0, tiled=True),
        lax.all_gather(bias_v, "fsdp", axis=0, tiled=True),
        lax.all_gather(w_out, "fsdp", axis=0, tiled=True),
        lax.all_gather(bias_out, "fsdp", axis=0, tiled=True),
        lax.all_gather(norm2_gain, "fsdp", axis=0, tiled=True),
        lax.all_gather(norm2_bias, "fsdp", axis=0, tiled=True),
        lax.all_gather(w_router, "fsdp", axis=0, tiled=True),
    )
    (
        gain_one,
        shift_one,
        qkv_full,
        query_bias,
        value_bias,
        out_full,
        out_bias,
        gain_two,
        shift_two,
        router_full,
    ) = gathered
    gain_one = gain_one.astype(jnp.float32)
    shift_one = shift_one.astype(jnp.float32)
    gain_two = gain_two.astype(jnp.float32)
    shift_two = shift_two.astype(jnp.float32)
    inputs = tokens.astype(jnp.float32)
    normed = norm_rows(inputs, gain_one, shift_one)
    normed_low = normed.astype(jnp.bfloat16)
    bias_row = jnp.concatenate([query_bias, jnp.zeros_like(query_bias), value_bias]).astype(
        jnp.float32
    )
    packed_low = (
        jnp.dot(normed_low, qkv_full, preferred_element_type=jnp.float32) + bias_row
    ).astype(jnp.bfloat16)
    image_shape = (image_total, IMG_TOK, HEADS, HEAD_DIM)
    queries = packed_low[:, :model_width].reshape(image_shape)
    all_keys = packed_low[:, model_width : 2 * model_width].reshape(image_shape)
    valued = packed_low[:, 2 * model_width :].reshape(image_shape)

    def score_block():
        return (
            jnp.einsum("iqhd,ikhd->hiqk", queries, all_keys, preferred_element_type=jnp.float32)
            * score_scale
        )

    scores = score_block()
    row_peak = jnp.max(scores, axis=-1, keepdims=True)
    exp_scores = jnp.exp(scores - row_peak)
    totals = jnp.sum(exp_scores, axis=-1, keepdims=True)
    log_total = row_peak + jnp.log(totals)
    attn_low = (exp_scores / totals).astype(jnp.bfloat16)
    mixed_low = (
        jnp.einsum("hiqk,ikhd->iqhd", attn_low, valued, preferred_element_type=jnp.float32)
        .reshape(rows_count, model_width)
        .astype(jnp.bfloat16)
    )
    middle = (
        inputs
        + jnp.dot(mixed_low, out_full, preferred_element_type=jnp.float32)
        + out_bias.astype(jnp.float32)
    )
    second_low = norm_rows(middle, gain_two, shift_two).astype(jnp.bfloat16)
    logits = jnp.dot(second_low, router_full, preferred_element_type=jnp.float32)
    expert_ids = jnp.arange(EXPERTS, dtype=jnp.int32)
    first_hot = (routes[:, 0:1] == expert_ids[None, :]).astype(jnp.float32)
    second_hot = (routes[:, 1:2] == expert_ids[None, :]).astype(jnp.float32)

    def gate_terms(logit_rows):
        router_probs = jax.nn.softmax(logit_rows, axis=-1)
        pick_one = jnp.sum(router_probs * first_hot, axis=-1)
        pick_two = jnp.sum(router_probs * second_hot, axis=-1)
        pick_total = pick_one + pick_two
        return (pick_one / pick_total, pick_two / pick_total, router_probs)

    (gate_first, gate_second, router_probs), gate_back = jax.vjp(gate_terms, logits)
    padded_rows = jnp.concatenate([second_low, jnp.zeros((1, model_width), jnp.bfloat16)], axis=0)
    sent_rows = padded_rows[slot_owner].reshape(EXPERTS, CAP, model_width)
    received = lax.all_to_all(sent_rows, "fsdp", split_axis=0, concat_axis=1, tiled=True)
    raised = (
        jnp.einsum("esd,edf->esf", received, expert_in, preferred_element_type=jnp.float32)
        + expert_in_bias.astype(jnp.float32)[:, None, :]
    )
    active, gelu_back = jax.vjp(jax.nn.gelu, raised)
    active_low = active.astype(jnp.bfloat16)
    produced = (
        jnp.einsum("esf,efd->esd", active_low, expert_out, preferred_element_type=jnp.float32)
        + expert_out_bias.astype(jnp.float32)[:, None, :]
    ).astype(jnp.bfloat16)
    returned = lax.all_to_all(produced, "fsdp", split_axis=1, concat_axis=0, tiled=True).reshape(
        EXPERTS * CAP, model_width
    )
    pair_rows = returned[safe_slot].astype(jnp.float32)
    pair_weight = jnp.concatenate([gate_first, gate_second]) * kept_float
    expert_sum = jnp.sum(
        (pair_rows * pair_weight[:, None]).reshape(2, rows_count, model_width), axis=0
    )
    outputs = (alive_float * (middle + expert_sum)).astype(jnp.bfloat16)
    upstream = cotangent.astype(jnp.float32) * alive_float
    pair_grad = jnp.concatenate([upstream, upstream], axis=0)
    gate_grads = jnp.sum(pair_grad * pair_rows, axis=1) * kept_float
    slot_gate = jnp.zeros((EXPERTS * CAP,), jnp.float32).at[target].set(pair_weight, mode="drop")
    padded_grad = jnp.concatenate([upstream, jnp.zeros((1, model_width), jnp.float32)], axis=0)
    slot_grads = (
        (padded_grad[slot_owner] * slot_gate[:, None])
        .astype(jnp.bfloat16)
        .reshape(EXPERTS, CAP, model_width)
    )
    grad_received = lax.all_to_all(slot_grads, "fsdp", split_axis=0, concat_axis=1, tiled=True)
    grad_active = jnp.einsum(
        "esd,efd->esf", grad_received, expert_out, preferred_element_type=jnp.float32
    )
    (grad_raised,) = gelu_back(grad_active)
    grad_raised_low = grad_raised.astype(jnp.bfloat16)
    grad_rows = jnp.einsum(
        "esf,edf->esd", grad_raised_low, expert_in, preferred_element_type=jnp.float32
    ).astype(jnp.bfloat16)
    back_rows = lax.all_to_all(grad_rows, "fsdp", split_axis=1, concat_axis=0, tiled=True).reshape(
        EXPERTS * CAP, model_width
    )
    expert_part = jnp.sum(
        (back_rows[safe_slot].astype(jnp.float32) * kept_float[:, None]).reshape(
            2, rows_count, model_width
        ),
        axis=0,
    )
    local_in = jnp.einsum(
        "esd,esf->edf", received, grad_raised_low, preferred_element_type=jnp.float32
    )
    local_in_bias = jnp.sum(grad_raised_low.astype(jnp.float32), axis=1)
    local_out = jnp.einsum(
        "esf,esd->efd", active_low, grad_received, preferred_element_type=jnp.float32
    )
    local_out_bias = jnp.sum(grad_received.astype(jnp.float32), axis=1)
    grad_in_weight, grad_in_bias, grad_out_weight, grad_out_expert_bias = (
        lax.psum_scatter(local_in, "rep", scatter_dimension=2, tiled=True),
        lax.psum_scatter(local_in_bias, "rep", scatter_dimension=1, tiled=True),
        lax.psum_scatter(local_out, "rep", scatter_dimension=1, tiled=True),
        lax.psum_scatter(local_out_bias, "rep", scatter_dimension=1, tiled=True),
    )
    prob_local = jnp.sum(router_probs * alive_float, axis=0)
    prob_total = lax.psum(prob_local, ("rep", "fsdp"))
    share = load_total / (2.0 * live_total)
    balance_loss = EXPERTS * jnp.sum(share * prob_total / live_total)
    aux_grad = alive_float * (EXPERTS * share / live_total)[None, :]
    (grad_logits,) = gate_back((gate_grads[:rows_count], gate_grads[rows_count:], aux_grad))
    grad_logits_low = grad_logits.astype(jnp.bfloat16)
    grad_router = jnp.dot(second_low.T, grad_logits_low, preferred_element_type=jnp.float32)
    grad_second = (
        jnp.dot(grad_logits_low, router_full.T, preferred_element_type=jnp.float32) + expert_part
    )
    _, norm_two_back = jax.vjp(norm_rows, middle, gain_two, shift_two)
    grad_mid_norm, grad_gain_two, grad_shift_two = norm_two_back(grad_second)
    grad_middle = upstream + grad_mid_norm
    grad_att_low = grad_middle.astype(jnp.bfloat16)
    grad_out_proj = jnp.dot(mixed_low.T, grad_att_low, preferred_element_type=jnp.float32)
    grad_out_bias = jnp.sum(grad_att_low.astype(jnp.float32), axis=0)
    grad_mixed = (
        jnp.dot(grad_att_low, out_full.T, preferred_element_type=jnp.float32)
        .astype(jnp.bfloat16)
        .reshape(image_shape)
    )
    recomputed = jnp.exp(score_block() - log_total)
    grad_weights = jnp.einsum(
        "iqhd,ikhd->hiqk", grad_mixed, valued, preferred_element_type=jnp.float32
    )
    grad_values = jnp.einsum(
        "hiqk,iqhd->ikhd",
        recomputed.astype(jnp.bfloat16),
        grad_mixed,
        preferred_element_type=jnp.float32,
    )
    inner_sum = jnp.sum(grad_weights * recomputed, axis=-1, keepdims=True)
    grad_scores = (recomputed * (grad_weights - inner_sum)).astype(jnp.bfloat16)
    grad_queries = (
        jnp.einsum("hiqk,ikhd->iqhd", grad_scores, all_keys, preferred_element_type=jnp.float32)
        * score_scale
    )
    grad_keys = (
        jnp.einsum("hiqk,iqhd->ikhd", grad_scores, queries, preferred_element_type=jnp.float32)
        * score_scale
    )
    grad_packed_low = jnp.concatenate(
        [
            grad_queries.reshape(rows_count, model_width),
            grad_keys.reshape(rows_count, model_width),
            grad_values.reshape(rows_count, model_width),
        ],
        axis=1,
    ).astype(jnp.bfloat16)
    grad_qkv = jnp.dot(normed_low.T, grad_packed_low, preferred_element_type=jnp.float32)
    packed_sums = jnp.sum(grad_packed_low.astype(jnp.float32), axis=0)
    grad_query_bias = packed_sums[:model_width]
    grad_value_bias = packed_sums[2 * model_width :]
    grad_normed = jnp.dot(grad_packed_low, qkv_full.T, preferred_element_type=jnp.float32)
    _, norm_one_back = jax.vjp(norm_rows, inputs, gain_one, shift_one)
    grad_input_norm, grad_gain_one, grad_shift_one = norm_one_back(grad_normed)
    grad_tokens = grad_middle + grad_input_norm
    local_grads = (
        grad_gain_one,
        grad_shift_one,
        grad_qkv,
        grad_query_bias,
        grad_value_bias,
        grad_out_proj,
        grad_out_bias,
        grad_gain_two,
        grad_shift_two,
        grad_router,
    )
    shares = (
        lax.psum_scatter(local_grads[0], "fsdp", scatter_dimension=0, tiled=True),
        lax.psum_scatter(local_grads[1], "fsdp", scatter_dimension=0, tiled=True),
        lax.psum_scatter(local_grads[2], "fsdp", scatter_dimension=0, tiled=True),
        lax.psum_scatter(local_grads[3], "fsdp", scatter_dimension=0, tiled=True),
        lax.psum_scatter(local_grads[4], "fsdp", scatter_dimension=0, tiled=True),
        lax.psum_scatter(local_grads[5], "fsdp", scatter_dimension=0, tiled=True),
        lax.psum_scatter(local_grads[6], "fsdp", scatter_dimension=0, tiled=True),
        lax.psum_scatter(local_grads[7], "fsdp", scatter_dimension=0, tiled=True),
        lax.psum_scatter(local_grads[8], "fsdp", scatter_dimension=0, tiled=True),
        lax.psum_scatter(local_grads[9], "fsdp", scatter_dimension=0, tiled=True),
    )
    owned = lax.psum(
        (
            shares[0],
            shares[1],
            shares[2],
            shares[3],
            shares[4],
            shares[5],
            shares[6],
            shares[7],
            shares[8],
            shares[9],
        ),
        "rep",
    )
    return (
        (outputs, grad_tokens, balance_loss)
        + tuple(owned)
        + (grad_in_weight, grad_in_bias, grad_out_weight, grad_out_expert_bias)
    )


def gelu_pair(value):
    root = 0.7978845608028654
    square = value * value
    bend = jnp.tanh(root * value * (1.0 + 0.044715 * square))
    half = 0.5 * (1.0 + bend)
    slope = half + 0.5 * value * (1.0 - bend * bend) * root * (1.0 + 3 * 0.044715 * square)
    return value * half, slope


def slice_grads_body(*refs, senders):
    parts, refs = refs[: sum(senders)], refs[sum(senders) :]
    in_ref, in_bias_ref, out_ref, keep_in, send_in, keep_out, send_out, d_bias, d_out_bias = refs
    core = lax.axis_index("rep") % 2
    width = in_ref.shape[1]

    def stacked(pieces):
        return jnp.concatenate([piece[...].reshape(-1, width) for piece in pieces], axis=0)

    rows = stacked(parts[: senders[0]])
    grads = stacked(parts[senders[0] :])
    first = in_ref[0]
    second = out_ref[0]
    raised = jnp.dot(rows, first, preferred_element_type=jnp.float32) + in_bias_ref[0].astype(
        jnp.float32
    )
    active, slope = gelu_pair(raised)
    active = active.astype(jnp.bfloat16)
    back = lax.dot_general(
        grads, second, (((1,), (1,)), ((), ())), preferred_element_type=jnp.float32
    )
    draised = (back * slope).astype(jnp.bfloat16)
    over_rows = (((0,), (0,)), ((), ()))
    g_in = lax.dot_general(rows, draised, over_rows, preferred_element_type=jnp.float32)
    g_out = lax.dot_general(active, grads, over_rows, preferred_element_type=jnp.float32)
    half = g_in.shape[1] // 2
    first_core = core == 0
    keep_in[0] = jnp.where(first_core, g_in[:, :half], g_in[:, half:])
    send_in[0] = jnp.where(first_core, g_in[:, half:], g_in[:, :half]).astype(jnp.bfloat16)
    keep_out[0] = jnp.where(first_core, g_out[:half], g_out[half:])
    send_out[0] = jnp.where(first_core, g_out[half:], g_out[:half]).astype(jnp.bfloat16)
    d_bias[0] = jnp.sum(draised.astype(jnp.float32), axis=0, keepdims=True)
    d_out_bias[0] = jnp.sum(grads.astype(jnp.float32), axis=0, keepdims=True)


def slice_grads(rows, grads, first, first_bias, second, chain, ident):
    experts, width, hidden = first.shape
    cap = rows[0].shape[2]
    slots = cap * sum(piece.shape[1] for piece in rows)
    part = 256
    half = part // 2
    f32 = jnp.float32
    def chip():
        return lax.axis_index("rep") // 2

    return run(
        lambda *refs: slice_grads_body(*refs, senders=(len(rows), len(grads))),
        (*rows, *grads, first, first_bias.reshape(experts, 1, hidden), second),
        [pl.BlockSpec((1,) + piece.shape[1:], lambda e: (e, 0, 0, 0)) for piece in (*rows, *grads)]
        + [
            pl.BlockSpec((1, width, part), lambda e: (e, 0, chip())),
            pl.BlockSpec((1, 1, part), lambda e: (e, 0, chip())),
            pl.BlockSpec((1, part, width), lambda e: (e, chip(), 0)),
        ],
        [by_image(width, half)] * 2 + [by_image(half, width)] * 2 + [by_image(1, part), by_image(1, width)],
        [
            jax.ShapeDtypeStruct((experts, width, half), f32),
            jax.ShapeDtypeStruct((experts, width, half), jnp.bfloat16),
            jax.ShapeDtypeStruct((experts, half, width), f32),
            jax.ShapeDtypeStruct((experts, half, width), jnp.bfloat16),
            jax.ShapeDtypeStruct((experts, 1, part), f32),
            jax.ShapeDtypeStruct((experts, 1, width), f32),
        ],
        grid=(experts,),
        cost=pl.CostEstimate(
            flops=8 * experts * slots * width * part,
            bytes_accessed=4 * experts * (slots * width + 3 * width * part),
            transcendentals=experts * slots * part,
        ),
        name="slice_grads",
        chain=chain,
        ident=ident,
    )


F32 = jnp.float32
BF16 = jnp.bfloat16
PAD = 208
ROOT_AXES = ("rep", "fsdp")
OVER_COLS = (((1,), (1,)), ((), ()))
OVER_ROWS = (((0,), (0,)), ((), ()))


def dot(left, right):
    return jnp.dot(left, right, preferred_element_type=F32)


def dot_cols(left, right):
    return lax.dot_general(left, right, OVER_COLS, preferred_element_type=F32)


def dot_rows(left, right):
    return lax.dot_general(left, right, OVER_ROWS, preferred_element_type=F32)


def iota(shape, axis):
    return lax.broadcasted_iota(jnp.int32, shape, axis)


def resident(shape):
    return pl.BlockSpec(shape, lambda *_: (0,) * len(shape))


def by_image(*shape):
    return pl.BlockSpec((1,) + shape, lambda i, *_: (i,) + (0,) * len(shape))


def scalar_spec():
    return pl.BlockSpec(memory_space=pltpu.SMEM)


def partner(link):
    device, side = lax.axis_index("rep"), lax.axis_index("fsdp")
    if link == "y":
        return {"rep": device, "fsdp": 1 - side}
    depth = device // 4
    step = {
        "core": 1 - 2 * (device % 2),
        "x": 2 - 4 * ((device // 2) % 2),
        "near": 4 - 8 * (depth % 2),
        "inner": 12 - 8 * depth,
        "skip": 8 - 16 * (depth // 2),
    }[link]
    return {"rep": device + step, "fsdp": side}


def only_if(condition, action):
    if condition is None:
        action()
    else:
        pl.when(condition)(action)


class Move:
    def __init__(self, link, source, target, needs=()):
        self.link, self.source, self.target, self.needs = link, source, target, needs

    def roles(self):
        depth = lax.axis_index("rep") // 4
        middle = (depth % 3) > 0
        if self.link == "inner":
            return middle, middle
        if self.link in ("outward", "skip"):
            return middle, (depth % 3) == 0
        return None, None

    def copy(self, refs, send, recv):
        return pltpu.make_async_remote_copy(
            src_ref=self.source(refs),
            dst_ref=self.target(refs),
            send_sem=send,
            recv_sem=recv,
            device_id=partner("near" if self.link == "outward" else self.link),
            device_id_type=pl.DeviceIdType.MESH,
        )


class Traffic:
    def __init__(self, sources, targets, rounds, steps):
        self.sources, self.targets, self.rounds, self.steps = sources, targets, rounds, steps

    def count(self):
        return sum(len(moves) for moves in self.rounds)

    def links(self):
        return {("near" if m.link == "outward" else m.link) for moves in self.rounds for m in moves}

    def start(self, which, refs, send, recv, arrived):
        moves = [m for moves in self.rounds for m in moves]
        at = sum(len(moves) for moves in self.rounds[:which])
        for k, move in enumerate(self.rounds[which]):
            for index in move.needs:
                if index not in arrived:
                    arrived.add(index)
                    only_if(moves[index].roles()[1], moves[index].copy(refs, send.at[index], recv.at[index]).wait_recv)
            only_if(move.roles()[0], move.copy(refs, send.at[at + k], recv.at[at + k]).start)

    def require(self, target, position, refs, send, recv, arrived):
        moves = [m for moves in self.rounds for m in moves]
        for index, move in enumerate(moves):
            if move.home[0] == target and move.home[1] <= position < move.home[1] + move.size and index not in arrived:
                arrived.add(index)
                only_if(move.roles()[1], move.copy(refs, send.at[index], recv.at[index]).wait_recv)

    def finish(self, refs, send, recv, arrived):
        moves = [m for moves in self.rounds for m in moves]
        for index, move in enumerate(moves):
            copy = move.copy(refs, send.at[index], recv.at[index])
            sends, receives = move.roles()
            only_if(sends, copy.wait_send)
            if index not in arrived:
                only_if(receives, copy.wait_recv)


def greet(links):
    barrier = pltpu.get_barrier_semaphore()
    middle = ((lax.axis_index("rep") // 4) % 3) > 0
    plain = [link for link in ("core", "x", "y", "near", "skip") if link in links]
    for link in plain:
        pl.semaphore_signal(barrier, inc=1, device_id=partner(link), device_id_type=pl.DeviceIdType.MESH)
    if "inner" in links:

        @pl.when(middle)
        def _():
            pl.semaphore_signal(
                barrier, inc=1, device_id=partner("inner"), device_id_type=pl.DeviceIdType.MESH
            )

    if "inner" in links:

        @pl.when(middle)
        def _():
            pl.semaphore_wait(barrier, len(plain) + 1)

        @pl.when(~middle)
        def _():
            if plain:
                pl.semaphore_wait(barrier, len(plain))

    else:
        pl.semaphore_wait(barrier, len(plain))


class Chain:
    def __init__(self, args, in_specs, out_specs, out_shape, scratch, links, actions):
        self.args, self.in_specs, self.out_specs, self.out_shape = args, in_specs, out_specs, out_shape
        self.scratch, self.links, self.actions = scratch, links, actions


def run(
    body, args, in_specs, out_specs, out_shape, *,
    name, grid=(1,), scratch=(), cost=None, traffic=None, chain=None, hook=None, ident=None,
):
    if (traffic is None or traffic.count() == 0) and chain is None:
        outs = pl.pallas_call(
            body, grid=grid, in_specs=in_specs, out_specs=out_specs, out_shape=out_shape,
            scratch_shapes=list(scratch), cost_estimate=cost, name=name,
        )(*args)
        return outs, [], []
    traffic = traffic or Traffic([], [], [], [])
    chain = chain or Chain([], [], [], [], [], set(), [])
    n_in, n_src, n_out, n_dst = len(args), len(traffic.sources), len(out_shape), len(traffic.targets)
    anywhere = pl.BlockSpec(memory_space=pl.ANY)
    sizes = (n_in, n_src, len(chain.args), n_out, n_dst, len(chain.out_shape), len(scratch), len(chain.scratch))
    links = traffic.links() | chain.links

    def carried(*refs):
        groups = []
        for size in sizes:
            groups.append(refs[:size])
            refs = refs[size:]
        ins, sources, chain_in, outs, targets, chain_out, held, chain_held = groups
        ends = (sources, targets)
        step = pl.program_id(0)
        pl.when(step == 0)(lambda: greet(links))
        arrived = set()
        for at in range(grid[0]):
            rounds = [which for which, when in enumerate(traffic.steps) if when == at]
            actions = [action for when, action in chain.actions[:-1] if when == at]
            if rounds or actions or hook:

                @pl.when(step == at)
                def _():
                    for which in rounds:
                        traffic.start(which, ends, *refs, arrived)
                    for action in actions:
                        action(*chain_in, *chain_out, *chain_held)
                    if hook:
                        hook(
                            at,
                            lambda target, position: traffic.require(target, position, ends, *refs, arrived),
                            targets, ins, held,
                        )

        body(*ins, *outs, *held)

        @pl.when(step == grid[0] - 1)
        def _():
            if traffic.count():
                traffic.finish(ends, *refs, arrived)
            if chain.actions:
                chain.actions[-1][1](*chain_in, *chain_out, *chain_held)

    count = traffic.count()
    semaphores = [pltpu.SemaphoreType.DMA((count,))] * 2 if count else []
    outs = pl.pallas_call(
        carried,
        grid=grid,
        in_specs=list(in_specs) + [anywhere] * n_src + list(chain.in_specs),
        out_specs=list(out_specs) + [anywhere] * n_dst + list(chain.out_specs),
        out_shape=list(out_shape) + list(traffic.targets) + list(chain.out_shape),
        scratch_shapes=list(scratch) + list(chain.scratch) + semaphores,
        compiler_params=pltpu.CompilerParams(collective_id=ident, has_side_effects=True),
        cost_estimate=cost,
        name=name,
    )(*args, *traffic.sources, *chain.args)
    return outs[:n_out], outs[n_out : n_out + n_dst], outs[n_out + n_dst :]


COT_PATHS = {
    (0, 0, 1): ("y", (0, 0, 0), -1.500),
    (0, 1, 0): ("x", (0, 0, 0), 2.243),
    (0, 1, 1): ("x", (0, 0, 1), 1.258),
    (1, 0, 0): ("near", (0, 0, 0), 1.763),
    (1, 0, 1): ("near", (0, 0, 1), 1.701),
    (1, 1, 0): ("near", (0, 1, 0), 3.477),
    (1, 1, 1): ("x", (1, 0, 1), 5.719),
    (2, 0, 0): ("inner", (0, 0, 0), 4.656),
    (2, 0, 1): ("y", (2, 0, 0), 2.464),
    (2, 1, 0): ("inner", (0, 1, 0), 0.237),
    (2, 1, 1): ("x", (2, 0, 1), 2.798),
    (3, 0, 0): ("inner", (1, 0, 0), 0.958),
    (3, 0, 1): ("y", (3, 0, 0), 2.984),
    (3, 1, 0): ("x", (3, 0, 0), 2.092),
    (3, 1, 1): ("inner", (1, 1, 1), 1.507),
}
ROW_PATHS = {
    (0, 0, 1): ("y", (0, 0, 0), -1.400),
    (0, 1, 0): ("x", (0, 0, 0), 1.939),
    (0, 1, 1): ("x", (0, 0, 1), 1.580),
    (1, 0, 0): ("near", (0, 0, 0), 1.441),
    (1, 0, 1): ("y", (1, 0, 0), 0.198),
    (1, 1, 0): ("near", (0, 1, 0), 2.429),
    (1, 1, 1): ("x", (1, 0, 1), 5.646),
    (2, 0, 0): ("inner", (0, 0, 0), 2.268),
    (2, 0, 1): ("y", (2, 0, 0), 2.650),
    (2, 1, 0): ("x", (2, 0, 0), 4.955),
    (2, 1, 1): ("x", (2, 0, 1), 4.985),
    (3, 0, 0): ("reach", (1, 0, 0), 1.374),
    (3, 0, 1): ("y", (3, 0, 0), 4.956),
    (3, 1, 0): ("x", (3, 0, 0), 2.903),
    (3, 1, 1): ("y", (3, 1, 0), 4.968),
}
FAR_FIRST = {(0, 0, 1): ("y", (0, 0, 0), -2.0)}
FAR_LAST = {(0, 0, 1): ("y", (0, 0, 0), 2.506)}
FRONT_ROOM, PAIR_ROOM, EXPERT_ROOM, OWN_ROOM, FINISH_ROOM, LAST_ROOM = 5, 9, 11, 4, 8, 25


class Network:
    def __init__(self):
        self.have, self.hops, self.weight, self.pieces = {}, {}, {}, {}

    def offer(self, name, array, hops, weight=1):
        self.hops[name], self.weight[name] = hops, weight
        self.pieces[name] = array.shape[0]
        for p in range(array.shape[0]):
            self.have[name, (0, 0, 0), p] = (array, p)

    def order(self, item):
        name, block, p = item
        return self.hops[name][block][2], block, p

    def missing(self):
        return [
            (name, block, p)
            for name in self.hops
            for block in self.hops[name]
            for p in range(self.pieces[name])
            if (name, block, p) not in self.have
        ]

    def complete(self, name, block):
        return all((name, block, p) in self.have for p in range(self.pieces[name]))

    def plan(self, room, steps, times):
        waiting = sorted(self.missing(), key=self.order)
        landed, rounds, going = {}, [[] for _ in steps], {}
        free = dict.fromkeys(("x", "y", "near", "inner"), 0.0)
        uses = {"reach": (("inner", 2), ("near", 1))}
        lag = 0.4

        def fill(link, now, weight, horizon):
            spans = [(on, max(free[on], now), n * weight) for on, n in uses.get(link, ((link, 1),))]
            if weight and any(begin >= horizon or begin + length > room + 0.01 for _, begin, length in spans):
                return None
            for on, begin, length in spans:
                if length:
                    free[on] = begin + length
            return max(begin + length for _, begin, length in spans) + lag

        for r, now in enumerate(times):
            horizon = times[r + 1] + 0.5 if r + 1 < len(times) else room
            for item in [i for i, (_, at) in going.items() if at <= now]:
                done = fill("near", now, self.weight[item[0]], horizon)
                if done is not None:
                    rounds[r].append(("outward", item, item))
                    landed[item] = done
                    del going[item]
            for item in waiting:
                name, block, p = item
                if item in landed or item in going:
                    continue
                link, source, _ = self.hops[name][block]
                source = (name, source, p)
                if source not in self.have and landed.get(source, now + 1) > now:
                    continue
                if link == "inner":
                    left = room - max(free["near"], now + 1) - sum(self.weight[i[0]] for i in going)
                    if r + 1 >= len(times) or left < 1 + self.weight[name] or times[-1] < now + self.weight[name] + lag:
                        continue
                done = fill(link, now, self.weight[name], horizon)
                if done is None:
                    continue
                if link == "reach":
                    rounds[r] += [("inner", source, item), ("skip", source, item)]
                else:
                    rounds[r].append((link, source, item))
                if link == "inner":
                    going[item] = (r, done)
                else:
                    landed[item] = done
        for item in list(going):
            rounds[-1].append(("outward", item, item))
            landed[item] = room
        sources, targets, homes = [], [], {}
        for name, block, p in sorted(landed):
            homes.setdefault((name, block), []).append(p)
        order = list(homes)
        for name, block in order:
            model = self.have[name, (0, 0, 0), 0][0]
            targets.append(jax.ShapeDtypeStruct((len(homes[name, block]),) + model.shape[1:], model.dtype))

        def home(item):
            name, block, p = item
            return order.index((name, block)), homes[name, block].index(p)

        def origin(item):
            if item in landed:
                return (1,) + home(item)
            array, at = self.have[item]
            for k, known in enumerate(sources):
                if known is array:
                    return 0, k, at
            sources.append(array)
            return 0, len(sources) - 1, at

        moves = []
        for chosen in rounds:
            spans = []
            for link, source, item in sorted(chosen, key=lambda c: (c[0] not in ("outward", "inner"), *c)):
                a, b = origin(source), home(item)
                if spans:
                    link_, a_, b_, n = spans[-1]
                    if link_ == link and a_[:2] == a[:2] and b_[0] == b[0] and a[2] == a_[2] + n and b[1] == b_[1] + n:
                        spans[-1] = (link, a_, b_, n + 1)
                        continue
                spans.append((link, a, b, 1))
            flat = [m for made in moves for m in made]
            placed = []
            for link, a, b, n in spans:
                needs = [
                    k
                    for k, m in enumerate(flat)
                    if a[0] == 1 and m.home[0] == a[1] and m.home[1] < a[2] + n and a[2] < m.home[1] + m.size
                ]
                placed.append(self.move(link, a, b, n, needs))
            moves.append(placed)
        while moves and not moves[-1]:
            moves.pop()
        traffic = Traffic(sources, targets, moves, steps[: len(moves)])
        return traffic, (order, homes, landed)

    def find(self, plan, name, block):
        order, homes, landed = plan
        found = []
        for p in range(self.pieces[name]):
            if (name, block, p) in landed:
                found.append((None, order.index((name, block)), homes[name, block].index(p)))
            else:
                array, at = self.have[name, block, p]
                found.append((array, None, at))
        return found

    def landing(self, plan, block):
        return max(plan[2].get((name, block, p), 0.0) for name in "CS" for p in range(self.pieces[name]))

    @staticmethod
    def move(link, origin, home, count, needs):
        def source(refs):
            return refs[origin[0]][origin[1]].at[pl.ds(origin[2], count)]

        def target(refs):
            return refs[1][home[0]].at[pl.ds(home[1], count)]

        made = Move(link, source, target, needs)
        made.home, made.size = home, count
        return made

    def land(self, plan, arrays):
        order, homes, _ = plan
        for key, array in zip(order, arrays):
            for at, p in enumerate(homes[key]):
                self.have[key[0], key[1], p] = (array, at)

    def block(self, name, block):
        return [self.have[name, block, p] for p in range(self.pieces[name])]


def evenly(room, steps, length, every=1):
    chosen = list(range(0, steps, every))
    return room, chosen, [step * length for step in chosen]


def gathering(room, senders, extra):
    busy = 2 * senders * 0.45
    times = [0.45 * step for step in range(2 * senders)]
    times += [busy + (step + 1) * max(0.5, room - busy) / (extra + 1) for step in range(extra)]
    return room, list(range(2 * senders + extra)), times


def standardise(values):
    average = jnp.mean(values, axis=-1, keepdims=True)
    centred = values - average
    variance = jnp.mean(centred * centred, axis=-1, keepdims=True)
    scale = lax.rsqrt(variance + 1e-06)
    return centred * scale, scale


def prep_body(count_ref, cap_ref, tok_ref, cot_ref, route_ref, tok_out, cot_out, route_out, ids_out, load_out, wide, narrow):
    pl.when(pl.program_id(0) == 0)(
        lambda: prep_rows(
            count_ref, cap_ref, tok_ref, cot_ref, route_ref, tok_out, cot_out, route_out, ids_out, load_out, wide, narrow
        )
    )


def prep_rows(count_ref, cap_ref, tok_ref, cot_ref, route_ref, tok_out, cot_out, route_out, ids_out, load_out, wide, narrow):
    images = tok_out.shape[0]
    total = tok_ref.shape[0]
    alive_images = count_ref[0]
    real = iota((PAD, 1), 0) < IMG_TOK

    def split(source, image):
        return source[pl.ds(image * IMG_TOK, PAD), :]

    wide[...] = jnp.zeros_like(wide)
    narrow[...] = jnp.zeros_like(narrow)
    wide[pl.ds(0, total), :] = tok_ref[...].astype(F32)
    for image in range(images):
        tok_out[image] = jnp.where(real, split(wide, image), 0.0).astype(BF16)
    wide[pl.ds(0, total), :] = cot_ref[...].astype(F32)
    narrow[pl.ds(0, total), :] = route_ref[...]
    routes = []
    lives = []
    for image in range(images):
        live = real & (image < alive_images)
        cot_out[image] = jnp.where(live, split(wide, image), 0.0).astype(BF16)
        picked = split(narrow, image)
        route_out[image] = picked
        routes.append(picked)
        lives.append(jnp.where(live, 1, 0))
    routes = jnp.concatenate(routes, axis=0)
    live = jnp.concatenate(lives, axis=0) > 0
    rows = images * PAD
    lane = iota((rows, 128), 1)
    first = (lane == routes[:, 0:1]) & live
    second = (lane == routes[:, 1:2] + EXPERTS) & live
    hot = jnp.where(first | second, 1.0, 0.0)
    below = jnp.where(iota((rows, rows), 0) > iota((rows, rows), 1), 1.0, 0.0).astype(BF16)
    before = dot(below, hot.astype(BF16))
    totals = jnp.sum(hot, axis=0, keepdims=True)
    place_one = jnp.sum(jnp.where(first, before, 0.0), axis=1, keepdims=True)
    place_two = jnp.sum(jnp.where(second, before, 0.0), axis=1, keepdims=True) + jnp.sum(
        jnp.where(lane == routes[:, 1:2], totals, 0.0), axis=1, keepdims=True
    )
    limit = cap_ref[0].astype(F32)
    keep_one = live & (place_one < limit)
    keep_two = live & (place_two < limit)
    slots = jnp.where(lane == 0, jnp.where(keep_one, routes[:, 0:1].astype(F32), -1.0), 0.0)
    slots = jnp.where(lane == 1, jnp.where(keep_one, place_one, 0.0), slots)
    slots = jnp.where(lane == 2, jnp.where(keep_two, routes[:, 1:2].astype(F32), -1.0), slots)
    slots = jnp.where(lane == 3, jnp.where(keep_two, place_two, 0.0), slots)
    for image in range(images):
        ids_out[image] = jnp.transpose(slots[image * PAD : (image + 1) * PAD])[0:8]
    lanes = iota((1, 128), 1)
    tokens_alive = (alive_images * IMG_TOK).astype(F32)
    load_out[0] = jnp.broadcast_to(jnp.where(lanes == 64, tokens_alive, totals), (8, 128))


def weight_traffic(wide, tall):
    def rows(array):
        half = array.shape[0] // 2
        return pl.ds(pl.multiple_of((lax.axis_index("rep") % 2) * half, 8), half)

    def fetch(at, array):
        return Move("y", lambda refs: refs[0][at].at[rows(array)], lambda refs: refs[1][at].at[rows(array)])

    def pass_on(at, array):
        there = lambda refs: refs[1][at].at[rows(array)]
        return Move("core", there, there, [at])

    arrays = (wide, tall)
    targets = [jax.ShapeDtypeStruct(a.shape, a.dtype) for a in arrays]
    rounds = [[make(at, a) for at, a in enumerate(arrays)] for make in (fetch, pass_on)]
    return Traffic(list(arrays), targets, rounds, [0, 1])


def prepare(tokens, cotangent, routes, image_count, capacity, wide, tall, ident):
    total, width = tokens.shape
    images = total // IMG_TOK
    shapes = [
        jax.ShapeDtypeStruct((images, PAD, width), BF16),
        jax.ShapeDtypeStruct((images, PAD, width), BF16),
        jax.ShapeDtypeStruct((images, PAD, 2), jnp.int32),
        jax.ShapeDtypeStruct((images, 8, PAD), F32),
        jax.ShapeDtypeStruct((1, 8, 128), F32),
    ]
    return run(
        prep_body,
        (image_count, capacity, tokens, cotangent, routes),
        [scalar_spec(), scalar_spec()] + [resident(a.shape) for a in (tokens, cotangent, routes)],
        [resident(a.shape) for a in shapes],
        shapes,
        grid=(2,),
        scratch=[pltpu.VMEM((1000, width), F32), pltpu.VMEM((1000, 2), jnp.int32)],
        cost=pl.CostEstimate(flops=300_000_000, bytes_accessed=6_000_000, transcendentals=0),
        name="prepare",
        traffic=weight_traffic(wide, tall),
        ident=ident,
    )


def place_halves(own, far, both):
    mine = lax.axis_index("fsdp")
    both[mine] = own[...]
    both[1 - mine] = far[...]


def vectors(wide_ref):
    return jnp.concatenate([wide_ref[0, 256:272, :256], wide_ref[1, 256:272, :256]], axis=1).astype(F32)


def front_body(
    count_ref, tok_ref, ids_ref, route_ref, wide_own, wide_far, tall_own, tall_far,
    packed_ref, prob_ref, mixed_ref, middle_ref, second_ref, soft_ref, sum_ref, wide_ref, tall_ref,
):
    @pl.when(pl.program_id(0) == 0)
    def _():
        sum_ref[...] = jnp.zeros_like(sum_ref)
        place_halves(wide_own, wide_far, wide_ref)
        place_halves(tall_own, tall_far, tall_ref)

    width = tok_ref.shape[-1]
    vec = vectors(wide_ref)
    inputs = tok_ref[0].astype(F32)
    normed = (standardise(inputs)[0] * vec[0:1] + vec[1:2]).astype(BF16)
    qkv = wide_ref[:, :256, :].reshape(width, 3 * width)
    raw = dot(normed, qkv)
    packed_ref[0, :, :width] = (raw[:, :width] + vec[2:3]).astype(BF16)
    packed_ref[0, :, width : 2 * width] = raw[:, width : 2 * width].astype(BF16)
    packed_ref[0, :, 2 * width :] = (raw[:, 2 * width :] + vec[3:4]).astype(BF16)
    low_lanes = iota((PAD, 128), 1) < HEAD_DIM
    real_key = iota((PAD, PAD), 1) < IMG_TOK
    for pair in range(HEADS // 2):
        at = pair * 128
        query = packed_ref[0, :, at : at + 128] * jnp.asarray(HEAD_DIM**-0.5, BF16)
        keys = packed_ref[0, :, width + at : width + at + 128]
        valued = packed_ref[0, :, 2 * width + at : 2 * width + at + 128]
        got = []
        for side in range(2):
            own = low_lanes if side == 0 else ~low_lanes
            scores = dot_cols(jnp.where(own, query, jnp.zeros_like(query)), keys)
            scores = jnp.where(real_key, scores, -1e30)
            raised = jnp.exp(scores - jnp.max(scores, axis=-1, keepdims=True))
            weights = (raised / jnp.sum(raised, axis=-1, keepdims=True)).astype(BF16)
            prob_ref[0, 2 * pair + side] = weights
            got.append(dot(weights, valued))
        mixed_ref[0, :, at : at + 128] = jnp.where(low_lanes, got[0], got[1]).astype(BF16)
    out_full = tall_ref[:, :, :width].reshape(width, width)
    router = tall_ref[:, :, width : width + 128].reshape(width, 128)
    middle = inputs + dot(mixed_ref[0], out_full) + vec[4:5]
    middle_ref[0] = middle
    second = standardise(middle)[0] * vec[5:6] + vec[6:7]
    lane = iota((PAD, 128), 1)
    logits = jnp.where(lane < EXPERTS, dot(second.astype(BF16), router), -1e30)
    soft = jnp.exp(logits - jnp.max(logits, axis=-1, keepdims=True))
    soft = soft / jnp.sum(soft, axis=-1, keepdims=True)
    route = route_ref[0]
    pick_one = jnp.sum(jnp.where(lane == route[:, 0:1], soft, 0.0), axis=-1, keepdims=True)
    pick_two = jnp.sum(jnp.where(lane == route[:, 1:2], soft, 0.0), axis=-1, keepdims=True)
    both = pick_one + pick_two
    live = (iota((PAD, 1), 0) < IMG_TOK) & (pl.program_id(0) < count_ref[0])
    alive = jnp.where(live, 1.0, 0.0)
    sum_ref[0] += jnp.broadcast_to(jnp.sum(soft * alive, axis=0, keepdims=True), (8, 128))
    soft = jnp.where(lane == EXPERTS + 4, pick_one / both, soft)
    soft = jnp.where(lane == EXPERTS + 5, pick_two / both, soft)
    soft_ref[0] = soft
    gates = jnp.transpose(soft)[EXPERTS : EXPERTS + 8]
    line = iota((8, PAD), 0)
    meta = jnp.where((line == 4) | (line == 5), gates, ids_ref[0])
    meta = jnp.concatenate([meta, jnp.zeros((8, width - PAD), F32)], axis=1)
    second_ref[0] = jnp.concatenate([second[: PAD - 8], meta], axis=0).astype(BF16)


def front(count, tok, ids, routes, wide, tall, traffic, ident):
    images, _, width = tok.shape
    shape = jax.ShapeDtypeStruct
    return run(
        front_body,
        (count, tok, ids, routes, *wide, *tall),
        [scalar_spec(), by_image(PAD, width), by_image(8, PAD), by_image(PAD, 2)]
        + [resident(wide[0].shape)] * 2
        + [resident(tall[0].shape)] * 2,
        [
            by_image(PAD, 3 * width),
            by_image(HEADS, PAD, PAD),
            by_image(PAD, width),
            by_image(PAD, width),
            by_image(PAD, width),
            by_image(PAD, 128),
            resident((1, 8, 128)),
        ],
        [
            shape((images, PAD, 3 * width), BF16),
            shape((images, HEADS, PAD, PAD), BF16),
            shape((images, PAD, width), BF16),
            shape((images, PAD, width), F32),
            shape((images, PAD, width), BF16),
            shape((images, PAD, 128), F32),
            shape((1, 8, 128), F32),
        ],
        grid=(images,),
        scratch=[pltpu.VMEM((2,) + wide[0].shape, BF16), pltpu.VMEM((2,) + tall[0].shape, BF16)],
        cost=pl.CostEstimate(flops=6_000_000_000, bytes_accessed=16_000_000, transcendentals=2_000_000),
        name="front",
        traffic=traffic,
        ident=ident,
    )


def slot_lines(meta):
    return meta[0:1] * CAP + meta[1:2], meta[2:3] * CAP + meta[3:4]


def gather(base, experts, senders, sequence, traffic, ident, chain=None):
    arrays, table = [], []
    for sender in sequence:
        if sender is None:
            table.append(None)
            continue
        for kind in range(2):
            spots = []
            for array, target, position in senders[sender][kind]:
                at = target
                if array is not None:
                    at = next((k for k, known in enumerate(arrays) if known is array), len(arrays))
                    if at == len(arrays):
                        arrays.append(array)
                spots.append((array is None, at, position))
            table.append((sender, kind, spots))
    images, width = len(table[0][2]), arrays[0].shape[-1]
    tokens, slots, count, steps = images * PAD, experts * CAP, len(senders), len(table)
    first = [next(k for k, entry in enumerate(table) if entry and entry[0] == sender) for sender in range(count)]

    def hook(step, require, targets, ins, held):
        sources, rows, loaded = ins[1:], held[0], held[2]

        def copies(entry):
            _, kind, spots = entry
            return [
                pltpu.make_async_copy(
                    (targets if arriving else sources)[at].at[position],
                    rows.at[kind, pl.ds(image * PAD, PAD)],
                    loaded.at[kind, image],
                )
                for image, (arriving, at, position) in enumerate(spots)
            ]

        def load(entry):
            for arriving, at, position in entry[2]:
                if arriving:
                    require(at, position)
            for copy in copies(entry):
                copy.start()

        if step == 0:
            load(table[0])
        if step + 1 < steps and table[step + 1]:
            load(table[step + 1])
        if table[step]:
            for copy in copies(table[step]):
                copy.wait()

    def body(base_ref, *refs):
        row_out, grad_out, rows, lines = refs[len(arrays) : len(arrays) + 4]
        step = pl.program_id(0)
        turns = [(k, entry[1]) for k, entry in enumerate(table) if entry]
        working, gated = step < 0, step < 0
        for k, kind in turns:
            working = working | (step == k)
            if kind:
                gated = gated | (step == k)

        @pl.when(working & ~gated)
        def _():
            for image in range(images):
                lines[image] = rows[0, image * PAD + PAD - 16 : (image + 1) * PAD, :PAD].astype(F32)[8:]

        @pl.when(working)
        def _():
            meta = jnp.concatenate([lines[image] for image in range(images)], axis=1)
            one, two = slot_lines(meta)
            weight_one = jnp.where(gated, meta[4:5], 1.0)
            weight_two = jnp.where(gated, meta[5:6], 1.0)
            slot = (iota((slots, tokens), 0) + base_ref[0]).astype(F32)
            pick = jnp.where(slot == one, weight_one, 0.0) + jnp.where(slot == two, weight_two, 0.0)
            got = dot(pick.astype(BF16), rows[jnp.where(gated, 1, 0)])
            got = got.astype(BF16).reshape(experts, 1, CAP, width)

            @pl.when(~gated)
            def _():
                row_out[...] = got

            @pl.when(gated)
            def _():
                grad_out[...] = got

    def place(d):
        turn = 0
        for at in first[1:]:
            turn += jnp.where(d >= at, 1, 0)
        return (0, turn, 0, 0)

    shape = jax.ShapeDtypeStruct((experts, count, CAP, width), BF16)
    return run(
        body,
        (base, *arrays),
        [scalar_spec()] + [pl.BlockSpec(memory_space=pl.ANY)] * len(arrays),
        [pl.BlockSpec((experts, 1, CAP, width), place)] * 2,
        [shape, shape],
        grid=(steps,),
        scratch=[
            pltpu.VMEM((2, tokens, width), BF16),
            pltpu.VMEM((images, 8, PAD), F32),
            pltpu.SemaphoreType.DMA((2, images)),
        ],
        cost=pl.CostEstimate(
            flops=4 * count * slots * tokens * width,
            bytes_accessed=4 * count * (tokens + slots) * width,
            transcendentals=0,
        ),
        name="gather",
        traffic=traffic,
        chain=chain,
        hook=hook,
        ident=ident,
    )


def expert_body(row_own, row_far, grad_own, grad_far, in_ref, in_bias_ref, out_ref, out_bias_ref, made_own, made_far, back_own, back_far):
    cap, width = row_own.shape[2:]
    hidden = in_ref.shape[2]
    rows = jnp.concatenate([row_own[0, 0], row_far[0, 0]], axis=0)
    grads = jnp.concatenate([grad_own[0, 0], grad_far[0, 0]], axis=0)
    made = jnp.zeros((2 * cap, width), F32)
    back = jnp.zeros((2 * cap, width), F32)
    chunk = 512
    for at in range(0, hidden, chunk):
        first = in_ref[0, :, at : at + chunk]
        second = out_ref[0, at : at + chunk, :]
        raised = dot(rows, first) + in_bias_ref[0, :, at : at + chunk].astype(F32)
        active, slope = gelu_pair(raised)
        made += dot(active.astype(BF16), second)
        draised = (dot_cols(grads, second) * slope).astype(BF16)
        back += dot_cols(draised, first)
    made = (made + out_bias_ref[0].astype(F32)).astype(BF16)
    back = back.astype(BF16)
    made_own[0], made_far[0] = made[:cap], made[cap:]
    back_own[0], back_far[0] = back[:cap], back[cap:]


def expert_layer(pair, first, first_bias, second, second_bias, chain, traffic, ident):
    experts, _, cap, width = pair[0].shape
    hidden = first.shape[2]
    rows = [pl.BlockSpec((1, 1, cap, width), lambda e, side=side: (e, side, 0, 0)) for side in range(2)]
    out = pl.BlockSpec((1, cap, width), lambda e: (e, 0, 0))
    return run(
        expert_body,
        (
            pair[0],
            pair[0],
            pair[1],
            pair[1],
            first,
            first_bias.reshape(experts, 1, hidden),
            second,
            second_bias.reshape(experts, 1, width),
        ),
        rows + rows + [by_image(width, hidden), by_image(1, hidden), by_image(hidden, width), by_image(1, width)],
        [out] * 4,
        [jax.ShapeDtypeStruct((experts, cap, width), BF16)] * 4,
        grid=(experts,),
        cost=pl.CostEstimate(
            flops=16 * experts * cap * width * hidden,
            bytes_accessed=4 * experts * width * hidden,
            transcendentals=2 * experts * cap * hidden,
        ),
        name="expert_layer",
        traffic=traffic,
        chain=chain,
        ident=ident,
    )


def combine_body(base_ref, rows, cot, made_ref, back_ref, sum_ref, row_ref, gate_ref):
    experts, cap, width = made_ref.shape
    slots = experts * cap
    meta = jnp.transpose(rows[PAD - 16 :, :PAD].astype(F32)[8:])
    slot = (iota((PAD, slots), 1) + base_ref[0]).astype(F32)
    one = jnp.where(slot == meta[:, 0:1] * CAP + meta[:, 1:2], 1.0, 0.0).astype(BF16)
    two = jnp.where(slot == meta[:, 2:3] * CAP + meta[:, 3:4], 1.0, 0.0).astype(BF16)
    made = made_ref[...].reshape(slots, width)
    made_one = dot(one, made)
    made_two = dot(two, made)
    sum_ref[0] = (meta[:, 4:5] * made_one + meta[:, 5:6] * made_two).astype(BF16)
    row_ref[0] = dot(one + two, back_ref[...].reshape(slots, width)).astype(BF16)
    cot = cot.astype(F32)
    grad_one = jnp.sum(cot * made_one, axis=1, keepdims=True)
    grad_two = jnp.sum(cot * made_two, axis=1, keepdims=True)
    lane = iota((PAD, 128), 1)
    wide = jnp.where(lane == 0, grad_one, jnp.where(lane == 1, grad_two, 0.0))
    gate_ref[0] = jnp.transpose(wide)[0:8]


def by_piece(pieces, *shape):
    arrays, first = [], []
    for image, (array, position) in enumerate(pieces):
        if not arrays or arrays[-1] is not array:
            arrays.append(array)
            first.append((image, position))
    specs = []
    for array, (image, position) in zip(arrays, first):

        def index(i, *_, image=image, position=position, last=array.shape[0] - 1):
            return (jnp.clip(i - image + position, 0, last),) + (0,) * len(shape)

        specs.append(pl.BlockSpec((1,) + shape, index))

    def read(refs):
        value = refs[0][0]
        for ref, (image, _) in zip(refs[1:], first[1:]):
            value = jnp.where(pl.program_id(0) >= image, ref[0], value)
        return value

    return arrays, specs, read


def combine(base, rows, cots, made, back, traffic, ident):
    width = made.shape[-1]
    images = len(rows)
    experts, cap, _ = made.shape
    row_arrays, row_specs, read_rows = by_piece(rows, PAD, width)
    cot_arrays, cot_specs, read_cots = by_piece(cots, PAD, width)
    split = len(row_arrays)

    def body(base_ref, made_ref, back_ref, *refs):
        inputs, outs = refs[: split + len(cot_arrays)], refs[split + len(cot_arrays) :]
        combine_body(base_ref, read_rows(inputs[:split]), read_cots(inputs[split:]), made_ref, back_ref, *outs)

    return run(
        body,
        (base, made, back, *row_arrays, *cot_arrays),
        [scalar_spec(), resident(made.shape), resident(back.shape), *row_specs, *cot_specs],
        [by_image(PAD, width), by_image(PAD, width), by_image(8, PAD)],
        [
            jax.ShapeDtypeStruct((images, PAD, width), BF16),
            jax.ShapeDtypeStruct((images, PAD, width), BF16),
            jax.ShapeDtypeStruct((images, 8, PAD), F32),
        ],
        grid=(images,),
        cost=pl.CostEstimate(
            flops=6 * images * PAD * experts * cap * width, bytes_accessed=6_000_000, transcendentals=0
        ),
        name="combine",
        traffic=traffic,
        ident=ident,
    )


def norm_back(grads, hat, scale, gain):
    scaled = grads * gain
    inner = jnp.mean(scaled * hat, axis=-1, keepdims=True)
    return scale * (scaled - jnp.mean(scaled, axis=-1, keepdims=True) - hat * inner)


def column_sum(values):
    return jnp.sum(values, axis=0, keepdims=True)


def finish_body(
    count_ref, tok_ref, cot_ref, packed_ref, prob_ref, mixed_ref, middle_ref, second_ref, soft_ref, route_ref,
    row_own, row_far, gate_own, gate_far, aux_ref,
    wide_own, wide_far, tall_own, tall_far, dtok_ref, pack_ref,
    dpacked, wide_ref, tall_ref, dqkv_ref, dout_ref, drouter_ref, dvec_ref,
):
    image = pl.program_id(0)
    width = tok_ref.shape[-1]

    @pl.when(image == 0)
    def _():
        place_halves(wide_own, wide_far, wide_ref)
        place_halves(tall_own, tall_far, tall_ref)

    vec = vectors(wide_ref)
    images = dtok_ref.shape[0] // IMG_TOK

    @pl.when(image == 0)
    def _():
        for ref in (dqkv_ref, dout_ref, drouter_ref, dvec_ref):
            ref[...] = jnp.zeros_like(ref)

    real = iota((PAD, 1), 0) < IMG_TOK
    alive = jnp.where(real & (image < count_ref[0]), 1.0, 0.0)
    middle = middle_ref[0]
    upstream = cot_ref[0].astype(F32)
    soft = soft_ref[0]
    route = route_ref[0]
    lane = iota((PAD, 128), 1)
    gate_grads = jnp.transpose(gate_own[0] + gate_far)
    push = (gate_grads[:, 0:1] - gate_grads[:, 1:2]) * soft[:, EXPERTS + 4 : EXPERTS + 5] * soft[:, EXPERTS + 5 : EXPERTS + 6]
    soft = jnp.where(lane < EXPERTS, soft, 0.0)
    aux = aux_ref[...] * alive
    dlogits = soft * (aux - jnp.sum(soft * aux, axis=-1, keepdims=True))
    dlogits += jnp.where(lane == route[:, 0:1], push, 0.0) - jnp.where(lane == route[:, 1:2], push, 0.0)
    dlogits = dlogits.astype(BF16)
    second = second_ref[0]
    router = tall_ref[:, :, width : width + 128].reshape(width, 128)
    drouter_ref[...] += dot_rows(second, dlogits)
    dsecond = dot_cols(dlogits, router) + (row_own[0].astype(F32) + row_far.astype(F32))
    hat, scale = standardise(middle)
    dmiddle = upstream + norm_back(dsecond, hat, scale, vec[5:6])
    dattn = dmiddle.astype(BF16)
    dvec_ref[EXPERTS + 4 : EXPERTS + 5] += column_sum(dattn.astype(F32))
    dvec_ref[EXPERTS + 5 : EXPERTS + 6] += column_sum(dsecond * hat)
    dvec_ref[EXPERTS + 6 : EXPERTS + 7] += column_sum(dsecond)
    dout_ref[...] += dot_rows(mixed_ref[0], dattn)
    out_full = tall_ref[:, :, :width].reshape(width, width)
    dmixed = dot_cols(dattn, out_full).astype(BF16)
    low_lanes = iota((PAD, 128), 1) < HEAD_DIM
    root = HEAD_DIM**-0.5
    for pair in range(HEADS // 2):
        at = pair * 128
        query = packed_ref[0, :, at : at + 128]
        keys = packed_ref[0, :, width + at : width + at + 128]
        valued = packed_ref[0, :, 2 * width + at : 2 * width + at + 128]
        grads = dmixed[:, at : at + 128]
        parts = []
        for side in range(2):
            own = low_lanes if side == 0 else ~low_lanes
            weights = prob_ref[0, 2 * pair + side]
            dweights = dot_cols(jnp.where(own, grads, jnp.zeros_like(grads)), valued)
            exact = weights.astype(F32)
            inner = jnp.sum(dweights * exact, axis=-1, keepdims=True)
            dscores = (exact * (dweights - inner)).astype(BF16)
            parts.append((dot(dscores, keys), dot_rows(dscores, query), dot_rows(weights, grads)))
        for third, factor in ((0, root), (1, root), (2, 1.0)):
            both = jnp.where(low_lanes, parts[0][third], parts[1][third]) * factor
            dpacked[:, third * width + at : third * width + at + 128] = both.astype(BF16)
    inputs = tok_ref[0].astype(F32)
    hat, scale = standardise(inputs)
    normed = (hat * vec[0:1] + vec[1:2]).astype(BF16)
    packed_grads = dpacked[...]
    dqkv_ref[...] += dot_rows(normed, packed_grads)
    dvec_ref[EXPERTS + 2 : EXPERTS + 3] += column_sum(packed_grads[:, :width].astype(F32))
    dvec_ref[EXPERTS + 3 : EXPERTS + 4] += column_sum(packed_grads[:, 2 * width :].astype(F32))
    qkv = wide_ref[:, :256, :].reshape(width, 3 * width)
    dnormed = dot_cols(packed_grads, qkv)
    dvec_ref[EXPERTS + 0 : EXPERTS + 1] += column_sum(dnormed * hat)
    dvec_ref[EXPERTS + 1 : EXPERTS + 2] += column_sum(dnormed)
    dtokens = dmiddle + norm_back(dnormed, hat, scale, vec[0:1])
    for k in range(images):

        @pl.when(image == k)
        def _():
            dtok_ref[pl.ds(k * IMG_TOK, IMG_TOK), :] = dtokens[:IMG_TOK]

    @pl.when(image == images - 1)
    def _():
        lines = jnp.transpose(dvec_ref[...])
        part = width // 8
        for owner in range(2):
            for half in range(2):
                for quarter in range(2):
                    at = ((owner * 2 + half) * 2 + quarter) * part
                    rows = slice(at, at + part)
                    spot = pack_ref.at[owner, half, quarter]
                    spot[:, : 3 * width] = dqkv_ref[rows].astype(BF16)
                    spot[:, 3 * width : 4 * width] = dout_ref[rows].astype(BF16)
                    spot[:, 4 * width :] = (drouter_ref[rows] + lines[rows]).astype(BF16)


def finish(count, tok, cot, saved, routes, row_own, row_far, gate_own, gate_far, aux, wide, tall, total, traffic, ident):
    images, _, width = tok.shape
    packed, prob, mixed, middle, second, soft = saved
    shape = jax.ShapeDtypeStruct
    tile = by_image(PAD, width)
    row_arrays = []
    for array, _, _ in row_far:
        if array is not None and not any(known is array for known in row_arrays):
            row_arrays.append(array)
    gate_arrays, gate_specs, read_gates = by_piece(gate_far, 8, PAD)
    lead, extra = len(row_arrays), len(row_arrays) + len(gate_arrays)

    def hook(step, require, targets, ins, held):
        array, target, position = row_far[step]
        if array is None:
            require(target, position)
            source = targets[target]
        else:
            source = next(ref for ref, known in zip(ins, row_arrays) if known is array)
        copy = pltpu.make_async_copy(source.at[position], held[-2], held[-1])
        copy.start()
        copy.wait()

    def body(*refs):
        pieces, far, refs = refs[:extra], refs[-2], list(refs[extra:-2])
        refs[11:11] = [far[...]]
        refs[13:13] = [read_gates(pieces[lead:])]
        finish_body(*refs)

    pack = (2, 2, 2, width // 8, 4 * width + 128)
    return run(
        body,
        (
            *row_arrays, *gate_arrays, count, tok, cot, packed, prob, mixed, middle, second, soft, routes,
            row_own, gate_own, aux, *wide, *tall,
        ),
        [
            *[pl.BlockSpec(memory_space=pl.ANY)] * lead,
            *gate_specs,
            scalar_spec(),
            tile,
            tile,
            by_image(PAD, 3 * width),
            by_image(HEADS, PAD, PAD),
            tile,
            tile,
            tile,
            by_image(PAD, 128),
            by_image(PAD, 2),
            tile,
            by_image(8, PAD),
            resident((1, 128)),
            resident(wide[0].shape),
            resident(wide[0].shape),
            resident(tall[0].shape),
            resident(tall[0].shape),
        ],
        [resident((total, width)), resident(pack)],
        [shape((total, width), F32), shape(pack, BF16)],
        grid=(images,),
        scratch=[
            pltpu.VMEM((PAD, 3 * width), BF16),
            pltpu.VMEM((2,) + wide[0].shape, BF16),
            pltpu.VMEM((2,) + tall[0].shape, BF16),
            pltpu.VMEM((width, 3 * width), F32),
            pltpu.VMEM((width, width), F32),
            pltpu.VMEM((width, 128), F32),
            pltpu.VMEM((128, width), F32),
            pltpu.VMEM((PAD, width), BF16),
            pltpu.SemaphoreType.DMA,
        ],
        cost=pl.CostEstimate(flops=12_000_000_000, bytes_accessed=24_000_000, transcendentals=0),
        name="finish",
        traffic=traffic,
        hook=hook,
        ident=ident,
    )


def add(left, right):
    return (left.astype(F32) + right.astype(F32)).astype(BF16)


class Exchange:
    def __init__(self, send, recv):
        self.send, self.recv = send, recv

    def at(self, index, link, source, target):
        move = Move(link, lambda _: source, lambda _: target)
        return move.roles(), move.copy(None, self.send.at[index], self.recv.at[index])


def begin(make):
    roles, copy = make()
    only_if(roles[0], copy.start)


def end(make):
    roles, copy = make()
    only_if(roles[0], copy.wait_send)
    only_if(roles[1], copy.wait_recv)


def sums_everywhere(load, soft_sum, steps):
    shape = (2,) + load.shape[1:]
    links = ("core", "y", "x", "near", "inner", "outward")

    def copies(load_ref, soft_ref, total, held, got, send, recv):
        made = Exchange(send, recv)
        return [
            lambda k=k, link=link: made.at(k, link, held.at[k], held.at[k] if link == "outward" else got.at[k])
            for k, link in enumerate(links)
        ]

    def first(*refs):
        load_ref, soft_ref, _, held = refs[:4]
        held[0, 0], held[0, 1] = load_ref[0], soft_ref[0]
        begin(copies(*refs)[0])

    def stage(k):
        def action(*refs):
            held, got = refs[3:5]
            end(copies(*refs)[k - 1])
            if links[k] == "outward":

                @pl.when(((lax.axis_index("rep") // 4) % 3) > 0)
                def _():
                    held[k] = held[k - 1] + got[k - 1]

            else:
                held[k] = held[k - 1] + got[k - 1]
            begin(copies(*refs)[k])

        return action

    def last(*refs):
        end(copies(*refs)[5])
        refs[2][...] = refs[3][5]

    return Chain(
        [load, soft_sum],
        [resident(load.shape)] * 2,
        [resident(shape)],
        [jax.ShapeDtypeStruct(shape, F32)],
        [pltpu.VMEM((6,) + shape, F32), pltpu.VMEM((5,) + shape, F32)] + [pltpu.SemaphoreType.DMA((6,))] * 2,
        {"core", "y", "x", "near", "inner"},
        list(zip(steps, [first] + [stage(k) for k in range(1, 6)])) + [(0, last)],
    )


def owner_sums(pack, steps):
    shape = pack.shape[2:]

    def first(pack_ref, part, near_in, half, far_in, send, recv):
        core = lax.axis_index("rep") % 2
        Exchange(send, recv).at(0, "core", pack_ref.at[:, 1 - core], near_in)[1].start()

    def second(pack_ref, part, near_in, half, far_in, send, recv):
        core, mine = lax.axis_index("rep") % 2, lax.axis_index("fsdp")
        Exchange(send, recv).at(0, "core", pack_ref.at[:, 1 - core], near_in)[1].wait()
        half[...] = add(pack_ref[:, core], near_in[...])
        Exchange(send, recv).at(1, "y", half.at[1 - mine], far_in)[1].start()

    def last(pack_ref, part, near_in, half, far_in, send, recv):
        mine = lax.axis_index("fsdp")
        Exchange(send, recv).at(1, "y", half.at[1 - mine], far_in)[1].wait()
        part[...] = add(half[mine], far_in[...])

    return Chain(
        [pack],
        [pl.BlockSpec(pack.shape, lambda *_: (0,) * 5, pipeline_mode=pl.Buffered(1))],
        [resident(shape)],
        [jax.ShapeDtypeStruct(shape, BF16)],
        [pltpu.VMEM((2,) + shape, BF16), pltpu.VMEM((2,) + shape, BF16), pltpu.VMEM(shape, BF16)]
        + [pltpu.SemaphoreType.DMA((2,))] * 2,
        {"core", "y"},
        [(steps[0], first), (steps[1], second), (0, last)],
    )


def copy_sums(part, steps):
    shape = part.shape[1:]

    def copies(part_ref, total, x_in, held, near_in, line, inner_in, full, send, recv):
        device = lax.axis_index("rep")
        core, side = device % 2, (device // 2) % 2
        made = Exchange(send, recv)
        mine = full.at[core, side]
        plans = [
            ("x", part_ref.at[1 - side], x_in),
            ("near", held, near_in),
            ("inner", line, inner_in),
            ("outward", mine, mine),
            ("x", mine, mine),
            ("core", full.at[core], full.at[core]),
        ]
        return [lambda k=k, plan=plan: made.at(k, *plan) for k, plan in enumerate(plans)]

    def first(*refs):
        begin(copies(*refs)[0])

    def second(*refs):
        part_ref, total, x_in, held = refs[:4]
        steps = copies(*refs)
        end(steps[0])
        side = (lax.axis_index("rep") // 2) % 2
        held[...] = add(part_ref[side], x_in[...])
        begin(steps[1])

    def third(*refs):
        part_ref, total, x_in, held, near_in, line = refs[:6]
        steps = copies(*refs)
        end(steps[1])
        line[...] = add(held[...], near_in[...])
        begin(steps[2])

    def fourth(*refs):
        part_ref, total, x_in, held, near_in, line, inner_in, full = refs[:8]
        steps = copies(*refs)
        device = lax.axis_index("rep")
        middle = ((device // 4) % 3) > 0
        end(steps[2])

        @pl.when(middle)
        def _():
            full[device % 2, (device // 2) % 2] = add(line[...], inner_in[...])

        begin(steps[3])

    def fifth(*refs):
        steps = copies(*refs)
        end(steps[3])
        begin(steps[4])

    def sixth(*refs):
        steps = copies(*refs)
        end(steps[4])
        begin(steps[5])

    def last(*refs):
        total, full = refs[1], refs[7]
        end(copies(*refs)[5])
        total[...] = full[...]

    whole = (2, 2) + shape
    return Chain(
        [part],
        [resident(part.shape)],
        [resident(whole)],
        [jax.ShapeDtypeStruct(whole, BF16)],
        [pltpu.VMEM(shape, BF16)] * 5 + [pltpu.VMEM(whole, BF16)] + [pltpu.SemaphoreType.DMA((6,))] * 2,
        {"core", "x", "near", "inner"},
        list(zip(steps, (first, second, third, fourth, fifth, sixth))) + [(0, last)],
    )


def emit(count, middle, sum_own, sum_far, total):
    images, _, width = middle.shape
    far_arrays, far_specs, read_far = by_piece(sum_far, PAD, width)

    def body(count_ref, middle_ref, own_ref, *refs):
        far, (out_ref, held) = refs[:-2], refs[-2:]
        image = pl.program_id(0)
        live = (iota((PAD, 1), 0) < IMG_TOK) & (image < count_ref[0])
        both = own_ref[0].astype(F32) + read_far(far).astype(F32)
        result = jnp.where(live, 1.0, 0.0) * (middle_ref[0] + both)
        for k in range(images):

            @pl.when(image == k)
            def _():
                held[pl.ds(k * IMG_TOK, IMG_TOK), :] = result[:IMG_TOK]

        @pl.when(image == images - 1)
        def _():
            out_ref[...] = held[pl.ds(0, total), :].astype(BF16)

    tile = by_image(PAD, width)
    return run(
        body,
        (count, middle, sum_own, *far_arrays),
        [scalar_spec(), tile, tile, *far_specs],
        [resident((total, width))],
        [jax.ShapeDtypeStruct((total, width), BF16)],
        grid=(images,),
        scratch=[pltpu.VMEM((1000, width), F32)],
        cost=pl.CostEstimate(flops=2_000_000, bytes_accessed=6_000_000, transcendentals=0),
        name="emit",
    )[0][0]


def by_slice(
    tokens, cotangent, routes, image_count, capacity, norm1_gain, norm1_bias, w_qkv, bias_q, bias_v, w_out, bias_out,
    norm2_gain, norm2_bias, w_router, expert_in, expert_in_bias, expert_out, expert_out_bias,
):
    total, width = tokens.shape
    local = expert_in.shape[0]
    device = lax.axis_index("rep")
    mine = lax.axis_index("fsdp")
    core = device % 2
    small = jnp.stack([norm1_gain, norm1_bias, bias_q, bias_v, bias_out, norm2_gain, norm2_bias])
    small = jnp.pad(small, ((0, 9), (0, 3 * width - small.shape[1])))
    wide = jnp.concatenate([w_qkv, small], axis=0)
    tall = jnp.concatenate([w_out, jnp.pad(w_router, ((0, 0), (0, 128 - EXPERTS)))], axis=1)
    (tok, cot, route, ids, load), (wide_far, tall_far), _ = prepare(
        tokens, cotangent, routes, image_count, capacity, wide, tall, 0
    )
    wide, tall = (wide, wide_far), (tall, tall_far)
    base = (mine * (local * CAP)).reshape(1)
    net = Network()
    net.offer("C", cot, COT_PATHS)
    idents = iter(range(1, 32))

    def staged(kernel, *args, rounds):
        traffic, plan = net.plan(*rounds)
        args = [arg(plan) if callable(arg) else arg for arg in args]
        outs, arrived, chained = kernel(*args, traffic, next(idents))
        net.land(plan, arrived)
        return (*outs, *chained)

    own, far = (0, 0, 0), (0, 0, 1)
    packed, prob, mixed, middle, second, soft, soft_sum = staged(
        front, image_count, tok, ids, route, wide, tall, rounds=evenly(FRONT_ROOM, 5, 0.68)
    )
    net.offer("S", second, ROW_PATHS)

    def sender(block):
        return net.block("S", block), net.block("C", block)

    def senders(blocks):
        return lambda plan: [(net.find(plan, "S", block), net.find(plan, "C", block)) for block in blocks]

    pair = staged(
        gather, base, local, senders([own, far]), [0, None, None, None, None, 1],
        rounds=(PAIR_ROOM, list(range(8)), [0.0, 0.45, 0.9, 1.9, 2.9, 3.9, 5.0, 6.0]),
    )
    made_own, made_far, back_own, back_far, sums = staged(
        expert_layer, pair, expert_in, expert_in_bias, expert_out, expert_out_bias,
        sums_everywhere(load, soft_sum, (0, 2, 5, 8, 11, 13)),
        rounds=evenly(EXPERT_ROOM, 16, 0.7, 2),
    )
    sum_far, drow_far, dgate_far = staged(
        combine, base, *sender(far), made_far, back_far, rounds=evenly(2, 5, 0.4, 2)
    )
    net.offer("D", drow_far, FAR_FIRST)
    net.offer("G", dgate_far, FAR_FIRST, 0)
    net.offer("M", sum_far, FAR_LAST)
    sum_own, drow_own, dgate_own = staged(
        combine, base, *sender(own), made_own, back_own, rounds=evenly(OWN_ROOM, 5, 0.4)
    )
    loads, prob_total = sums[0, 0:1], sums[1, 0:1]
    live = loads[:, 64:65]
    share = (loads[:, :EXPERTS] + loads[:, EXPERTS : 2 * EXPERTS]) / (2.0 * live)
    aux = jnp.pad(EXPERTS * share / live, ((0, 0), (0, 128 - EXPERTS)))
    grad_tokens, pack = staged(
        finish, image_count, tok, cot, (packed, prob, mixed, middle, second, soft), route, drow_own,
        lambda plan: net.find(plan, "D", far), dgate_own, net.block("G", far), aux, wide, tall, total,
        rounds=evenly(FINISH_ROOM, 5, 1.5),
    )
    blocks = [block for block in COT_PATHS if block != far]
    count = 2 * len(blocks) + 2
    traffic, plan = net.plan(LAST_ROOM, list(range(count)), [LAST_ROOM * k / count for k in range(count)])
    blocks.sort(key=lambda block: net.landing(plan, block))
    outs, arrived, (part,) = gather(
        base, local, senders(blocks)(plan), list(range(len(blocks))) + [None, None],
        traffic, next(idents), owner_sums(pack, (0, 6)),
    )
    net.land(plan, arrived)
    slots = [pair, outs]
    outputs = emit(image_count, middle, sum_own, net.block("M", far), total)
    row_slots = [pair[0] for pair in slots]
    grad_slots = [pair[1] for pair in slots]
    (keep_in, send_in, keep_out, send_out, d_bias, d_out_bias), _, (owned,) = slice_grads(
        row_slots, grad_slots, expert_in, expert_in_bias, expert_out, copy_sums(part, (0, 3, 6, 9, 12, 15)), next(idents)
    )
    owned = owned.reshape(width // 2, -1).astype(F32)
    swap = [(i, i ^ 1) for i in range(16)]
    got_in, got_out, got_bias, got_out_bias = (
        lax.ppermute(v, "rep", swap) for v in (send_in, send_out, d_bias, d_out_bias)
    )
    bias = (d_bias + got_bias)[:, 0]
    out_bias = (d_out_bias + got_out_bias)[:, 0]
    half = bias.shape[1] // 2
    piece = width // 16
    expert_grads = (
        keep_in + got_in.astype(F32),
        lax.dynamic_slice_in_dim(bias, core * half, half, axis=1),
        keep_out + got_out.astype(F32),
        lax.dynamic_slice_in_dim(out_bias, device * piece, piece, axis=1),
    )

    balance_loss = jnp.sum(aux * prob_total)
    lines = jnp.transpose(owned[:, 4 * width + EXPERTS : 4 * width + EXPERTS + 8])
    owned = (
        lines[0],
        lines[1],
        owned[:, : 3 * width],
        lines[2],
        lines[3],
        owned[:, 3 * width : 4 * width],
        lines[4],
        lines[5],
        lines[6],
        owned[:, 4 * width : 4 * width + EXPERTS],
    )
    return (outputs, grad_tokens, balance_loss) + owned + expert_grads


def solution(mesh):
    in_specs = (
        P(("rep", "fsdp"), None),
        P(("rep", "fsdp"), None),
        P(("rep", "fsdp"), None),
        P(("rep", "fsdp")),
        P(("rep", "fsdp")),
        P("fsdp"),
        P("fsdp"),
        P("fsdp", None),
        P("fsdp"),
        P("fsdp"),
        P("fsdp", None),
        P("fsdp"),
        P("fsdp"),
        P("fsdp"),
        P("fsdp", None),
        P("fsdp", None, None),
        P("fsdp", None),
        P("fsdp", None, None),
        P("fsdp", None),
    )
    out_specs = (
        P(("rep", "fsdp"), None),
        P(("rep", "fsdp"), None),
        P(),
        P("fsdp"),
        P("fsdp"),
        P("fsdp", None),
        P("fsdp"),
        P("fsdp"),
        P("fsdp", None),
        P("fsdp"),
        P("fsdp"),
        P("fsdp"),
        P("fsdp", None),
        P("fsdp", None, "rep"),
        P("fsdp", "rep"),
        P("fsdp", "rep", None),
        P("fsdp", "rep"),
    )
    program = by_slice if mesh.shape["rep"] == 16 and mesh.shape["fsdp"] == 2 else shards
    return jax.shard_map(program, mesh=mesh, in_specs=in_specs, out_specs=out_specs, check_vma=False)
```

```python
import jax
import jax.numpy as jnp
from jax import lax
from jax.experimental import pallas as pl
from jax.experimental.pallas import tpu as pltpu
from jax.sharding import PartitionSpec as P

HEADS = 8
HEAD_DIM = 64
EXPERTS = 32
IMG_TOK = 197
CAP = 80


def norm_rows(values, norm_gain, offset):
    average = jnp.mean(values, axis=-1, keepdims=True)
    centred = values - average
    variance = jnp.mean(centred * centred, axis=-1, keepdims=True)
    return centred * lax.rsqrt(variance + 1e-06) * norm_gain + offset


def slot_table(choices, alive_mask, limit, row_total):
    pair_expert = jnp.concatenate([choices[:, 0], choices[:, 1]])
    live_pairs = jnp.concatenate([alive_mask, alive_mask])
    expert_ids = jnp.arange(EXPERTS, dtype=jnp.int32)
    onehot = ((pair_expert[:, None] == expert_ids[None, :]) & live_pairs[:, None]).astype(jnp.int32)
    before = jnp.cumsum(onehot, axis=0) - onehot
    position = jnp.sum(before * onehot, axis=1)
    kept_pairs = live_pairs & (position < limit)
    pair_slot = pair_expert * CAP + position
    pair_token = jnp.concatenate(
        [jnp.arange(row_total, dtype=jnp.int32), jnp.arange(row_total, dtype=jnp.int32)]
    )
    slot_owner = jnp.full((EXPERTS * CAP,), row_total, jnp.int32)
    target = jnp.where(kept_pairs, pair_slot, EXPERTS * CAP)
    slot_owner = slot_owner.at[target].set(pair_token, mode="drop")
    safe_slot = jnp.where(kept_pairs, pair_slot, 0)
    return (slot_owner, kept_pairs, safe_slot, target, onehot)


def shards(
    tokens,
    cotangent,
    routes,
    image_count,
    capacity,
    norm1_gain,
    norm1_bias,
    w_qkv,
    bias_q,
    bias_v,
    w_out,
    bias_out,
    norm2_gain,
    norm2_bias,
    w_router,
    expert_in,
    expert_in_bias,
    expert_out,
    expert_out_bias,
):
    rows_count = tokens.shape[0]
    model_width = tokens.shape[1]
    image_total = rows_count // IMG_TOK
    score_scale = HEAD_DIM ** (-0.5)
    image_rows = jnp.arange(rows_count, dtype=jnp.int32) // IMG_TOK
    alive_mask = image_rows < image_count[0]
    alive_float = alive_mask.astype(jnp.float32)[:, None]
    slot_owner, kept_pairs, safe_slot, target, onehot = slot_table(
        routes, alive_mask, capacity[0], rows_count
    )
    kept_float = kept_pairs.astype(jnp.float32)
    load_local = jnp.sum(onehot.astype(jnp.float32), axis=0)
    live_local = jnp.sum(alive_float)
    load_total, live_total = lax.psum((load_local, live_local), ("rep", "fsdp"))
    gathered = (
        lax.all_gather(norm1_gain, "fsdp", axis=0, tiled=True),
        lax.all_gather(norm1_bias, "fsdp", axis=0, tiled=True),
        lax.all_gather(w_qkv, "fsdp", axis=0, tiled=True),
        lax.all_gather(bias_q, "fsdp", axis=0, tiled=True),
        lax.all_gather(bias_v, "fsdp", axis=0, tiled=True),
        lax.all_gather(w_out, "fsdp", axis=0, tiled=True),
        lax.all_gather(bias_out, "fsdp", axis=0, tiled=True),
        lax.all_gather(norm2_gain, "fsdp", axis=0, tiled=True),
        lax.all_gather(norm2_bias, "fsdp", axis=0, tiled=True),
        lax.all_gather(w_router, "fsdp", axis=0, tiled=True),
    )
    (
        gain_one,
        shift_one,
        qkv_full,
        query_bias,
        value_bias,
        out_full,
        out_bias,
        gain_two,
        shift_two,
        router_full,
    ) = gathered
    gain_one = gain_one.astype(jnp.float32)
    shift_one = shift_one.astype(jnp.float32)
    gain_two = gain_two.astype(jnp.float32)
    shift_two = shift_two.astype(jnp.float32)
    inputs = tokens.astype(jnp.float32)
    normed = norm_rows(inputs, gain_one, shift_one)
    normed_low = normed.astype(jnp.bfloat16)
    bias_row = jnp.concatenate([query_bias, jnp.zeros_like(query_bias), value_bias]).astype(
        jnp.float32
    )
    packed_low = (
        jnp.dot(normed_low, qkv_full, preferred_element_type=jnp.float32) + bias_row
    ).astype(jnp.bfloat16)
    image_shape = (image_total, IMG_TOK, HEADS, HEAD_DIM)
    queries = packed_low[:, :model_width].reshape(image_shape)
    all_keys = packed_low[:, model_width : 2 * model_width].reshape(image_shape)
    valued = packed_low[:, 2 * model_width :].reshape(image_shape)

    def score_block():
        return (
            jnp.einsum("iqhd,ikhd->hiqk", queries, all_keys, preferred_element_type=jnp.float32)
            * score_scale
        )

    scores = score_block()
    row_peak = jnp.max(scores, axis=-1, keepdims=True)
    exp_scores = jnp.exp(scores - row_peak)
    totals = jnp.sum(exp_scores, axis=-1, keepdims=True)
    log_total = row_peak + jnp.log(totals)
    attn_low = (exp_scores / totals).astype(jnp.bfloat16)
    mixed_low = (
        jnp.einsum("hiqk,ikhd->iqhd", attn_low, valued, preferred_element_type=jnp.float32)
        .reshape(rows_count, model_width)
        .astype(jnp.bfloat16)
    )
    middle = (
        inputs
        + jnp.dot(mixed_low, out_full, preferred_element_type=jnp.float32)
        + out_bias.astype(jnp.float32)
    )
    second_low = norm_rows(middle, gain_two, shift_two).astype(jnp.bfloat16)
    logits = jnp.dot(second_low, router_full, preferred_element_type=jnp.float32)
    expert_ids = jnp.arange(EXPERTS, dtype=jnp.int32)
    first_hot = (routes[:, 0:1] == expert_ids[None, :]).astype(jnp.float32)
    second_hot = (routes[:, 1:2] == expert_ids[None, :]).astype(jnp.float32)

    def gate_terms(logit_rows):
        router_probs = jax.nn.softmax(logit_rows, axis=-1)
        pick_one = jnp.sum(router_probs * first_hot, axis=-1)
        pick_two = jnp.sum(router_probs * second_hot, axis=-1)
        pick_total = pick_one + pick_two
        return (pick_one / pick_total, pick_two / pick_total, router_probs)

    (gate_first, gate_second, router_probs), gate_back = jax.vjp(gate_terms, logits)
    padded_rows = jnp.concatenate([second_low, jnp.zeros((1, model_width), jnp.bfloat16)], axis=0)
    sent_rows = padded_rows[slot_owner].reshape(EXPERTS, CAP, model_width)
    received = lax.all_to_all(sent_rows, "fsdp", split_axis=0, concat_axis=1, tiled=True)
    raised = (
        jnp.einsum("esd,edf->esf", received, expert_in, preferred_element_type=jnp.float32)
        + expert_in_bias.astype(jnp.float32)[:, None, :]
    )
    active, gelu_back = jax.vjp(jax.nn.gelu, raised)
    active_low = active.astype(jnp.bfloat16)
    produced = (
        jnp.einsum("esf,efd->esd", active_low, expert_out, preferred_element_type=jnp.float32)
        + expert_out_bias.astype(jnp.float32)[:, None, :]
    ).astype(jnp.bfloat16)
    returned = lax.all_to_all(produced, "fsdp", split_axis=1, concat_axis=0, tiled=True).reshape(
        EXPERTS * CAP, model_width
    )
    pair_rows = returned[safe_slot].astype(jnp.float32)
    pair_weight = jnp.concatenate([gate_first, gate_second]) * kept_float
    expert_sum = jnp.sum(
        (pair_rows * pair_weight[:, None]).reshape(2, rows_count, model_width), axis=0
    )
    outputs = (alive_float * (middle + expert_sum)).astype(jnp.bfloat16)
    upstream = cotangent.astype(jnp.float32) * alive_float
    pair_grad = jnp.concatenate([upstream, upstream], axis=0)
    gate_grads = jnp.sum(pair_grad * pair_rows, axis=1) * kept_float
    slot_gate = jnp.zeros((EXPERTS * CAP,), jnp.float32).at[target].set(pair_weight, mode="drop")
    padded_grad = jnp.concatenate([upstream, jnp.zeros((1, model_width), jnp.float32)], axis=0)
    slot_grads = (
        (padded_grad[slot_owner] * slot_gate[:, None])
        .astype(jnp.bfloat16)
        .reshape(EXPERTS, CAP, model_width)
    )
    grad_received = lax.all_to_all(slot_grads, "fsdp", split_axis=0, concat_axis=1, tiled=True)
    grad_active = jnp.einsum(
        "esd,efd->esf", grad_received, expert_out, preferred_element_type=jnp.float32
    )
    (grad_raised,) = gelu_back(grad_active)
    grad_raised_low = grad_raised.astype(jnp.bfloat16)
    grad_rows = jnp.einsum(
        "esf,edf->esd", grad_raised_low, expert_in, preferred_element_type=jnp.float32
    ).astype(jnp.bfloat16)
    back_rows = lax.all_to_all(grad_rows, "fsdp", split_axis=1, concat_axis=0, tiled=True).reshape(
        EXPERTS * CAP, model_width
    )
    expert_part = jnp.sum(
        (back_rows[safe_slot].astype(jnp.float32) * kept_float[:, None]).reshape(
            2, rows_count, model_width
        ),
        axis=0,
    )
    local_in = jnp.einsum(
        "esd,esf->edf", received, grad_raised_low, preferred_element_type=jnp.float32
    )
    local_in_bias = jnp.sum(grad_raised_low.astype(jnp.float32), axis=1)
    local_out = jnp.einsum(
        "esf,esd->efd", active_low, grad_received, preferred_element_type=jnp.float32
    )
    local_out_bias = jnp.sum(grad_received.astype(jnp.float32), axis=1)
    grad_in_weight, grad_in_bias, grad_out_weight, grad_out_expert_bias = (
        lax.psum_scatter(local_in, "rep", scatter_dimension=2, tiled=True),
        lax.psum_scatter(local_in_bias, "rep", scatter_dimension=1, tiled=True),
        lax.psum_scatter(local_out, "rep", scatter_dimension=1, tiled=True),
        lax.psum_scatter(local_out_bias, "rep", scatter_dimension=1, tiled=True),
    )
    prob_local = jnp.sum(router_probs * alive_float, axis=0)
    prob_total = lax.psum(prob_local, ("rep", "fsdp"))
    share = load_total / (2.0 * live_total)
    balance_loss = EXPERTS * jnp.sum(share * prob_total / live_total)
    aux_grad = alive_float * (EXPERTS * share / live_total)[None, :]
    (grad_logits,) = gate_back((gate_grads[:rows_count], gate_grads[rows_count:], aux_grad))
    grad_logits_low = grad_logits.astype(jnp.bfloat16)
    grad_router = jnp.dot(second_low.T, grad_logits_low, preferred_element_type=jnp.float32)
    grad_second = (
        jnp.dot(grad_logits_low, router_full.T, preferred_element_type=jnp.float32) + expert_part
    )
    _, norm_two_back = jax.vjp(norm_rows, middle, gain_two, shift_two)
    grad_mid_norm, grad_gain_two, grad_shift_two = norm_two_back(grad_second)
    grad_middle = upstream + grad_mid_norm
    grad_att_low = grad_middle.astype(jnp.bfloat16)
    grad_out_proj = jnp.dot(mixed_low.T, grad_att_low, preferred_element_type=jnp.float32)
    grad_out_bias = jnp.sum(grad_att_low.astype(jnp.float32), axis=0)
    grad_mixed = (
        jnp.dot(grad_att_low, out_full.T, preferred_element_type=jnp.float32)
        .astype(jnp.bfloat16)
        .reshape(image_shape)
    )
    recomputed = jnp.exp(score_block() - log_total)
    grad_weights = jnp.einsum(
        "iqhd,ikhd->hiqk", grad_mixed, valued, preferred_element_type=jnp.float32
    )
    grad_values = jnp.einsum(
        "hiqk,iqhd->ikhd",
        recomputed.astype(jnp.bfloat16),
        grad_mixed,
        preferred_element_type=jnp.float32,
    )
    inner_sum = jnp.sum(grad_weights * recomputed, axis=-1, keepdims=True)
    grad_scores = (recomputed * (grad_weights - inner_sum)).astype(jnp.bfloat16)
    grad_queries = (
        jnp.einsum("hiqk,ikhd->iqhd", grad_scores, all_keys, preferred_element_type=jnp.float32)
        * score_scale
    )
    grad_keys = (
        jnp.einsum("hiqk,iqhd->ikhd", grad_scores, queries, preferred_element_type=jnp.float32)
        * score_scale
    )
    grad_packed_low = jnp.concatenate(
        [
            grad_queries.reshape(rows_count, model_width),
            grad_keys.reshape(rows_count, model_width),
            grad_values.reshape(rows_count, model_width),
        ],
        axis=1,
    ).astype(jnp.bfloat16)
    grad_qkv = jnp.dot(normed_low.T, grad_packed_low, preferred_element_type=jnp.float32)
    packed_sums = jnp.sum(grad_packed_low.astype(jnp.float32), axis=0)
    grad_query_bias = packed_sums[:model_width]
    grad_value_bias = packed_sums[2 * model_width :]
    grad_normed = jnp.dot(grad_packed_low, qkv_full.T, preferred_element_type=jnp.float32)
    _, norm_one_back = jax.vjp(norm_rows, inputs, gain_one, shift_one)
    grad_input_norm, grad_gain_one, grad_shift_one = norm_one_back(grad_normed)
    grad_tokens = grad_middle + grad_input_norm
    local_grads = (
        grad_gain_one,
        grad_shift_one,
        grad_qkv,
        grad_query_bias,
        grad_value_bias,
        grad_out_proj,
        grad_out_bias,
        grad_gain_two,
        grad_shift_two,
        grad_router,
    )
    shares = (
        lax.psum_scatter(local_grads[0], "fsdp", scatter_dimension=0, tiled=True),
        lax.psum_scatter(local_grads[1], "fsdp", scatter_dimension=0, tiled=True),
        lax.psum_scatter(local_grads[2], "fsdp", scatter_dimension=0, tiled=True),
        lax.psum_scatter(local_grads[3], "fsdp", scatter_dimension=0, tiled=True),
        lax.psum_scatter(local_grads[4], "fsdp", scatter_dimension=0, tiled=True),
        lax.psum_scatter(local_grads[5], "fsdp", scatter_dimension=0, tiled=True),
        lax.psum_scatter(local_grads[6], "fsdp", scatter_dimension=0, tiled=True),
        lax.psum_scatter(local_grads[7], "fsdp", scatter_dimension=0, tiled=True),
        lax.psum_scatter(local_grads[8], "fsdp", scatter_dimension=0, tiled=True),
        lax.psum_scatter(local_grads[9], "fsdp", scatter_dimension=0, tiled=True),
    )
    owned = lax.psum(
        (
            shares[0],
            shares[1],
            shares[2],
            shares[3],
            shares[4],
            shares[5],
            shares[6],
            shares[7],
            shares[8],
            shares[9],
        ),
        "rep",
    )
    return (
        (outputs, grad_tokens, balance_loss)
        + tuple(owned)
        + (grad_in_weight, grad_in_bias, grad_out_weight, grad_out_expert_bias)
    )


def gelu_pair(value):
    root = 0.7978845608028654
    square = value * value
    bend = jnp.tanh(root * value * (1.0 + 0.044715 * square))
    half = 0.5 * (1.0 + bend)
    slope = half + 0.5 * value * (1.0 - bend * bend) * root * (1.0 + 3 * 0.044715 * square)
    return value * half, slope


def slice_grads_body(*refs, senders):
    parts, refs = refs[: sum(senders)], refs[sum(senders) :]
    in_ref, in_bias_ref, out_ref, keep_in, send_in, keep_out, send_out, d_bias, d_out_bias = refs
    core = lax.axis_index("rep") % 2
    width = in_ref.shape[1]

    def stacked(pieces):
        return jnp.concatenate([piece[...].reshape(-1, width) for piece in pieces], axis=0)

    rows = stacked(parts[: senders[0]])
    grads = stacked(parts[senders[0] :])
    first = in_ref[0]
    second = out_ref[0]
    raised = jnp.dot(rows, first, preferred_element_type=jnp.float32) + own_line(in_bias_ref)
    active, slope = gelu_pair(raised)
    active = active.astype(jnp.bfloat16)
    back = lax.dot_general(
        grads, second, (((1,), (1,)), ((), ())), preferred_element_type=jnp.float32
    )
    draised = (back * slope).astype(jnp.bfloat16)
    over_rows = (((0,), (0,)), ((), ()))
    g_in = lax.dot_general(rows, draised, over_rows, preferred_element_type=jnp.float32)
    g_out = lax.dot_general(active, grads, over_rows, preferred_element_type=jnp.float32)
    half = g_in.shape[1] // 2
    first_core = core == 0
    keep_in[0] = jnp.where(first_core, g_in[:, :half], g_in[:, half:])
    send_in[0] = jnp.where(first_core, g_in[:, half:], g_in[:, :half]).astype(jnp.bfloat16)
    keep_out[0] = jnp.where(first_core, g_out[:half], g_out[half:])
    send_out[0] = jnp.where(first_core, g_out[half:], g_out[:half]).astype(jnp.bfloat16)
    d_bias[0] = jnp.sum(draised.astype(jnp.float32), axis=0, keepdims=True)
    d_out_bias[0] = jnp.sum(grads.astype(jnp.float32), axis=0, keepdims=True)


def slice_grads(rows, grads, first, first_bias, second, chain, ident):
    experts, width, hidden = first.shape
    cap = rows[0].shape[2]
    slots = cap * sum(piece.shape[1] for piece in rows)
    part = 256
    half = part // 2
    f32 = jnp.float32
    def chip():
        return lax.axis_index("rep") // 2

    return run(
        lambda *refs: slice_grads_body(*refs, senders=(len(rows), len(grads))),
        (*rows, *grads, first, first_bias, second),
        [pl.BlockSpec((1,) + piece.shape[1:], lambda e: (e, 0, 0, 0)) for piece in (*rows, *grads)]
        + [
            pl.BlockSpec((1, width, part), lambda e: (e, 0, chip())),
            pl.BlockSpec((experts, part), lambda e: (0, chip())),
            pl.BlockSpec((1, part, width), lambda e: (e, chip(), 0)),
        ],
        [by_image(width, half)] * 2 + [by_image(half, width)] * 2 + [by_image(1, part), by_image(1, width)],
        [
            jax.ShapeDtypeStruct((experts, width, half), f32),
            jax.ShapeDtypeStruct((experts, width, half), jnp.bfloat16),
            jax.ShapeDtypeStruct((experts, half, width), f32),
            jax.ShapeDtypeStruct((experts, half, width), jnp.bfloat16),
            jax.ShapeDtypeStruct((experts, 1, part), f32),
            jax.ShapeDtypeStruct((experts, 1, width), f32),
        ],
        grid=(experts,),
        cost=pl.CostEstimate(
            flops=8 * experts * slots * width * part,
            bytes_accessed=4 * experts * (slots * width + 3 * width * part),
            transcendentals=experts * slots * part,
        ),
        name="slice_grads",
        chain=chain,
        ident=ident,
    )


F32 = jnp.float32
BF16 = jnp.bfloat16
PAD = 208
ROOT_AXES = ("rep", "fsdp")
OVER_COLS = (((1,), (1,)), ((), ()))
OVER_ROWS = (((0,), (0,)), ((), ()))


def dot(left, right):
    return jnp.dot(left, right, preferred_element_type=F32)


def dot_cols(left, right):
    return lax.dot_general(left, right, OVER_COLS, preferred_element_type=F32)


def dot_rows(left, right):
    return lax.dot_general(left, right, OVER_ROWS, preferred_element_type=F32)


def iota(shape, axis):
    return lax.broadcasted_iota(jnp.int32, shape, axis)


def resident(shape):
    return pl.BlockSpec(shape, lambda *_: (0,) * len(shape))


def by_image(*shape):
    return pl.BlockSpec((1,) + shape, lambda i, *_: (i,) + (0,) * len(shape))


def scalar_spec():
    return pl.BlockSpec(memory_space=pltpu.SMEM)


def partner(link):
    device, side = lax.axis_index("rep"), lax.axis_index("fsdp")
    if link == "y":
        return {"rep": device, "fsdp": 1 - side}
    depth = device // 4
    step = {
        "core": 1 - 2 * (device % 2),
        "x": 2 - 4 * ((device // 2) % 2),
        "near": 4 - 8 * (depth % 2),
        "inner": 12 - 8 * depth,
        "skip": 8 - 16 * (depth // 2),
    }[link]
    return {"rep": device + step, "fsdp": side}


def only_if(condition, action):
    if condition is None:
        action()
    else:
        pl.when(condition)(action)


class Move:
    def __init__(self, link, source, target, needs=()):
        self.link, self.source, self.target, self.needs = link, source, target, needs

    def roles(self):
        depth = lax.axis_index("rep") // 4
        middle = (depth % 3) > 0
        if self.link == "inner":
            return middle, middle
        if self.link in ("outward", "skip"):
            return middle, (depth % 3) == 0
        return None, None

    def copy(self, refs, send, recv):
        return pltpu.make_async_remote_copy(
            src_ref=self.source(refs),
            dst_ref=self.target(refs),
            send_sem=send,
            recv_sem=recv,
            device_id=partner("near" if self.link == "outward" else self.link),
            device_id_type=pl.DeviceIdType.MESH,
        )


class Traffic:
    def __init__(self, sources, targets, rounds, steps):
        self.sources, self.targets, self.rounds, self.steps = sources, targets, rounds, steps

    def count(self):
        return sum(len(moves) for moves in self.rounds)

    def links(self):
        return {("near" if m.link == "outward" else m.link) for moves in self.rounds for m in moves}

    def start(self, which, refs, send, recv, arrived):
        moves = [m for moves in self.rounds for m in moves]
        at = sum(len(moves) for moves in self.rounds[:which])
        for k, move in enumerate(self.rounds[which]):
            for index in move.needs:
                if index not in arrived:
                    arrived.add(index)
                    only_if(moves[index].roles()[1], moves[index].copy(refs, send.at[index], recv.at[index]).wait_recv)
            only_if(move.roles()[0], move.copy(refs, send.at[at + k], recv.at[at + k]).start)

    def require(self, target, position, refs, send, recv, arrived):
        moves = [m for moves in self.rounds for m in moves]
        for index, move in enumerate(moves):
            if move.home[0] == target and move.home[1] <= position < move.home[1] + move.size and index not in arrived:
                arrived.add(index)
                only_if(move.roles()[1], move.copy(refs, send.at[index], recv.at[index]).wait_recv)

    def finish(self, refs, send, recv, arrived):
        moves = [m for moves in self.rounds for m in moves]
        for index, move in enumerate(moves):
            copy = move.copy(refs, send.at[index], recv.at[index])
            sends, receives = move.roles()
            only_if(sends, copy.wait_send)
            if index not in arrived:
                only_if(receives, copy.wait_recv)


def greet(links):
    barrier = pltpu.get_barrier_semaphore()
    middle = ((lax.axis_index("rep") // 4) % 3) > 0
    plain = [link for link in ("core", "x", "y", "near", "skip") if link in links]
    for link in plain:
        pl.semaphore_signal(barrier, inc=1, device_id=partner(link), device_id_type=pl.DeviceIdType.MESH)
    if "inner" in links:

        @pl.when(middle)
        def _():
            pl.semaphore_signal(
                barrier, inc=1, device_id=partner("inner"), device_id_type=pl.DeviceIdType.MESH
            )

    if "inner" in links:

        @pl.when(middle)
        def _():
            pl.semaphore_wait(barrier, len(plain) + 1)

        @pl.when(~middle)
        def _():
            if plain:
                pl.semaphore_wait(barrier, len(plain))

    else:
        pl.semaphore_wait(barrier, len(plain))


class Chain:
    def __init__(self, args, in_specs, out_specs, out_shape, scratch, links, actions):
        self.args, self.in_specs, self.out_specs, self.out_shape = args, in_specs, out_specs, out_shape
        self.scratch, self.links, self.actions = scratch, links, actions


def run(
    body, args, in_specs, out_specs, out_shape, *,
    name, grid=(1,), scratch=(), cost=None, traffic=None, chain=None, hook=None, ident=None,
):
    if (traffic is None or traffic.count() == 0) and chain is None:
        outs = pl.pallas_call(
            body, grid=grid, in_specs=in_specs, out_specs=out_specs, out_shape=out_shape,
            scratch_shapes=list(scratch), cost_estimate=cost, name=name,
        )(*args)
        return outs, [], []
    traffic = traffic or Traffic([], [], [], [])
    chain = chain or Chain([], [], [], [], [], set(), [])
    n_in, n_src, n_out, n_dst = len(args), len(traffic.sources), len(out_shape), len(traffic.targets)
    anywhere = pl.BlockSpec(memory_space=pl.ANY)
    sizes = (n_in, n_src, len(chain.args), n_out, n_dst, len(chain.out_shape), len(scratch), len(chain.scratch))
    links = traffic.links() | chain.links

    def carried(*refs):
        groups = []
        for size in sizes:
            groups.append(refs[:size])
            refs = refs[size:]
        ins, sources, chain_in, outs, targets, chain_out, held, chain_held = groups
        ends = (sources, targets)
        step = pl.program_id(0)
        pl.when(step == 0)(lambda: greet(links))
        arrived = set()
        for at in range(grid[0]):
            rounds = [which for which, when in enumerate(traffic.steps) if when == at]
            actions = [action for when, action in chain.actions[:-1] if when == at]
            if rounds or actions or hook:

                @pl.when(step == at)
                def _():
                    for which in rounds:
                        traffic.start(which, ends, *refs, arrived)
                    for action in actions:
                        action(*chain_in, *chain_out, *chain_held)
                    if hook:
                        hook(
                            at,
                            lambda target, position: traffic.require(target, position, ends, *refs, arrived),
                            targets, ins, held,
                        )

        body(*ins, *outs, *held)

        @pl.when(step == grid[0] - 1)
        def _():
            if traffic.count():
                traffic.finish(ends, *refs, arrived)
            if chain.actions:
                chain.actions[-1][1](*chain_in, *chain_out, *chain_held)

    count = traffic.count()
    semaphores = [pltpu.SemaphoreType.DMA((count,))] * 2 if count else []
    outs = pl.pallas_call(
        carried,
        grid=grid,
        in_specs=list(in_specs) + [anywhere] * n_src + list(chain.in_specs),
        out_specs=list(out_specs) + [anywhere] * n_dst + list(chain.out_specs),
        out_shape=list(out_shape) + list(traffic.targets) + list(chain.out_shape),
        scratch_shapes=list(scratch) + list(chain.scratch) + semaphores,
        compiler_params=pltpu.CompilerParams(collective_id=ident, has_side_effects=True),
        cost_estimate=cost,
        name=name,
    )(*args, *traffic.sources, *chain.args)
    return outs[:n_out], outs[n_out : n_out + n_dst], outs[n_out + n_dst :]


COT_PATHS = {
    (0, 0, 1): ("y", (0, 0, 0), -1.500),
    (0, 1, 0): ("x", (0, 0, 0), 2.243),
    (0, 1, 1): ("x", (0, 0, 1), 1.258),
    (1, 0, 0): ("near", (0, 0, 0), 1.763),
    (1, 0, 1): ("near", (0, 0, 1), 1.701),
    (1, 1, 0): ("near", (0, 1, 0), 3.477),
    (1, 1, 1): ("x", (1, 0, 1), 5.719),
    (2, 0, 0): ("inner", (0, 0, 0), 4.656),
    (2, 0, 1): ("y", (2, 0, 0), 2.464),
    (2, 1, 0): ("inner", (0, 1, 0), 0.237),
    (2, 1, 1): ("x", (2, 0, 1), 2.798),
    (3, 0, 0): ("inner", (1, 0, 0), 0.958),
    (3, 0, 1): ("y", (3, 0, 0), 2.984),
    (3, 1, 0): ("x", (3, 0, 0), 2.092),
    (3, 1, 1): ("inner", (1, 1, 1), 1.507),
}
ROW_PATHS = {
    (0, 0, 1): ("y", (0, 0, 0), -1.400),
    (0, 1, 0): ("x", (0, 0, 0), 1.939),
    (0, 1, 1): ("x", (0, 0, 1), 1.580),
    (1, 0, 0): ("near", (0, 0, 0), 1.441),
    (1, 0, 1): ("y", (1, 0, 0), 0.198),
    (1, 1, 0): ("near", (0, 1, 0), 2.429),
    (1, 1, 1): ("x", (1, 0, 1), 5.646),
    (2, 0, 0): ("inner", (0, 0, 0), 2.268),
    (2, 0, 1): ("y", (2, 0, 0), 2.650),
    (2, 1, 0): ("x", (2, 0, 0), 4.955),
    (2, 1, 1): ("x", (2, 0, 1), 4.985),
    (3, 0, 0): ("reach", (1, 0, 0), 1.374),
    (3, 0, 1): ("y", (3, 0, 0), 4.956),
    (3, 1, 0): ("x", (3, 0, 0), 2.903),
    (3, 1, 1): ("y", (3, 1, 0), 4.968),
}
FAR_FIRST = {(0, 0, 1): ("y", (0, 0, 0), -2.0)}
FAR_LAST = {(0, 0, 1): ("y", (0, 0, 0), 2.506)}
FRONT_ROOM, PAIR_ROOM, EXPERT_ROOM, OWN_ROOM, FINISH_ROOM, LAST_ROOM = 5, 9, 11, 4, 8, 25


class Network:
    def __init__(self):
        self.have, self.hops, self.weight, self.pieces = {}, {}, {}, {}

    def offer(self, name, array, hops, weight=1):
        self.hops[name], self.weight[name] = hops, weight
        self.pieces[name] = array.shape[0]
        for p in range(array.shape[0]):
            self.have[name, (0, 0, 0), p] = (array, p)

    def order(self, item):
        name, block, p = item
        return self.hops[name][block][2], block, p

    def missing(self):
        return [
            (name, block, p)
            for name in self.hops
            for block in self.hops[name]
            for p in range(self.pieces[name])
            if (name, block, p) not in self.have
        ]

    def complete(self, name, block):
        return all((name, block, p) in self.have for p in range(self.pieces[name]))

    def plan(self, room, steps, times):
        waiting = sorted(self.missing(), key=self.order)
        landed, rounds, going = {}, [[] for _ in steps], {}
        free = dict.fromkeys(("x", "y", "near", "inner"), 0.0)
        uses = {"reach": (("inner", 2), ("near", 1))}
        lag = 0.4

        def fill(link, now, weight, horizon):
            spans = [(on, max(free[on], now), n * weight) for on, n in uses.get(link, ((link, 1),))]
            if weight and any(begin >= horizon or begin + length > room + 0.01 for _, begin, length in spans):
                return None
            for on, begin, length in spans:
                if length:
                    free[on] = begin + length
            return max(begin + length for _, begin, length in spans) + lag

        for r, now in enumerate(times):
            horizon = times[r + 1] + 0.5 if r + 1 < len(times) else room
            for item in [i for i, (_, at) in going.items() if at <= now]:
                done = fill("near", now, self.weight[item[0]], horizon)
                if done is not None:
                    rounds[r].append(("outward", item, item))
                    landed[item] = done
                    del going[item]
            for item in waiting:
                name, block, p = item
                if item in landed or item in going:
                    continue
                link, source, _ = self.hops[name][block]
                source = (name, source, p)
                if source not in self.have and landed.get(source, now + 1) > now:
                    continue
                if link == "inner":
                    left = room - max(free["near"], now + 1) - sum(self.weight[i[0]] for i in going)
                    if r + 1 >= len(times) or left < 1 + self.weight[name] or times[-1] < now + self.weight[name] + lag:
                        continue
                done = fill(link, now, self.weight[name], horizon)
                if done is None:
                    continue
                if link == "reach":
                    rounds[r] += [("inner", source, item), ("skip", source, item)]
                else:
                    rounds[r].append((link, source, item))
                if link == "inner":
                    going[item] = (r, done)
                else:
                    landed[item] = done
        for item in list(going):
            rounds[-1].append(("outward", item, item))
            landed[item] = room
        sources, targets, homes = [], [], {}
        for name, block, p in sorted(landed):
            homes.setdefault((name, block), []).append(p)
        order = list(homes)
        for name, block in order:
            model = self.have[name, (0, 0, 0), 0][0]
            targets.append(jax.ShapeDtypeStruct((len(homes[name, block]),) + model.shape[1:], model.dtype))

        def home(item):
            name, block, p = item
            return order.index((name, block)), homes[name, block].index(p)

        def origin(item):
            if item in landed:
                return (1,) + home(item)
            array, at = self.have[item]
            for k, known in enumerate(sources):
                if known is array:
                    return 0, k, at
            sources.append(array)
            return 0, len(sources) - 1, at

        moves = []
        for chosen in rounds:
            spans = []
            for link, source, item in sorted(chosen, key=lambda c: (c[0] not in ("outward", "inner"), *c)):
                a, b = origin(source), home(item)
                if spans:
                    link_, a_, b_, n = spans[-1]
                    if link_ == link and a_[:2] == a[:2] and b_[0] == b[0] and a[2] == a_[2] + n and b[1] == b_[1] + n:
                        spans[-1] = (link, a_, b_, n + 1)
                        continue
                spans.append((link, a, b, 1))
            flat = [m for made in moves for m in made]
            placed = []
            for link, a, b, n in spans:
                needs = [
                    k
                    for k, m in enumerate(flat)
                    if a[0] == 1 and m.home[0] == a[1] and m.home[1] < a[2] + n and a[2] < m.home[1] + m.size
                ]
                placed.append(self.move(link, a, b, n, needs))
            moves.append(placed)
        while moves and not moves[-1]:
            moves.pop()
        traffic = Traffic(sources, targets, moves, steps[: len(moves)])
        return traffic, (order, homes, landed)

    def find(self, plan, name, block):
        order, homes, landed = plan
        found = []
        for p in range(self.pieces[name]):
            if (name, block, p) in landed:
                found.append((None, order.index((name, block)), homes[name, block].index(p)))
            else:
                array, at = self.have[name, block, p]
                found.append((array, None, at))
        return found

    def landing(self, plan, block):
        return max(plan[2].get((name, block, p), 0.0) for name in "CS" for p in range(self.pieces[name]))

    @staticmethod
    def move(link, origin, home, count, needs):
        def source(refs):
            return refs[origin[0]][origin[1]].at[pl.ds(origin[2], count)]

        def target(refs):
            return refs[1][home[0]].at[pl.ds(home[1], count)]

        made = Move(link, source, target, needs)
        made.home, made.size = home, count
        return made

    def land(self, plan, arrays):
        order, homes, _ = plan
        for key, array in zip(order, arrays):
            for at, p in enumerate(homes[key]):
                self.have[key[0], key[1], p] = (array, at)

    def block(self, name, block):
        return [self.have[name, block, p] for p in range(self.pieces[name])]


def evenly(room, steps, length, every=1):
    chosen = list(range(0, steps, every))
    return room, chosen, [step * length for step in chosen]


def gathering(room, senders, extra):
    busy = 2 * senders * 0.45
    times = [0.45 * step for step in range(2 * senders)]
    times += [busy + (step + 1) * max(0.5, room - busy) / (extra + 1) for step in range(extra)]
    return room, list(range(2 * senders + extra)), times


def standardise(values):
    average = jnp.mean(values, axis=-1, keepdims=True)
    centred = values - average
    variance = jnp.mean(centred * centred, axis=-1, keepdims=True)
    scale = lax.rsqrt(variance + 1e-06)
    return centred * scale, scale


def prep_body(count_ref, cap_ref, tok_ref, cot_ref, route_ref, tok_out, cot_out, route_out, ids_out, load_out, wide, narrow):
    pl.when(pl.program_id(0) == 0)(
        lambda: prep_rows(
            count_ref, cap_ref, tok_ref, cot_ref, route_ref, tok_out, cot_out, route_out, ids_out, load_out, wide, narrow
        )
    )


def prep_rows(count_ref, cap_ref, tok_ref, cot_ref, route_ref, tok_out, cot_out, route_out, ids_out, load_out, wide, narrow):
    images = tok_out.shape[0]
    total = tok_ref.shape[0]
    alive_images = count_ref[0]
    real = iota((PAD, 1), 0) < IMG_TOK

    def split(source, image):
        return source[pl.ds(image * IMG_TOK, PAD), :]

    wide[...] = jnp.zeros_like(wide)
    narrow[...] = jnp.zeros_like(narrow)
    wide[pl.ds(0, total), :] = tok_ref[...].astype(F32)
    for image in range(images):
        tok_out[image] = jnp.where(real, split(wide, image), 0.0).astype(BF16)
    wide[pl.ds(0, total), :] = cot_ref[...].astype(F32)
    narrow[pl.ds(0, total), :] = route_ref[...]
    routes = []
    lives = []
    for image in range(images):
        live = real & (image < alive_images)
        cot_out[image] = jnp.where(live, split(wide, image), 0.0).astype(BF16)
        picked = split(narrow, image)
        route_out[image] = picked
        routes.append(picked)
        lives.append(jnp.where(live, 1, 0))
    routes = jnp.concatenate(routes, axis=0)
    live = jnp.concatenate(lives, axis=0) > 0
    rows = images * PAD
    lane = iota((rows, 128), 1)
    first = (lane == routes[:, 0:1]) & live
    second = (lane == routes[:, 1:2] + EXPERTS) & live
    hot = jnp.where(first | second, 1.0, 0.0)
    below = jnp.where(iota((rows, rows), 0) > iota((rows, rows), 1), 1.0, 0.0).astype(BF16)
    before = dot(below, hot.astype(BF16))
    totals = jnp.sum(hot, axis=0, keepdims=True)
    place_one = jnp.sum(jnp.where(first, before, 0.0), axis=1, keepdims=True)
    place_two = jnp.sum(jnp.where(second, before, 0.0), axis=1, keepdims=True) + jnp.sum(
        jnp.where(lane == routes[:, 1:2], totals, 0.0), axis=1, keepdims=True
    )
    limit = cap_ref[0].astype(F32)
    keep_one = live & (place_one < limit)
    keep_two = live & (place_two < limit)
    slots = jnp.where(lane == 0, jnp.where(keep_one, routes[:, 0:1].astype(F32), -1.0), 0.0)
    slots = jnp.where(lane == 1, jnp.where(keep_one, place_one, 0.0), slots)
    slots = jnp.where(lane == 2, jnp.where(keep_two, routes[:, 1:2].astype(F32), -1.0), slots)
    slots = jnp.where(lane == 3, jnp.where(keep_two, place_two, 0.0), slots)
    for image in range(images):
        ids_out[image] = jnp.transpose(slots[image * PAD : (image + 1) * PAD])[0:8]
    lanes = iota((1, 128), 1)
    tokens_alive = (alive_images * IMG_TOK).astype(F32)
    load_out[0] = jnp.broadcast_to(jnp.where(lanes == 64, tokens_alive, totals), (8, 128))


def pack_body(*refs):
    lines, (qkv_ref, out_ref, router_ref, wide_ref, tall_ref) = refs[:-5], refs[-5:]
    rows, part = qkv_ref.shape[0], lines[0].shape[0]
    wide_ref[:rows] = qkv_ref[...]
    table = jnp.zeros((16, part), F32)
    for k, ref in enumerate(lines):
        line = jnp.broadcast_to(ref[...].astype(F32).reshape(1, part), (16, part))
        table = jnp.where(iota((16, part), 0) == k, line, table)
    wide_ref[rows:] = jnp.zeros((16, wide_ref.shape[1]), BF16)
    wide_ref[rows:, :part] = table.astype(BF16)
    width = out_ref.shape[1]
    tall_ref[:, :width] = out_ref[...]
    tall_ref[:, width:] = jnp.zeros((rows, 128), BF16)
    tall_ref[:, width : width + EXPERTS] = router_ref[...]


def pack_weights(lines, w_qkv, w_out, w_router):
    rows = w_qkv.shape[0]
    return pl.pallas_call(
        pack_body,
        in_specs=[pl.BlockSpec(memory_space=pltpu.VMEM)] * (len(lines) + 3),
        out_specs=[pl.BlockSpec(memory_space=pltpu.VMEM)] * 2,
        out_shape=[
            jax.ShapeDtypeStruct((rows + 16, w_qkv.shape[1]), BF16),
            jax.ShapeDtypeStruct((rows, w_out.shape[1] + 128), BF16),
        ],
        cost_estimate=pl.CostEstimate(flops=1_000_000, bytes_accessed=2_500_000, transcendentals=0),
        name="pack_weights",
    )(*lines, w_qkv, w_out, w_router)


def weight_traffic(wide, tall):
    def rows(array):
        half = array.shape[0] // 2
        return pl.ds(pl.multiple_of((lax.axis_index("rep") % 2) * half, 8), half)

    def fetch(at, array):
        return Move("y", lambda refs: refs[0][at].at[rows(array)], lambda refs: refs[1][at].at[rows(array)])

    def pass_on(at, array):
        there = lambda refs: refs[1][at].at[rows(array)]
        return Move("core", there, there, [at])

    arrays = (wide, tall)
    targets = [jax.ShapeDtypeStruct(a.shape, a.dtype) for a in arrays]
    rounds = [[make(at, a) for at, a in enumerate(arrays)] for make in (fetch, pass_on)]
    return Traffic(list(arrays), targets, rounds, [0, 1])


def prepare(tokens, cotangent, routes, image_count, capacity, wide, tall, ident):
    total, width = tokens.shape
    images = total // IMG_TOK
    shapes = [
        jax.ShapeDtypeStruct((images, PAD, width), BF16),
        jax.ShapeDtypeStruct((images, PAD, width), BF16),
        jax.ShapeDtypeStruct((images, PAD, 2), jnp.int32),
        jax.ShapeDtypeStruct((images, 8, PAD), F32),
        jax.ShapeDtypeStruct((1, 8, 128), F32),
    ]
    return run(
        prep_body,
        (image_count, capacity, tokens, cotangent, routes),
        [scalar_spec(), scalar_spec()] + [resident(a.shape) for a in (tokens, cotangent, routes)],
        [resident(a.shape) for a in shapes],
        shapes,
        grid=(2,),
        scratch=[pltpu.VMEM((1000, width), F32), pltpu.VMEM((1000, 2), jnp.int32)],
        cost=pl.CostEstimate(flops=300_000_000, bytes_accessed=6_000_000, transcendentals=0),
        name="prepare",
        traffic=weight_traffic(wide, tall),
        ident=ident,
    )


def place_halves(own, far, both):
    mine = lax.axis_index("fsdp")
    both[mine] = own[...]
    both[1 - mine] = far[...]


def vectors(wide_ref):
    return jnp.concatenate([wide_ref[0, 256:272, :256], wide_ref[1, 256:272, :256]], axis=1).astype(F32)


def front_body(
    count_ref, tok_ref, ids_ref, route_ref, wide_own, wide_far, tall_own, tall_far,
    packed_ref, prob_ref, mixed_ref, middle_ref, second_ref, soft_ref, sum_ref, wide_ref, tall_ref,
):
    @pl.when(pl.program_id(0) == 0)
    def _():
        sum_ref[...] = jnp.zeros_like(sum_ref)
        place_halves(wide_own, wide_far, wide_ref)
        place_halves(tall_own, tall_far, tall_ref)

    width = tok_ref.shape[-1]
    vec = vectors(wide_ref)
    inputs = tok_ref[0].astype(F32)
    normed = (standardise(inputs)[0] * vec[0:1] + vec[1:2]).astype(BF16)
    qkv = wide_ref[:, :256, :].reshape(width, 3 * width)
    raw = dot(normed, qkv)
    packed_ref[0, :, :width] = (raw[:, :width] + vec[2:3]).astype(BF16)
    packed_ref[0, :, width : 2 * width] = raw[:, width : 2 * width].astype(BF16)
    packed_ref[0, :, 2 * width :] = (raw[:, 2 * width :] + vec[3:4]).astype(BF16)
    low_lanes = iota((PAD, 128), 1) < HEAD_DIM
    real_key = iota((PAD, PAD), 1) < IMG_TOK
    for pair in range(HEADS // 2):
        at = pair * 128
        query = packed_ref[0, :, at : at + 128] * jnp.asarray(HEAD_DIM**-0.5, BF16)
        keys = packed_ref[0, :, width + at : width + at + 128]
        valued = packed_ref[0, :, 2 * width + at : 2 * width + at + 128]
        got = []
        for side in range(2):
            own = low_lanes if side == 0 else ~low_lanes
            scores = dot_cols(jnp.where(own, query, jnp.zeros_like(query)), keys)
            scores = jnp.where(real_key, scores, -1e30)
            raised = jnp.exp(scores - jnp.max(scores, axis=-1, keepdims=True))
            weights = (raised / jnp.sum(raised, axis=-1, keepdims=True)).astype(BF16)
            prob_ref[0, 2 * pair + side] = weights
            got.append(dot(weights, valued))
        mixed_ref[0, :, at : at + 128] = jnp.where(low_lanes, got[0], got[1]).astype(BF16)
    out_full = tall_ref[:, :, :width].reshape(width, width)
    router = tall_ref[:, :, width : width + 128].reshape(width, 128)
    middle = inputs + dot(mixed_ref[0], out_full) + vec[4:5]
    middle_ref[0] = middle
    second = standardise(middle)[0] * vec[5:6] + vec[6:7]
    lane = iota((PAD, 128), 1)
    logits = jnp.where(lane < EXPERTS, dot(second.astype(BF16), router), -1e30)
    soft = jnp.exp(logits - jnp.max(logits, axis=-1, keepdims=True))
    soft = soft / jnp.sum(soft, axis=-1, keepdims=True)
    route = route_ref[0]
    pick_one = jnp.sum(jnp.where(lane == route[:, 0:1], soft, 0.0), axis=-1, keepdims=True)
    pick_two = jnp.sum(jnp.where(lane == route[:, 1:2], soft, 0.0), axis=-1, keepdims=True)
    both = pick_one + pick_two
    live = (iota((PAD, 1), 0) < IMG_TOK) & (pl.program_id(0) < count_ref[0])
    alive = jnp.where(live, 1.0, 0.0)
    sum_ref[0] += jnp.broadcast_to(jnp.sum(soft * alive, axis=0, keepdims=True), (8, 128))
    soft = jnp.where(lane == EXPERTS + 4, pick_one / both, soft)
    soft = jnp.where(lane == EXPERTS + 5, pick_two / both, soft)
    soft_ref[0] = soft
    gates = jnp.transpose(soft)[EXPERTS : EXPERTS + 8]
    line = iota((8, PAD), 0)
    meta = jnp.where((line == 4) | (line == 5), gates, ids_ref[0])
    meta = jnp.concatenate([meta, jnp.zeros((8, width - PAD), F32)], axis=1)
    second_ref[0] = jnp.concatenate([second[: PAD - 8], meta], axis=0).astype(BF16)


def front(count, tok, ids, routes, wide, tall, traffic, ident):
    images, _, width = tok.shape
    shape = jax.ShapeDtypeStruct
    return run(
        front_body,
        (count, tok, ids, routes, *wide, *tall),
        [scalar_spec(), by_image(PAD, width), by_image(8, PAD), by_image(PAD, 2)]
        + [resident(wide[0].shape)] * 2
        + [resident(tall[0].shape)] * 2,
        [
            by_image(PAD, 3 * width),
            by_image(HEADS, PAD, PAD),
            by_image(PAD, width),
            by_image(PAD, width),
            by_image(PAD, width),
            by_image(PAD, 128),
            resident((1, 8, 128)),
        ],
        [
            shape((images, PAD, 3 * width), BF16),
            shape((images, HEADS, PAD, PAD), BF16),
            shape((images, PAD, width), BF16),
            shape((images, PAD, width), F32),
            shape((images, PAD, width), BF16),
            shape((images, PAD, 128), F32),
            shape((1, 8, 128), F32),
        ],
        grid=(images,),
        scratch=[pltpu.VMEM((2,) + wide[0].shape, BF16), pltpu.VMEM((2,) + tall[0].shape, BF16)],
        cost=pl.CostEstimate(flops=6_000_000_000, bytes_accessed=16_000_000, transcendentals=2_000_000),
        name="front",
        traffic=traffic,
        ident=ident,
    )


def slot_lines(meta):
    return meta[0:1] * CAP + meta[1:2], meta[2:3] * CAP + meta[3:4]


def gather(base, experts, senders, sequence, traffic, ident, chain=None):
    arrays, table = [], []
    for sender in sequence:
        if sender is None:
            table.append(None)
            continue
        for kind in range(2):
            spots = []
            for array, target, position in senders[sender][kind]:
                at = target
                if array is not None:
                    at = next((k for k, known in enumerate(arrays) if known is array), len(arrays))
                    if at == len(arrays):
                        arrays.append(array)
                spots.append((array is None, at, position))
            table.append((sender, kind, spots))
    images, width = len(table[0][2]), arrays[0].shape[-1]
    tokens, slots, count, steps = images * PAD, experts * CAP, len(senders), len(table)
    first = [next(k for k, entry in enumerate(table) if entry and entry[0] == sender) for sender in range(count)]

    def hook(step, require, targets, ins, held):
        sources, rows, loaded = ins[1:], held[0], held[2]

        def copies(entry):
            _, kind, spots = entry
            return [
                pltpu.make_async_copy(
                    (targets if arriving else sources)[at].at[position],
                    rows.at[kind, pl.ds(image * PAD, PAD)],
                    loaded.at[kind, image],
                )
                for image, (arriving, at, position) in enumerate(spots)
            ]

        def load(entry):
            for arriving, at, position in entry[2]:
                if arriving:
                    require(at, position)
            for copy in copies(entry):
                copy.start()

        if step == 0:
            load(table[0])
        if step + 1 < steps and table[step + 1]:
            load(table[step + 1])
        if table[step]:
            for copy in copies(table[step]):
                copy.wait()

    def body(base_ref, *refs):
        row_out, grad_out, rows, lines = refs[len(arrays) : len(arrays) + 4]
        step = pl.program_id(0)
        turns = [(k, entry[1]) for k, entry in enumerate(table) if entry]
        working, gated = step < 0, step < 0
        for k, kind in turns:
            working = working | (step == k)
            if kind:
                gated = gated | (step == k)

        @pl.when(working & ~gated)
        def _():
            for image in range(images):
                lines[image] = rows[0, image * PAD + PAD - 16 : (image + 1) * PAD, :PAD].astype(F32)[8:]

        @pl.when(working)
        def _():
            meta = jnp.concatenate([lines[image] for image in range(images)], axis=1)
            one, two = slot_lines(meta)
            weight_one = jnp.where(gated, meta[4:5], 1.0)
            weight_two = jnp.where(gated, meta[5:6], 1.0)
            slot = (iota((slots, tokens), 0) + base_ref[0]).astype(F32)
            pick = jnp.where(slot == one, weight_one, 0.0) + jnp.where(slot == two, weight_two, 0.0)
            got = dot(pick.astype(BF16), rows[jnp.where(gated, 1, 0)])
            got = got.astype(BF16).reshape(experts, 1, CAP, width)

            @pl.when(~gated)
            def _():
                row_out[...] = got

            @pl.when(gated)
            def _():
                grad_out[...] = got

    def place(d):
        turn = 0
        for at in first[1:]:
            turn += jnp.where(d >= at, 1, 0)
        return (0, turn, 0, 0)

    shape = jax.ShapeDtypeStruct((experts, count, CAP, width), BF16)
    return run(
        body,
        (base, *arrays),
        [scalar_spec()] + [pl.BlockSpec(memory_space=pl.ANY)] * len(arrays),
        [pl.BlockSpec((experts, 1, CAP, width), place)] * 2,
        [shape, shape],
        grid=(steps,),
        scratch=[
            pltpu.VMEM((2, tokens, width), BF16),
            pltpu.VMEM((images, 8, PAD), F32),
            pltpu.SemaphoreType.DMA((2, images)),
        ],
        cost=pl.CostEstimate(
            flops=4 * count * slots * tokens * width,
            bytes_accessed=4 * count * (tokens + slots) * width,
            transcendentals=0,
        ),
        name="gather",
        traffic=traffic,
        chain=chain,
        hook=hook,
        ident=ident,
    )


def own_line(ref):
    table = ref[...].astype(F32)
    return jnp.sum(jnp.where(iota(table.shape, 0) == pl.program_id(0), table, 0.0), axis=0, keepdims=True)


def expert_body(row_own, row_far, grad_own, grad_far, in_ref, in_bias_ref, out_ref, out_bias_ref, made_own, made_far, back_own, back_far):
    cap, width = row_own.shape[2:]
    hidden = in_ref.shape[2]
    rows = jnp.concatenate([row_own[0, 0], row_far[0, 0]], axis=0)
    grads = jnp.concatenate([grad_own[0, 0], grad_far[0, 0]], axis=0)
    in_bias = own_line(in_bias_ref)
    made = jnp.zeros((2 * cap, width), F32)
    back = jnp.zeros((2 * cap, width), F32)
    chunk = 512
    for at in range(0, hidden, chunk):
        first = in_ref[0, :, at : at + chunk]
        second = out_ref[0, at : at + chunk, :]
        raised = dot(rows, first) + in_bias[:, at : at + chunk]
        active, slope = gelu_pair(raised)
        made += dot(active.astype(BF16), second)
        draised = (dot_cols(grads, second) * slope).astype(BF16)
        back += dot_cols(draised, first)
    made = (made + own_line(out_bias_ref)).astype(BF16)
    back = back.astype(BF16)
    made_own[0], made_far[0] = made[:cap], made[cap:]
    back_own[0], back_far[0] = back[:cap], back[cap:]


def expert_layer(pair, first, first_bias, second, second_bias, chain, traffic, ident):
    experts, _, cap, width = pair[0].shape
    hidden = first.shape[2]
    rows = [pl.BlockSpec((1, 1, cap, width), lambda e, side=side: (e, side, 0, 0)) for side in range(2)]
    out = pl.BlockSpec((1, cap, width), lambda e: (e, 0, 0))
    return run(
        expert_body,
        (
            pair[0],
            pair[0],
            pair[1],
            pair[1],
            first,
            first_bias,
            second,
            second_bias,
        ),
        rows + rows + [by_image(width, hidden), resident(first_bias.shape), by_image(hidden, width), resident(second_bias.shape)],
        [out] * 4,
        [jax.ShapeDtypeStruct((experts, cap, width), BF16)] * 4,
        grid=(experts,),
        cost=pl.CostEstimate(
            flops=16 * experts * cap * width * hidden,
            bytes_accessed=4 * experts * width * hidden,
            transcendentals=2 * experts * cap * hidden,
        ),
        name="expert_layer",
        traffic=traffic,
        chain=chain,
        ident=ident,
    )


def combine_body(base_ref, rows, cot, made_ref, back_ref, sum_ref, row_ref, gate_ref):
    experts, cap, width = made_ref.shape
    slots = experts * cap
    meta = jnp.transpose(rows[PAD - 16 :, :PAD].astype(F32)[8:])
    slot = (iota((PAD, slots), 1) + base_ref[0]).astype(F32)
    one = jnp.where(slot == meta[:, 0:1] * CAP + meta[:, 1:2], 1.0, 0.0).astype(BF16)
    two = jnp.where(slot == meta[:, 2:3] * CAP + meta[:, 3:4], 1.0, 0.0).astype(BF16)
    made = made_ref[...].reshape(slots, width)
    made_one = dot(one, made)
    made_two = dot(two, made)
    sum_ref[0] = (meta[:, 4:5] * made_one + meta[:, 5:6] * made_two).astype(BF16)
    row_ref[0] = dot(one + two, back_ref[...].reshape(slots, width)).astype(BF16)
    cot = cot.astype(F32)
    grad_one = jnp.sum(cot * made_one, axis=1, keepdims=True)
    grad_two = jnp.sum(cot * made_two, axis=1, keepdims=True)
    lane = iota((PAD, 128), 1)
    wide = jnp.where(lane == 0, grad_one, jnp.where(lane == 1, grad_two, 0.0))
    gate_ref[0] = jnp.transpose(wide)[0:8]


def by_piece(pieces, *shape):
    arrays, first = [], []
    for image, (array, position) in enumerate(pieces):
        if not arrays or arrays[-1] is not array:
            arrays.append(array)
            first.append((image, position))
    specs = []
    for array, (image, position) in zip(arrays, first):

        def index(i, *_, image=image, position=position, last=array.shape[0] - 1):
            return (jnp.clip(i - image + position, 0, last),) + (0,) * len(shape)

        specs.append(pl.BlockSpec((1,) + shape, index))

    def read(refs):
        value = refs[0][0]
        for ref, (image, _) in zip(refs[1:], first[1:]):
            value = jnp.where(pl.program_id(0) >= image, ref[0], value)
        return value

    return arrays, specs, read


def combine(base, rows, cots, made, back, traffic, ident):
    width = made.shape[-1]
    images = len(rows)
    experts, cap, _ = made.shape
    row_arrays, row_specs, read_rows = by_piece(rows, PAD, width)
    cot_arrays, cot_specs, read_cots = by_piece(cots, PAD, width)
    split = len(row_arrays)

    def body(base_ref, made_ref, back_ref, *refs):
        inputs, outs = refs[: split + len(cot_arrays)], refs[split + len(cot_arrays) :]
        combine_body(base_ref, read_rows(inputs[:split]), read_cots(inputs[split:]), made_ref, back_ref, *outs)

    return run(
        body,
        (base, made, back, *row_arrays, *cot_arrays),
        [scalar_spec(), resident(made.shape), resident(back.shape), *row_specs, *cot_specs],
        [by_image(PAD, width), by_image(PAD, width), by_image(8, PAD)],
        [
            jax.ShapeDtypeStruct((images, PAD, width), BF16),
            jax.ShapeDtypeStruct((images, PAD, width), BF16),
            jax.ShapeDtypeStruct((images, 8, PAD), F32),
        ],
        grid=(images,),
        cost=pl.CostEstimate(
            flops=6 * images * PAD * experts * cap * width, bytes_accessed=6_000_000, transcendentals=0
        ),
        name="combine",
        traffic=traffic,
        ident=ident,
    )


def norm_back(grads, hat, scale, gain):
    scaled = grads * gain
    inner = jnp.mean(scaled * hat, axis=-1, keepdims=True)
    return scale * (scaled - jnp.mean(scaled, axis=-1, keepdims=True) - hat * inner)


def column_sum(values):
    return jnp.sum(values, axis=0, keepdims=True)


def finish_body(
    count_ref, tok_ref, cot_ref, packed_ref, prob_ref, mixed_ref, middle_ref, second_ref, soft_ref, route_ref,
    row_own, row_far, gate_own, gate_far, aux_ref,
    wide_own, wide_far, tall_own, tall_far, dtok_ref, pack_ref,
    dpacked, wide_ref, tall_ref, dqkv_ref, dout_ref, drouter_ref, dvec_ref,
):
    image = pl.program_id(0)
    width = tok_ref.shape[-1]

    @pl.when(image == 0)
    def _():
        place_halves(wide_own, wide_far, wide_ref)
        place_halves(tall_own, tall_far, tall_ref)

    vec = vectors(wide_ref)
    images = dtok_ref.shape[0] // IMG_TOK

    @pl.when(image == 0)
    def _():
        for ref in (dqkv_ref, dout_ref, drouter_ref, dvec_ref):
            ref[...] = jnp.zeros_like(ref)

    real = iota((PAD, 1), 0) < IMG_TOK
    alive = jnp.where(real & (image < count_ref[0]), 1.0, 0.0)
    middle = middle_ref[0]
    upstream = cot_ref[0].astype(F32)
    soft = soft_ref[0]
    route = route_ref[0]
    lane = iota((PAD, 128), 1)
    gate_grads = jnp.transpose(gate_own[0] + gate_far)
    push = (gate_grads[:, 0:1] - gate_grads[:, 1:2]) * soft[:, EXPERTS + 4 : EXPERTS + 5] * soft[:, EXPERTS + 5 : EXPERTS + 6]
    soft = jnp.where(lane < EXPERTS, soft, 0.0)
    aux = aux_ref[...] * alive
    dlogits = soft * (aux - jnp.sum(soft * aux, axis=-1, keepdims=True))
    dlogits += jnp.where(lane == route[:, 0:1], push, 0.0) - jnp.where(lane == route[:, 1:2], push, 0.0)
    dlogits = dlogits.astype(BF16)
    second = second_ref[0]
    router = tall_ref[:, :, width : width + 128].reshape(width, 128)
    drouter_ref[...] += dot_rows(second, dlogits)
    dsecond = dot_cols(dlogits, router) + (row_own[0].astype(F32) + row_far.astype(F32))
    hat, scale = standardise(middle)
    dmiddle = upstream + norm_back(dsecond, hat, scale, vec[5:6])
    dattn = dmiddle.astype(BF16)
    dvec_ref[EXPERTS + 4 : EXPERTS + 5] += column_sum(dattn.astype(F32))
    dvec_ref[EXPERTS + 5 : EXPERTS + 6] += column_sum(dsecond * hat)
    dvec_ref[EXPERTS + 6 : EXPERTS + 7] += column_sum(dsecond)
    dout_ref[...] += dot_rows(mixed_ref[0], dattn)
    out_full = tall_ref[:, :, :width].reshape(width, width)
    dmixed = dot_cols(dattn, out_full).astype(BF16)
    low_lanes = iota((PAD, 128), 1) < HEAD_DIM
    root = HEAD_DIM**-0.5
    for pair in range(HEADS // 2):
        at = pair * 128
        query = packed_ref[0, :, at : at + 128]
        keys = packed_ref[0, :, width + at : width + at + 128]
        valued = packed_ref[0, :, 2 * width + at : 2 * width + at + 128]
        grads = dmixed[:, at : at + 128]
        parts = []
        for side in range(2):
            own = low_lanes if side == 0 else ~low_lanes
            weights = prob_ref[0, 2 * pair + side]
            dweights = dot_cols(jnp.where(own, grads, jnp.zeros_like(grads)), valued)
            exact = weights.astype(F32)
            inner = jnp.sum(dweights * exact, axis=-1, keepdims=True)
            dscores = (exact * (dweights - inner)).astype(BF16)
            parts.append((dot(dscores, keys), dot_rows(dscores, query), dot_rows(weights, grads)))
        for third, factor in ((0, root), (1, root), (2, 1.0)):
            both = jnp.where(low_lanes, parts[0][third], parts[1][third]) * factor
            dpacked[:, third * width + at : third * width + at + 128] = both.astype(BF16)
    inputs = tok_ref[0].astype(F32)
    hat, scale = standardise(inputs)
    normed = (hat * vec[0:1] + vec[1:2]).astype(BF16)
    packed_grads = dpacked[...]
    dqkv_ref[...] += dot_rows(normed, packed_grads)
    dvec_ref[EXPERTS + 2 : EXPERTS + 3] += column_sum(packed_grads[:, :width].astype(F32))
    dvec_ref[EXPERTS + 3 : EXPERTS + 4] += column_sum(packed_grads[:, 2 * width :].astype(F32))
    qkv = wide_ref[:, :256, :].reshape(width, 3 * width)
    dnormed = dot_cols(packed_grads, qkv)
    dvec_ref[EXPERTS + 0 : EXPERTS + 1] += column_sum(dnormed * hat)
    dvec_ref[EXPERTS + 1 : EXPERTS + 2] += column_sum(dnormed)
    dtokens = dmiddle + norm_back(dnormed, hat, scale, vec[0:1])
    for k in range(images):

        @pl.when(image == k)
        def _():
            dtok_ref[pl.ds(k * IMG_TOK, IMG_TOK), :] = dtokens[:IMG_TOK]

    @pl.when(image == images - 1)
    def _():
        lines = jnp.transpose(dvec_ref[...])
        part = width // 8
        for owner in range(2):
            for half in range(2):
                for quarter in range(2):
                    at = ((owner * 2 + half) * 2 + quarter) * part
                    rows = slice(at, at + part)
                    spot = pack_ref.at[owner, half, quarter]
                    spot[:, : 3 * width] = dqkv_ref[rows].astype(BF16)
                    spot[:, 3 * width : 4 * width] = dout_ref[rows].astype(BF16)
                    spot[:, 4 * width :] = (drouter_ref[rows] + lines[rows]).astype(BF16)


def finish(count, tok, cot, saved, routes, row_own, row_far, gate_own, gate_far, aux, wide, tall, total, traffic, ident):
    images, _, width = tok.shape
    packed, prob, mixed, middle, second, soft = saved
    shape = jax.ShapeDtypeStruct
    tile = by_image(PAD, width)
    row_arrays = []
    for array, _, _ in row_far:
        if array is not None and not any(known is array for known in row_arrays):
            row_arrays.append(array)
    gate_arrays, gate_specs, read_gates = by_piece(gate_far, 8, PAD)
    lead, extra = len(row_arrays), len(row_arrays) + len(gate_arrays)

    def hook(step, require, targets, ins, held):
        array, target, position = row_far[step]
        if array is None:
            require(target, position)
            source = targets[target]
        else:
            source = next(ref for ref, known in zip(ins, row_arrays) if known is array)
        copy = pltpu.make_async_copy(source.at[position], held[-2], held[-1])
        copy.start()
        copy.wait()

    def body(*refs):
        pieces, far, refs = refs[:extra], refs[-2], list(refs[extra:-2])
        refs[11:11] = [far[...]]
        refs[13:13] = [read_gates(pieces[lead:])]
        finish_body(*refs)

    pack = (2, 2, 2, width // 8, 4 * width + 128)
    return run(
        body,
        (
            *row_arrays, *gate_arrays, count, tok, cot, packed, prob, mixed, middle, second, soft, routes,
            row_own, gate_own, aux, *wide, *tall,
        ),
        [
            *[pl.BlockSpec(memory_space=pl.ANY)] * lead,
            *gate_specs,
            scalar_spec(),
            tile,
            tile,
            by_image(PAD, 3 * width),
            by_image(HEADS, PAD, PAD),
            tile,
            tile,
            tile,
            by_image(PAD, 128),
            by_image(PAD, 2),
            tile,
            by_image(8, PAD),
            resident((1, 128)),
            resident(wide[0].shape),
            resident(wide[0].shape),
            resident(tall[0].shape),
            resident(tall[0].shape),
        ],
        [resident((total, width)), resident(pack)],
        [shape((total, width), F32), shape(pack, BF16)],
        grid=(images,),
        scratch=[
            pltpu.VMEM((PAD, 3 * width), BF16),
            pltpu.VMEM((2,) + wide[0].shape, BF16),
            pltpu.VMEM((2,) + tall[0].shape, BF16),
            pltpu.VMEM((width, 3 * width), F32),
            pltpu.VMEM((width, width), F32),
            pltpu.VMEM((width, 128), F32),
            pltpu.VMEM((128, width), F32),
            pltpu.VMEM((PAD, width), BF16),
            pltpu.SemaphoreType.DMA,
        ],
        cost=pl.CostEstimate(flops=12_000_000_000, bytes_accessed=24_000_000, transcendentals=0),
        name="finish",
        traffic=traffic,
        hook=hook,
        ident=ident,
    )


def add(left, right):
    return (left.astype(F32) + right.astype(F32)).astype(BF16)


class Exchange:
    def __init__(self, send, recv):
        self.send, self.recv = send, recv

    def at(self, index, link, source, target):
        move = Move(link, lambda _: source, lambda _: target)
        return move.roles(), move.copy(None, self.send.at[index], self.recv.at[index])


def begin(make):
    roles, copy = make()
    only_if(roles[0], copy.start)


def end(make):
    roles, copy = make()
    only_if(roles[0], copy.wait_send)
    only_if(roles[1], copy.wait_recv)


def sums_everywhere(load, soft_sum, steps):
    shape = (2,) + load.shape[1:]
    links = ("core", "y", "x", "near", "inner", "outward")

    def copies(load_ref, soft_ref, total, held, got, send, recv):
        made = Exchange(send, recv)
        return [
            lambda k=k, link=link: made.at(k, link, held.at[k], held.at[k] if link == "outward" else got.at[k])
            for k, link in enumerate(links)
        ]

    def first(*refs):
        load_ref, soft_ref, _, held = refs[:4]
        held[0, 0], held[0, 1] = load_ref[0], soft_ref[0]
        begin(copies(*refs)[0])

    def stage(k):
        def action(*refs):
            held, got = refs[3:5]
            end(copies(*refs)[k - 1])
            if links[k] == "outward":

                @pl.when(((lax.axis_index("rep") // 4) % 3) > 0)
                def _():
                    held[k] = held[k - 1] + got[k - 1]

            else:
                held[k] = held[k - 1] + got[k - 1]
            begin(copies(*refs)[k])

        return action

    def last(*refs):
        end(copies(*refs)[5])
        refs[2][...] = refs[3][5]

    return Chain(
        [load, soft_sum],
        [resident(load.shape)] * 2,
        [resident(shape)],
        [jax.ShapeDtypeStruct(shape, F32)],
        [pltpu.VMEM((6,) + shape, F32), pltpu.VMEM((5,) + shape, F32)] + [pltpu.SemaphoreType.DMA((6,))] * 2,
        {"core", "y", "x", "near", "inner"},
        list(zip(steps, [first] + [stage(k) for k in range(1, 6)])) + [(0, last)],
    )


def owner_sums(pack, steps):
    shape = pack.shape[2:]

    def first(pack_ref, part, near_in, half, far_in, send, recv):
        core = lax.axis_index("rep") % 2
        Exchange(send, recv).at(0, "core", pack_ref.at[:, 1 - core], near_in)[1].start()

    def second(pack_ref, part, near_in, half, far_in, send, recv):
        core, mine = lax.axis_index("rep") % 2, lax.axis_index("fsdp")
        Exchange(send, recv).at(0, "core", pack_ref.at[:, 1 - core], near_in)[1].wait()
        half[...] = add(pack_ref[:, core], near_in[...])
        Exchange(send, recv).at(1, "y", half.at[1 - mine], far_in)[1].start()

    def last(pack_ref, part, near_in, half, far_in, send, recv):
        mine = lax.axis_index("fsdp")
        Exchange(send, recv).at(1, "y", half.at[1 - mine], far_in)[1].wait()
        part[...] = add(half[mine], far_in[...])

    return Chain(
        [pack],
        [pl.BlockSpec(pack.shape, lambda *_: (0,) * 5, pipeline_mode=pl.Buffered(1))],
        [resident(shape)],
        [jax.ShapeDtypeStruct(shape, BF16)],
        [pltpu.VMEM((2,) + shape, BF16), pltpu.VMEM((2,) + shape, BF16), pltpu.VMEM(shape, BF16)]
        + [pltpu.SemaphoreType.DMA((2,))] * 2,
        {"core", "y"},
        [(steps[0], first), (steps[1], second), (0, last)],
    )


def copy_sums(part, steps):
    shape = part.shape[1:]

    def copies(part_ref, total, x_in, held, near_in, line, inner_in, full, send, recv):
        device = lax.axis_index("rep")
        core, side = device % 2, (device // 2) % 2
        made = Exchange(send, recv)
        mine = full.at[core, side]
        plans = [
            ("x", part_ref.at[1 - side], x_in),
            ("near", held, near_in),
            ("inner", line, inner_in),
            ("outward", mine, mine),
            ("x", mine, mine),
            ("core", full.at[core], full.at[core]),
        ]
        return [lambda k=k, plan=plan: made.at(k, *plan) for k, plan in enumerate(plans)]

    def first(*refs):
        begin(copies(*refs)[0])

    def second(*refs):
        part_ref, total, x_in, held = refs[:4]
        steps = copies(*refs)
        end(steps[0])
        side = (lax.axis_index("rep") // 2) % 2
        held[...] = add(part_ref[side], x_in[...])
        begin(steps[1])

    def third(*refs):
        part_ref, total, x_in, held, near_in, line = refs[:6]
        steps = copies(*refs)
        end(steps[1])
        line[...] = add(held[...], near_in[...])
        begin(steps[2])

    def fourth(*refs):
        part_ref, total, x_in, held, near_in, line, inner_in, full = refs[:8]
        steps = copies(*refs)
        device = lax.axis_index("rep")
        middle = ((device // 4) % 3) > 0
        end(steps[2])

        @pl.when(middle)
        def _():
            full[device % 2, (device // 2) % 2] = add(line[...], inner_in[...])

        begin(steps[3])

    def fifth(*refs):
        steps = copies(*refs)
        end(steps[3])
        begin(steps[4])

    def sixth(*refs):
        steps = copies(*refs)
        end(steps[4])
        begin(steps[5])

    def last(*refs):
        total, full = refs[1], refs[7]
        end(copies(*refs)[5])
        total[...] = full[...]

    whole = (2, 2) + shape
    return Chain(
        [part],
        [resident(part.shape)],
        [resident(whole)],
        [jax.ShapeDtypeStruct(whole, BF16)],
        [pltpu.VMEM(shape, BF16)] * 5 + [pltpu.VMEM(whole, BF16)] + [pltpu.SemaphoreType.DMA((6,))] * 2,
        {"core", "x", "near", "inner"},
        list(zip(steps, (first, second, third, fourth, fifth, sixth))) + [(0, last)],
    )


def emit(count, middle, sum_own, sum_far, total):
    images, _, width = middle.shape
    far_arrays, far_specs, read_far = by_piece(sum_far, PAD, width)

    def body(count_ref, middle_ref, own_ref, *refs):
        far, (out_ref, held) = refs[:-2], refs[-2:]
        image = pl.program_id(0)
        live = (iota((PAD, 1), 0) < IMG_TOK) & (image < count_ref[0])
        both = own_ref[0].astype(F32) + read_far(far).astype(F32)
        result = jnp.where(live, 1.0, 0.0) * (middle_ref[0] + both)
        for k in range(images):

            @pl.when(image == k)
            def _():
                held[pl.ds(k * IMG_TOK, IMG_TOK), :] = result[:IMG_TOK]

        @pl.when(image == images - 1)
        def _():
            out_ref[...] = held[pl.ds(0, total), :].astype(BF16)

    tile = by_image(PAD, width)
    return run(
        body,
        (count, middle, sum_own, *far_arrays),
        [scalar_spec(), tile, tile, *far_specs],
        [resident((total, width))],
        [jax.ShapeDtypeStruct((total, width), BF16)],
        grid=(images,),
        scratch=[pltpu.VMEM((1000, width), F32)],
        cost=pl.CostEstimate(flops=2_000_000, bytes_accessed=6_000_000, transcendentals=0),
        name="emit",
    )[0][0]


def by_slice(
    tokens, cotangent, routes, image_count, capacity, norm1_gain, norm1_bias, w_qkv, bias_q, bias_v, w_out, bias_out,
    norm2_gain, norm2_bias, w_router, expert_in, expert_in_bias, expert_out, expert_out_bias,
):
    total, width = tokens.shape
    local = expert_in.shape[0]
    device = lax.axis_index("rep")
    mine = lax.axis_index("fsdp")
    core = device % 2
    wide, tall = pack_weights(
        (norm1_gain, norm1_bias, bias_q, bias_v, bias_out, norm2_gain, norm2_bias), w_qkv, w_out, w_router
    )
    (tok, cot, route, ids, load), (wide_far, tall_far), _ = prepare(
        tokens, cotangent, routes, image_count, capacity, wide, tall, 0
    )
    wide, tall = (wide, wide_far), (tall, tall_far)
    base = (mine * (local * CAP)).reshape(1)
    net = Network()
    net.offer("C", cot, COT_PATHS)
    idents = iter(range(1, 32))

    def staged(kernel, *args, rounds):
        traffic, plan = net.plan(*rounds)
        args = [arg(plan) if callable(arg) else arg for arg in args]
        outs, arrived, chained = kernel(*args, traffic, next(idents))
        net.land(plan, arrived)
        return (*outs, *chained)

    own, far = (0, 0, 0), (0, 0, 1)
    packed, prob, mixed, middle, second, soft, soft_sum = staged(
        front, image_count, tok, ids, route, wide, tall, rounds=evenly(FRONT_ROOM, 5, 0.68)
    )
    net.offer("S", second, ROW_PATHS)

    def sender(block):
        return net.block("S", block), net.block("C", block)

    def senders(blocks):
        return lambda plan: [(net.find(plan, "S", block), net.find(plan, "C", block)) for block in blocks]

    pair = staged(
        gather, base, local, senders([own, far]), [0, None, None, None, None, 1],
        rounds=(PAIR_ROOM, list(range(8)), [0.0, 0.45, 0.9, 1.9, 2.9, 3.9, 5.0, 6.0]),
    )
    made_own, made_far, back_own, back_far, sums = staged(
        expert_layer, pair, expert_in, expert_in_bias, expert_out, expert_out_bias,
        sums_everywhere(load, soft_sum, (0, 2, 5, 8, 11, 13)),
        rounds=evenly(EXPERT_ROOM, 16, 0.7, 2),
    )
    sum_far, drow_far, dgate_far = staged(
        combine, base, *sender(far), made_far, back_far, rounds=evenly(2, 5, 0.4, 2)
    )
    net.offer("D", drow_far, FAR_FIRST)
    net.offer("G", dgate_far, FAR_FIRST, 0)
    net.offer("M", sum_far, FAR_LAST)
    sum_own, drow_own, dgate_own = staged(
        combine, base, *sender(own), made_own, back_own, rounds=evenly(OWN_ROOM, 5, 0.4)
    )
    loads, prob_total = sums[0, 0:1], sums[1, 0:1]
    live = loads[:, 64:65]
    share = (loads[:, :EXPERTS] + loads[:, EXPERTS : 2 * EXPERTS]) / (2.0 * live)
    aux = jnp.pad(EXPERTS * share / live, ((0, 0), (0, 128 - EXPERTS)))
    grad_tokens, pack = staged(
        finish, image_count, tok, cot, (packed, prob, mixed, middle, second, soft), route, drow_own,
        lambda plan: net.find(plan, "D", far), dgate_own, net.block("G", far), aux, wide, tall, total,
        rounds=evenly(FINISH_ROOM, 5, 1.5),
    )
    blocks = [block for block in COT_PATHS if block != far]
    count = 2 * len(blocks) + 2
    traffic, plan = net.plan(LAST_ROOM, list(range(count)), [LAST_ROOM * k / count for k in range(count)])
    blocks.sort(key=lambda block: net.landing(plan, block))
    outs, arrived, (part,) = gather(
        base, local, senders(blocks)(plan), list(range(len(blocks))) + [None, None],
        traffic, next(idents), owner_sums(pack, (0, 6)),
    )
    net.land(plan, arrived)
    slots = [pair, outs]
    outputs = emit(image_count, middle, sum_own, net.block("M", far), total)
    row_slots = [pair[0] for pair in slots]
    grad_slots = [pair[1] for pair in slots]
    (keep_in, send_in, keep_out, send_out, d_bias, d_out_bias), _, (owned,) = slice_grads(
        row_slots, grad_slots, expert_in, expert_in_bias, expert_out, copy_sums(part, (0, 3, 6, 9, 12, 15)), next(idents)
    )
    owned = owned.reshape(width // 2, -1).astype(F32)
    swap = [(i, i ^ 1) for i in range(16)]
    got_in, got_out, got_bias, got_out_bias = (
        lax.ppermute(v, "rep", swap) for v in (send_in, send_out, d_bias, d_out_bias)
    )
    bias = (d_bias + got_bias)[:, 0]
    out_bias = (d_out_bias + got_out_bias)[:, 0]
    half = bias.shape[1] // 2
    piece = width // 16
    expert_grads = (
        keep_in + got_in.astype(F32),
        lax.dynamic_slice_in_dim(bias, core * half, half, axis=1),
        keep_out + got_out.astype(F32),
        lax.dynamic_slice_in_dim(out_bias, device * piece, piece, axis=1),
    )

    balance_loss = jnp.sum(aux * prob_total)
    lines = jnp.transpose(owned[:, 4 * width + EXPERTS : 4 * width + EXPERTS + 8])
    owned = (
        lines[0],
        lines[1],
        owned[:, : 3 * width],
        lines[2],
        lines[3],
        owned[:, 3 * width : 4 * width],
        lines[4],
        lines[5],
        lines[6],
        owned[:, 4 * width : 4 * width + EXPERTS],
    )
    return (outputs, grad_tokens, balance_loss) + owned + expert_grads


def solution(mesh):
    in_specs = (
        P(("rep", "fsdp"), None),
        P(("rep", "fsdp"), None),
        P(("rep", "fsdp"), None),
        P(("rep", "fsdp")),
        P(("rep", "fsdp")),
        P("fsdp"),
        P("fsdp"),
        P("fsdp", None),
        P("fsdp"),
        P("fsdp"),
        P("fsdp", None),
        P("fsdp"),
        P("fsdp"),
        P("fsdp"),
        P("fsdp", None),
        P("fsdp", None, None),
        P("fsdp", None),
        P("fsdp", None, None),
        P("fsdp", None),
    )
    out_specs = (
        P(("rep", "fsdp"), None),
        P(("rep", "fsdp"), None),
        P(),
        P("fsdp"),
        P("fsdp"),
        P("fsdp", None),
        P("fsdp"),
        P("fsdp"),
        P("fsdp", None),
        P("fsdp"),
        P("fsdp"),
        P("fsdp"),
        P("fsdp", None),
        P("fsdp", None, "rep"),
        P("fsdp", "rep"),
        P("fsdp", "rep", None),
        P("fsdp", "rep"),
    )
    program = by_slice if mesh.shape["rep"] == 16 and mesh.shape["fsdp"] == 2 else shards
    return jax.shard_map(program, mesh=mesh, in_specs=in_specs, out_specs=out_specs, check_vma=False)
```

```python
import jax
import jax.numpy as jnp
from jax import lax
from jax.experimental import pallas as pl
from jax.experimental.pallas import tpu as pltpu
from jax.sharding import PartitionSpec as P

HEADS = 8
HEAD_DIM = 64
EXPERTS = 32
IMG_TOK = 197
CAP = 80


def norm_rows(values, norm_gain, offset):
    average = jnp.mean(values, axis=-1, keepdims=True)
    centred = values - average
    variance = jnp.mean(centred * centred, axis=-1, keepdims=True)
    return centred * lax.rsqrt(variance + 1e-06) * norm_gain + offset


def slot_table(choices, alive_mask, limit, row_total):
    pair_expert = jnp.concatenate([choices[:, 0], choices[:, 1]])
    live_pairs = jnp.concatenate([alive_mask, alive_mask])
    expert_ids = jnp.arange(EXPERTS, dtype=jnp.int32)
    onehot = ((pair_expert[:, None] == expert_ids[None, :]) & live_pairs[:, None]).astype(jnp.int32)
    before = jnp.cumsum(onehot, axis=0) - onehot
    position = jnp.sum(before * onehot, axis=1)
    kept_pairs = live_pairs & (position < limit)
    pair_slot = pair_expert * CAP + position
    pair_token = jnp.concatenate(
        [jnp.arange(row_total, dtype=jnp.int32), jnp.arange(row_total, dtype=jnp.int32)]
    )
    slot_owner = jnp.full((EXPERTS * CAP,), row_total, jnp.int32)
    target = jnp.where(kept_pairs, pair_slot, EXPERTS * CAP)
    slot_owner = slot_owner.at[target].set(pair_token, mode="drop")
    safe_slot = jnp.where(kept_pairs, pair_slot, 0)
    return (slot_owner, kept_pairs, safe_slot, target, onehot)


def shards(
    tokens,
    cotangent,
    routes,
    image_count,
    capacity,
    norm1_gain,
    norm1_bias,
    w_qkv,
    bias_q,
    bias_v,
    w_out,
    bias_out,
    norm2_gain,
    norm2_bias,
    w_router,
    expert_in,
    expert_in_bias,
    expert_out,
    expert_out_bias,
):
    rows_count = tokens.shape[0]
    model_width = tokens.shape[1]
    image_total = rows_count // IMG_TOK
    score_scale = HEAD_DIM ** (-0.5)
    image_rows = jnp.arange(rows_count, dtype=jnp.int32) // IMG_TOK
    alive_mask = image_rows < image_count[0]
    alive_float = alive_mask.astype(jnp.float32)[:, None]
    slot_owner, kept_pairs, safe_slot, target, onehot = slot_table(
        routes, alive_mask, capacity[0], rows_count
    )
    kept_float = kept_pairs.astype(jnp.float32)
    load_local = jnp.sum(onehot.astype(jnp.float32), axis=0)
    live_local = jnp.sum(alive_float)
    load_total, live_total = lax.psum((load_local, live_local), ("rep", "fsdp"))
    gathered = (
        lax.all_gather(norm1_gain, "fsdp", axis=0, tiled=True),
        lax.all_gather(norm1_bias, "fsdp", axis=0, tiled=True),
        lax.all_gather(w_qkv, "fsdp", axis=0, tiled=True),
        lax.all_gather(bias_q, "fsdp", axis=0, tiled=True),
        lax.all_gather(bias_v, "fsdp", axis=0, tiled=True),
        lax.all_gather(w_out, "fsdp", axis=0, tiled=True),
        lax.all_gather(bias_out, "fsdp", axis=0, tiled=True),
        lax.all_gather(norm2_gain, "fsdp", axis=0, tiled=True),
        lax.all_gather(norm2_bias, "fsdp", axis=0, tiled=True),
        lax.all_gather(w_router, "fsdp", axis=0, tiled=True),
    )
    (
        gain_one,
        shift_one,
        qkv_full,
        query_bias,
        value_bias,
        out_full,
        out_bias,
        gain_two,
        shift_two,
        router_full,
    ) = gathered
    gain_one = gain_one.astype(jnp.float32)
    shift_one = shift_one.astype(jnp.float32)
    gain_two = gain_two.astype(jnp.float32)
    shift_two = shift_two.astype(jnp.float32)
    inputs = tokens.astype(jnp.float32)
    normed = norm_rows(inputs, gain_one, shift_one)
    normed_low = normed.astype(jnp.bfloat16)
    bias_row = jnp.concatenate([query_bias, jnp.zeros_like(query_bias), value_bias]).astype(
        jnp.float32
    )
    packed_low = (
        jnp.dot(normed_low, qkv_full, preferred_element_type=jnp.float32) + bias_row
    ).astype(jnp.bfloat16)
    image_shape = (image_total, IMG_TOK, HEADS, HEAD_DIM)
    queries = packed_low[:, :model_width].reshape(image_shape)
    all_keys = packed_low[:, model_width : 2 * model_width].reshape(image_shape)
    valued = packed_low[:, 2 * model_width :].reshape(image_shape)

    def score_block():
        return (
            jnp.einsum("iqhd,ikhd->hiqk", queries, all_keys, preferred_element_type=jnp.float32)
            * score_scale
        )

    scores = score_block()
    row_peak = jnp.max(scores, axis=-1, keepdims=True)
    exp_scores = jnp.exp(scores - row_peak)
    totals = jnp.sum(exp_scores, axis=-1, keepdims=True)
    log_total = row_peak + jnp.log(totals)
    attn_low = (exp_scores / totals).astype(jnp.bfloat16)
    mixed_low = (
        jnp.einsum("hiqk,ikhd->iqhd", attn_low, valued, preferred_element_type=jnp.float32)
        .reshape(rows_count, model_width)
        .astype(jnp.bfloat16)
    )
    middle = (
        inputs
        + jnp.dot(mixed_low, out_full, preferred_element_type=jnp.float32)
        + out_bias.astype(jnp.float32)
    )
    second_low = norm_rows(middle, gain_two, shift_two).astype(jnp.bfloat16)
    logits = jnp.dot(second_low, router_full, preferred_element_type=jnp.float32)
    expert_ids = jnp.arange(EXPERTS, dtype=jnp.int32)
    first_hot = (routes[:, 0:1] == expert_ids[None, :]).astype(jnp.float32)
    second_hot = (routes[:, 1:2] == expert_ids[None, :]).astype(jnp.float32)

    def gate_terms(logit_rows):
        router_probs = jax.nn.softmax(logit_rows, axis=-1)
        pick_one = jnp.sum(router_probs * first_hot, axis=-1)
        pick_two = jnp.sum(router_probs * second_hot, axis=-1)
        pick_total = pick_one + pick_two
        return (pick_one / pick_total, pick_two / pick_total, router_probs)

    (gate_first, gate_second, router_probs), gate_back = jax.vjp(gate_terms, logits)
    padded_rows = jnp.concatenate([second_low, jnp.zeros((1, model_width), jnp.bfloat16)], axis=0)
    sent_rows = padded_rows[slot_owner].reshape(EXPERTS, CAP, model_width)
    received = lax.all_to_all(sent_rows, "fsdp", split_axis=0, concat_axis=1, tiled=True)
    raised = (
        jnp.einsum("esd,edf->esf", received, expert_in, preferred_element_type=jnp.float32)
        + expert_in_bias.astype(jnp.float32)[:, None, :]
    )
    active, gelu_back = jax.vjp(jax.nn.gelu, raised)
    active_low = active.astype(jnp.bfloat16)
    produced = (
        jnp.einsum("esf,efd->esd", active_low, expert_out, preferred_element_type=jnp.float32)
        + expert_out_bias.astype(jnp.float32)[:, None, :]
    ).astype(jnp.bfloat16)
    returned = lax.all_to_all(produced, "fsdp", split_axis=1, concat_axis=0, tiled=True).reshape(
        EXPERTS * CAP, model_width
    )
    pair_rows = returned[safe_slot].astype(jnp.float32)
    pair_weight = jnp.concatenate([gate_first, gate_second]) * kept_float
    expert_sum = jnp.sum(
        (pair_rows * pair_weight[:, None]).reshape(2, rows_count, model_width), axis=0
    )
    outputs = (alive_float * (middle + expert_sum)).astype(jnp.bfloat16)
    upstream = cotangent.astype(jnp.float32) * alive_float
    pair_grad = jnp.concatenate([upstream, upstream], axis=0)
    gate_grads = jnp.sum(pair_grad * pair_rows, axis=1) * kept_float
    slot_gate = jnp.zeros((EXPERTS * CAP,), jnp.float32).at[target].set(pair_weight, mode="drop")
    padded_grad = jnp.concatenate([upstream, jnp.zeros((1, model_width), jnp.float32)], axis=0)
    slot_grads = (
        (padded_grad[slot_owner] * slot_gate[:, None])
        .astype(jnp.bfloat16)
        .reshape(EXPERTS, CAP, model_width)
    )
    grad_received = lax.all_to_all(slot_grads, "fsdp", split_axis=0, concat_axis=1, tiled=True)
    grad_active = jnp.einsum(
        "esd,efd->esf", grad_received, expert_out, preferred_element_type=jnp.float32
    )
    (grad_raised,) = gelu_back(grad_active)
    grad_raised_low = grad_raised.astype(jnp.bfloat16)
    grad_rows = jnp.einsum(
        "esf,edf->esd", grad_raised_low, expert_in, preferred_element_type=jnp.float32
    ).astype(jnp.bfloat16)
    back_rows = lax.all_to_all(grad_rows, "fsdp", split_axis=1, concat_axis=0, tiled=True).reshape(
        EXPERTS * CAP, model_width
    )
    expert_part = jnp.sum(
        (back_rows[safe_slot].astype(jnp.float32) * kept_float[:, None]).reshape(
            2, rows_count, model_width
        ),
        axis=0,
    )
    local_in = jnp.einsum(
        "esd,esf->edf", received, grad_raised_low, preferred_element_type=jnp.float32
    )
    local_in_bias = jnp.sum(grad_raised_low.astype(jnp.float32), axis=1)
    local_out = jnp.einsum(
        "esf,esd->efd", active_low, grad_received, preferred_element_type=jnp.float32
    )
    local_out_bias = jnp.sum(grad_received.astype(jnp.float32), axis=1)
    grad_in_weight, grad_in_bias, grad_out_weight, grad_out_expert_bias = (
        lax.psum_scatter(local_in, "rep", scatter_dimension=2, tiled=True),
        lax.psum_scatter(local_in_bias, "rep", scatter_dimension=1, tiled=True),
        lax.psum_scatter(local_out, "rep", scatter_dimension=1, tiled=True),
        lax.psum_scatter(local_out_bias, "rep", scatter_dimension=1, tiled=True),
    )
    prob_local = jnp.sum(router_probs * alive_float, axis=0)
    prob_total = lax.psum(prob_local, ("rep", "fsdp"))
    share = load_total / (2.0 * live_total)
    balance_loss = EXPERTS * jnp.sum(share * prob_total / live_total)
    aux_grad = alive_float * (EXPERTS * share / live_total)[None, :]
    (grad_logits,) = gate_back((gate_grads[:rows_count], gate_grads[rows_count:], aux_grad))
    grad_logits_low = grad_logits.astype(jnp.bfloat16)
    grad_router = jnp.dot(second_low.T, grad_logits_low, preferred_element_type=jnp.float32)
    grad_second = (
        jnp.dot(grad_logits_low, router_full.T, preferred_element_type=jnp.float32) + expert_part
    )
    _, norm_two_back = jax.vjp(norm_rows, middle, gain_two, shift_two)
    grad_mid_norm, grad_gain_two, grad_shift_two = norm_two_back(grad_second)
    grad_middle = upstream + grad_mid_norm
    grad_att_low = grad_middle.astype(jnp.bfloat16)
    grad_out_proj = jnp.dot(mixed_low.T, grad_att_low, preferred_element_type=jnp.float32)
    grad_out_bias = jnp.sum(grad_att_low.astype(jnp.float32), axis=0)
    grad_mixed = (
        jnp.dot(grad_att_low, out_full.T, preferred_element_type=jnp.float32)
        .astype(jnp.bfloat16)
        .reshape(image_shape)
    )
    recomputed = jnp.exp(score_block() - log_total)
    grad_weights = jnp.einsum(
        "iqhd,ikhd->hiqk", grad_mixed, valued, preferred_element_type=jnp.float32
    )
    grad_values = jnp.einsum(
        "hiqk,iqhd->ikhd",
        recomputed.astype(jnp.bfloat16),
        grad_mixed,
        preferred_element_type=jnp.float32,
    )
    inner_sum = jnp.sum(grad_weights * recomputed, axis=-1, keepdims=True)
    grad_scores = (recomputed * (grad_weights - inner_sum)).astype(jnp.bfloat16)
    grad_queries = (
        jnp.einsum("hiqk,ikhd->iqhd", grad_scores, all_keys, preferred_element_type=jnp.float32)
        * score_scale
    )
    grad_keys = (
        jnp.einsum("hiqk,iqhd->ikhd", grad_scores, queries, preferred_element_type=jnp.float32)
        * score_scale
    )
    grad_packed_low = jnp.concatenate(
        [
            grad_queries.reshape(rows_count, model_width),
            grad_keys.reshape(rows_count, model_width),
            grad_values.reshape(rows_count, model_width),
        ],
        axis=1,
    ).astype(jnp.bfloat16)
    grad_qkv = jnp.dot(normed_low.T, grad_packed_low, preferred_element_type=jnp.float32)
    packed_sums = jnp.sum(grad_packed_low.astype(jnp.float32), axis=0)
    grad_query_bias = packed_sums[:model_width]
    grad_value_bias = packed_sums[2 * model_width :]
    grad_normed = jnp.dot(grad_packed_low, qkv_full.T, preferred_element_type=jnp.float32)
    _, norm_one_back = jax.vjp(norm_rows, inputs, gain_one, shift_one)
    grad_input_norm, grad_gain_one, grad_shift_one = norm_one_back(grad_normed)
    grad_tokens = grad_middle + grad_input_norm
    local_grads = (
        grad_gain_one,
        grad_shift_one,
        grad_qkv,
        grad_query_bias,
        grad_value_bias,
        grad_out_proj,
        grad_out_bias,
        grad_gain_two,
        grad_shift_two,
        grad_router,
    )
    shares = (
        lax.psum_scatter(local_grads[0], "fsdp", scatter_dimension=0, tiled=True),
        lax.psum_scatter(local_grads[1], "fsdp", scatter_dimension=0, tiled=True),
        lax.psum_scatter(local_grads[2], "fsdp", scatter_dimension=0, tiled=True),
        lax.psum_scatter(local_grads[3], "fsdp", scatter_dimension=0, tiled=True),
        lax.psum_scatter(local_grads[4], "fsdp", scatter_dimension=0, tiled=True),
        lax.psum_scatter(local_grads[5], "fsdp", scatter_dimension=0, tiled=True),
        lax.psum_scatter(local_grads[6], "fsdp", scatter_dimension=0, tiled=True),
        lax.psum_scatter(local_grads[7], "fsdp", scatter_dimension=0, tiled=True),
        lax.psum_scatter(local_grads[8], "fsdp", scatter_dimension=0, tiled=True),
        lax.psum_scatter(local_grads[9], "fsdp", scatter_dimension=0, tiled=True),
    )
    owned = lax.psum(
        (
            shares[0],
            shares[1],
            shares[2],
            shares[3],
            shares[4],
            shares[5],
            shares[6],
            shares[7],
            shares[8],
            shares[9],
        ),
        "rep",
    )
    return (
        (outputs, grad_tokens, balance_loss)
        + tuple(owned)
        + (grad_in_weight, grad_in_bias, grad_out_weight, grad_out_expert_bias)
    )


def gelu_pair(value):
    root = 0.7978845608028654
    square = value * value
    bend = jnp.tanh(root * value * (1.0 + 0.044715 * square))
    half = 0.5 * (1.0 + bend)
    slope = half + 0.5 * value * (1.0 - bend * bend) * root * (1.0 + 3 * 0.044715 * square)
    return value * half, slope


def slice_grads_body(*refs, senders):
    parts, refs = refs[: sum(senders)], refs[sum(senders) :]
    in_ref, in_bias_ref, out_ref, keep_in, send_in, keep_out, send_out, d_bias, d_out_bias = refs
    core = lax.axis_index("rep") % 2
    width = in_ref.shape[1]

    def stacked(pieces):
        return jnp.concatenate([piece[...].reshape(-1, width) for piece in pieces], axis=0)

    rows = stacked(parts[: senders[0]])
    grads = stacked(parts[senders[0] :])
    first = in_ref[0]
    second = out_ref[0]
    raised = jnp.dot(rows, first, preferred_element_type=jnp.float32) + own_line(in_bias_ref)
    active, slope = gelu_pair(raised)
    active = active.astype(jnp.bfloat16)
    back = lax.dot_general(
        grads, second, (((1,), (1,)), ((), ())), preferred_element_type=jnp.float32
    )
    draised = (back * slope).astype(jnp.bfloat16)
    over_rows = (((0,), (0,)), ((), ()))
    g_in = lax.dot_general(rows, draised, over_rows, preferred_element_type=jnp.float32)
    g_out = lax.dot_general(active, grads, over_rows, preferred_element_type=jnp.float32)
    half = g_in.shape[1] // 2
    first_core = core == 0
    keep_in[0] = jnp.where(first_core, g_in[:, :half], g_in[:, half:])
    send_in[0] = jnp.where(first_core, g_in[:, half:], g_in[:, :half]).astype(jnp.bfloat16)
    keep_out[0] = jnp.where(first_core, g_out[:half], g_out[half:])
    send_out[0] = jnp.where(first_core, g_out[half:], g_out[:half]).astype(jnp.bfloat16)
    d_bias[0] = jnp.sum(draised.astype(jnp.float32), axis=0, keepdims=True)
    d_out_bias[0] = jnp.sum(grads.astype(jnp.float32), axis=0, keepdims=True)


def slice_grads(rows, grads, first, first_bias, second, chain, ident):
    experts, width, hidden = first.shape
    cap = rows[0].shape[2]
    slots = cap * sum(piece.shape[1] for piece in rows)
    part = 256
    half = part // 2
    f32 = jnp.float32
    def chip():
        return lax.axis_index("rep") // 2

    return run(
        lambda *refs: slice_grads_body(*refs, senders=(len(rows), len(grads))),
        (*rows, *grads, first, first_bias, second),
        [pl.BlockSpec((1,) + piece.shape[1:], lambda e: (e, 0, 0, 0)) for piece in (*rows, *grads)]
        + [
            pl.BlockSpec((1, width, part), lambda e: (e, 0, chip())),
            pl.BlockSpec((experts, part), lambda e: (0, chip())),
            pl.BlockSpec((1, part, width), lambda e: (e, chip(), 0)),
        ],
        [by_image(width, half)] * 2 + [by_image(half, width)] * 2 + [by_image(1, part), by_image(1, width)],
        [
            jax.ShapeDtypeStruct((experts, width, half), f32),
            jax.ShapeDtypeStruct((experts, width, half), jnp.bfloat16),
            jax.ShapeDtypeStruct((experts, half, width), f32),
            jax.ShapeDtypeStruct((experts, half, width), jnp.bfloat16),
            jax.ShapeDtypeStruct((experts, 1, part), f32),
            jax.ShapeDtypeStruct((experts, 1, width), f32),
        ],
        grid=(experts,),
        cost=pl.CostEstimate(
            flops=8 * experts * slots * width * part,
            bytes_accessed=4 * experts * (slots * width + 3 * width * part),
            transcendentals=experts * slots * part,
        ),
        name="slice_grads",
        chain=chain,
        ident=ident,
    )


F32 = jnp.float32
BF16 = jnp.bfloat16
PAD = 208
ROOT_AXES = ("rep", "fsdp")
OVER_COLS = (((1,), (1,)), ((), ()))
OVER_ROWS = (((0,), (0,)), ((), ()))


def dot(left, right):
    return jnp.dot(left, right, preferred_element_type=F32)


def dot_cols(left, right):
    return lax.dot_general(left, right, OVER_COLS, preferred_element_type=F32)


def dot_rows(left, right):
    return lax.dot_general(left, right, OVER_ROWS, preferred_element_type=F32)


def iota(shape, axis):
    return lax.broadcasted_iota(jnp.int32, shape, axis)


def resident(shape):
    return pl.BlockSpec(shape, lambda *_: (0,) * len(shape))


def by_image(*shape):
    return pl.BlockSpec((1,) + shape, lambda i, *_: (i,) + (0,) * len(shape))


def scalar_spec():
    return pl.BlockSpec(memory_space=pltpu.SMEM)


def partner(link):
    device, side = lax.axis_index("rep"), lax.axis_index("fsdp")
    if link == "y":
        return {"rep": device, "fsdp": 1 - side}
    depth = device // 4
    step = {
        "core": 1 - 2 * (device % 2),
        "x": 2 - 4 * ((device // 2) % 2),
        "near": 4 - 8 * (depth % 2),
        "inner": 12 - 8 * depth,
        "skip": 8 - 16 * (depth // 2),
    }[link]
    return {"rep": device + step, "fsdp": side}


def only_if(condition, action):
    if condition is None:
        action()
    else:
        pl.when(condition)(action)


class Move:
    def __init__(self, link, source, target, needs=()):
        self.link, self.source, self.target, self.needs = link, source, target, needs

    def roles(self):
        depth = lax.axis_index("rep") // 4
        middle = (depth % 3) > 0
        if self.link == "inner":
            return middle, middle
        if self.link in ("outward", "skip"):
            return middle, (depth % 3) == 0
        return None, None

    def copy(self, refs, send, recv):
        return pltpu.make_async_remote_copy(
            src_ref=self.source(refs),
            dst_ref=self.target(refs),
            send_sem=send,
            recv_sem=recv,
            device_id=partner("near" if self.link == "outward" else self.link),
            device_id_type=pl.DeviceIdType.MESH,
        )


class Traffic:
    def __init__(self, sources, targets, rounds, steps):
        self.sources, self.targets, self.rounds, self.steps = sources, targets, rounds, steps

    def count(self):
        return sum(len(moves) for moves in self.rounds)

    def links(self):
        return {("near" if m.link == "outward" else m.link) for moves in self.rounds for m in moves}

    def start(self, which, refs, send, recv, arrived):
        moves = [m for moves in self.rounds for m in moves]
        at = sum(len(moves) for moves in self.rounds[:which])
        for k, move in enumerate(self.rounds[which]):
            for index in move.needs:
                if index not in arrived:
                    arrived.add(index)
                    only_if(moves[index].roles()[1], moves[index].copy(refs, send.at[index], recv.at[index]).wait_recv)
            only_if(move.roles()[0], move.copy(refs, send.at[at + k], recv.at[at + k]).start)

    def require(self, target, position, refs, send, recv, arrived):
        moves = [m for moves in self.rounds for m in moves]
        for index, move in enumerate(moves):
            if move.home[0] == target and move.home[1] <= position < move.home[1] + move.size and index not in arrived:
                arrived.add(index)
                only_if(move.roles()[1], move.copy(refs, send.at[index], recv.at[index]).wait_recv)

    def finish(self, refs, send, recv, arrived):
        moves = [m for moves in self.rounds for m in moves]
        for index, move in enumerate(moves):
            copy = move.copy(refs, send.at[index], recv.at[index])
            sends, receives = move.roles()
            only_if(sends, copy.wait_send)
            if index not in arrived:
                only_if(receives, copy.wait_recv)


def greet(links):
    barrier = pltpu.get_barrier_semaphore()
    middle = ((lax.axis_index("rep") // 4) % 3) > 0
    plain = [link for link in ("core", "x", "y", "near", "skip") if link in links]
    for link in plain:
        pl.semaphore_signal(barrier, inc=1, device_id=partner(link), device_id_type=pl.DeviceIdType.MESH)
    if "inner" in links:

        @pl.when(middle)
        def _():
            pl.semaphore_signal(
                barrier, inc=1, device_id=partner("inner"), device_id_type=pl.DeviceIdType.MESH
            )

    if "inner" in links:

        @pl.when(middle)
        def _():
            pl.semaphore_wait(barrier, len(plain) + 1)

        @pl.when(~middle)
        def _():
            if plain:
                pl.semaphore_wait(barrier, len(plain))

    else:
        pl.semaphore_wait(barrier, len(plain))


class Chain:
    def __init__(self, args, in_specs, out_specs, out_shape, scratch, links, actions):
        self.args, self.in_specs, self.out_specs, self.out_shape = args, in_specs, out_specs, out_shape
        self.scratch, self.links, self.actions = scratch, links, actions


def run(
    body, args, in_specs, out_specs, out_shape, *,
    name, grid=(1,), scratch=(), cost=None, traffic=None, chain=None, hook=None, ident=None,
):
    if (traffic is None or traffic.count() == 0) and chain is None:
        outs = pl.pallas_call(
            body, grid=grid, in_specs=in_specs, out_specs=out_specs, out_shape=out_shape,
            scratch_shapes=list(scratch), cost_estimate=cost, name=name,
        )(*args)
        return outs, [], []
    traffic = traffic or Traffic([], [], [], [])
    chain = chain or Chain([], [], [], [], [], set(), [])
    n_in, n_src, n_out, n_dst = len(args), len(traffic.sources), len(out_shape), len(traffic.targets)
    anywhere = pl.BlockSpec(memory_space=pl.ANY)
    sizes = (n_in, n_src, len(chain.args), n_out, n_dst, len(chain.out_shape), len(scratch), len(chain.scratch))
    links = traffic.links() | chain.links

    def carried(*refs):
        groups = []
        for size in sizes:
            groups.append(refs[:size])
            refs = refs[size:]
        ins, sources, chain_in, outs, targets, chain_out, held, chain_held = groups
        ends = (sources, targets)
        step = pl.program_id(0)
        pl.when(step == 0)(lambda: greet(links))
        arrived = set()
        for at in range(grid[0]):
            rounds = [which for which, when in enumerate(traffic.steps) if when == at]
            actions = [action for when, action in chain.actions[:-1] if when == at]
            if rounds or actions or hook:

                @pl.when(step == at)
                def _():
                    for which in rounds:
                        traffic.start(which, ends, *refs, arrived)
                    for action in actions:
                        action(*chain_in, *chain_out, *chain_held)
                    if hook:
                        hook(
                            at,
                            lambda target, position: traffic.require(target, position, ends, *refs, arrived),
                            targets, ins, held,
                        )

        body(*ins, *outs, *held)

        @pl.when(step == grid[0] - 1)
        def _():
            if traffic.count():
                traffic.finish(ends, *refs, arrived)
            if chain.actions:
                chain.actions[-1][1](*chain_in, *chain_out, *chain_held)

    count = traffic.count()
    semaphores = [pltpu.SemaphoreType.DMA((count,))] * 2 if count else []
    outs = pl.pallas_call(
        carried,
        grid=grid,
        in_specs=list(in_specs) + [anywhere] * n_src + list(chain.in_specs),
        out_specs=list(out_specs) + [anywhere] * n_dst + list(chain.out_specs),
        out_shape=list(out_shape) + list(traffic.targets) + list(chain.out_shape),
        scratch_shapes=list(scratch) + list(chain.scratch) + semaphores,
        compiler_params=pltpu.CompilerParams(collective_id=ident, has_side_effects=True),
        cost_estimate=cost,
        name=name,
    )(*args, *traffic.sources, *chain.args)
    return outs[:n_out], outs[n_out : n_out + n_dst], outs[n_out + n_dst :]


COT_PATHS = {
    (0, 0, 1): ("y", (0, 0, 0), -1.500),
    (0, 1, 0): ("x", (0, 0, 0), 2.243),
    (0, 1, 1): ("x", (0, 0, 1), 1.258),
    (1, 0, 0): ("near", (0, 0, 0), 1.763),
    (1, 0, 1): ("near", (0, 0, 1), 1.701),
    (1, 1, 0): ("near", (0, 1, 0), 3.477),
    (1, 1, 1): ("x", (1, 0, 1), 5.719),
    (2, 0, 0): ("inner", (0, 0, 0), 4.656),
    (2, 0, 1): ("y", (2, 0, 0), 2.464),
    (2, 1, 0): ("inner", (0, 1, 0), 0.237),
    (2, 1, 1): ("x", (2, 0, 1), 2.798),
    (3, 0, 0): ("inner", (1, 0, 0), 0.958),
    (3, 0, 1): ("y", (3, 0, 0), 2.984),
    (3, 1, 0): ("x", (3, 0, 0), 2.092),
    (3, 1, 1): ("inner", (1, 1, 1), 1.507),
}
ROW_PATHS = {
    (0, 0, 1): ("y", (0, 0, 0), -1.400),
    (0, 1, 0): ("x", (0, 0, 0), 1.939),
    (0, 1, 1): ("x", (0, 0, 1), 1.580),
    (1, 0, 0): ("near", (0, 0, 0), 1.441),
    (1, 0, 1): ("y", (1, 0, 0), 0.198),
    (1, 1, 0): ("near", (0, 1, 0), 2.429),
    (1, 1, 1): ("x", (1, 0, 1), 5.646),
    (2, 0, 0): ("inner", (0, 0, 0), 2.268),
    (2, 0, 1): ("y", (2, 0, 0), 2.650),
    (2, 1, 0): ("x", (2, 0, 0), 4.955),
    (2, 1, 1): ("x", (2, 0, 1), 4.985),
    (3, 0, 0): ("reach", (1, 0, 0), 1.374),
    (3, 0, 1): ("y", (3, 0, 0), 4.956),
    (3, 1, 0): ("x", (3, 0, 0), 2.903),
    (3, 1, 1): ("y", (3, 1, 0), 4.968),
}
FAR_FIRST = {(0, 0, 1): ("y", (0, 0, 0), -2.0)}
FAR_LAST = {(0, 0, 1): ("y", (0, 0, 0), 2.506)}
FRONT_ROOM, PAIR_ROOM, EXPERT_ROOM, OWN_ROOM, FINISH_ROOM, LAST_ROOM = 5, 9, 11, 4, 8, 25


class Network:
    def __init__(self):
        self.have, self.hops, self.weight, self.pieces = {}, {}, {}, {}

    def offer(self, name, array, hops, weight=1):
        self.hops[name], self.weight[name] = hops, weight
        self.pieces[name] = array.shape[0]
        for p in range(array.shape[0]):
            self.have[name, (0, 0, 0), p] = (array, p)

    def order(self, item):
        name, block, p = item
        return self.hops[name][block][2], block, p

    def missing(self):
        return [
            (name, block, p)
            for name in self.hops
            for block in self.hops[name]
            for p in range(self.pieces[name])
            if (name, block, p) not in self.have
        ]

    def complete(self, name, block):
        return all((name, block, p) in self.have for p in range(self.pieces[name]))

    def plan(self, room, steps, times):
        waiting = sorted(self.missing(), key=self.order)
        landed, rounds, going = {}, [[] for _ in steps], {}
        free = dict.fromkeys(("x", "y", "near", "inner"), 0.0)
        uses = {"reach": (("inner", 2), ("near", 1))}
        lag = 0.4

        def fill(link, now, weight, horizon):
            spans = [(on, max(free[on], now), n * weight) for on, n in uses.get(link, ((link, 1),))]
            if weight and any(begin >= horizon or begin + length > room + 0.01 for _, begin, length in spans):
                return None
            for on, begin, length in spans:
                if length:
                    free[on] = begin + length
            return max(begin + length for _, begin, length in spans) + lag

        for r, now in enumerate(times):
            horizon = times[r + 1] + 0.5 if r + 1 < len(times) else room
            for item in [i for i, (_, at) in going.items() if at <= now]:
                done = fill("near", now, self.weight[item[0]], horizon)
                if done is not None:
                    rounds[r].append(("outward", item, item))
                    landed[item] = done
                    del going[item]
            for item in waiting:
                name, block, p = item
                if item in landed or item in going:
                    continue
                link, source, _ = self.hops[name][block]
                source = (name, source, p)
                if source not in self.have and landed.get(source, now + 1) > now:
                    continue
                if link == "inner":
                    left = room - max(free["near"], now + 1) - sum(self.weight[i[0]] for i in going)
                    if r + 1 >= len(times) or left < 1 + self.weight[name] or times[-1] < now + self.weight[name] + lag:
                        continue
                done = fill(link, now, self.weight[name], horizon)
                if done is None:
                    continue
                if link == "reach":
                    rounds[r] += [("inner", source, item), ("skip", source, item)]
                else:
                    rounds[r].append((link, source, item))
                if link == "inner":
                    going[item] = (r, done)
                else:
                    landed[item] = done
        for item in list(going):
            rounds[-1].append(("outward", item, item))
            landed[item] = room
        sources, targets, homes = [], [], {}
        for name, block, p in sorted(landed):
            homes.setdefault((name, block), []).append(p)
        order = list(homes)
        for name, block in order:
            model = self.have[name, (0, 0, 0), 0][0]
            targets.append(jax.ShapeDtypeStruct((len(homes[name, block]),) + model.shape[1:], model.dtype))

        def home(item):
            name, block, p = item
            return order.index((name, block)), homes[name, block].index(p)

        def origin(item):
            if item in landed:
                return (1,) + home(item)
            array, at = self.have[item]
            for k, known in enumerate(sources):
                if known is array:
                    return 0, k, at
            sources.append(array)
            return 0, len(sources) - 1, at

        moves = []
        for chosen in rounds:
            spans = []
            for link, source, item in sorted(chosen, key=lambda c: (c[0] not in ("outward", "inner"), *c)):
                a, b = origin(source), home(item)
                if spans:
                    link_, a_, b_, n = spans[-1]
                    if link_ == link and a_[:2] == a[:2] and b_[0] == b[0] and a[2] == a_[2] + n and b[1] == b_[1] + n:
                        spans[-1] = (link, a_, b_, n + 1)
                        continue
                spans.append((link, a, b, 1))
            flat = [m for made in moves for m in made]
            placed = []
            for link, a, b, n in spans:
                needs = [
                    k
                    for k, m in enumerate(flat)
                    if a[0] == 1 and m.home[0] == a[1] and m.home[1] < a[2] + n and a[2] < m.home[1] + m.size
                ]
                placed.append(self.move(link, a, b, n, needs))
            moves.append(placed)
        while moves and not moves[-1]:
            moves.pop()
        traffic = Traffic(sources, targets, moves, steps[: len(moves)])
        return traffic, (order, homes, landed)

    def find(self, plan, name, block):
        order, homes, landed = plan
        found = []
        for p in range(self.pieces[name]):
            if (name, block, p) in landed:
                found.append((None, order.index((name, block)), homes[name, block].index(p)))
            else:
                array, at = self.have[name, block, p]
                found.append((array, None, at))
        return found

    def landing(self, plan, block):
        return max(plan[2].get((name, block, p), 0.0) for name in "CS" for p in range(self.pieces[name]))

    @staticmethod
    def move(link, origin, home, count, needs):
        def source(refs):
            return refs[origin[0]][origin[1]].at[pl.ds(origin[2], count)]

        def target(refs):
            return refs[1][home[0]].at[pl.ds(home[1], count)]

        made = Move(link, source, target, needs)
        made.home, made.size = home, count
        return made

    def land(self, plan, arrays):
        order, homes, _ = plan
        for key, array in zip(order, arrays):
            for at, p in enumerate(homes[key]):
                self.have[key[0], key[1], p] = (array, at)

    def block(self, name, block):
        return [self.have[name, block, p] for p in range(self.pieces[name])]


def evenly(room, steps, length, every=1):
    chosen = list(range(0, steps, every))
    return room, chosen, [step * length for step in chosen]


def gathering(room, senders, extra):
    busy = 2 * senders * 0.45
    times = [0.45 * step for step in range(2 * senders)]
    times += [busy + (step + 1) * max(0.5, room - busy) / (extra + 1) for step in range(extra)]
    return room, list(range(2 * senders + extra)), times


def standardise(values):
    average = jnp.mean(values, axis=-1, keepdims=True)
    centred = values - average
    variance = jnp.mean(centred * centred, axis=-1, keepdims=True)
    scale = lax.rsqrt(variance + 1e-06)
    return centred * scale, scale


def prep_body(count_ref, cap_ref, tok_ref, cot_ref, route_ref, tok_out, cot_out, route_out, ids_out, load_out, wide, narrow):
    pl.when(pl.program_id(0) == 0)(
        lambda: prep_rows(
            count_ref, cap_ref, tok_ref, cot_ref, route_ref, tok_out, cot_out, route_out, ids_out, load_out, wide, narrow
        )
    )


def prep_rows(count_ref, cap_ref, tok_ref, cot_ref, route_ref, tok_out, cot_out, route_out, ids_out, load_out, wide, narrow):
    images = tok_out.shape[0]
    total = tok_ref.shape[0]
    alive_images = count_ref[0]
    real = iota((PAD, 1), 0) < IMG_TOK

    def split(source, image):
        return source[pl.ds(image * IMG_TOK, PAD), :]

    wide[...] = jnp.zeros_like(wide)
    narrow[...] = jnp.zeros_like(narrow)
    wide[pl.ds(0, total), :] = tok_ref[...].astype(F32)
    for image in range(images):
        tok_out[image] = jnp.where(real, split(wide, image), 0.0).astype(BF16)
    wide[pl.ds(0, total), :] = cot_ref[...].astype(F32)
    narrow[pl.ds(0, total), :] = route_ref[...]
    routes = []
    lives = []
    for image in range(images):
        live = real & (image < alive_images)
        cot_out[image] = jnp.where(live, split(wide, image), 0.0).astype(BF16)
        picked = split(narrow, image)
        route_out[image] = picked
        routes.append(picked)
        lives.append(jnp.where(live, 1, 0))
    routes = jnp.concatenate(routes, axis=0)
    live = jnp.concatenate(lives, axis=0) > 0
    rows = images * PAD
    lane = iota((rows, 128), 1)
    first = (lane == routes[:, 0:1]) & live
    second = (lane == routes[:, 1:2] + EXPERTS) & live
    hot = jnp.where(first | second, 1.0, 0.0)
    below = jnp.where(iota((rows, rows), 0) > iota((rows, rows), 1), 1.0, 0.0).astype(BF16)
    before = dot(below, hot.astype(BF16))
    totals = jnp.sum(hot, axis=0, keepdims=True)
    place_one = jnp.sum(jnp.where(first, before, 0.0), axis=1, keepdims=True)
    place_two = jnp.sum(jnp.where(second, before, 0.0), axis=1, keepdims=True) + jnp.sum(
        jnp.where(lane == routes[:, 1:2], totals, 0.0), axis=1, keepdims=True
    )
    limit = cap_ref[0].astype(F32)
    keep_one = live & (place_one < limit)
    keep_two = live & (place_two < limit)
    slots = jnp.where(lane == 0, jnp.where(keep_one, routes[:, 0:1].astype(F32), -1.0), 0.0)
    slots = jnp.where(lane == 1, jnp.where(keep_one, place_one, 0.0), slots)
    slots = jnp.where(lane == 2, jnp.where(keep_two, routes[:, 1:2].astype(F32), -1.0), slots)
    slots = jnp.where(lane == 3, jnp.where(keep_two, place_two, 0.0), slots)
    for image in range(images):
        ids_out[image] = jnp.transpose(slots[image * PAD : (image + 1) * PAD])[0:8]
    lanes = iota((1, 128), 1)
    tokens_alive = (alive_images * IMG_TOK).astype(F32)
    load_out[0] = jnp.broadcast_to(jnp.where(lanes == 64, tokens_alive, totals), (8, 128))


def pack_body(*refs):
    lines, (qkv_ref, out_ref, router_ref, wide_ref, tall_ref) = refs[:-5], refs[-5:]
    rows, part = qkv_ref.shape[0], lines[0].shape[0]
    wide_ref[:rows] = qkv_ref[...]
    table = jnp.zeros((16, part), F32)
    for k, ref in enumerate(lines):
        line = jnp.broadcast_to(ref[...].astype(F32).reshape(1, part), (16, part))
        table = jnp.where(iota((16, part), 0) == k, line, table)
    wide_ref[rows:] = jnp.zeros((16, wide_ref.shape[1]), BF16)
    wide_ref[rows:, :part] = table.astype(BF16)
    width = out_ref.shape[1]
    tall_ref[:, :width] = out_ref[...]
    tall_ref[:, width:] = jnp.zeros((rows, 128), BF16)
    tall_ref[:, width : width + EXPERTS] = router_ref[...]


def pack_weights(lines, w_qkv, w_out, w_router):
    rows = w_qkv.shape[0]
    return pl.pallas_call(
        pack_body,
        in_specs=[pl.BlockSpec(memory_space=pltpu.VMEM)] * (len(lines) + 3),
        out_specs=[pl.BlockSpec(memory_space=pltpu.VMEM)] * 2,
        out_shape=[
            jax.ShapeDtypeStruct((rows + 16, w_qkv.shape[1]), BF16),
            jax.ShapeDtypeStruct((rows, w_out.shape[1] + 128), BF16),
        ],
        cost_estimate=pl.CostEstimate(flops=1_000_000, bytes_accessed=2_500_000, transcendentals=0),
        name="pack_weights",
    )(*lines, w_qkv, w_out, w_router)


def weight_traffic(wide, tall):
    def rows(array):
        half = array.shape[0] // 2
        return pl.ds(pl.multiple_of((lax.axis_index("rep") % 2) * half, 8), half)

    def fetch(at, array):
        return Move("y", lambda refs: refs[0][at].at[rows(array)], lambda refs: refs[1][at].at[rows(array)])

    def pass_on(at, array):
        there = lambda refs: refs[1][at].at[rows(array)]
        return Move("core", there, there, [at])

    arrays = (wide, tall)
    targets = [jax.ShapeDtypeStruct(a.shape, a.dtype) for a in arrays]
    rounds = [[make(at, a) for at, a in enumerate(arrays)] for make in (fetch, pass_on)]
    return Traffic(list(arrays), targets, rounds, [0, 1])


def prepare(tokens, cotangent, routes, image_count, capacity, wide, tall, ident):
    total, width = tokens.shape
    images = total // IMG_TOK
    shapes = [
        jax.ShapeDtypeStruct((images, PAD, width), BF16),
        jax.ShapeDtypeStruct((images, PAD, width), BF16),
        jax.ShapeDtypeStruct((images, PAD, 2), jnp.int32),
        jax.ShapeDtypeStruct((images, 8, PAD), F32),
        jax.ShapeDtypeStruct((1, 8, 128), F32),
    ]
    return run(
        prep_body,
        (image_count, capacity, tokens, cotangent, routes),
        [scalar_spec(), scalar_spec()] + [resident(a.shape) for a in (tokens, cotangent, routes)],
        [resident(a.shape) for a in shapes],
        shapes,
        grid=(2,),
        scratch=[pltpu.VMEM((1000, width), F32), pltpu.VMEM((1000, 2), jnp.int32)],
        cost=pl.CostEstimate(flops=300_000_000, bytes_accessed=6_000_000, transcendentals=0),
        name="prepare",
        traffic=weight_traffic(wide, tall),
        ident=ident,
    )


def place_halves(own, far, both):
    mine = lax.axis_index("fsdp")
    both[mine] = own[...]
    both[1 - mine] = far[...]


def vectors(wide_ref):
    return jnp.concatenate([wide_ref[0, 256:272, :256], wide_ref[1, 256:272, :256]], axis=1).astype(F32)


def front_body(
    count_ref, tok_ref, ids_ref, route_ref, wide_own, wide_far, tall_own, tall_far,
    packed_ref, prob_ref, mixed_ref, middle_ref, second_ref, soft_ref, sum_ref, wide_ref, tall_ref,
):
    @pl.when(pl.program_id(0) == 0)
    def _():
        sum_ref[...] = jnp.zeros_like(sum_ref)
        place_halves(wide_own, wide_far, wide_ref)
        place_halves(tall_own, tall_far, tall_ref)

    width = tok_ref.shape[-1]
    vec = vectors(wide_ref)
    inputs = tok_ref[0].astype(F32)
    normed = (standardise(inputs)[0] * vec[0:1] + vec[1:2]).astype(BF16)
    qkv = wide_ref[:, :256, :].reshape(width, 3 * width)
    raw = dot(normed, qkv)
    packed_ref[0, :, :width] = (raw[:, :width] + vec[2:3]).astype(BF16)
    packed_ref[0, :, width : 2 * width] = raw[:, width : 2 * width].astype(BF16)
    packed_ref[0, :, 2 * width :] = (raw[:, 2 * width :] + vec[3:4]).astype(BF16)
    low_lanes = iota((PAD, 128), 1) < HEAD_DIM
    real_key = iota((PAD, PAD), 1) < IMG_TOK
    for pair in range(HEADS // 2):
        at = pair * 128
        query = packed_ref[0, :, at : at + 128] * jnp.asarray(HEAD_DIM**-0.5, BF16)
        keys = packed_ref[0, :, width + at : width + at + 128]
        valued = packed_ref[0, :, 2 * width + at : 2 * width + at + 128]
        got = []
        for side in range(2):
            own = low_lanes if side == 0 else ~low_lanes
            scores = dot_cols(jnp.where(own, query, jnp.zeros_like(query)), keys)
            scores = jnp.where(real_key, scores, -1e30)
            raised = jnp.exp(scores - jnp.max(scores, axis=-1, keepdims=True))
            weights = (raised / jnp.sum(raised, axis=-1, keepdims=True)).astype(BF16)
            prob_ref[0, 2 * pair + side] = weights
            got.append(dot(weights, valued))
        mixed_ref[0, :, at : at + 128] = jnp.where(low_lanes, got[0], got[1]).astype(BF16)
    out_full = tall_ref[:, :, :width].reshape(width, width)
    router = tall_ref[:, :, width : width + 128].reshape(width, 128)
    middle = inputs + dot(mixed_ref[0], out_full) + vec[4:5]
    middle_ref[0] = middle
    second = standardise(middle)[0] * vec[5:6] + vec[6:7]
    lane = iota((PAD, 128), 1)
    logits = jnp.where(lane < EXPERTS, dot(second.astype(BF16), router), -1e30)
    soft = jnp.exp(logits - jnp.max(logits, axis=-1, keepdims=True))
    soft = soft / jnp.sum(soft, axis=-1, keepdims=True)
    route = route_ref[0]
    pick_one = jnp.sum(jnp.where(lane == route[:, 0:1], soft, 0.0), axis=-1, keepdims=True)
    pick_two = jnp.sum(jnp.where(lane == route[:, 1:2], soft, 0.0), axis=-1, keepdims=True)
    both = pick_one + pick_two
    live = (iota((PAD, 1), 0) < IMG_TOK) & (pl.program_id(0) < count_ref[0])
    alive = jnp.where(live, 1.0, 0.0)
    sum_ref[0] += jnp.broadcast_to(jnp.sum(soft * alive, axis=0, keepdims=True), (8, 128))
    soft = jnp.where(lane == EXPERTS + 4, pick_one / both, soft)
    soft = jnp.where(lane == EXPERTS + 5, pick_two / both, soft)
    soft_ref[0] = soft
    gates = jnp.transpose(soft)[EXPERTS : EXPERTS + 8]
    line = iota((8, PAD), 0)
    meta = jnp.where((line == 4) | (line == 5), gates, ids_ref[0])
    meta = jnp.concatenate([meta, jnp.zeros((8, width - PAD), F32)], axis=1)
    second_ref[0] = jnp.concatenate([second[: PAD - 8], meta], axis=0).astype(BF16)


def front(count, tok, ids, routes, wide, tall, traffic, ident):
    images, _, width = tok.shape
    shape = jax.ShapeDtypeStruct
    return run(
        front_body,
        (count, tok, ids, routes, *wide, *tall),
        [scalar_spec(), by_image(PAD, width), by_image(8, PAD), by_image(PAD, 2)]
        + [resident(wide[0].shape)] * 2
        + [resident(tall[0].shape)] * 2,
        [
            by_image(PAD, 3 * width),
            by_image(HEADS, PAD, PAD),
            by_image(PAD, width),
            by_image(PAD, width),
            by_image(PAD, width),
            by_image(PAD, 128),
            resident((1, 8, 128)),
        ],
        [
            shape((images, PAD, 3 * width), BF16),
            shape((images, HEADS, PAD, PAD), BF16),
            shape((images, PAD, width), BF16),
            shape((images, PAD, width), F32),
            shape((images, PAD, width), BF16),
            shape((images, PAD, 128), F32),
            shape((1, 8, 128), F32),
        ],
        grid=(images,),
        scratch=[pltpu.VMEM((2,) + wide[0].shape, BF16), pltpu.VMEM((2,) + tall[0].shape, BF16)],
        cost=pl.CostEstimate(flops=6_000_000_000, bytes_accessed=16_000_000, transcendentals=2_000_000),
        name="front",
        traffic=traffic,
        ident=ident,
    )


def slot_lines(meta):
    return meta[0:1] * CAP + meta[1:2], meta[2:3] * CAP + meta[3:4]


def gather(base, experts, senders, sequence, traffic, ident, chain=None):
    arrays, table = [], []
    for sender in sequence:
        if sender is None:
            table.append(None)
            continue
        for kind in range(2):
            spots = []
            for array, target, position in senders[sender][kind]:
                at = target
                if array is not None:
                    at = next((k for k, known in enumerate(arrays) if known is array), len(arrays))
                    if at == len(arrays):
                        arrays.append(array)
                spots.append((array is None, at, position))
            table.append((sender, kind, spots))
    images, width = len(table[0][2]), arrays[0].shape[-1]
    tokens, slots, count, steps = images * PAD, experts * CAP, len(senders), len(table)
    first = [next(k for k, entry in enumerate(table) if entry and entry[0] == sender) for sender in range(count)]

    def hook(step, require, targets, ins, held):
        sources, rows, loaded = ins[1:], held[0], held[2]

        def copies(entry):
            _, kind, spots = entry
            return [
                pltpu.make_async_copy(
                    (targets if arriving else sources)[at].at[position],
                    rows.at[kind, pl.ds(image * PAD, PAD)],
                    loaded.at[kind, image],
                )
                for image, (arriving, at, position) in enumerate(spots)
            ]

        def load(entry):
            for arriving, at, position in entry[2]:
                if arriving:
                    require(at, position)
            for copy in copies(entry):
                copy.start()

        if step == 0:
            load(table[0])
        if step + 1 < steps and table[step + 1]:
            load(table[step + 1])
        if table[step]:
            for copy in copies(table[step]):
                copy.wait()

    def body(base_ref, *refs):
        row_out, grad_out, rows, lines = refs[len(arrays) : len(arrays) + 4]
        step = pl.program_id(0)
        turns = [(k, entry[1]) for k, entry in enumerate(table) if entry]
        working, gated = step < 0, step < 0
        for k, kind in turns:
            working = working | (step == k)
            if kind:
                gated = gated | (step == k)

        @pl.when(working & ~gated)
        def _():
            for image in range(images):
                lines[image] = rows[0, image * PAD + PAD - 16 : (image + 1) * PAD, :PAD].astype(F32)[8:]

        @pl.when(working)
        def _():
            meta = jnp.concatenate([lines[image] for image in range(images)], axis=1)
            one, two = slot_lines(meta)
            weight_one = jnp.where(gated, meta[4:5], 1.0)
            weight_two = jnp.where(gated, meta[5:6], 1.0)
            slot = (iota((slots, tokens), 0) + base_ref[0]).astype(F32)
            pick = jnp.where(slot == one, weight_one, 0.0) + jnp.where(slot == two, weight_two, 0.0)
            got = dot(pick.astype(BF16), rows[jnp.where(gated, 1, 0)])
            got = got.astype(BF16).reshape(experts, 1, CAP, width)

            @pl.when(~gated)
            def _():
                row_out[...] = got

            @pl.when(gated)
            def _():
                grad_out[...] = got

    def place(d):
        turn = 0
        for at in first[1:]:
            turn += jnp.where(d >= at, 1, 0)
        return (0, turn, 0, 0)

    shape = jax.ShapeDtypeStruct((experts, count, CAP, width), BF16)
    return run(
        body,
        (base, *arrays),
        [scalar_spec()] + [pl.BlockSpec(memory_space=pl.ANY)] * len(arrays),
        [pl.BlockSpec((experts, 1, CAP, width), place)] * 2,
        [shape, shape],
        grid=(steps,),
        scratch=[
            pltpu.VMEM((2, tokens, width), BF16),
            pltpu.VMEM((images, 8, PAD), F32),
            pltpu.SemaphoreType.DMA((2, images)),
        ],
        cost=pl.CostEstimate(
            flops=4 * count * slots * tokens * width,
            bytes_accessed=4 * count * (tokens + slots) * width,
            transcendentals=0,
        ),
        name="gather",
        traffic=traffic,
        chain=chain,
        hook=hook,
        ident=ident,
    )


def own_line(ref):
    table = ref[...].astype(F32)
    return jnp.sum(jnp.where(iota(table.shape, 0) == pl.program_id(0), table, 0.0), axis=0, keepdims=True)


def expert_body(row_own, row_far, grad_own, grad_far, in_ref, in_bias_ref, out_ref, out_bias_ref, made_own, made_far, back_own, back_far):
    cap, width = row_own.shape[2:]
    hidden = in_ref.shape[2]
    rows = jnp.concatenate([row_own[0, 0], row_far[0, 0]], axis=0)
    grads = jnp.concatenate([grad_own[0, 0], grad_far[0, 0]], axis=0)
    in_bias = own_line(in_bias_ref)
    made = jnp.zeros((2 * cap, width), F32)
    back = jnp.zeros((2 * cap, width), F32)
    chunk = 512
    for at in range(0, hidden, chunk):
        first = in_ref[0, :, at : at + chunk]
        second = out_ref[0, at : at + chunk, :]
        raised = dot(rows, first) + in_bias[:, at : at + chunk]
        active, slope = gelu_pair(raised)
        made += dot(active.astype(BF16), second)
        draised = (dot_cols(grads, second) * slope).astype(BF16)
        back += dot_cols(draised, first)
    made = (made + own_line(out_bias_ref)).astype(BF16)
    back = back.astype(BF16)
    made_own[0], made_far[0] = made[:cap], made[cap:]
    back_own[0], back_far[0] = back[:cap], back[cap:]


def expert_layer(pair, first, first_bias, second, second_bias, chain, traffic, ident):
    experts, _, cap, width = pair[0].shape
    hidden = first.shape[2]
    rows = [pl.BlockSpec((1, 1, cap, width), lambda e, side=side: (e, side, 0, 0)) for side in range(2)]
    out = pl.BlockSpec((1, cap, width), lambda e: (e, 0, 0))
    return run(
        expert_body,
        (
            pair[0],
            pair[0],
            pair[1],
            pair[1],
            first,
            first_bias,
            second,
            second_bias,
        ),
        rows + rows + [by_image(width, hidden), resident(first_bias.shape), by_image(hidden, width), resident(second_bias.shape)],
        [out] * 4,
        [jax.ShapeDtypeStruct((experts, cap, width), BF16)] * 4,
        grid=(experts,),
        cost=pl.CostEstimate(
            flops=16 * experts * cap * width * hidden,
            bytes_accessed=4 * experts * width * hidden,
            transcendentals=2 * experts * cap * hidden,
        ),
        name="expert_layer",
        traffic=traffic,
        chain=chain,
        ident=ident,
    )


def combine_body(base_ref, rows, cot, made_ref, back_ref, sum_ref, row_ref, gate_ref):
    experts, cap, width = made_ref.shape
    slots = experts * cap
    meta = jnp.transpose(rows[PAD - 16 :, :PAD].astype(F32)[8:])
    slot = (iota((PAD, slots), 1) + base_ref[0]).astype(F32)
    one = jnp.where(slot == meta[:, 0:1] * CAP + meta[:, 1:2], 1.0, 0.0).astype(BF16)
    two = jnp.where(slot == meta[:, 2:3] * CAP + meta[:, 3:4], 1.0, 0.0).astype(BF16)
    made = made_ref[...].reshape(slots, width)
    made_one = dot(one, made)
    made_two = dot(two, made)
    sum_ref[0] = (meta[:, 4:5] * made_one + meta[:, 5:6] * made_two).astype(BF16)
    row_ref[0] = dot(one + two, back_ref[...].reshape(slots, width)).astype(BF16)
    cot = cot.astype(F32)
    grad_one = jnp.sum(cot * made_one, axis=1, keepdims=True)
    grad_two = jnp.sum(cot * made_two, axis=1, keepdims=True)
    lane = iota((PAD, 128), 1)
    wide = jnp.where(lane == 0, grad_one, jnp.where(lane == 1, grad_two, 0.0))
    gate_ref[0] = jnp.transpose(wide)[0:8]


def by_piece(pieces, *shape):
    arrays, first = [], []
    for image, (array, position) in enumerate(pieces):
        if not arrays or arrays[-1] is not array:
            arrays.append(array)
            first.append((image, position))
    specs = []
    for array, (image, position) in zip(arrays, first):

        def index(i, *_, image=image, position=position, last=array.shape[0] - 1):
            return (jnp.clip(i - image + position, 0, last),) + (0,) * len(shape)

        specs.append(pl.BlockSpec((1,) + shape, index))

    def read(refs):
        value = refs[0][0]
        for ref, (image, _) in zip(refs[1:], first[1:]):
            value = jnp.where(pl.program_id(0) >= image, ref[0], value)
        return value

    return arrays, specs, read


def combine(base, rows, cots, made, back, traffic, ident):
    width = made.shape[-1]
    images = len(rows)
    experts, cap, _ = made.shape
    row_arrays, row_specs, read_rows = by_piece(rows, PAD, width)
    cot_arrays, cot_specs, read_cots = by_piece(cots, PAD, width)
    split = len(row_arrays)

    def body(base_ref, made_ref, back_ref, *refs):
        inputs, outs = refs[: split + len(cot_arrays)], refs[split + len(cot_arrays) :]
        combine_body(base_ref, read_rows(inputs[:split]), read_cots(inputs[split:]), made_ref, back_ref, *outs)

    return run(
        body,
        (base, made, back, *row_arrays, *cot_arrays),
        [scalar_spec(), resident(made.shape), resident(back.shape), *row_specs, *cot_specs],
        [by_image(PAD, width), by_image(PAD, width), by_image(8, PAD)],
        [
            jax.ShapeDtypeStruct((images, PAD, width), BF16),
            jax.ShapeDtypeStruct((images, PAD, width), BF16),
            jax.ShapeDtypeStruct((images, 8, PAD), F32),
        ],
        grid=(images,),
        cost=pl.CostEstimate(
            flops=6 * images * PAD * experts * cap * width, bytes_accessed=6_000_000, transcendentals=0
        ),
        name="combine",
        traffic=traffic,
        ident=ident,
    )


def norm_back(grads, hat, scale, gain):
    scaled = grads * gain
    inner = jnp.mean(scaled * hat, axis=-1, keepdims=True)
    return scale * (scaled - jnp.mean(scaled, axis=-1, keepdims=True) - hat * inner)


def column_sum(values):
    return jnp.sum(values, axis=0, keepdims=True)


def finish_body(
    count_ref, tok_ref, cot_ref, packed_ref, prob_ref, mixed_ref, middle_ref, second_ref, soft_ref, route_ref,
    row_own, row_far, gate_own, gate_far, aux_ref,
    wide_own, wide_far, tall_own, tall_far, dtok_ref, pack_ref, loss_ref,
    dpacked, wide_ref, tall_ref, dqkv_ref, dout_ref, drouter_ref, dvec_ref,
):
    image = pl.program_id(0)
    width = tok_ref.shape[-1]

    @pl.when(image == 0)
    def _():
        place_halves(wide_own, wide_far, wide_ref)
        place_halves(tall_own, tall_far, tall_ref)

    vec = vectors(wide_ref)
    images = dtok_ref.shape[0] // IMG_TOK

    @pl.when(image == 0)
    def _():
        for ref in (dqkv_ref, dout_ref, drouter_ref, dvec_ref):
            ref[...] = jnp.zeros_like(ref)

    real = iota((PAD, 1), 0) < IMG_TOK
    alive = jnp.where(real & (image < count_ref[0]), 1.0, 0.0)
    middle = middle_ref[0]
    upstream = cot_ref[0].astype(F32)
    soft = soft_ref[0]
    route = route_ref[0]
    lane = iota((PAD, 128), 1)
    gate_grads = jnp.transpose(gate_own[0] + gate_far)
    push = (gate_grads[:, 0:1] - gate_grads[:, 1:2]) * soft[:, EXPERTS + 4 : EXPERTS + 5] * soft[:, EXPERTS + 5 : EXPERTS + 6]
    soft = jnp.where(lane < EXPERTS, soft, 0.0)
    loads = aux_ref[0]
    lanes = iota(loads.shape, 1)
    live = jnp.sum(jnp.where(lanes == 2 * EXPERTS, loads, 0.0), axis=1, keepdims=True)
    share = (loads + pltpu.roll(loads, 128 - EXPERTS, 1)) / (2.0 * live)
    push_all = jnp.where(lanes < EXPERTS, EXPERTS * share / live, 0.0)
    loss = jnp.sum(push_all * aux_ref[1], axis=1, keepdims=True)
    loss_ref[...] = jnp.broadcast_to(loss, loads.shape)
    aux = push_all[0:1] * alive
    dlogits = soft * (aux - jnp.sum(soft * aux, axis=-1, keepdims=True))
    dlogits += jnp.where(lane == route[:, 0:1], push, 0.0) - jnp.where(lane == route[:, 1:2], push, 0.0)
    dlogits = dlogits.astype(BF16)
    second = second_ref[0]
    router = tall_ref[:, :, width : width + 128].reshape(width, 128)
    drouter_ref[...] += dot_rows(second, dlogits)
    dsecond = dot_cols(dlogits, router) + (row_own[0].astype(F32) + row_far.astype(F32))
    hat, scale = standardise(middle)
    dmiddle = upstream + norm_back(dsecond, hat, scale, vec[5:6])
    dattn = dmiddle.astype(BF16)
    dvec_ref[EXPERTS + 4 : EXPERTS + 5] += column_sum(dattn.astype(F32))
    dvec_ref[EXPERTS + 5 : EXPERTS + 6] += column_sum(dsecond * hat)
    dvec_ref[EXPERTS + 6 : EXPERTS + 7] += column_sum(dsecond)
    dout_ref[...] += dot_rows(mixed_ref[0], dattn)
    out_full = tall_ref[:, :, :width].reshape(width, width)
    dmixed = dot_cols(dattn, out_full).astype(BF16)
    low_lanes = iota((PAD, 128), 1) < HEAD_DIM
    root = HEAD_DIM**-0.5
    for pair in range(HEADS // 2):
        at = pair * 128
        query = packed_ref[0, :, at : at + 128]
        keys = packed_ref[0, :, width + at : width + at + 128]
        valued = packed_ref[0, :, 2 * width + at : 2 * width + at + 128]
        grads = dmixed[:, at : at + 128]
        parts = []
        for side in range(2):
            own = low_lanes if side == 0 else ~low_lanes
            weights = prob_ref[0, 2 * pair + side]
            dweights = dot_cols(jnp.where(own, grads, jnp.zeros_like(grads)), valued)
            exact = weights.astype(F32)
            inner = jnp.sum(dweights * exact, axis=-1, keepdims=True)
            dscores = (exact * (dweights - inner)).astype(BF16)
            parts.append((dot(dscores, keys), dot_rows(dscores, query), dot_rows(weights, grads)))
        for third, factor in ((0, root), (1, root), (2, 1.0)):
            both = jnp.where(low_lanes, parts[0][third], parts[1][third]) * factor
            dpacked[:, third * width + at : third * width + at + 128] = both.astype(BF16)
    inputs = tok_ref[0].astype(F32)
    hat, scale = standardise(inputs)
    normed = (hat * vec[0:1] + vec[1:2]).astype(BF16)
    packed_grads = dpacked[...]
    dqkv_ref[...] += dot_rows(normed, packed_grads)
    dvec_ref[EXPERTS + 2 : EXPERTS + 3] += column_sum(packed_grads[:, :width].astype(F32))
    dvec_ref[EXPERTS + 3 : EXPERTS + 4] += column_sum(packed_grads[:, 2 * width :].astype(F32))
    qkv = wide_ref[:, :256, :].reshape(width, 3 * width)
    dnormed = dot_cols(packed_grads, qkv)
    dvec_ref[EXPERTS + 0 : EXPERTS + 1] += column_sum(dnormed * hat)
    dvec_ref[EXPERTS + 1 : EXPERTS + 2] += column_sum(dnormed)
    dtokens = dmiddle + norm_back(dnormed, hat, scale, vec[0:1])
    for k in range(images):

        @pl.when(image == k)
        def _():
            dtok_ref[pl.ds(k * IMG_TOK, IMG_TOK), :] = dtokens[:IMG_TOK]

    @pl.when(image == images - 1)
    def _():
        lines = jnp.transpose(dvec_ref[...])
        part = width // 8
        for owner in range(2):
            for half in range(2):
                for quarter in range(2):
                    at = ((owner * 2 + half) * 2 + quarter) * part
                    rows = slice(at, at + part)
                    spot = pack_ref.at[owner, half, quarter]
                    spot[:, : 3 * width] = dqkv_ref[rows].astype(BF16)
                    spot[:, 3 * width : 4 * width] = dout_ref[rows].astype(BF16)
                    spot[:, 4 * width :] = (drouter_ref[rows] + lines[rows]).astype(BF16)


def finish(count, tok, cot, saved, routes, row_own, row_far, gate_own, gate_far, aux, wide, tall, total, traffic, ident):
    images, _, width = tok.shape
    packed, prob, mixed, middle, second, soft = saved
    shape = jax.ShapeDtypeStruct
    tile = by_image(PAD, width)
    row_arrays = []
    for array, _, _ in row_far:
        if array is not None and not any(known is array for known in row_arrays):
            row_arrays.append(array)
    gate_arrays, gate_specs, read_gates = by_piece(gate_far, 8, PAD)
    lead, extra = len(row_arrays), len(row_arrays) + len(gate_arrays)

    def hook(step, require, targets, ins, held):
        array, target, position = row_far[step]
        if array is None:
            require(target, position)
            source = targets[target]
        else:
            source = next(ref for ref, known in zip(ins, row_arrays) if known is array)
        copy = pltpu.make_async_copy(source.at[position], held[-2], held[-1])
        copy.start()
        copy.wait()

    def body(*refs):
        pieces, far, refs = refs[:extra], refs[-2], list(refs[extra:-2])
        refs[11:11] = [far[...]]
        refs[13:13] = [read_gates(pieces[lead:])]
        finish_body(*refs)

    pack = (2, 2, 2, width // 8, 4 * width + 128)
    return run(
        body,
        (
            *row_arrays, *gate_arrays, count, tok, cot, packed, prob, mixed, middle, second, soft, routes,
            row_own, gate_own, aux, *wide, *tall,
        ),
        [
            *[pl.BlockSpec(memory_space=pl.ANY)] * lead,
            *gate_specs,
            scalar_spec(),
            tile,
            tile,
            by_image(PAD, 3 * width),
            by_image(HEADS, PAD, PAD),
            tile,
            tile,
            tile,
            by_image(PAD, 128),
            by_image(PAD, 2),
            tile,
            by_image(8, PAD),
            resident((2, 8, 128)),
            resident(wide[0].shape),
            resident(wide[0].shape),
            resident(tall[0].shape),
            resident(tall[0].shape),
        ],
        [resident((total, width)), resident(pack), resident((8, 128))],
        [shape((total, width), F32), shape(pack, BF16), shape((8, 128), F32)],
        grid=(images,),
        scratch=[
            pltpu.VMEM((PAD, 3 * width), BF16),
            pltpu.VMEM((2,) + wide[0].shape, BF16),
            pltpu.VMEM((2,) + tall[0].shape, BF16),
            pltpu.VMEM((width, 3 * width), F32),
            pltpu.VMEM((width, width), F32),
            pltpu.VMEM((width, 128), F32),
            pltpu.VMEM((128, width), F32),
            pltpu.VMEM((PAD, width), BF16),
            pltpu.SemaphoreType.DMA,
        ],
        cost=pl.CostEstimate(flops=12_000_000_000, bytes_accessed=24_000_000, transcendentals=0),
        name="finish",
        traffic=traffic,
        hook=hook,
        ident=ident,
    )


def add(left, right):
    return (left.astype(F32) + right.astype(F32)).astype(BF16)


class Exchange:
    def __init__(self, send, recv):
        self.send, self.recv = send, recv

    def at(self, index, link, source, target):
        move = Move(link, lambda _: source, lambda _: target)
        return move.roles(), move.copy(None, self.send.at[index], self.recv.at[index])


def begin(make):
    roles, copy = make()
    only_if(roles[0], copy.start)


def end(make):
    roles, copy = make()
    only_if(roles[0], copy.wait_send)
    only_if(roles[1], copy.wait_recv)


def sums_everywhere(load, soft_sum, steps):
    shape = (2,) + load.shape[1:]
    links = ("core", "y", "x", "near", "inner", "outward")

    def copies(load_ref, soft_ref, total, held, got, send, recv):
        made = Exchange(send, recv)
        return [
            lambda k=k, link=link: made.at(k, link, held.at[k], held.at[k] if link == "outward" else got.at[k])
            for k, link in enumerate(links)
        ]

    def first(*refs):
        load_ref, soft_ref, _, held = refs[:4]
        held[0, 0], held[0, 1] = load_ref[0], soft_ref[0]
        begin(copies(*refs)[0])

    def stage(k):
        def action(*refs):
            held, got = refs[3:5]
            end(copies(*refs)[k - 1])
            if links[k] == "outward":

                @pl.when(((lax.axis_index("rep") // 4) % 3) > 0)
                def _():
                    held[k] = held[k - 1] + got[k - 1]

            else:
                held[k] = held[k - 1] + got[k - 1]
            begin(copies(*refs)[k])

        return action

    def last(*refs):
        end(copies(*refs)[5])
        refs[2][...] = refs[3][5]

    return Chain(
        [load, soft_sum],
        [resident(load.shape)] * 2,
        [resident(shape)],
        [jax.ShapeDtypeStruct(shape, F32)],
        [pltpu.VMEM((6,) + shape, F32), pltpu.VMEM((5,) + shape, F32)] + [pltpu.SemaphoreType.DMA((6,))] * 2,
        {"core", "y", "x", "near", "inner"},
        list(zip(steps, [first] + [stage(k) for k in range(1, 6)])) + [(0, last)],
    )


def owner_sums(pack, steps):
    shape = pack.shape[2:]

    def first(pack_ref, part, near_in, half, far_in, send, recv):
        core = lax.axis_index("rep") % 2
        Exchange(send, recv).at(0, "core", pack_ref.at[:, 1 - core], near_in)[1].start()

    def second(pack_ref, part, near_in, half, far_in, send, recv):
        core, mine = lax.axis_index("rep") % 2, lax.axis_index("fsdp")
        Exchange(send, recv).at(0, "core", pack_ref.at[:, 1 - core], near_in)[1].wait()
        half[...] = add(pack_ref[:, core], near_in[...])
        Exchange(send, recv).at(1, "y", half.at[1 - mine], far_in)[1].start()

    def last(pack_ref, part, near_in, half, far_in, send, recv):
        mine = lax.axis_index("fsdp")
        Exchange(send, recv).at(1, "y", half.at[1 - mine], far_in)[1].wait()
        part[...] = add(half[mine], far_in[...])

    return Chain(
        [pack],
        [pl.BlockSpec(pack.shape, lambda *_: (0,) * 5, pipeline_mode=pl.Buffered(1))],
        [resident(shape)],
        [jax.ShapeDtypeStruct(shape, BF16)],
        [pltpu.VMEM((2,) + shape, BF16), pltpu.VMEM((2,) + shape, BF16), pltpu.VMEM(shape, BF16)]
        + [pltpu.SemaphoreType.DMA((2,))] * 2,
        {"core", "y"},
        [(steps[0], first), (steps[1], second), (0, last)],
    )


def copy_sums(part, steps):
    shape = part.shape[1:]

    def copies(part_ref, total, x_in, held, near_in, line, inner_in, full, send, recv):
        device = lax.axis_index("rep")
        core, side = device % 2, (device // 2) % 2
        made = Exchange(send, recv)
        mine = full.at[core, side]
        plans = [
            ("x", part_ref.at[1 - side], x_in),
            ("near", held, near_in),
            ("inner", line, inner_in),
            ("outward", mine, mine),
            ("x", mine, mine),
            ("core", full.at[core], full.at[core]),
        ]
        return [lambda k=k, plan=plan: made.at(k, *plan) for k, plan in enumerate(plans)]

    def first(*refs):
        begin(copies(*refs)[0])

    def second(*refs):
        part_ref, total, x_in, held = refs[:4]
        steps = copies(*refs)
        end(steps[0])
        side = (lax.axis_index("rep") // 2) % 2
        held[...] = add(part_ref[side], x_in[...])
        begin(steps[1])

    def third(*refs):
        part_ref, total, x_in, held, near_in, line = refs[:6]
        steps = copies(*refs)
        end(steps[1])
        line[...] = add(held[...], near_in[...])
        begin(steps[2])

    def fourth(*refs):
        part_ref, total, x_in, held, near_in, line, inner_in, full = refs[:8]
        steps = copies(*refs)
        device = lax.axis_index("rep")
        middle = ((device // 4) % 3) > 0
        end(steps[2])

        @pl.when(middle)
        def _():
            full[device % 2, (device // 2) % 2] = add(line[...], inner_in[...])

        begin(steps[3])

    def fifth(*refs):
        steps = copies(*refs)
        end(steps[3])
        begin(steps[4])

    def sixth(*refs):
        steps = copies(*refs)
        end(steps[4])
        begin(steps[5])

    def last(*refs):
        total, full = refs[1], refs[7]
        end(copies(*refs)[5])
        total[...] = full[...]

    whole = (2, 2) + shape
    return Chain(
        [part],
        [resident(part.shape)],
        [resident(whole)],
        [jax.ShapeDtypeStruct(whole, BF16)],
        [pltpu.VMEM(shape, BF16)] * 5 + [pltpu.VMEM(whole, BF16)] + [pltpu.SemaphoreType.DMA((6,))] * 2,
        {"core", "x", "near", "inner"},
        list(zip(steps, (first, second, third, fourth, fifth, sixth))) + [(0, last)],
    )


def emit(count, middle, sum_own, sum_far, total):
    images, _, width = middle.shape
    far_arrays, far_specs, read_far = by_piece(sum_far, PAD, width)

    def body(count_ref, middle_ref, own_ref, *refs):
        far, (out_ref, held) = refs[:-2], refs[-2:]
        image = pl.program_id(0)
        live = (iota((PAD, 1), 0) < IMG_TOK) & (image < count_ref[0])
        both = own_ref[0].astype(F32) + read_far(far).astype(F32)
        result = jnp.where(live, 1.0, 0.0) * (middle_ref[0] + both)
        for k in range(images):

            @pl.when(image == k)
            def _():
                held[pl.ds(k * IMG_TOK, IMG_TOK), :] = result[:IMG_TOK]

        @pl.when(image == images - 1)
        def _():
            out_ref[...] = held[pl.ds(0, total), :].astype(BF16)

    tile = by_image(PAD, width)
    return run(
        body,
        (count, middle, sum_own, *far_arrays),
        [scalar_spec(), tile, tile, *far_specs],
        [resident((total, width))],
        [jax.ShapeDtypeStruct((total, width), BF16)],
        grid=(images,),
        scratch=[pltpu.VMEM((1000, width), F32)],
        cost=pl.CostEstimate(flops=2_000_000, bytes_accessed=6_000_000, transcendentals=0),
        name="emit",
    )[0][0]


def by_slice(
    tokens, cotangent, routes, image_count, capacity, norm1_gain, norm1_bias, w_qkv, bias_q, bias_v, w_out, bias_out,
    norm2_gain, norm2_bias, w_router, expert_in, expert_in_bias, expert_out, expert_out_bias,
):
    total, width = tokens.shape
    local = expert_in.shape[0]
    device = lax.axis_index("rep")
    mine = lax.axis_index("fsdp")
    core = device % 2
    wide, tall = pack_weights(
        (norm1_gain, norm1_bias, bias_q, bias_v, bias_out, norm2_gain, norm2_bias), w_qkv, w_out, w_router
    )
    (tok, cot, route, ids, load), (wide_far, tall_far), _ = prepare(
        tokens, cotangent, routes, image_count, capacity, wide, tall, 0
    )
    wide, tall = (wide, wide_far), (tall, tall_far)
    base = (mine * (local * CAP)).reshape(1)
    net = Network()
    net.offer("C", cot, COT_PATHS)
    idents = iter(range(1, 32))

    def staged(kernel, *args, rounds):
        traffic, plan = net.plan(*rounds)
        args = [arg(plan) if callable(arg) else arg for arg in args]
        outs, arrived, chained = kernel(*args, traffic, next(idents))
        net.land(plan, arrived)
        return (*outs, *chained)

    own, far = (0, 0, 0), (0, 0, 1)
    packed, prob, mixed, middle, second, soft, soft_sum = staged(
        front, image_count, tok, ids, route, wide, tall, rounds=evenly(FRONT_ROOM, 5, 0.68)
    )
    net.offer("S", second, ROW_PATHS)

    def sender(block):
        return net.block("S", block), net.block("C", block)

    def senders(blocks):
        return lambda plan: [(net.find(plan, "S", block), net.find(plan, "C", block)) for block in blocks]

    pair = staged(
        gather, base, local, senders([own, far]), [0, None, None, None, None, 1],
        rounds=(PAIR_ROOM, list(range(8)), [0.0, 0.45, 0.9, 1.9, 2.9, 3.9, 5.0, 6.0]),
    )
    made_own, made_far, back_own, back_far, sums = staged(
        expert_layer, pair, expert_in, expert_in_bias, expert_out, expert_out_bias,
        sums_everywhere(load, soft_sum, (0, 2, 5, 8, 11, 13)),
        rounds=evenly(EXPERT_ROOM, 16, 0.7, 2),
    )
    sum_far, drow_far, dgate_far = staged(
        combine, base, *sender(far), made_far, back_far, rounds=evenly(2, 5, 0.4, 2)
    )
    net.offer("D", drow_far, FAR_FIRST)
    net.offer("G", dgate_far, FAR_FIRST, 0)
    net.offer("M", sum_far, FAR_LAST)
    sum_own, drow_own, dgate_own = staged(
        combine, base, *sender(own), made_own, back_own, rounds=evenly(OWN_ROOM, 5, 0.4)
    )
    grad_tokens, pack, loss = staged(
        finish, image_count, tok, cot, (packed, prob, mixed, middle, second, soft), route, drow_own,
        lambda plan: net.find(plan, "D", far), dgate_own, net.block("G", far), sums, wide, tall, total,
        rounds=evenly(FINISH_ROOM, 5, 1.5),
    )
    blocks = [block for block in COT_PATHS if block != far]
    count = 2 * len(blocks) + 2
    traffic, plan = net.plan(LAST_ROOM, list(range(count)), [LAST_ROOM * k / count for k in range(count)])
    blocks.sort(key=lambda block: net.landing(plan, block))
    outs, arrived, (part,) = gather(
        base, local, senders(blocks)(plan), list(range(len(blocks))) + [None, None],
        traffic, next(idents), owner_sums(pack, (0, 6)),
    )
    net.land(plan, arrived)
    slots = [pair, outs]
    outputs = emit(image_count, middle, sum_own, net.block("M", far), total)
    row_slots = [pair[0] for pair in slots]
    grad_slots = [pair[1] for pair in slots]
    (keep_in, send_in, keep_out, send_out, d_bias, d_out_bias), _, (owned,) = slice_grads(
        row_slots, grad_slots, expert_in, expert_in_bias, expert_out, copy_sums(part, (0, 3, 6, 9, 12, 15)), next(idents)
    )
    owned = owned.reshape(width // 2, -1).astype(F32)
    swap = [(i, i ^ 1) for i in range(16)]
    got_in, got_out, got_bias, got_out_bias = (
        lax.ppermute(v, "rep", swap) for v in (send_in, send_out, d_bias, d_out_bias)
    )
    bias = (d_bias + got_bias)[:, 0]
    out_bias = (d_out_bias + got_out_bias)[:, 0]
    half = bias.shape[1] // 2
    piece = width // 16
    expert_grads = (
        keep_in + got_in.astype(F32),
        lax.dynamic_slice_in_dim(bias, core * half, half, axis=1),
        keep_out + got_out.astype(F32),
        lax.dynamic_slice_in_dim(out_bias, device * piece, piece, axis=1),
    )

    balance_loss = loss[0, 0]
    lines = jnp.transpose(owned[:, 4 * width + EXPERTS : 4 * width + EXPERTS + 8])
    owned = (
        lines[0],
        lines[1],
        owned[:, : 3 * width],
        lines[2],
        lines[3],
        owned[:, 3 * width : 4 * width],
        lines[4],
        lines[5],
        lines[6],
        owned[:, 4 * width : 4 * width + EXPERTS],
    )
    return (outputs, grad_tokens, balance_loss) + owned + expert_grads


def solution(mesh):
    in_specs = (
        P(("rep", "fsdp"), None),
        P(("rep", "fsdp"), None),
        P(("rep", "fsdp"), None),
        P(("rep", "fsdp")),
        P(("rep", "fsdp")),
        P("fsdp"),
        P("fsdp"),
        P("fsdp", None),
        P("fsdp"),
        P("fsdp"),
        P("fsdp", None),
        P("fsdp"),
        P("fsdp"),
        P("fsdp"),
        P("fsdp", None),
        P("fsdp", None, None),
        P("fsdp", None),
        P("fsdp", None, None),
        P("fsdp", None),
    )
    out_specs = (
        P(("rep", "fsdp"), None),
        P(("rep", "fsdp"), None),
        P(),
        P("fsdp"),
        P("fsdp"),
        P("fsdp", None),
        P("fsdp"),
        P("fsdp"),
        P("fsdp", None),
        P("fsdp"),
        P("fsdp"),
        P("fsdp"),
        P("fsdp", None),
        P("fsdp", None, "rep"),
        P("fsdp", "rep"),
        P("fsdp", "rep", None),
        P("fsdp", "rep"),
    )
    program = by_slice if mesh.shape["rep"] == 16 and mesh.shape["fsdp"] == 2 else shards
    return jax.shard_map(program, mesh=mesh, in_specs=in_specs, out_specs=out_specs, check_vma=False)
```

```python
import jax
import jax.numpy as jnp
from jax import lax
from jax.experimental import pallas as pl
from jax.experimental.pallas import tpu as pltpu
from jax.sharding import PartitionSpec as P

HEADS = 8
HEAD_DIM = 64
EXPERTS = 32
IMG_TOK = 197
CAP = 80


def norm_rows(values, norm_gain, offset):
    average = jnp.mean(values, axis=-1, keepdims=True)
    centred = values - average
    variance = jnp.mean(centred * centred, axis=-1, keepdims=True)
    return centred * lax.rsqrt(variance + 1e-06) * norm_gain + offset


def slot_table(choices, alive_mask, limit, row_total):
    pair_expert = jnp.concatenate([choices[:, 0], choices[:, 1]])
    live_pairs = jnp.concatenate([alive_mask, alive_mask])
    expert_ids = jnp.arange(EXPERTS, dtype=jnp.int32)
    onehot = ((pair_expert[:, None] == expert_ids[None, :]) & live_pairs[:, None]).astype(jnp.int32)
    before = jnp.cumsum(onehot, axis=0) - onehot
    position = jnp.sum(before * onehot, axis=1)
    kept_pairs = live_pairs & (position < limit)
    pair_slot = pair_expert * CAP + position
    pair_token = jnp.concatenate(
        [jnp.arange(row_total, dtype=jnp.int32), jnp.arange(row_total, dtype=jnp.int32)]
    )
    slot_owner = jnp.full((EXPERTS * CAP,), row_total, jnp.int32)
    target = jnp.where(kept_pairs, pair_slot, EXPERTS * CAP)
    slot_owner = slot_owner.at[target].set(pair_token, mode="drop")
    safe_slot = jnp.where(kept_pairs, pair_slot, 0)
    return (slot_owner, kept_pairs, safe_slot, target, onehot)


def shards(
    tokens,
    cotangent,
    routes,
    image_count,
    capacity,
    norm1_gain,
    norm1_bias,
    w_qkv,
    bias_q,
    bias_v,
    w_out,
    bias_out,
    norm2_gain,
    norm2_bias,
    w_router,
    expert_in,
    expert_in_bias,
    expert_out,
    expert_out_bias,
):
    rows_count = tokens.shape[0]
    model_width = tokens.shape[1]
    image_total = rows_count // IMG_TOK
    score_scale = HEAD_DIM ** (-0.5)
    image_rows = jnp.arange(rows_count, dtype=jnp.int32) // IMG_TOK
    alive_mask = image_rows < image_count[0]
    alive_float = alive_mask.astype(jnp.float32)[:, None]
    slot_owner, kept_pairs, safe_slot, target, onehot = slot_table(
        routes, alive_mask, capacity[0], rows_count
    )
    kept_float = kept_pairs.astype(jnp.float32)
    load_local = jnp.sum(onehot.astype(jnp.float32), axis=0)
    live_local = jnp.sum(alive_float)
    load_total, live_total = lax.psum((load_local, live_local), ("rep", "fsdp"))
    gathered = (
        lax.all_gather(norm1_gain, "fsdp", axis=0, tiled=True),
        lax.all_gather(norm1_bias, "fsdp", axis=0, tiled=True),
        lax.all_gather(w_qkv, "fsdp", axis=0, tiled=True),
        lax.all_gather(bias_q, "fsdp", axis=0, tiled=True),
        lax.all_gather(bias_v, "fsdp", axis=0, tiled=True),
        lax.all_gather(w_out, "fsdp", axis=0, tiled=True),
        lax.all_gather(bias_out, "fsdp", axis=0, tiled=True),
        lax.all_gather(norm2_gain, "fsdp", axis=0, tiled=True),
        lax.all_gather(norm2_bias, "fsdp", axis=0, tiled=True),
        lax.all_gather(w_router, "fsdp", axis=0, tiled=True),
    )
    (
        gain_one,
        shift_one,
        qkv_full,
        query_bias,
        value_bias,
        out_full,
        out_bias,
        gain_two,
        shift_two,
        router_full,
    ) = gathered
    gain_one = gain_one.astype(jnp.float32)
    shift_one = shift_one.astype(jnp.float32)
    gain_two = gain_two.astype(jnp.float32)
    shift_two = shift_two.astype(jnp.float32)
    inputs = tokens.astype(jnp.float32)
    normed = norm_rows(inputs, gain_one, shift_one)
    normed_low = normed.astype(jnp.bfloat16)
    bias_row = jnp.concatenate([query_bias, jnp.zeros_like(query_bias), value_bias]).astype(
        jnp.float32
    )
    packed_low = (
        jnp.dot(normed_low, qkv_full, preferred_element_type=jnp.float32) + bias_row
    ).astype(jnp.bfloat16)
    image_shape = (image_total, IMG_TOK, HEADS, HEAD_DIM)
    queries = packed_low[:, :model_width].reshape(image_shape)
    all_keys = packed_low[:, model_width : 2 * model_width].reshape(image_shape)
    valued = packed_low[:, 2 * model_width :].reshape(image_shape)

    def score_block():
        return (
            jnp.einsum("iqhd,ikhd->hiqk", queries, all_keys, preferred_element_type=jnp.float32)
            * score_scale
        )

    scores = score_block()
    row_peak = jnp.max(scores, axis=-1, keepdims=True)
    exp_scores = jnp.exp(scores - row_peak)
    totals = jnp.sum(exp_scores, axis=-1, keepdims=True)
    log_total = row_peak + jnp.log(totals)
    attn_low = (exp_scores / totals).astype(jnp.bfloat16)
    mixed_low = (
        jnp.einsum("hiqk,ikhd->iqhd", attn_low, valued, preferred_element_type=jnp.float32)
        .reshape(rows_count, model_width)
        .astype(jnp.bfloat16)
    )
    middle = (
        inputs
        + jnp.dot(mixed_low, out_full, preferred_element_type=jnp.float32)
        + out_bias.astype(jnp.float32)
    )
    second_low = norm_rows(middle, gain_two, shift_two).astype(jnp.bfloat16)
    logits = jnp.dot(second_low, router_full, preferred_element_type=jnp.float32)
    expert_ids = jnp.arange(EXPERTS, dtype=jnp.int32)
    first_hot = (routes[:, 0:1] == expert_ids[None, :]).astype(jnp.float32)
    second_hot = (routes[:, 1:2] == expert_ids[None, :]).astype(jnp.float32)

    def gate_terms(logit_rows):
        router_probs = jax.nn.softmax(logit_rows, axis=-1)
        pick_one = jnp.sum(router_probs * first_hot, axis=-1)
        pick_two = jnp.sum(router_probs * second_hot, axis=-1)
        pick_total = pick_one + pick_two
        return (pick_one / pick_total, pick_two / pick_total, router_probs)

    (gate_first, gate_second, router_probs), gate_back = jax.vjp(gate_terms, logits)
    padded_rows = jnp.concatenate([second_low, jnp.zeros((1, model_width), jnp.bfloat16)], axis=0)
    sent_rows = padded_rows[slot_owner].reshape(EXPERTS, CAP, model_width)
    received = lax.all_to_all(sent_rows, "fsdp", split_axis=0, concat_axis=1, tiled=True)
    raised = (
        jnp.einsum("esd,edf->esf", received, expert_in, preferred_element_type=jnp.float32)
        + expert_in_bias.astype(jnp.float32)[:, None, :]
    )
    active, gelu_back = jax.vjp(jax.nn.gelu, raised)
    active_low = active.astype(jnp.bfloat16)
    produced = (
        jnp.einsum("esf,efd->esd", active_low, expert_out, preferred_element_type=jnp.float32)
        + expert_out_bias.astype(jnp.float32)[:, None, :]
    ).astype(jnp.bfloat16)
    returned = lax.all_to_all(produced, "fsdp", split_axis=1, concat_axis=0, tiled=True).reshape(
        EXPERTS * CAP, model_width
    )
    pair_rows = returned[safe_slot].astype(jnp.float32)
    pair_weight = jnp.concatenate([gate_first, gate_second]) * kept_float
    expert_sum = jnp.sum(
        (pair_rows * pair_weight[:, None]).reshape(2, rows_count, model_width), axis=0
    )
    outputs = (alive_float * (middle + expert_sum)).astype(jnp.bfloat16)
    upstream = cotangent.astype(jnp.float32) * alive_float
    pair_grad = jnp.concatenate([upstream, upstream], axis=0)
    gate_grads = jnp.sum(pair_grad * pair_rows, axis=1) * kept_float
    slot_gate = jnp.zeros((EXPERTS * CAP,), jnp.float32).at[target].set(pair_weight, mode="drop")
    padded_grad = jnp.concatenate([upstream, jnp.zeros((1, model_width), jnp.float32)], axis=0)
    slot_grads = (
        (padded_grad[slot_owner] * slot_gate[:, None])
        .astype(jnp.bfloat16)
        .reshape(EXPERTS, CAP, model_width)
    )
    grad_received = lax.all_to_all(slot_grads, "fsdp", split_axis=0, concat_axis=1, tiled=True)
    grad_active = jnp.einsum(
        "esd,efd->esf", grad_received, expert_out, preferred_element_type=jnp.float32
    )
    (grad_raised,) = gelu_back(grad_active)
    grad_raised_low = grad_raised.astype(jnp.bfloat16)
    grad_rows = jnp.einsum(
        "esf,edf->esd", grad_raised_low, expert_in, preferred_element_type=jnp.float32
    ).astype(jnp.bfloat16)
    back_rows = lax.all_to_all(grad_rows, "fsdp", split_axis=1, concat_axis=0, tiled=True).reshape(
        EXPERTS * CAP, model_width
    )
    expert_part = jnp.sum(
        (back_rows[safe_slot].astype(jnp.float32) * kept_float[:, None]).reshape(
            2, rows_count, model_width
        ),
        axis=0,
    )
    local_in = jnp.einsum(
        "esd,esf->edf", received, grad_raised_low, preferred_element_type=jnp.float32
    )
    local_in_bias = jnp.sum(grad_raised_low.astype(jnp.float32), axis=1)
    local_out = jnp.einsum(
        "esf,esd->efd", active_low, grad_received, preferred_element_type=jnp.float32
    )
    local_out_bias = jnp.sum(grad_received.astype(jnp.float32), axis=1)
    grad_in_weight, grad_in_bias, grad_out_weight, grad_out_expert_bias = (
        lax.psum_scatter(local_in, "rep", scatter_dimension=2, tiled=True),
        lax.psum_scatter(local_in_bias, "rep", scatter_dimension=1, tiled=True),
        lax.psum_scatter(local_out, "rep", scatter_dimension=1, tiled=True),
        lax.psum_scatter(local_out_bias, "rep", scatter_dimension=1, tiled=True),
    )
    prob_local = jnp.sum(router_probs * alive_float, axis=0)
    prob_total = lax.psum(prob_local, ("rep", "fsdp"))
    share = load_total / (2.0 * live_total)
    balance_loss = EXPERTS * jnp.sum(share * prob_total / live_total)
    aux_grad = alive_float * (EXPERTS * share / live_total)[None, :]
    (grad_logits,) = gate_back((gate_grads[:rows_count], gate_grads[rows_count:], aux_grad))
    grad_logits_low = grad_logits.astype(jnp.bfloat16)
    grad_router = jnp.dot(second_low.T, grad_logits_low, preferred_element_type=jnp.float32)
    grad_second = (
        jnp.dot(grad_logits_low, router_full.T, preferred_element_type=jnp.float32) + expert_part
    )
    _, norm_two_back = jax.vjp(norm_rows, middle, gain_two, shift_two)
    grad_mid_norm, grad_gain_two, grad_shift_two = norm_two_back(grad_second)
    grad_middle = upstream + grad_mid_norm
    grad_att_low = grad_middle.astype(jnp.bfloat16)
    grad_out_proj = jnp.dot(mixed_low.T, grad_att_low, preferred_element_type=jnp.float32)
    grad_out_bias = jnp.sum(grad_att_low.astype(jnp.float32), axis=0)
    grad_mixed = (
        jnp.dot(grad_att_low, out_full.T, preferred_element_type=jnp.float32)
        .astype(jnp.bfloat16)
        .reshape(image_shape)
    )
    recomputed = jnp.exp(score_block() - log_total)
    grad_weights = jnp.einsum(
        "iqhd,ikhd->hiqk", grad_mixed, valued, preferred_element_type=jnp.float32
    )
    grad_values = jnp.einsum(
        "hiqk,iqhd->ikhd",
        recomputed.astype(jnp.bfloat16),
        grad_mixed,
        preferred_element_type=jnp.float32,
    )
    inner_sum = jnp.sum(grad_weights * recomputed, axis=-1, keepdims=True)
    grad_scores = (recomputed * (grad_weights - inner_sum)).astype(jnp.bfloat16)
    grad_queries = (
        jnp.einsum("hiqk,ikhd->iqhd", grad_scores, all_keys, preferred_element_type=jnp.float32)
        * score_scale
    )
    grad_keys = (
        jnp.einsum("hiqk,iqhd->ikhd", grad_scores, queries, preferred_element_type=jnp.float32)
        * score_scale
    )
    grad_packed_low = jnp.concatenate(
        [
            grad_queries.reshape(rows_count, model_width),
            grad_keys.reshape(rows_count, model_width),
            grad_values.reshape(rows_count, model_width),
        ],
        axis=1,
    ).astype(jnp.bfloat16)
    grad_qkv = jnp.dot(normed_low.T, grad_packed_low, preferred_element_type=jnp.float32)
    packed_sums = jnp.sum(grad_packed_low.astype(jnp.float32), axis=0)
    grad_query_bias = packed_sums[:model_width]
    grad_value_bias = packed_sums[2 * model_width :]
    grad_normed = jnp.dot(grad_packed_low, qkv_full.T, preferred_element_type=jnp.float32)
    _, norm_one_back = jax.vjp(norm_rows, inputs, gain_one, shift_one)
    grad_input_norm, grad_gain_one, grad_shift_one = norm_one_back(grad_normed)
    grad_tokens = grad_middle + grad_input_norm
    local_grads = (
        grad_gain_one,
        grad_shift_one,
        grad_qkv,
        grad_query_bias,
        grad_value_bias,
        grad_out_proj,
        grad_out_bias,
        grad_gain_two,
        grad_shift_two,
        grad_router,
    )
    shares = (
        lax.psum_scatter(local_grads[0], "fsdp", scatter_dimension=0, tiled=True),
        lax.psum_scatter(local_grads[1], "fsdp", scatter_dimension=0, tiled=True),
        lax.psum_scatter(local_grads[2], "fsdp", scatter_dimension=0, tiled=True),
        lax.psum_scatter(local_grads[3], "fsdp", scatter_dimension=0, tiled=True),
        lax.psum_scatter(local_grads[4], "fsdp", scatter_dimension=0, tiled=True),
        lax.psum_scatter(local_grads[5], "fsdp", scatter_dimension=0, tiled=True),
        lax.psum_scatter(local_grads[6], "fsdp", scatter_dimension=0, tiled=True),
        lax.psum_scatter(local_grads[7], "fsdp", scatter_dimension=0, tiled=True),
        lax.psum_scatter(local_grads[8], "fsdp", scatter_dimension=0, tiled=True),
        lax.psum_scatter(local_grads[9], "fsdp", scatter_dimension=0, tiled=True),
    )
    owned = lax.psum(
        (
            shares[0],
            shares[1],
            shares[2],
            shares[3],
            shares[4],
            shares[5],
            shares[6],
            shares[7],
            shares[8],
            shares[9],
        ),
        "rep",
    )
    return (
        (outputs, grad_tokens, balance_loss)
        + tuple(owned)
        + (grad_in_weight, grad_in_bias, grad_out_weight, grad_out_expert_bias)
    )


def gelu_pair(value):
    root = 0.7978845608028654
    square = value * value
    bend = jnp.tanh(root * value * (1.0 + 0.044715 * square))
    half = 0.5 * (1.0 + bend)
    slope = half + 0.5 * value * (1.0 - bend * bend) * root * (1.0 + 3 * 0.044715 * square)
    return value * half, slope


def slice_grads_body(*refs, senders):
    parts, refs = refs[: sum(senders)], refs[sum(senders) :]
    in_ref, in_bias_ref, out_ref, keep_in, send_in, keep_out, send_out, d_bias, d_out_bias = refs
    core = lax.axis_index("rep") % 2
    width = in_ref.shape[1]

    def stacked(pieces):
        return jnp.concatenate([piece[...].reshape(-1, width) for piece in pieces], axis=0)

    rows = stacked(parts[: senders[0]])
    grads = stacked(parts[senders[0] :])
    first = in_ref[0]
    second = out_ref[0]
    raised = jnp.dot(rows, first, preferred_element_type=jnp.float32) + own_line(in_bias_ref)
    active, slope = gelu_pair(raised)
    active = active.astype(jnp.bfloat16)
    back = lax.dot_general(
        grads, second, (((1,), (1,)), ((), ())), preferred_element_type=jnp.float32
    )
    draised = (back * slope).astype(jnp.bfloat16)
    over_rows = (((0,), (0,)), ((), ()))
    g_in = lax.dot_general(rows, draised, over_rows, preferred_element_type=jnp.float32)
    g_out = lax.dot_general(active, grads, over_rows, preferred_element_type=jnp.float32)
    half = g_in.shape[1] // 2
    first_core = core == 0
    keep_in[0] = jnp.where(first_core, g_in[:, :half], g_in[:, half:])
    send_in[0] = jnp.where(first_core, g_in[:, half:], g_in[:, :half]).astype(jnp.bfloat16)
    keep_out[0] = jnp.where(first_core, g_out[:half], g_out[half:])
    send_out[0] = jnp.where(first_core, g_out[half:], g_out[:half]).astype(jnp.bfloat16)
    d_bias[0] = jnp.sum(draised.astype(jnp.float32), axis=0, keepdims=True)
    d_out_bias[0] = jnp.sum(grads.astype(jnp.float32), axis=0, keepdims=True)


def slice_grads(rows, grads, first, first_bias, second, chain, ident):
    experts, width, hidden = first.shape
    cap = rows[0].shape[2]
    slots = cap * sum(piece.shape[1] for piece in rows)
    part = 256
    half = part // 2
    f32 = jnp.float32
    def chip():
        return lax.axis_index("rep") // 2

    return run(
        lambda *refs: slice_grads_body(*refs, senders=(len(rows), len(grads))),
        (*rows, *grads, first, first_bias, second),
        [pl.BlockSpec((1,) + piece.shape[1:], lambda e: (e, 0, 0, 0)) for piece in (*rows, *grads)]
        + [
            pl.BlockSpec((1, width, part), lambda e: (e, 0, chip())),
            pl.BlockSpec((experts, part), lambda e: (0, chip())),
            pl.BlockSpec((1, part, width), lambda e: (e, chip(), 0)),
        ],
        [by_image(width, half)] * 2 + [by_image(half, width)] * 2 + [by_image(1, part), by_image(1, width)],
        [
            jax.ShapeDtypeStruct((experts, width, half), f32),
            jax.ShapeDtypeStruct((experts, width, half), jnp.bfloat16),
            jax.ShapeDtypeStruct((experts, half, width), f32),
            jax.ShapeDtypeStruct((experts, half, width), jnp.bfloat16),
            jax.ShapeDtypeStruct((experts, 1, part), f32),
            jax.ShapeDtypeStruct((experts, 1, width), f32),
        ],
        grid=(experts,),
        cost=pl.CostEstimate(
            flops=8 * experts * slots * width * part,
            bytes_accessed=4 * experts * (slots * width + 3 * width * part),
            transcendentals=experts * slots * part,
        ),
        name="slice_grads",
        chain=chain,
        ident=ident,
    )


F32 = jnp.float32
BF16 = jnp.bfloat16
PAD = 208
ROOT_AXES = ("rep", "fsdp")
OVER_COLS = (((1,), (1,)), ((), ()))
OVER_ROWS = (((0,), (0,)), ((), ()))


def dot(left, right):
    return jnp.dot(left, right, preferred_element_type=F32)


def dot_cols(left, right):
    return lax.dot_general(left, right, OVER_COLS, preferred_element_type=F32)


def dot_rows(left, right):
    return lax.dot_general(left, right, OVER_ROWS, preferred_element_type=F32)


def iota(shape, axis):
    return lax.broadcasted_iota(jnp.int32, shape, axis)


def resident(shape):
    return pl.BlockSpec(shape, lambda *_: (0,) * len(shape))


def by_image(*shape):
    return pl.BlockSpec((1,) + shape, lambda i, *_: (i,) + (0,) * len(shape))


def scalar_spec():
    return pl.BlockSpec(memory_space=pltpu.SMEM)


def partner(link):
    device, side = lax.axis_index("rep"), lax.axis_index("fsdp")
    if link == "y":
        return {"rep": device, "fsdp": 1 - side}
    depth = device // 4
    step = {
        "core": 1 - 2 * (device % 2),
        "x": 2 - 4 * ((device // 2) % 2),
        "near": 4 - 8 * (depth % 2),
        "inner": 12 - 8 * depth,
        "skip": 8 - 16 * (depth // 2),
    }[link]
    return {"rep": device + step, "fsdp": side}


def only_if(condition, action):
    if condition is None:
        action()
    else:
        pl.when(condition)(action)


class Move:
    def __init__(self, link, source, target, needs=()):
        self.link, self.source, self.target, self.needs = link, source, target, needs

    def roles(self):
        depth = lax.axis_index("rep") // 4
        middle = (depth % 3) > 0
        if self.link == "inner":
            return middle, middle
        if self.link in ("outward", "skip"):
            return middle, (depth % 3) == 0
        return None, None

    def copy(self, refs, send, recv):
        return pltpu.make_async_remote_copy(
            src_ref=self.source(refs),
            dst_ref=self.target(refs),
            send_sem=send,
            recv_sem=recv,
            device_id=partner("near" if self.link == "outward" else self.link),
            device_id_type=pl.DeviceIdType.MESH,
        )


class Traffic:
    def __init__(self, sources, targets, rounds, steps):
        self.sources, self.targets, self.rounds, self.steps = sources, targets, rounds, steps

    def count(self):
        return sum(len(moves) for moves in self.rounds)

    def links(self):
        return {("near" if m.link == "outward" else m.link) for moves in self.rounds for m in moves}

    def start(self, which, refs, send, recv, arrived):
        moves = [m for moves in self.rounds for m in moves]
        at = sum(len(moves) for moves in self.rounds[:which])
        for k, move in enumerate(self.rounds[which]):
            for index in move.needs:
                if index not in arrived:
                    arrived.add(index)
                    only_if(moves[index].roles()[1], moves[index].copy(refs, send.at[index], recv.at[index]).wait_recv)
            only_if(move.roles()[0], move.copy(refs, send.at[at + k], recv.at[at + k]).start)

    def require(self, target, position, refs, send, recv, arrived):
        moves = [m for moves in self.rounds for m in moves]
        for index, move in enumerate(moves):
            if move.home[0] == target and move.home[1] <= position < move.home[1] + move.size and index not in arrived:
                arrived.add(index)
                only_if(move.roles()[1], move.copy(refs, send.at[index], recv.at[index]).wait_recv)

    def finish(self, refs, send, recv, arrived):
        moves = [m for moves in self.rounds for m in moves]
        for index, move in enumerate(moves):
            copy = move.copy(refs, send.at[index], recv.at[index])
            sends, receives = move.roles()
            only_if(sends, copy.wait_send)
            if index not in arrived:
                only_if(receives, copy.wait_recv)


def greet(links):
    barrier = pltpu.get_barrier_semaphore()
    middle = ((lax.axis_index("rep") // 4) % 3) > 0
    plain = [link for link in ("core", "x", "y", "near", "skip") if link in links]
    for link in plain:
        pl.semaphore_signal(barrier, inc=1, device_id=partner(link), device_id_type=pl.DeviceIdType.MESH)
    if "inner" in links:

        @pl.when(middle)
        def _():
            pl.semaphore_signal(
                barrier, inc=1, device_id=partner("inner"), device_id_type=pl.DeviceIdType.MESH
            )

    if "inner" in links:

        @pl.when(middle)
        def _():
            pl.semaphore_wait(barrier, len(plain) + 1)

        @pl.when(~middle)
        def _():
            if plain:
                pl.semaphore_wait(barrier, len(plain))

    else:
        pl.semaphore_wait(barrier, len(plain))


class Chain:
    def __init__(self, args, in_specs, out_specs, out_shape, scratch, links, actions):
        self.args, self.in_specs, self.out_specs, self.out_shape = args, in_specs, out_specs, out_shape
        self.scratch, self.links, self.actions = scratch, links, actions


def run(
    body, args, in_specs, out_specs, out_shape, *,
    name, grid=(1,), scratch=(), cost=None, traffic=None, chain=None, hook=None, ident=None,
):
    if (traffic is None or traffic.count() == 0) and chain is None:
        outs = pl.pallas_call(
            body, grid=grid, in_specs=in_specs, out_specs=out_specs, out_shape=out_shape,
            scratch_shapes=list(scratch), cost_estimate=cost, name=name,
        )(*args)
        return outs, [], []
    traffic = traffic or Traffic([], [], [], [])
    chain = chain or Chain([], [], [], [], [], set(), [])
    n_in, n_src, n_out, n_dst = len(args), len(traffic.sources), len(out_shape), len(traffic.targets)
    anywhere = pl.BlockSpec(memory_space=pl.ANY)
    sizes = (n_in, n_src, len(chain.args), n_out, n_dst, len(chain.out_shape), len(scratch), len(chain.scratch))
    links = traffic.links() | chain.links

    def carried(*refs):
        groups = []
        for size in sizes:
            groups.append(refs[:size])
            refs = refs[size:]
        ins, sources, chain_in, outs, targets, chain_out, held, chain_held = groups
        ends = (sources, targets)
        step = pl.program_id(0)
        pl.when(step == 0)(lambda: greet(links))
        arrived = set()
        for at in range(grid[0]):
            rounds = [which for which, when in enumerate(traffic.steps) if when == at]
            actions = [action for when, action in chain.actions[:-1] if when == at]
            if rounds or actions or hook:

                @pl.when(step == at)
                def _():
                    for which in rounds:
                        traffic.start(which, ends, *refs, arrived)
                    for action in actions:
                        action(*chain_in, *chain_out, *chain_held)
                    if hook:
                        hook(
                            at,
                            lambda target, position: traffic.require(target, position, ends, *refs, arrived),
                            targets, ins, held,
                        )

        body(*ins, *outs, *held)

        @pl.when(step == grid[0] - 1)
        def _():
            if traffic.count():
                traffic.finish(ends, *refs, arrived)
            if chain.actions:
                chain.actions[-1][1](*chain_in, *chain_out, *chain_held)

    count = traffic.count()
    semaphores = [pltpu.SemaphoreType.DMA((count,))] * 2 if count else []
    outs = pl.pallas_call(
        carried,
        grid=grid,
        in_specs=list(in_specs) + [anywhere] * n_src + list(chain.in_specs),
        out_specs=list(out_specs) + [anywhere] * n_dst + list(chain.out_specs),
        out_shape=list(out_shape) + list(traffic.targets) + list(chain.out_shape),
        scratch_shapes=list(scratch) + list(chain.scratch) + semaphores,
        compiler_params=pltpu.CompilerParams(collective_id=ident, has_side_effects=True),
        cost_estimate=cost,
        name=name,
    )(*args, *traffic.sources, *chain.args)
    return outs[:n_out], outs[n_out : n_out + n_dst], outs[n_out + n_dst :]


COT_PATHS = {
    (0, 0, 1): ("y", (0, 0, 0), -1.500),
    (0, 1, 0): ("x", (0, 0, 0), 2.243),
    (0, 1, 1): ("x", (0, 0, 1), 1.258),
    (1, 0, 0): ("near", (0, 0, 0), 1.763),
    (1, 0, 1): ("near", (0, 0, 1), 1.701),
    (1, 1, 0): ("near", (0, 1, 0), 3.477),
    (1, 1, 1): ("x", (1, 0, 1), 5.719),
    (2, 0, 0): ("inner", (0, 0, 0), 4.656),
    (2, 0, 1): ("y", (2, 0, 0), 2.464),
    (2, 1, 0): ("inner", (0, 1, 0), 0.237),
    (2, 1, 1): ("x", (2, 0, 1), 2.798),
    (3, 0, 0): ("inner", (1, 0, 0), 0.958),
    (3, 0, 1): ("y", (3, 0, 0), 2.984),
    (3, 1, 0): ("x", (3, 0, 0), 2.092),
    (3, 1, 1): ("inner", (1, 1, 1), 1.507),
}
ROW_PATHS = {
    (0, 0, 1): ("y", (0, 0, 0), -1.400),
    (0, 1, 0): ("x", (0, 0, 0), 1.939),
    (0, 1, 1): ("x", (0, 0, 1), 1.580),
    (1, 0, 0): ("near", (0, 0, 0), 1.441),
    (1, 0, 1): ("y", (1, 0, 0), 0.198),
    (1, 1, 0): ("near", (0, 1, 0), 2.429),
    (1, 1, 1): ("x", (1, 0, 1), 5.646),
    (2, 0, 0): ("inner", (0, 0, 0), 2.268),
    (2, 0, 1): ("y", (2, 0, 0), 2.650),
    (2, 1, 0): ("x", (2, 0, 0), 4.955),
    (2, 1, 1): ("x", (2, 0, 1), 4.985),
    (3, 0, 0): ("reach", (1, 0, 0), 1.374),
    (3, 0, 1): ("y", (3, 0, 0), 4.956),
    (3, 1, 0): ("x", (3, 0, 0), 2.903),
    (3, 1, 1): ("y", (3, 1, 0), 4.968),
}
FAR_FIRST = {(0, 0, 1): ("y", (0, 0, 0), -2.0)}
FAR_LAST = {(0, 0, 1): ("y", (0, 0, 0), 2.506)}
FRONT_ROOM, PAIR_ROOM, EXPERT_ROOM, OWN_ROOM, FINISH_ROOM, LAST_ROOM = 5, 9, 11, 4, 8, 25


class Network:
    def __init__(self):
        self.have, self.hops, self.weight, self.pieces = {}, {}, {}, {}

    def offer(self, name, array, hops, weight=1):
        self.hops[name], self.weight[name] = hops, weight
        self.pieces[name] = array.shape[0]
        for p in range(array.shape[0]):
            self.have[name, (0, 0, 0), p] = (array, p)

    def order(self, item):
        name, block, p = item
        return self.hops[name][block][2], block, p

    def missing(self):
        return [
            (name, block, p)
            for name in self.hops
            for block in self.hops[name]
            for p in range(self.pieces[name])
            if (name, block, p) not in self.have
        ]

    def complete(self, name, block):
        return all((name, block, p) in self.have for p in range(self.pieces[name]))

    def plan(self, room, steps, times):
        waiting = sorted(self.missing(), key=self.order)
        landed, rounds, going = {}, [[] for _ in steps], {}
        free = dict.fromkeys(("x", "y", "near", "inner"), 0.0)
        uses = {"reach": (("inner", 2), ("near", 1))}
        lag = 0.4

        def fill(link, now, weight, horizon):
            spans = [(on, max(free[on], now), n * weight) for on, n in uses.get(link, ((link, 1),))]
            if weight and any(begin >= horizon or begin + length > room + 0.01 for _, begin, length in spans):
                return None
            for on, begin, length in spans:
                if length:
                    free[on] = begin + length
            return max(begin + length for _, begin, length in spans) + lag

        for r, now in enumerate(times):
            horizon = times[r + 1] + 0.5 if r + 1 < len(times) else room
            for item in [i for i, (_, at) in going.items() if at <= now]:
                done = fill("near", now, self.weight[item[0]], horizon)
                if done is not None:
                    rounds[r].append(("outward", item, item))
                    landed[item] = done
                    del going[item]
            for item in waiting:
                name, block, p = item
                if item in landed or item in going:
                    continue
                link, source, _ = self.hops[name][block]
                source = (name, source, p)
                if source not in self.have and landed.get(source, now + 1) > now:
                    continue
                if link == "inner":
                    left = room - max(free["near"], now + 1) - sum(self.weight[i[0]] for i in going)
                    if r + 1 >= len(times) or left < 1 + self.weight[name] or times[-1] < now + self.weight[name] + lag:
                        continue
                done = fill(link, now, self.weight[name], horizon)
                if done is None:
                    continue
                if link == "reach":
                    rounds[r] += [("inner", source, item), ("skip", source, item)]
                else:
                    rounds[r].append((link, source, item))
                if link == "inner":
                    going[item] = (r, done)
                else:
                    landed[item] = done
        for item in list(going):
            rounds[-1].append(("outward", item, item))
            landed[item] = room
        sources, targets, homes = [], [], {}
        for name, block, p in sorted(landed):
            homes.setdefault((name, block), []).append(p)
        order = list(homes)
        for name, block in order:
            model = self.have[name, (0, 0, 0), 0][0]
            targets.append(jax.ShapeDtypeStruct((len(homes[name, block]),) + model.shape[1:], model.dtype))

        def home(item):
            name, block, p = item
            return order.index((name, block)), homes[name, block].index(p)

        def origin(item):
            if item in landed:
                return (1,) + home(item)
            array, at = self.have[item]
            for k, known in enumerate(sources):
                if known is array:
                    return 0, k, at
            sources.append(array)
            return 0, len(sources) - 1, at

        moves = []
        for chosen in rounds:
            spans = []
            for link, source, item in sorted(chosen, key=lambda c: (c[0] not in ("outward", "inner"), *c)):
                a, b = origin(source), home(item)
                if spans:
                    link_, a_, b_, n = spans[-1]
                    if link_ == link and a_[:2] == a[:2] and b_[0] == b[0] and a[2] == a_[2] + n and b[1] == b_[1] + n:
                        spans[-1] = (link, a_, b_, n + 1)
                        continue
                spans.append((link, a, b, 1))
            flat = [m for made in moves for m in made]
            placed = []
            for link, a, b, n in spans:
                needs = [
                    k
                    for k, m in enumerate(flat)
                    if a[0] == 1 and m.home[0] == a[1] and m.home[1] < a[2] + n and a[2] < m.home[1] + m.size
                ]
                placed.append(self.move(link, a, b, n, needs))
            moves.append(placed)
        while moves and not moves[-1]:
            moves.pop()
        traffic = Traffic(sources, targets, moves, steps[: len(moves)])
        return traffic, (order, homes, landed)

    def find(self, plan, name, block):
        order, homes, landed = plan
        found = []
        for p in range(self.pieces[name]):
            if (name, block, p) in landed:
                found.append((None, order.index((name, block)), homes[name, block].index(p)))
            else:
                array, at = self.have[name, block, p]
                found.append((array, None, at))
        return found

    def landing(self, plan, block):
        return max(plan[2].get((name, block, p), 0.0) for name in "CS" for p in range(self.pieces[name]))

    @staticmethod
    def move(link, origin, home, count, needs):
        def source(refs):
            return refs[origin[0]][origin[1]].at[pl.ds(origin[2], count)]

        def target(refs):
            return refs[1][home[0]].at[pl.ds(home[1], count)]

        made = Move(link, source, target, needs)
        made.home, made.size = home, count
        return made

    def land(self, plan, arrays):
        order, homes, _ = plan
        for key, array in zip(order, arrays):
            for at, p in enumerate(homes[key]):
                self.have[key[0], key[1], p] = (array, at)

    def block(self, name, block):
        return [self.have[name, block, p] for p in range(self.pieces[name])]


def evenly(room, steps, length, every=1):
    chosen = list(range(0, steps, every))
    return room, chosen, [step * length for step in chosen]


def gathering(room, senders, extra):
    busy = 2 * senders * 0.45
    times = [0.45 * step for step in range(2 * senders)]
    times += [busy + (step + 1) * max(0.5, room - busy) / (extra + 1) for step in range(extra)]
    return room, list(range(2 * senders + extra)), times


def standardise(values):
    average = jnp.mean(values, axis=-1, keepdims=True)
    centred = values - average
    variance = jnp.mean(centred * centred, axis=-1, keepdims=True)
    scale = lax.rsqrt(variance + 1e-06)
    return centred * scale, scale


def prep_body(count_ref, cap_ref, tok_ref, cot_ref, route_ref, tok_out, cot_out, route_out, ids_out, load_out, wide, narrow, lines):
    pl.when(pl.program_id(0) == 0)(
        lambda: prep_rows(
            count_ref, cap_ref, tok_ref, cot_ref, route_ref, tok_out, cot_out, route_out, ids_out, load_out, wide, narrow, lines
        )
    )


def prep_rows(count_ref, cap_ref, tok_ref, cot_ref, route_ref, tok_out, cot_out, route_out, ids_out, load_out, wide, narrow, lines):
    images = tok_out.shape[0]
    total = tok_ref.shape[0]
    alive_images = count_ref[0]
    real = iota((PAD, 1), 0) < IMG_TOK

    def split(source, image):
        return source[pl.ds(image * IMG_TOK, PAD), :]

    wide[...] = jnp.zeros_like(wide)
    narrow[...] = jnp.zeros_like(narrow)
    wide[pl.ds(0, total), :] = tok_ref[...].astype(F32)
    for image in range(images):
        tok_out[image] = jnp.where(real, split(wide, image), 0.0).astype(BF16)
    wide[pl.ds(0, total), :] = cot_ref[...].astype(F32)
    lines[...] = jnp.zeros_like(lines)
    lines[0:2, 0:total] = route_ref[...].astype(F32)
    narrow[...] = jnp.transpose(lines[...])[: narrow.shape[0], :2].astype(jnp.int32)
    routes = []
    lives = []
    for image in range(images):
        live = real & (image < alive_images)
        cot_out[image] = jnp.where(live, split(wide, image), 0.0).astype(BF16)
        picked = split(narrow, image)
        route_out[image] = picked
        routes.append(picked)
        lives.append(jnp.where(live, 1, 0))
    routes = jnp.concatenate(routes, axis=0)
    live = jnp.concatenate(lives, axis=0) > 0
    rows = images * PAD
    lane = iota((rows, 128), 1)
    first = (lane == routes[:, 0:1]) & live
    second = (lane == routes[:, 1:2] + EXPERTS) & live
    hot = jnp.where(first | second, 1.0, 0.0)
    below = jnp.where(iota((rows, rows), 0) > iota((rows, rows), 1), 1.0, 0.0).astype(BF16)
    before = dot(below, hot.astype(BF16))
    totals = jnp.sum(hot, axis=0, keepdims=True)
    place_one = jnp.sum(jnp.where(first, before, 0.0), axis=1, keepdims=True)
    place_two = jnp.sum(jnp.where(second, before, 0.0), axis=1, keepdims=True) + jnp.sum(
        jnp.where(lane == routes[:, 1:2], totals, 0.0), axis=1, keepdims=True
    )
    limit = cap_ref[0].astype(F32)
    keep_one = live & (place_one < limit)
    keep_two = live & (place_two < limit)
    slots = jnp.where(lane == 0, jnp.where(keep_one, routes[:, 0:1].astype(F32), -1.0), 0.0)
    slots = jnp.where(lane == 1, jnp.where(keep_one, place_one, 0.0), slots)
    slots = jnp.where(lane == 2, jnp.where(keep_two, routes[:, 1:2].astype(F32), -1.0), slots)
    slots = jnp.where(lane == 3, jnp.where(keep_two, place_two, 0.0), slots)
    for image in range(images):
        ids_out[image] = jnp.transpose(slots[image * PAD : (image + 1) * PAD])[0:8]
    lanes = iota((1, 128), 1)
    tokens_alive = (alive_images * IMG_TOK).astype(F32)
    load_out[0] = jnp.broadcast_to(jnp.where(lanes == 64, tokens_alive, totals), (8, 128))


def pack_body(*refs):
    lines, (qkv_ref, out_ref, router_ref, wide_ref, tall_ref) = refs[:-5], refs[-5:]
    rows, part = qkv_ref.shape[0], lines[0].shape[0]
    wide_ref[:rows] = qkv_ref[...]
    table = jnp.zeros((16, part), F32)
    for k, ref in enumerate(lines):
        line = jnp.broadcast_to(ref[...].astype(F32).reshape(1, part), (16, part))
        table = jnp.where(iota((16, part), 0) == k, line, table)
    wide_ref[rows:] = jnp.zeros((16, wide_ref.shape[1]), BF16)
    wide_ref[rows:, :part] = table.astype(BF16)
    width = out_ref.shape[1]
    tall_ref[:, :width] = out_ref[...]
    tall_ref[:, width:] = jnp.zeros((rows, 128), BF16)
    tall_ref[:, width : width + EXPERTS] = router_ref[...]


def pack_weights(lines, w_qkv, w_out, w_router):
    rows = w_qkv.shape[0]
    return pl.pallas_call(
        pack_body,
        in_specs=[pl.BlockSpec(memory_space=pltpu.VMEM)] * (len(lines) + 3),
        out_specs=[pl.BlockSpec(memory_space=pltpu.VMEM)] * 2,
        out_shape=[
            jax.ShapeDtypeStruct((rows + 16, w_qkv.shape[1]), BF16),
            jax.ShapeDtypeStruct((rows, w_out.shape[1] + 128), BF16),
        ],
        cost_estimate=pl.CostEstimate(flops=1_000_000, bytes_accessed=2_500_000, transcendentals=0),
        name="pack_weights",
    )(*lines, w_qkv, w_out, w_router)


def weight_traffic(wide, tall):
    def rows(array):
        half = array.shape[0] // 2
        return pl.ds(pl.multiple_of((lax.axis_index("rep") % 2) * half, 8), half)

    def fetch(at, array):
        return Move("y", lambda refs: refs[0][at].at[rows(array)], lambda refs: refs[1][at].at[rows(array)])

    def pass_on(at, array):
        there = lambda refs: refs[1][at].at[rows(array)]
        return Move("core", there, there, [at])

    arrays = (wide, tall)
    targets = [jax.ShapeDtypeStruct(a.shape, a.dtype) for a in arrays]
    rounds = [[make(at, a) for at, a in enumerate(arrays)] for make in (fetch, pass_on)]
    return Traffic(list(arrays), targets, rounds, [0, 1])


def prepare(tokens, cotangent, routes, image_count, capacity, wide, tall, ident):
    total, width = tokens.shape
    images = total // IMG_TOK
    shapes = [
        jax.ShapeDtypeStruct((images, PAD, width), BF16),
        jax.ShapeDtypeStruct((images, PAD, width), BF16),
        jax.ShapeDtypeStruct((images, PAD, 2), jnp.int32),
        jax.ShapeDtypeStruct((images, 8, PAD), F32),
        jax.ShapeDtypeStruct((1, 8, 128), F32),
    ]
    return run(
        prep_body,
        (image_count, capacity, tokens, cotangent, routes),
        [scalar_spec(), scalar_spec()] + [resident(a.shape) for a in (tokens, cotangent, routes)],
        [resident(a.shape) for a in shapes],
        shapes,
        grid=(2,),
        scratch=[pltpu.VMEM((1000, width), F32), pltpu.VMEM((1000, 2), jnp.int32), pltpu.VMEM((8, 1024), F32)],
        cost=pl.CostEstimate(flops=300_000_000, bytes_accessed=6_000_000, transcendentals=0),
        name="prepare",
        traffic=weight_traffic(wide, tall),
        ident=ident,
    )


def place_halves(own, far, both):
    mine = lax.axis_index("fsdp")
    both[mine] = own[...]
    both[1 - mine] = far[...]


def vectors(wide_ref):
    return jnp.concatenate([wide_ref[0, 256:272, :256], wide_ref[1, 256:272, :256]], axis=1).astype(F32)


def front_body(
    count_ref, tok_ref, ids_ref, route_ref, wide_own, wide_far, tall_own, tall_far,
    packed_ref, prob_ref, mixed_ref, middle_ref, second_ref, soft_ref, sum_ref, wide_ref, tall_ref,
):
    @pl.when(pl.program_id(0) == 0)
    def _():
        sum_ref[...] = jnp.zeros_like(sum_ref)
        place_halves(wide_own, wide_far, wide_ref)
        place_halves(tall_own, tall_far, tall_ref)

    width = tok_ref.shape[-1]
    vec = vectors(wide_ref)
    inputs = tok_ref[0].astype(F32)
    normed = (standardise(inputs)[0] * vec[0:1] + vec[1:2]).astype(BF16)
    qkv = wide_ref[:, :256, :].reshape(width, 3 * width)
    raw = dot(normed, qkv)
    packed_ref[0, :, :width] = (raw[:, :width] + vec[2:3]).astype(BF16)
    packed_ref[0, :, width : 2 * width] = raw[:, width : 2 * width].astype(BF16)
    packed_ref[0, :, 2 * width :] = (raw[:, 2 * width :] + vec[3:4]).astype(BF16)
    low_lanes = iota((PAD, 128), 1) < HEAD_DIM
    real_key = iota((PAD, PAD), 1) < IMG_TOK
    for pair in range(HEADS // 2):
        at = pair * 128
        query = packed_ref[0, :, at : at + 128] * jnp.asarray(HEAD_DIM**-0.5, BF16)
        keys = packed_ref[0, :, width + at : width + at + 128]
        valued = packed_ref[0, :, 2 * width + at : 2 * width + at + 128]
        got = []
        for side in range(2):
            own = low_lanes if side == 0 else ~low_lanes
            scores = dot_cols(jnp.where(own, query, jnp.zeros_like(query)), keys)
            scores = jnp.where(real_key, scores, -1e30)
            raised = jnp.exp(scores - jnp.max(scores, axis=-1, keepdims=True))
            weights = (raised / jnp.sum(raised, axis=-1, keepdims=True)).astype(BF16)
            prob_ref[0, 2 * pair + side] = weights
            got.append(dot(weights, valued))
        mixed_ref[0, :, at : at + 128] = jnp.where(low_lanes, got[0], got[1]).astype(BF16)
    out_full = tall_ref[:, :, :width].reshape(width, width)
    router = tall_ref[:, :, width : width + 128].reshape(width, 128)
    middle = inputs + dot(mixed_ref[0], out_full) + vec[4:5]
    middle_ref[0] = middle
    second = standardise(middle)[0] * vec[5:6] + vec[6:7]
    lane = iota((PAD, 128), 1)
    logits = jnp.where(lane < EXPERTS, dot(second.astype(BF16), router), -1e30)
    soft = jnp.exp(logits - jnp.max(logits, axis=-1, keepdims=True))
    soft = soft / jnp.sum(soft, axis=-1, keepdims=True)
    route = route_ref[0]
    pick_one = jnp.sum(jnp.where(lane == route[:, 0:1], soft, 0.0), axis=-1, keepdims=True)
    pick_two = jnp.sum(jnp.where(lane == route[:, 1:2], soft, 0.0), axis=-1, keepdims=True)
    both = pick_one + pick_two
    live = (iota((PAD, 1), 0) < IMG_TOK) & (pl.program_id(0) < count_ref[0])
    alive = jnp.where(live, 1.0, 0.0)
    sum_ref[0] += jnp.broadcast_to(jnp.sum(soft * alive, axis=0, keepdims=True), (8, 128))
    soft = jnp.where(lane == EXPERTS + 4, pick_one / both, soft)
    soft = jnp.where(lane == EXPERTS + 5, pick_two / both, soft)
    soft_ref[0] = soft
    gates = jnp.transpose(soft)[EXPERTS : EXPERTS + 8]
    line = iota((8, PAD), 0)
    meta = jnp.where((line == 4) | (line == 5), gates, ids_ref[0])
    meta = jnp.concatenate([meta, jnp.zeros((8, width - PAD), F32)], axis=1)
    second_ref[0] = jnp.concatenate([second[: PAD - 8], meta], axis=0).astype(BF16)


def front(count, tok, ids, routes, wide, tall, traffic, ident):
    images, _, width = tok.shape
    shape = jax.ShapeDtypeStruct
    return run(
        front_body,
        (count, tok, ids, routes, *wide, *tall),
        [scalar_spec(), by_image(PAD, width), by_image(8, PAD), by_image(PAD, 2)]
        + [resident(wide[0].shape)] * 2
        + [resident(tall[0].shape)] * 2,
        [
            by_image(PAD, 3 * width),
            by_image(HEADS, PAD, PAD),
            by_image(PAD, width),
            by_image(PAD, width),
            by_image(PAD, width),
            by_image(PAD, 128),
            resident((1, 8, 128)),
        ],
        [
            shape((images, PAD, 3 * width), BF16),
            shape((images, HEADS, PAD, PAD), BF16),
            shape((images, PAD, width), BF16),
            shape((images, PAD, width), F32),
            shape((images, PAD, width), BF16),
            shape((images, PAD, 128), F32),
            shape((1, 8, 128), F32),
        ],
        grid=(images,),
        scratch=[pltpu.VMEM((2,) + wide[0].shape, BF16), pltpu.VMEM((2,) + tall[0].shape, BF16)],
        cost=pl.CostEstimate(flops=6_000_000_000, bytes_accessed=16_000_000, transcendentals=2_000_000),
        name="front",
        traffic=traffic,
        ident=ident,
    )


def slot_lines(meta):
    return meta[0:1] * CAP + meta[1:2], meta[2:3] * CAP + meta[3:4]


def gather(base, experts, senders, sequence, traffic, ident, chain=None):
    arrays, table = [], []
    for sender in sequence:
        if sender is None:
            table.append(None)
            continue
        for kind in range(2):
            spots = []
            for array, target, position in senders[sender][kind]:
                at = target
                if array is not None:
                    at = next((k for k, known in enumerate(arrays) if known is array), len(arrays))
                    if at == len(arrays):
                        arrays.append(array)
                spots.append((array is None, at, position))
            table.append((sender, kind, spots))
    images, width = len(table[0][2]), arrays[0].shape[-1]
    tokens, slots, count, steps = images * PAD, experts * CAP, len(senders), len(table)
    first = [next(k for k, entry in enumerate(table) if entry and entry[0] == sender) for sender in range(count)]

    def hook(step, require, targets, ins, held):
        sources, rows, loaded = ins[1:], held[0], held[2]

        def copies(entry):
            _, kind, spots = entry
            return [
                pltpu.make_async_copy(
                    (targets if arriving else sources)[at].at[position],
                    rows.at[kind, pl.ds(image * PAD, PAD)],
                    loaded.at[kind, image],
                )
                for image, (arriving, at, position) in enumerate(spots)
            ]

        def load(entry):
            for arriving, at, position in entry[2]:
                if arriving:
                    require(at, position)
            for copy in copies(entry):
                copy.start()

        if step == 0:
            load(table[0])
        if step + 1 < steps and table[step + 1]:
            load(table[step + 1])
        if table[step]:
            for copy in copies(table[step]):
                copy.wait()

    def body(base_ref, *refs):
        row_out, grad_out, rows, lines = refs[len(arrays) : len(arrays) + 4]
        step = pl.program_id(0)
        turns = [(k, entry[1]) for k, entry in enumerate(table) if entry]
        working, gated = step < 0, step < 0
        for k, kind in turns:
            working = working | (step == k)
            if kind:
                gated = gated | (step == k)

        @pl.when(working & ~gated)
        def _():
            for image in range(images):
                lines[image] = rows[0, image * PAD + PAD - 16 : (image + 1) * PAD, :PAD].astype(F32)[8:]

        @pl.when(working)
        def _():
            meta = jnp.concatenate([lines[image] for image in range(images)], axis=1)
            one, two = slot_lines(meta)
            weight_one = jnp.where(gated, meta[4:5], 1.0)
            weight_two = jnp.where(gated, meta[5:6], 1.0)
            slot = (iota((slots, tokens), 0) + base_ref[0]).astype(F32)
            pick = jnp.where(slot == one, weight_one, 0.0) + jnp.where(slot == two, weight_two, 0.0)
            got = dot(pick.astype(BF16), rows[jnp.where(gated, 1, 0)])
            got = got.astype(BF16).reshape(experts, 1, CAP, width)

            @pl.when(~gated)
            def _():
                row_out[...] = got

            @pl.when(gated)
            def _():
                grad_out[...] = got

    def place(d):
        turn = 0
        for at in first[1:]:
            turn += jnp.where(d >= at, 1, 0)
        return (0, turn, 0, 0)

    shape = jax.ShapeDtypeStruct((experts, count, CAP, width), BF16)
    return run(
        body,
        (base, *arrays),
        [scalar_spec()] + [pl.BlockSpec(memory_space=pl.ANY)] * len(arrays),
        [pl.BlockSpec((experts, 1, CAP, width), place)] * 2,
        [shape, shape],
        grid=(steps,),
        scratch=[
            pltpu.VMEM((2, tokens, width), BF16),
            pltpu.VMEM((images, 8, PAD), F32),
            pltpu.SemaphoreType.DMA((2, images)),
        ],
        cost=pl.CostEstimate(
            flops=4 * count * slots * tokens * width,
            bytes_accessed=4 * count * (tokens + slots) * width,
            transcendentals=0,
        ),
        name="gather",
        traffic=traffic,
        chain=chain,
        hook=hook,
        ident=ident,
    )


def own_line(ref):
    table = ref[...].astype(F32)
    return jnp.sum(jnp.where(iota(table.shape, 0) == pl.program_id(0), table, 0.0), axis=0, keepdims=True)


def expert_body(row_own, row_far, grad_own, grad_far, in_ref, in_bias_ref, out_ref, out_bias_ref, made_own, made_far, back_own, back_far):
    cap, width = row_own.shape[2:]
    hidden = in_ref.shape[2]
    rows = jnp.concatenate([row_own[0, 0], row_far[0, 0]], axis=0)
    grads = jnp.concatenate([grad_own[0, 0], grad_far[0, 0]], axis=0)
    in_bias = own_line(in_bias_ref)
    made = jnp.zeros((2 * cap, width), F32)
    back = jnp.zeros((2 * cap, width), F32)
    chunk = 512
    for at in range(0, hidden, chunk):
        first = in_ref[0, :, at : at + chunk]
        second = out_ref[0, at : at + chunk, :]
        raised = dot(rows, first) + in_bias[:, at : at + chunk]
        active, slope = gelu_pair(raised)
        made += dot(active.astype(BF16), second)
        draised = (dot_cols(grads, second) * slope).astype(BF16)
        back += dot_cols(draised, first)
    made = (made + own_line(out_bias_ref)).astype(BF16)
    back = back.astype(BF16)
    made_own[0], made_far[0] = made[:cap], made[cap:]
    back_own[0], back_far[0] = back[:cap], back[cap:]


def expert_layer(pair, first, first_bias, second, second_bias, chain, traffic, ident):
    experts, _, cap, width = pair[0].shape
    hidden = first.shape[2]
    rows = [pl.BlockSpec((1, 1, cap, width), lambda e, side=side: (e, side, 0, 0)) for side in range(2)]
    out = pl.BlockSpec((1, cap, width), lambda e: (e, 0, 0))
    return run(
        expert_body,
        (
            pair[0],
            pair[0],
            pair[1],
            pair[1],
            first,
            first_bias,
            second,
            second_bias,
        ),
        rows + rows + [by_image(width, hidden), resident(first_bias.shape), by_image(hidden, width), resident(second_bias.shape)],
        [out] * 4,
        [jax.ShapeDtypeStruct((experts, cap, width), BF16)] * 4,
        grid=(experts,),
        cost=pl.CostEstimate(
            flops=16 * experts * cap * width * hidden,
            bytes_accessed=4 * experts * width * hidden,
            transcendentals=2 * experts * cap * hidden,
        ),
        name="expert_layer",
        traffic=traffic,
        chain=chain,
        ident=ident,
    )


def combine_body(base_ref, rows, cot, made_ref, back_ref, sum_ref, row_ref, gate_ref):
    experts, cap, width = made_ref.shape
    slots = experts * cap
    meta = jnp.transpose(rows[PAD - 16 :, :PAD].astype(F32)[8:])
    slot = (iota((PAD, slots), 1) + base_ref[0]).astype(F32)
    one = jnp.where(slot == meta[:, 0:1] * CAP + meta[:, 1:2], 1.0, 0.0).astype(BF16)
    two = jnp.where(slot == meta[:, 2:3] * CAP + meta[:, 3:4], 1.0, 0.0).astype(BF16)
    made = made_ref[...].reshape(slots, width)
    made_one = dot(one, made)
    made_two = dot(two, made)
    sum_ref[0] = (meta[:, 4:5] * made_one + meta[:, 5:6] * made_two).astype(BF16)
    row_ref[0] = dot(one + two, back_ref[...].reshape(slots, width)).astype(BF16)
    cot = cot.astype(F32)
    grad_one = jnp.sum(cot * made_one, axis=1, keepdims=True)
    grad_two = jnp.sum(cot * made_two, axis=1, keepdims=True)
    lane = iota((PAD, 128), 1)
    wide = jnp.where(lane == 0, grad_one, jnp.where(lane == 1, grad_two, 0.0))
    gate_ref[0] = jnp.transpose(wide)[0:8]


def by_piece(pieces, *shape):
    arrays, first = [], []
    for image, (array, position) in enumerate(pieces):
        if not arrays or arrays[-1] is not array:
            arrays.append(array)
            first.append((image, position))
    specs = []
    for array, (image, position) in zip(arrays, first):

        def index(i, *_, image=image, position=position, last=array.shape[0] - 1):
            return (jnp.clip(i - image + position, 0, last),) + (0,) * len(shape)

        specs.append(pl.BlockSpec((1,) + shape, index))

    def read(refs):
        value = refs[0][0]
        for ref, (image, _) in zip(refs[1:], first[1:]):
            value = jnp.where(pl.program_id(0) >= image, ref[0], value)
        return value

    return arrays, specs, read


def combine(base, rows, cots, made, back, traffic, ident):
    width = made.shape[-1]
    images = len(rows)
    experts, cap, _ = made.shape
    row_arrays, row_specs, read_rows = by_piece(rows, PAD, width)
    cot_arrays, cot_specs, read_cots = by_piece(cots, PAD, width)
    split = len(row_arrays)

    def body(base_ref, made_ref, back_ref, *refs):
        inputs, outs = refs[: split + len(cot_arrays)], refs[split + len(cot_arrays) :]
        combine_body(base_ref, read_rows(inputs[:split]), read_cots(inputs[split:]), made_ref, back_ref, *outs)

    return run(
        body,
        (base, made, back, *row_arrays, *cot_arrays),
        [scalar_spec(), resident(made.shape), resident(back.shape), *row_specs, *cot_specs],
        [by_image(PAD, width), by_image(PAD, width), by_image(8, PAD)],
        [
            jax.ShapeDtypeStruct((images, PAD, width), BF16),
            jax.ShapeDtypeStruct((images, PAD, width), BF16),
            jax.ShapeDtypeStruct((images, 8, PAD), F32),
        ],
        grid=(images,),
        cost=pl.CostEstimate(
            flops=6 * images * PAD * experts * cap * width, bytes_accessed=6_000_000, transcendentals=0
        ),
        name="combine",
        traffic=traffic,
        ident=ident,
    )


def norm_back(grads, hat, scale, gain):
    scaled = grads * gain
    inner = jnp.mean(scaled * hat, axis=-1, keepdims=True)
    return scale * (scaled - jnp.mean(scaled, axis=-1, keepdims=True) - hat * inner)


def column_sum(values):
    return jnp.sum(values, axis=0, keepdims=True)


def finish_body(
    count_ref, tok_ref, cot_ref, packed_ref, prob_ref, mixed_ref, middle_ref, second_ref, soft_ref, route_ref,
    row_own, row_far, gate_own, gate_far, aux_ref,
    wide_own, wide_far, tall_own, tall_far, dtok_ref, pack_ref, loss_ref,
    dpacked, wide_ref, tall_ref, dqkv_ref, dout_ref, drouter_ref, dvec_ref,
):
    image = pl.program_id(0)
    width = tok_ref.shape[-1]

    @pl.when(image == 0)
    def _():
        place_halves(wide_own, wide_far, wide_ref)
        place_halves(tall_own, tall_far, tall_ref)

    vec = vectors(wide_ref)
    images = dtok_ref.shape[0] // IMG_TOK

    @pl.when(image == 0)
    def _():
        for ref in (dqkv_ref, dout_ref, drouter_ref, dvec_ref):
            ref[...] = jnp.zeros_like(ref)

    real = iota((PAD, 1), 0) < IMG_TOK
    alive = jnp.where(real & (image < count_ref[0]), 1.0, 0.0)
    middle = middle_ref[0]
    upstream = cot_ref[0].astype(F32)
    soft = soft_ref[0]
    route = route_ref[0]
    lane = iota((PAD, 128), 1)
    gate_grads = jnp.transpose(gate_own[0] + gate_far)
    push = (gate_grads[:, 0:1] - gate_grads[:, 1:2]) * soft[:, EXPERTS + 4 : EXPERTS + 5] * soft[:, EXPERTS + 5 : EXPERTS + 6]
    soft = jnp.where(lane < EXPERTS, soft, 0.0)
    loads = aux_ref[0]
    lanes = iota(loads.shape, 1)
    live = jnp.sum(jnp.where(lanes == 2 * EXPERTS, loads, 0.0), axis=1, keepdims=True)
    share = (loads + pltpu.roll(loads, 128 - EXPERTS, 1)) / (2.0 * live)
    push_all = jnp.where(lanes < EXPERTS, EXPERTS * share / live, 0.0)
    loss = jnp.sum(push_all * aux_ref[1], axis=1, keepdims=True)
    loss_ref[...] = jnp.broadcast_to(loss, loads.shape)
    aux = push_all[0:1] * alive
    dlogits = soft * (aux - jnp.sum(soft * aux, axis=-1, keepdims=True))
    dlogits += jnp.where(lane == route[:, 0:1], push, 0.0) - jnp.where(lane == route[:, 1:2], push, 0.0)
    dlogits = dlogits.astype(BF16)
    second = second_ref[0]
    router = tall_ref[:, :, width : width + 128].reshape(width, 128)
    drouter_ref[...] += dot_rows(second, dlogits)
    dsecond = dot_cols(dlogits, router) + (row_own[0].astype(F32) + row_far.astype(F32))
    hat, scale = standardise(middle)
    dmiddle = upstream + norm_back(dsecond, hat, scale, vec[5:6])
    dattn = dmiddle.astype(BF16)
    dvec_ref[EXPERTS + 4 : EXPERTS + 5] += column_sum(dattn.astype(F32))
    dvec_ref[EXPERTS + 5 : EXPERTS + 6] += column_sum(dsecond * hat)
    dvec_ref[EXPERTS + 6 : EXPERTS + 7] += column_sum(dsecond)
    dout_ref[...] += dot_rows(mixed_ref[0], dattn)
    out_full = tall_ref[:, :, :width].reshape(width, width)
    dmixed = dot_cols(dattn, out_full).astype(BF16)
    low_lanes = iota((PAD, 128), 1) < HEAD_DIM
    root = HEAD_DIM**-0.5
    for pair in range(HEADS // 2):
        at = pair * 128
        query = packed_ref[0, :, at : at + 128]
        keys = packed_ref[0, :, width + at : width + at + 128]
        valued = packed_ref[0, :, 2 * width + at : 2 * width + at + 128]
        grads = dmixed[:, at : at + 128]
        parts = []
        for side in range(2):
            own = low_lanes if side == 0 else ~low_lanes
            weights = prob_ref[0, 2 * pair + side]
            dweights = dot_cols(jnp.where(own, grads, jnp.zeros_like(grads)), valued)
            exact = weights.astype(F32)
            inner = jnp.sum(dweights * exact, axis=-1, keepdims=True)
            dscores = (exact * (dweights - inner)).astype(BF16)
            parts.append((dot(dscores, keys), dot_rows(dscores, query), dot_rows(weights, grads)))
        for third, factor in ((0, root), (1, root), (2, 1.0)):
            both = jnp.where(low_lanes, parts[0][third], parts[1][third]) * factor
            dpacked[:, third * width + at : third * width + at + 128] = both.astype(BF16)
    inputs = tok_ref[0].astype(F32)
    hat, scale = standardise(inputs)
    normed = (hat * vec[0:1] + vec[1:2]).astype(BF16)
    packed_grads = dpacked[...]
    dqkv_ref[...] += dot_rows(normed, packed_grads)
    dvec_ref[EXPERTS + 2 : EXPERTS + 3] += column_sum(packed_grads[:, :width].astype(F32))
    dvec_ref[EXPERTS + 3 : EXPERTS + 4] += column_sum(packed_grads[:, 2 * width :].astype(F32))
    qkv = wide_ref[:, :256, :].reshape(width, 3 * width)
    dnormed = dot_cols(packed_grads, qkv)
    dvec_ref[EXPERTS + 0 : EXPERTS + 1] += column_sum(dnormed * hat)
    dvec_ref[EXPERTS + 1 : EXPERTS + 2] += column_sum(dnormed)
    dtokens = dmiddle + norm_back(dnormed, hat, scale, vec[0:1])
    for k in range(images):

        @pl.when(image == k)
        def _():
            dtok_ref[pl.ds(k * IMG_TOK, IMG_TOK), :] = dtokens[:IMG_TOK]

    @pl.when(image == images - 1)
    def _():
        lines = jnp.transpose(dvec_ref[...])
        part = width // 8
        for owner in range(2):
            for half in range(2):
                for quarter in range(2):
                    at = ((owner * 2 + half) * 2 + quarter) * part
                    rows = slice(at, at + part)
                    spot = pack_ref.at[owner, half, quarter]
                    spot[:, : 3 * width] = dqkv_ref[rows].astype(BF16)
                    spot[:, 3 * width : 4 * width] = dout_ref[rows].astype(BF16)
                    spot[:, 4 * width :] = (drouter_ref[rows] + lines[rows]).astype(BF16)


def finish(count, tok, cot, saved, routes, row_own, row_far, gate_own, gate_far, aux, wide, tall, total, traffic, ident):
    images, _, width = tok.shape
    packed, prob, mixed, middle, second, soft = saved
    shape = jax.ShapeDtypeStruct
    tile = by_image(PAD, width)
    row_arrays = []
    for array, _, _ in row_far:
        if array is not None and not any(known is array for known in row_arrays):
            row_arrays.append(array)
    gate_arrays, gate_specs, read_gates = by_piece(gate_far, 8, PAD)
    lead, extra = len(row_arrays), len(row_arrays) + len(gate_arrays)

    def hook(step, require, targets, ins, held):
        array, target, position = row_far[step]
        if array is None:
            require(target, position)
            source = targets[target]
        else:
            source = next(ref for ref, known in zip(ins, row_arrays) if known is array)
        copy = pltpu.make_async_copy(source.at[position], held[-2], held[-1])
        copy.start()
        copy.wait()

    def body(*refs):
        pieces, far, refs = refs[:extra], refs[-2], list(refs[extra:-2])
        refs[11:11] = [far[...]]
        refs[13:13] = [read_gates(pieces[lead:])]
        finish_body(*refs)

    pack = (2, 2, 2, width // 8, 4 * width + 128)
    return run(
        body,
        (
            *row_arrays, *gate_arrays, count, tok, cot, packed, prob, mixed, middle, second, soft, routes,
            row_own, gate_own, aux, *wide, *tall,
        ),
        [
            *[pl.BlockSpec(memory_space=pl.ANY)] * lead,
            *gate_specs,
            scalar_spec(),
            tile,
            tile,
            by_image(PAD, 3 * width),
            by_image(HEADS, PAD, PAD),
            tile,
            tile,
            tile,
            by_image(PAD, 128),
            by_image(PAD, 2),
            tile,
            by_image(8, PAD),
            resident((2, 8, 128)),
            resident(wide[0].shape),
            resident(wide[0].shape),
            resident(tall[0].shape),
            resident(tall[0].shape),
        ],
        [resident((total, width)), resident(pack), resident((8, 128))],
        [shape((total, width), F32), shape(pack, BF16), shape((8, 128), F32)],
        grid=(images,),
        scratch=[
            pltpu.VMEM((PAD, 3 * width), BF16),
            pltpu.VMEM((2,) + wide[0].shape, BF16),
            pltpu.VMEM((2,) + tall[0].shape, BF16),
            pltpu.VMEM((width, 3 * width), F32),
            pltpu.VMEM((width, width), F32),
            pltpu.VMEM((width, 128), F32),
            pltpu.VMEM((128, width), F32),
            pltpu.VMEM((PAD, width), BF16),
            pltpu.SemaphoreType.DMA,
        ],
        cost=pl.CostEstimate(flops=12_000_000_000, bytes_accessed=24_000_000, transcendentals=0),
        name="finish",
        traffic=traffic,
        hook=hook,
        ident=ident,
    )


def add(left, right):
    return (left.astype(F32) + right.astype(F32)).astype(BF16)


class Exchange:
    def __init__(self, send, recv):
        self.send, self.recv = send, recv

    def at(self, index, link, source, target):
        move = Move(link, lambda _: source, lambda _: target)
        return move.roles(), move.copy(None, self.send.at[index], self.recv.at[index])


def begin(make):
    roles, copy = make()
    only_if(roles[0], copy.start)


def end(make):
    roles, copy = make()
    only_if(roles[0], copy.wait_send)
    only_if(roles[1], copy.wait_recv)


def sums_everywhere(load, soft_sum, steps):
    shape = (2,) + load.shape[1:]
    links = ("core", "y", "x", "near", "inner", "outward")

    def copies(load_ref, soft_ref, total, held, got, send, recv):
        made = Exchange(send, recv)
        return [
            lambda k=k, link=link: made.at(k, link, held.at[k], held.at[k] if link == "outward" else got.at[k])
            for k, link in enumerate(links)
        ]

    def first(*refs):
        load_ref, soft_ref, _, held = refs[:4]
        held[0, 0], held[0, 1] = load_ref[0], soft_ref[0]
        begin(copies(*refs)[0])

    def stage(k):
        def action(*refs):
            held, got = refs[3:5]
            end(copies(*refs)[k - 1])
            if links[k] == "outward":

                @pl.when(((lax.axis_index("rep") // 4) % 3) > 0)
                def _():
                    held[k] = held[k - 1] + got[k - 1]

            else:
                held[k] = held[k - 1] + got[k - 1]
            begin(copies(*refs)[k])

        return action

    def last(*refs):
        end(copies(*refs)[5])
        refs[2][...] = refs[3][5]

    return Chain(
        [load, soft_sum],
        [resident(load.shape)] * 2,
        [resident(shape)],
        [jax.ShapeDtypeStruct(shape, F32)],
        [pltpu.VMEM((6,) + shape, F32), pltpu.VMEM((5,) + shape, F32)] + [pltpu.SemaphoreType.DMA((6,))] * 2,
        {"core", "y", "x", "near", "inner"},
        list(zip(steps, [first] + [stage(k) for k in range(1, 6)])) + [(0, last)],
    )


def owner_sums(pack, steps):
    shape = pack.shape[2:]

    def first(pack_ref, part, near_in, half, far_in, send, recv):
        core = lax.axis_index("rep") % 2
        Exchange(send, recv).at(0, "core", pack_ref.at[:, 1 - core], near_in)[1].start()

    def second(pack_ref, part, near_in, half, far_in, send, recv):
        core, mine = lax.axis_index("rep") % 2, lax.axis_index("fsdp")
        Exchange(send, recv).at(0, "core", pack_ref.at[:, 1 - core], near_in)[1].wait()
        half[...] = add(pack_ref[:, core], near_in[...])
        Exchange(send, recv).at(1, "y", half.at[1 - mine], far_in)[1].start()

    def last(pack_ref, part, near_in, half, far_in, send, recv):
        mine = lax.axis_index("fsdp")
        Exchange(send, recv).at(1, "y", half.at[1 - mine], far_in)[1].wait()
        part[...] = add(half[mine], far_in[...])

    return Chain(
        [pack],
        [pl.BlockSpec(pack.shape, lambda *_: (0,) * 5, pipeline_mode=pl.Buffered(1))],
        [resident(shape)],
        [jax.ShapeDtypeStruct(shape, BF16)],
        [pltpu.VMEM((2,) + shape, BF16), pltpu.VMEM((2,) + shape, BF16), pltpu.VMEM(shape, BF16)]
        + [pltpu.SemaphoreType.DMA((2,))] * 2,
        {"core", "y"},
        [(steps[0], first), (steps[1], second), (0, last)],
    )


def copy_sums(part, steps):
    shape = part.shape[1:]

    def copies(part_ref, total, x_in, held, near_in, line, inner_in, full, send, recv):
        device = lax.axis_index("rep")
        core, side = device % 2, (device // 2) % 2
        made = Exchange(send, recv)
        mine = full.at[core, side]
        plans = [
            ("x", part_ref.at[1 - side], x_in),
            ("near", held, near_in),
            ("inner", line, inner_in),
            ("outward", mine, mine),
            ("x", mine, mine),
            ("core", full.at[core], full.at[core]),
        ]
        return [lambda k=k, plan=plan: made.at(k, *plan) for k, plan in enumerate(plans)]

    def first(*refs):
        begin(copies(*refs)[0])

    def second(*refs):
        part_ref, total, x_in, held = refs[:4]
        steps = copies(*refs)
        end(steps[0])
        side = (lax.axis_index("rep") // 2) % 2
        held[...] = add(part_ref[side], x_in[...])
        begin(steps[1])

    def third(*refs):
        part_ref, total, x_in, held, near_in, line = refs[:6]
        steps = copies(*refs)
        end(steps[1])
        line[...] = add(held[...], near_in[...])
        begin(steps[2])

    def fourth(*refs):
        part_ref, total, x_in, held, near_in, line, inner_in, full = refs[:8]
        steps = copies(*refs)
        device = lax.axis_index("rep")
        middle = ((device // 4) % 3) > 0
        end(steps[2])

        @pl.when(middle)
        def _():
            full[device % 2, (device // 2) % 2] = add(line[...], inner_in[...])

        begin(steps[3])

    def fifth(*refs):
        steps = copies(*refs)
        end(steps[3])
        begin(steps[4])

    def sixth(*refs):
        steps = copies(*refs)
        end(steps[4])
        begin(steps[5])

    def last(*refs):
        total, full = refs[1], refs[7]
        end(copies(*refs)[5])
        total[...] = full[...]

    whole = (2, 2) + shape
    return Chain(
        [part],
        [resident(part.shape)],
        [resident(whole)],
        [jax.ShapeDtypeStruct(whole, BF16)],
        [pltpu.VMEM(shape, BF16)] * 5 + [pltpu.VMEM(whole, BF16)] + [pltpu.SemaphoreType.DMA((6,))] * 2,
        {"core", "x", "near", "inner"},
        list(zip(steps, (first, second, third, fourth, fifth, sixth))) + [(0, last)],
    )


def emit(count, middle, sum_own, sum_far, total):
    images, _, width = middle.shape
    far_arrays, far_specs, read_far = by_piece(sum_far, PAD, width)

    def body(count_ref, middle_ref, own_ref, *refs):
        far, (out_ref, held) = refs[:-2], refs[-2:]
        image = pl.program_id(0)
        live = (iota((PAD, 1), 0) < IMG_TOK) & (image < count_ref[0])
        both = own_ref[0].astype(F32) + read_far(far).astype(F32)
        result = jnp.where(live, 1.0, 0.0) * (middle_ref[0] + both)
        for k in range(images):

            @pl.when(image == k)
            def _():
                held[pl.ds(k * IMG_TOK, IMG_TOK), :] = result[:IMG_TOK]

        @pl.when(image == images - 1)
        def _():
            out_ref[...] = held[pl.ds(0, total), :].astype(BF16)

    tile = by_image(PAD, width)
    return run(
        body,
        (count, middle, sum_own, *far_arrays),
        [scalar_spec(), tile, tile, *far_specs],
        [resident((total, width))],
        [jax.ShapeDtypeStruct((total, width), BF16)],
        grid=(images,),
        scratch=[pltpu.VMEM((1000, width), F32)],
        cost=pl.CostEstimate(flops=2_000_000, bytes_accessed=6_000_000, transcendentals=0),
        name="emit",
    )[0][0]


def by_slice(
    tokens, cotangent, routes, image_count, capacity, norm1_gain, norm1_bias, w_qkv, bias_q, bias_v, w_out, bias_out,
    norm2_gain, norm2_bias, w_router, expert_in, expert_in_bias, expert_out, expert_out_bias,
):
    total, width = tokens.shape
    local = expert_in.shape[0]
    device = lax.axis_index("rep")
    mine = lax.axis_index("fsdp")
    core = device % 2
    wide, tall = pack_weights(
        (norm1_gain, norm1_bias, bias_q, bias_v, bias_out, norm2_gain, norm2_bias), w_qkv, w_out, w_router
    )
    (tok, cot, route, ids, load), (wide_far, tall_far), _ = prepare(
        tokens, cotangent, routes.T, image_count, capacity, wide, tall, 0
    )
    wide, tall = (wide, wide_far), (tall, tall_far)
    base = (mine * (local * CAP)).reshape(1)
    net = Network()
    net.offer("C", cot, COT_PATHS)
    idents = iter(range(1, 32))

    def staged(kernel, *args, rounds):
        traffic, plan = net.plan(*rounds)
        args = [arg(plan) if callable(arg) else arg for arg in args]
        outs, arrived, chained = kernel(*args, traffic, next(idents))
        net.land(plan, arrived)
        return (*outs, *chained)

    own, far = (0, 0, 0), (0, 0, 1)
    packed, prob, mixed, middle, second, soft, soft_sum = staged(
        front, image_count, tok, ids, route, wide, tall, rounds=evenly(FRONT_ROOM, 5, 0.68)
    )
    net.offer("S", second, ROW_PATHS)

    def sender(block):
        return net.block("S", block), net.block("C", block)

    def senders(blocks):
        return lambda plan: [(net.find(plan, "S", block), net.find(plan, "C", block)) for block in blocks]

    pair = staged(
        gather, base, local, senders([own, far]), [0, None, None, None, None, 1],
        rounds=(PAIR_ROOM, list(range(8)), [0.0, 0.45, 0.9, 1.9, 2.9, 3.9, 5.0, 6.0]),
    )
    made_own, made_far, back_own, back_far, sums = staged(
        expert_layer, pair, expert_in, expert_in_bias, expert_out, expert_out_bias,
        sums_everywhere(load, soft_sum, (0, 2, 5, 8, 11, 13)),
        rounds=evenly(EXPERT_ROOM, 16, 0.7, 2),
    )
    sum_far, drow_far, dgate_far = staged(
        combine, base, *sender(far), made_far, back_far, rounds=evenly(2, 5, 0.4, 2)
    )
    net.offer("D", drow_far, FAR_FIRST)
    net.offer("G", dgate_far, FAR_FIRST, 0)
    net.offer("M", sum_far, FAR_LAST)
    sum_own, drow_own, dgate_own = staged(
        combine, base, *sender(own), made_own, back_own, rounds=evenly(OWN_ROOM, 5, 0.4)
    )
    grad_tokens, pack, loss = staged(
        finish, image_count, tok, cot, (packed, prob, mixed, middle, second, soft), route, drow_own,
        lambda plan: net.find(plan, "D", far), dgate_own, net.block("G", far), sums, wide, tall, total,
        rounds=evenly(FINISH_ROOM, 5, 1.5),
    )
    blocks = [block for block in COT_PATHS if block != far]
    count = 2 * len(blocks) + 2
    traffic, plan = net.plan(LAST_ROOM, list(range(count)), [LAST_ROOM * k / count for k in range(count)])
    blocks.sort(key=lambda block: net.landing(plan, block))
    outs, arrived, (part,) = gather(
        base, local, senders(blocks)(plan), list(range(len(blocks))) + [None, None],
        traffic, next(idents), owner_sums(pack, (0, 6)),
    )
    net.land(plan, arrived)
    slots = [pair, outs]
    outputs = emit(image_count, middle, sum_own, net.block("M", far), total)
    row_slots = [pair[0] for pair in slots]
    grad_slots = [pair[1] for pair in slots]
    (keep_in, send_in, keep_out, send_out, d_bias, d_out_bias), _, (owned,) = slice_grads(
        row_slots, grad_slots, expert_in, expert_in_bias, expert_out, copy_sums(part, (0, 3, 6, 9, 12, 15)), next(idents)
    )
    owned = owned.reshape(width // 2, -1).astype(F32)
    swap = [(i, i ^ 1) for i in range(16)]
    got_in, got_out, got_bias, got_out_bias = (
        lax.ppermute(v, "rep", swap) for v in (send_in, send_out, d_bias, d_out_bias)
    )
    bias = (d_bias + got_bias)[:, 0]
    out_bias = (d_out_bias + got_out_bias)[:, 0]
    half = bias.shape[1] // 2
    piece = width // 16
    expert_grads = (
        keep_in + got_in.astype(F32),
        lax.dynamic_slice_in_dim(bias, core * half, half, axis=1),
        keep_out + got_out.astype(F32),
        lax.dynamic_slice_in_dim(out_bias, device * piece, piece, axis=1),
    )

    balance_loss = loss[0, 0]
    lines = jnp.transpose(owned[:, 4 * width + EXPERTS : 4 * width + EXPERTS + 8])
    owned = (
        lines[0],
        lines[1],
        owned[:, : 3 * width],
        lines[2],
        lines[3],
        owned[:, 3 * width : 4 * width],
        lines[4],
        lines[5],
        lines[6],
        owned[:, 4 * width : 4 * width + EXPERTS],
    )
    return (outputs, grad_tokens, balance_loss) + owned + expert_grads


def solution(mesh):
    in_specs = (
        P(("rep", "fsdp"), None),
        P(("rep", "fsdp"), None),
        P(("rep", "fsdp"), None),
        P(("rep", "fsdp")),
        P(("rep", "fsdp")),
        P("fsdp"),
        P("fsdp"),
        P("fsdp", None),
        P("fsdp"),
        P("fsdp"),
        P("fsdp", None),
        P("fsdp"),
        P("fsdp"),
        P("fsdp"),
        P("fsdp", None),
        P("fsdp", None, None),
        P("fsdp", None),
        P("fsdp", None, None),
        P("fsdp", None),
    )
    out_specs = (
        P(("rep", "fsdp"), None),
        P(("rep", "fsdp"), None),
        P(),
        P("fsdp"),
        P("fsdp"),
        P("fsdp", None),
        P("fsdp"),
        P("fsdp"),
        P("fsdp", None),
        P("fsdp"),
        P("fsdp"),
        P("fsdp"),
        P("fsdp", None),
        P("fsdp", None, "rep"),
        P("fsdp", "rep"),
        P("fsdp", "rep", None),
        P("fsdp", "rep"),
    )
    program = by_slice if mesh.shape["rep"] == 16 and mesh.shape["fsdp"] == 2 else shards
    return jax.shard_map(program, mesh=mesh, in_specs=in_specs, out_specs=out_specs, check_vma=False)
```
